32 devices in a mesh: seq: 8 (over z, core), dp: 4 (over y, x).
Axes of the slice: x: 2, y: 2, z: 4, core: 2. Of those that a mesh axis runs over, the one named last changes fastest.
Arguments:
- tokens: float32 [4, 4096, 768], P('dp', 'seq'), as said below
- segment_lens: int32 [4, 64], P('dp', 'seq'), may hold values from 16 to 64, as said below
- query_weight: float32 [768, 768], replicated, may hold values from -0.375 to 0.375
- query_bias: float32 [768], replicated, may hold values from -3 to 3
- key_weight: float32 [768, 768], replicated, may hold values from -0.375 to 0.375
- value_weight: float32 [768, 768], replicated, may hold values from -0.21875 to 0.21875
- value_bias: float32 [768], replicated, may hold values from -3 to 3
- conv_taps: float32 [33, 12], replicated, may hold values from -0.3 to 0.3
- output_weight: float32 [768, 768], replicated, may hold values from -0.5 to 0.5
- output_bias: float32 [768], replicated, may hold values from -2 to 2
- first_gain: float32 [768], replicated, may hold values from 0.25 to 1.75
- first_bias: float32 [768], replicated, may hold values from -2 to 2
- inner_weight: float32 [768, 3072], replicated, may hold values from -0.21875 to 0.21875
- inner_bias: float32 [3072], replicated, may hold values from -3 to 3
- outer_weight: float32 [3072, 768], replicated, may hold values from -0.15625 to 0.15625
- outer_bias: float32 [768], replicated, may hold values from -2 to 2
- second_gain: float32 [768], replicated, may hold values from 0.25 to 1.75
- second_bias: float32 [768], replicated, may hold values from -2 to 2
- cotangent: float32 [4, 4096, 768], P('dp', 'seq'), may hold values from -6 to 6
Outputs:
- layer_out: float32 [4, 4096, 768], P('dp', 'seq')
- input_grad: float32 [4, 4096, 768], P('dp', 'seq')
- grad_query_weight: float32 [768, 768], replicated
- grad_query_bias: float32 [768], replicated
- grad_key_weight: float32 [768, 768], replicated
- grad_value_weight: float32 [768, 768], replicated
- grad_value_bias: float32 [768], replicated
- grad_conv_taps: float32 [33, 12], replicated
- grad_output_weight: float32 [768, 768], replicated
- grad_output_bias: float32 [768], replicated
- grad_first_gain: float32 [768], replicated
- grad_first_bias: float32 [768], replicated
- grad_inner_weight: float32 [768, 3072], replicated
- grad_inner_bias: float32 [3072], replicated
- grad_outer_weight: float32 [3072, 768], replicated
- grad_outer_bias: float32 [768], replicated
- grad_second_gain: float32 [768], replicated
- grad_second_bias: float32 [768], replicated
The draws below stay inside these ranges and needn't reach their ends.
Inputs may be any that keep to these rules, and one draw needn't show every extreme that they name: `segment_lens`: each landmark segment holds 16 to 64 tokens, and every sequence has a segment of exactly 64. `tokens`: entries at padding slots take no part in any output.
All inputs are finite; a program needn't handle non-finite values.
Results may differ from the reference program's by a relative error of at most 0.0003.
Values sent between devices are 32-bit elements; how exact they have to be, the bound alone decides.
A program may use at most 320 MiB of HBM per device.

```python
import jax
import jax.numpy as jnp
from jax import lax

D = 768
HEADS = 12
DH = 64
FF = 3072
LM = 64
CONV = 33
NEWTON = 6
SEGCAP = 64
LM_DEV = 8
SLOTS = 4096
SEQS = 4


def segment_lengths(key):
    drawn = jax.random.randint(jax.random.fold_in(key, 11), (SEQS, LM), SEGCAP // 4, SEGCAP + 1)
    chosen = jax.random.randint(jax.random.fold_in(key, 12), (SEQS, 1), 0, LM)
    return jnp.where(jnp.arange(LM)[None, :] == chosen, SEGCAP, drawn).astype(jnp.int32)


def draw_segment_lens(key, part):
    return segment_lengths(key)


def pick_rows(lookup, indices):
    return lookup[indices]


def draw_tokens(key, part):
    lengths = segment_lengths(key)
    blocks = LM // LM_DEV
    segment_ends = jnp.cumsum(lengths.reshape(SEQS, blocks, LM_DEV), axis=2)
    slot_ids = jnp.arange(LM_DEV * SEGCAP)
    local_seg = jnp.sum((slot_ids[None, None, :, None] >= segment_ends[:, :, None, :]).astype(jnp.int32), axis=3)
    landmark = jnp.minimum(local_seg, LM_DEV - 1) + LM_DEV * jnp.arange(blocks)[None, :, None]
    landmark = landmark.reshape(SEQS, SLOTS)
    common = jax.random.normal(jax.random.fold_in(key, 21), (SEQS, LM, D))
    noise_part = 0.6 * jax.random.normal(jax.random.fold_in(key, 22), (SEQS, SLOTS, D))
    return (0.8 * jax.vmap(pick_rows)(common, landmark) + noise_part).astype(jnp.float32)


def level_of(key, extent, cuts, low, high):
    def one(position, parts):
        draws = jax.random.uniform(jax.random.fold_in(jax.random.fold_in(key, 6), position), (parts,), jnp.float32, low / len(cuts), high / len(cuts))
        return jnp.repeat(jnp.exp(draws), extent[position] // parts).reshape((-1,) + (1,) * (len(extent) - position - 1))

    gain = one(*cuts[0])
    for cut in cuts[1:]:
        gain = gain * one(*cut)
    return gain


def normal_values(stream_key, shape, deviation, reach, pieces=(), held_as=jnp.bfloat16):
    gain = level_of(stream_key, shape, pieces, -0.22, 0.18) if pieces else 1.0
    array = jax.random.normal(stream_key, shape, jnp.float32) * deviation * gain
    return jnp.minimum(jnp.maximum(array, -reach), reach).astype(held_as)


def setup_inputs(seed: int = 0) -> dict:
    streams_of = jax.random.split(jax.random.key(seed), 20)
    tokens = draw_tokens(jax.random.fold_in(streams_of[19], 71), 0)
    segment_lens = draw_segment_lens(jax.random.fold_in(streams_of[19], 71), 0)
    query_weight = normal_values(streams_of[2], (D, D), (D // 3) ** -0.5, 0.375, (), jnp.float32)
    query_bias = normal_values(streams_of[3], (D,), 0.5, 3.0, (), jnp.float32)
    key_weight = normal_values(streams_of[4], (D, D), (D // 3) ** -0.5, 0.375, (), jnp.float32)
    value_weight = normal_values(streams_of[5], (D, D), D ** -0.5, 0.21875, (), jnp.float32)
    value_bias = normal_values(streams_of[6], (D,), 0.5, 3.0, (), jnp.float32)
    conv_taps = normal_values(streams_of[7], (CONV, HEADS), 0.06, 0.3, (), jnp.float32)
    output_weight = normal_values(streams_of[8], (D, D), (D // 6) ** -0.5, 0.5, (), jnp.float32)
    output_bias = normal_values(streams_of[9], (D,), 0.3, 2.0, (), jnp.float32)
    first_gain = jnp.clip(1.0 + 0.15 * jax.random.normal(streams_of[10], (D,), jnp.float32), 0.25, 1.75)
    first_bias = normal_values(streams_of[11], (D,), 0.3, 2.0, (), jnp.float32)
    inner_weight = normal_values(streams_of[12], (D, FF), D ** -0.5, 0.21875, (), jnp.float32)
    inner_bias = normal_values(streams_of[13], (FF,), 0.5, 3.0, (), jnp.float32)
    outer_weight = normal_values(streams_of[14], (FF, D), (FF // 2) ** -0.5, 0.15625, (), jnp.float32)
    outer_bias = normal_values(streams_of[15], (D,), 0.3, 2.0, (), jnp.float32)
    second_gain = jnp.clip(1.0 + 0.15 * jax.random.normal(streams_of[16], (D,), jnp.float32), 0.25, 1.75)
    second_bias = normal_values(streams_of[17], (D,), 0.3, 2.0, (), jnp.float32)
    cotangent = normal_values(streams_of[18], (SEQS, SLOTS, D), 1.0, 6.0, ((0, 4), (1, 8)), jnp.float32)
    return dict(tokens=tokens, segment_lens=segment_lens, query_weight=query_weight, query_bias=query_bias, key_weight=key_weight, value_weight=value_weight, value_bias=value_bias, conv_taps=conv_taps, output_weight=output_weight, output_bias=output_bias, first_gain=first_gain, first_bias=first_bias, inner_weight=inner_weight, inner_bias=inner_bias, outer_weight=outer_weight, outer_bias=outer_bias, second_gain=second_gain, second_bias=second_bias, cotangent=cotangent)


@jax.custom_vjp
def low(v):
    return lax.optimization_barrier(v.astype(jnp.bfloat16)).astype(jnp.float32)

@jax.custom_vjp
def low_back(v):
    return v

def low_keep(v):
    return (low(v), None)

def low_pass(kept, grad):
    return (grad,)

def back_keep(v):
    return (v, None)

def back_low(kept, grad):
    return (low(grad),)
low.defvjp(low_keep, low_pass)
low_back.defvjp(back_keep, back_low)
highest = lax.Precision.HIGHEST
norm_eps = 1e-05
root_half = 0.7071067811865476
masked_score = -1e+30

def matmul(left, right):
    return jnp.dot(left, right, precision=highest, preferred_element_type=jnp.float32)

def contract(form, left, right):
    return jnp.einsum(form, left, right, precision=highest, preferred_element_type=jnp.float32)

def layer_norm(summed, scale_gain, offset):
    centered = summed - lax.optimization_barrier(jnp.mean(summed, axis=-1, keepdims=True))
    spread = lax.optimization_barrier(jnp.mean(centered * centered, axis=-1, keepdims=True))
    return centered * lax.rsqrt(spread + norm_eps) * scale_gain + offset

def normalize_rows(scores):
    top_score = lax.optimization_barrier(jnp.max(scores, axis=-1, keepdims=True))
    raised = jnp.exp(scores - top_score)
    return raised / lax.optimization_barrier(jnp.sum(raised, axis=-1, keepdims=True))

def newton_inverse(kernel):
    colsum = lax.optimization_barrier(jnp.sum(kernel, axis=-2))
    scaling = jnp.sqrt(lax.optimization_barrier(jnp.sum(colsum * colsum, axis=-1)))
    iterate = jnp.swapaxes(kernel, -1, -2) / scaling[..., None, None]
    identity = jnp.eye(kernel.shape[-1], dtype=jnp.float32)
    for newton_step in range(NEWTON):
        product = contract('...ij,...jk->...ik', kernel, iterate)
        factor = 7.0 * identity - product
        factor = 15.0 * identity - contract('...ij,...jk->...ik', product, factor)
        factor = 13.0 * identity - contract('...ij,...jk->...ik', product, factor)
        iterate = 0.25 * contract('...ij,...jk->...ik', iterate, factor)
    return iterate

def sequence_forward(tokens, segment_lens, weights):
    query_weight, query_bias, key_weight, value_weight, value_bias, conv_taps, output_weight, output_bias, first_gain, first_bias, inner_weight, inner_bias, outer_weight, outer_bias, second_gain, second_bias = weights
    rim_width = (CONV - 1) // 2
    score_scale = DH ** (-0.5)
    block_len = LM_DEV * SEGCAP
    grouped = segment_lens.reshape(LM // LM_DEV, LM_DEV).astype(jnp.int32)
    block_count = lax.optimization_barrier(jnp.sum(grouped, axis=1)).astype(jnp.int32)
    block_start = (jnp.cumsum(block_count) - block_count).astype(jnp.int32)
    segment_ends = jnp.cumsum(grouped, axis=1).astype(jnp.int32)
    slot_ids = jnp.arange(SLOTS, dtype=jnp.int32)
    owner_block = (slot_ids // block_len).astype(jnp.int32)
    offsets = (slot_ids % block_len).astype(jnp.int32)
    valid = offsets < block_count[owner_block]
    local_seg = lax.optimization_barrier(jnp.sum((offsets[:, None] >= segment_ends[owner_block]).astype(jnp.int32), axis=1)).astype(jnp.int32)
    landmark = (owner_block * LM_DEV + local_seg).astype(jnp.int32)
    positions = (block_start[owner_block] + offsets).astype(jnp.int32)
    member = ((landmark[:, None] == jnp.arange(LM, dtype=jnp.int32)[None, :]) & valid[:, None]).astype(jnp.float32)
    slot_mask = valid.astype(jnp.float32)[:, None]
    inverse_len = 1.0 / segment_lens.astype(jnp.float32)
    queries = matmul(tokens, query_weight) + query_bias
    key_rows = matmul(tokens, key_weight)
    values = matmul(tokens, value_weight) + value_bias
    query_land = matmul(member.T, queries) * inverse_len[:, None]
    key_land = matmul(member.T, key_rows) * inverse_len[:, None]
    query_heads = queries.reshape(SLOTS, HEADS, DH)
    key_heads = key_rows.reshape(SLOTS, HEADS, DH)
    value_heads = values.reshape(SLOTS, HEADS, DH)
    land_query = query_land.reshape(LM, HEADS, DH)
    land_key = key_land.reshape(LM, HEADS, DH)
    near = normalize_rows(contract('thd,jhd->htj', query_heads, land_key) * score_scale)
    core = normalize_rows(contract('ihd,jhd->hij', land_query, land_key) * score_scale)
    inverse = newton_inverse(core)
    far_scores = contract('ihd,thd->hit', land_query, key_heads) * score_scale
    far = normalize_rows(jnp.where(valid[None, None, :], far_scores, masked_score))
    mixed = contract('hit,thd->hid', far, value_heads)
    blend = contract('hij,hjd->hid', inverse, mixed)
    attention = contract('htj,hjd->thd', near, blend).reshape(SLOTS, D)
    target = jnp.where(valid, positions + rim_width, SLOTS + 2 * rim_width).astype(jnp.int32)
    compact = jnp.zeros((SLOTS + 2 * rim_width + 1, D), jnp.float32).at[target].add(values * slot_mask)
    feature_taps = jnp.repeat(conv_taps, DH, axis=1)
    running = feature_taps[0] * compact[0:SLOTS]
    for offset in range(1, CONV):
        running = running + feature_taps[offset] * compact[offset:offset + SLOTS]
    conv_out = running[jnp.where(valid, positions, 0).astype(jnp.int32)]
    context = attention + conv_out
    hidden_one = layer_norm(tokens + (matmul(context, output_weight) + output_bias), first_gain, first_bias)
    pre_act = matmul(hidden_one, inner_weight) + inner_bias
    activated = 0.5 * pre_act * (1.0 + lax.erf(pre_act * root_half))
    branch = matmul(activated, outer_weight) + outer_bias
    return layer_norm(hidden_one + branch, second_gain, second_bias) * slot_mask

def reference(tokens, segment_lens, query_weight, query_bias, key_weight, value_weight, value_bias, conv_taps, output_weight, output_bias, first_gain, first_bias, inner_weight, inner_bias, outer_weight, outer_bias, second_gain, second_bias, cotangent):
    weights = (query_weight, query_bias, key_weight, value_weight, value_bias, conv_taps, output_weight, output_bias, first_gain, first_bias, inner_weight, inner_bias, outer_weight, outer_bias, second_gain, second_bias)

    def forward(source, params):

        def per_sequence(sequence_pair):
            return sequence_forward(sequence_pair[0], sequence_pair[1], params)
        return lax.map(jax.checkpoint(per_sequence), (source, segment_lens))
    layer_out, pullback = jax.vjp(forward, tokens, weights)
    grad_tokens, grad_weights = pullback(cotangent)
    return (layer_out, grad_tokens, grad_weights[0], grad_weights[1], grad_weights[2], grad_weights[3], grad_weights[4], grad_weights[5], grad_weights[6], grad_weights[7], grad_weights[8], grad_weights[9], grad_weights[10], grad_weights[11], grad_weights[12], grad_weights[13], grad_weights[14], grad_weights[15])
```

```python
from functools import partial
import math

import jax
import jax.numpy as jnp
from jax import lax
from jax.experimental import pallas as pl
from jax.experimental.pallas import tpu as pltpu
from jax.sharding import PartitionSpec as P

HEADS = 12
DH = 64
CONV = 33
NEWTON = 6
RIM = (CONV - 1) // 2
LANES = 128
PAIRS = HEADS * DH // LANES
QUAD = 256
SCALE = DH ** (-0.5)
EPS = 1e-05
ROOT_HALF = 0.7071067811865476
INV_ROOT_TAU = 0.3989422804014327
MASKED = -1e30
f32 = jnp.float32
HI = lax.Precision.HIGH
TOP = lax.Precision.HIGHEST
MESH = pl.DeviceIdType.MESH
VMEM_CAP = 60 << 20


def _dg(a, b, ca, cb, prec):
    return lax.dot_general(
        a, b, (((ca,), (cb,)), ((), ())), precision=prec, preferred_element_type=f32
    )


def mm(a, b, prec=HI):
    return _dg(a, b, 1, 0, prec)


def mm_t(a, b, prec=HI):
    return _dg(a, b, 1, 1, prec)


def t_mm(a, b, prec=HI):
    return _dg(a, b, 0, 0, prec)


def head_mask(size):
    row = lax.broadcasted_iota(jnp.int32, (size, size), 0) >> 6
    col = lax.broadcasted_iota(jnp.int32, (size, size), 1) >> 6
    return row == col


def spread(rows, mask):
    return jnp.where(mask, jnp.concatenate([rows] * (mask.shape[0] // DH), axis=0), 0.0)


def fold(square, mask):
    kept = jnp.where(mask, square, 0.0)
    total = kept[:DH]
    for at in range(DH, mask.shape[0], DH):
        total = total + kept[at : at + DH]
    return total


def seg_ends(lens_ref, count):
    ends = []
    total = 0
    for j in range(count):
        total = total + lens_ref[0, j]
        ends.append(total)
    return ends


def member_rows(ends, slots):
    shape = (len(ends), slots)
    row = lax.broadcasted_iota(jnp.int32, shape, 0)
    col = lax.broadcasted_iota(jnp.int32, shape, 1)
    low = jnp.zeros(shape, jnp.int32)
    high = jnp.zeros(shape, jnp.int32)
    before = 0
    for j, end in enumerate(ends):
        low = jnp.where(row == j, before, low)
        high = jnp.where(row == j, end, high)
        before = end
    return jnp.where((col >= low) & (col < high), 1.0, 0.0)


def inverse_lens(lens_ref, count):
    row = lax.broadcasted_iota(jnp.int32, (count, 1), 0)
    out = jnp.zeros((count, 1), f32)
    for j in range(count):
        out = jnp.where(row == j, lens_ref[0, j].astype(f32), out)
    return 1.0 / out


def valid_rows(count, slots):
    return lax.broadcasted_iota(jnp.int32, (slots, 1), 0) < count


def rims_of(matrix, count):
    slots = matrix.shape[0]
    row = lax.broadcasted_iota(jnp.int32, (2 * RIM, slots), 0)
    col = lax.broadcasted_iota(jnp.int32, (2 * RIM, slots), 1)
    want = jnp.where(row < RIM, row, row - 2 * RIM + count)
    return mm(jnp.where(col == want, 1.0, 0.0), matrix)


def fill_extended(ext_ref, middle, left, right, count):
    slots = middle.shape[0]
    ext_ref[0:RIM, :] = left
    ext_ref[RIM : RIM + slots, :] = middle
    tail = ext_ref.shape[0] - RIM - slots
    ext_ref[RIM + slots :, :] = jnp.zeros((tail, middle.shape[1]), f32)
    rows = slots + RIM
    row = lax.broadcasted_iota(jnp.int32, (rows, RIM), 0)
    col = lax.broadcasted_iota(jnp.int32, (rows, RIM), 1)
    put = jnp.where(row == col + count, 1.0, 0.0)
    ext_ref[RIM : RIM + rows, :] += mm(put, right)


CONV_ROWS = 64


def shifted(ext_ref, r0, l0):
    slab = ext_ref[pl.ds(r0, CONV_ROWS + 40), pl.ds(l0, LANES)]
    for b in range(8):
        moved = slab[b : b + CONV_ROWS + 32]
        for a in range(5):
            if 8 * a + b < CONV:
                yield 8 * a + b, moved[8 * a : 8 * a + CONV_ROWS]


def conv_into(out_ref, ext_ref, taps_ref, slots, flip, add):
    def block(i, carry):
        r0 = pl.multiple_of((i // PAIRS) * CONV_ROWS, CONV_ROWS)
        l0 = pl.multiple_of((i % PAIRS) * LANES, LANES)
        acc = jnp.zeros((CONV_ROWS, LANES), f32)
        for c, part in shifted(ext_ref, r0, l0):
            at = CONV - 1 - c if flip else c
            acc = acc + taps_ref[at : at + 1, pl.ds(l0, LANES)] * part
        here = (pl.ds(r0, CONV_ROWS), pl.ds(l0, LANES))
        if add:
            out_ref[here] += acc
        else:
            out_ref[here] = acc
        return carry

    lax.fori_loop(0, (slots // CONV_ROWS) * PAIRS, block, 0)


def taps_grad_into(scr_ref, grad_ref, ext_ref, slots):
    scr_ref[...] = jnp.zeros_like(scr_ref)

    def block(i, carry):
        r0 = pl.multiple_of((i // PAIRS) * CONV_ROWS, CONV_ROWS)
        l0 = pl.multiple_of((i % PAIRS) * LANES, LANES)
        grad = grad_ref[pl.ds(r0, CONV_ROWS), pl.ds(l0, LANES)]
        for c, part in shifted(ext_ref, r0, l0):
            prod = grad * part
            total = prod[0:8]
            for at in range(8, CONV_ROWS, 8):
                total = total + prod[at : at + 8]
            scr_ref[c, :, pl.ds(l0, LANES)] += total
        return carry

    lax.fori_loop(0, (slots // CONV_ROWS) * PAIRS, block, 0)


def whole(shape=None):
    return pl.BlockSpec(memory_space=pltpu.VMEM)


def smem():
    return pl.BlockSpec(memory_space=pltpu.SMEM)


def params(**more):
    return pltpu.CompilerParams(vmem_limit_bytes=VMEM_CAP, **more)


def shape(*dims):
    return jax.ShapeDtypeStruct(dims, f32)


def project_kernel(
    lens_ref, x_ref, wq_ref, wk_ref, wv_ref, bq_ref, bv_ref,
    q_ref, k_ref, v_ref, land_ref, rim_ref,
):
    slots = x_ref.shape[0]
    segs = land_ref.shape[1]
    ends = seg_ends(lens_ref, segs)
    member = member_rows(ends, slots)
    inv = inverse_lens(lens_ref, segs)
    x = x_ref[...]
    q = mm(x, wq_ref[...]) + bq_ref[...][None, :]
    k = mm(x, wk_ref[...])
    v = mm(x, wv_ref[...]) + bv_ref[...][None, :]
    v = jnp.where(valid_rows(ends[-1], slots), v, 0.0)
    q_ref[...] = q
    k_ref[...] = k
    v_ref[...] = v
    land_ref[0] = mm(member, q) * inv
    land_ref[1] = mm(member, k) * inv
    rim_ref[...] = rims_of(v, ends[-1])


def project(lens, x, wq, wk, wv, bq, bv):
    slots, width = x.shape
    segs = lens.shape[1]
    col = 256
    wspec = pl.BlockSpec((width, col), lambda i: (0, i))
    bspec = pl.BlockSpec((col,), lambda i: (i,))
    ospec = pl.BlockSpec((slots, col), lambda i: (0, i))
    return pl.pallas_call(
        project_kernel,
        grid=(width // col,),
        in_specs=[smem(), pl.BlockSpec((slots, width), lambda i: (0, 0)), wspec, wspec, wspec, bspec, bspec],
        out_specs=[
            ospec, ospec, ospec,
            pl.BlockSpec((2, segs, col), lambda i: (0, 0, i)),
            pl.BlockSpec((2 * RIM, col), lambda i: (0, i)),
        ],
        out_shape=[
            shape(slots, width), shape(slots, width), shape(slots, width),
            shape(2, segs, width), shape(2 * RIM, width),
        ],
        compiler_params=params(),
        name="project",
    )(lens, x, wq, wk, wv, bq, bv)


def greet_all(n):
    me = lax.axis_index("seq")
    barrier = pltpu.get_barrier_semaphore()
    for d in range(1, n):
        pl.semaphore_signal(
            barrier, inc=1, device_id={"seq": lax.rem(me + d, n)}, device_id_type=MESH
        )
    pl.semaphore_wait(barrier, n - 1)
    return me


def to_seq(src, dst, send, recv, target):
    return pltpu.make_async_remote_copy(
        src, dst, send, recv, device_id={"seq": target}, device_id_type=MESH
    )


def rim_copies(n, me, rim_ref, left_ref, right_ref, rsend, rrecv):
    up = to_seq(rim_ref.at[pl.ds(RIM, RIM)], left_ref, rsend.at[0], rrecv.at[0], lax.rem(me + 1, n))
    down = to_seq(rim_ref.at[pl.ds(0, RIM)], right_ref, rsend.at[1], rrecv.at[1], lax.rem(me + n - 1, n))
    return up, down


def rim_start(n, me, up, down, left_ref, right_ref):
    @pl.when(me < n - 1)
    def _():
        up.start()

    @pl.when(me > 0)
    def _():
        down.start()

    @pl.when(me == 0)
    def _():
        left_ref[...] = jnp.zeros_like(left_ref)

    @pl.when(me == n - 1)
    def _():
        right_ref[...] = jnp.zeros_like(right_ref)


def rim_wait(n, me, up, down):
    @pl.when(me > 0)
    def _():
        up.wait_recv()
        down.wait_send()

    @pl.when(me < n - 1)
    def _():
        down.wait_recv()
        up.wait_send()


def land_exchange_kernel(
    n, mine_ref, rim_ref, all_ref, left_ref, right_ref, send, recv, rsend, rrecv
):
    me = greet_all(n)
    up, down = rim_copies(n, me, rim_ref, left_ref, right_ref, rsend, rrecv)
    copies = []
    for d in range(1, n):
        copy = to_seq(
            mine_ref, all_ref.at[me], send.at[d], recv.at[me], lax.rem(me + d, n)
        )
        copy.start()
        copies.append(copy)
    rim_start(n, me, up, down, left_ref, right_ref)
    all_ref[me] = mine_ref[...]
    for d in range(1, n):
        source = lax.rem(me + d, n)
        to_seq(mine_ref, all_ref.at[source], send.at[d], recv.at[source], source).wait_recv()
    rim_wait(n, me, up, down)
    for copy in copies:
        copy.wait_send()


def land_exchange(n, mine, rim):
    _, segs, width = mine.shape
    dma = pltpu.SemaphoreType.DMA
    return pl.pallas_call(
        partial(land_exchange_kernel, n),
        in_specs=[whole()] * 2,
        out_specs=[whole()] * 3,
        out_shape=[shape(n, 2, segs, width), shape(RIM, width), shape(RIM, width)],
        scratch_shapes=[dma((n,)), dma((n,)), dma((2,)), dma((2,))],
        compiler_params=params(collective_id=1, has_side_effects=True),
        name="land_exchange",
    )(mine, rim)


MSG = DH + 8


def eye(size):
    row = lax.broadcasted_iota(jnp.int32, (size, size), 0)
    col = lax.broadcasted_iota(jnp.int32, (size, size), 1)
    return jnp.where(row == col, 1.0, 0.0)


def pair_sums(row):
    lane = lax.broadcasted_iota(jnp.int32, row.shape, 1)
    first = jnp.sum(jnp.where(lane < DH, row, 0.0), axis=1, keepdims=True)
    second = jnp.sum(jnp.where(lane < DH, 0.0, row), axis=1, keepdims=True)
    return jnp.where(lane < DH, first, second)


def core_of(query, key, mask):
    scores = jnp.where(mask, mm_t(query, key, TOP) * SCALE, MASKED)
    raised = jnp.exp(scores - jnp.max(scores, axis=1, keepdims=True))
    return raised / jnp.sum(raised, axis=1, keepdims=True)


def far_exchange_kernel(
    n, f_ref, ql_ref, kl_ref, b_ref, core_ref, zs_ref, ps_ref, rs_ref, qs_ref, mx_ref,
    land, s1, r1, s2, r2,
):
    me = greet_all(n)
    for p in range(PAIRS):

        @pl.when(me != p)
        def _(p=p):
            to_seq(f_ref.at[p], land.at[me], s1.at[p], r1.at[me], p).start()

    @pl.when(me < PAIRS)
    def _():
        mask = head_mask(LANES)
        lanes = pl.ds(pl.multiple_of(me * LANES, LANES), LANES)
        query = spread(ql_ref[:, lanes], mask)
        key = spread(kl_ref[:, lanes], mask)
        core = core_of(query, key, mask)
        core_ref[...] = core
        colsum = jnp.sum(core, axis=0, keepdims=True)
        sigma = jnp.sqrt(pair_sums(colsum * colsum))
        z = core.T / sigma
        unit = eye(LANES)
        for step in range(NEWTON):
            zs_ref[step] = z
            prod = mm(core, z, TOP)
            ps_ref[step] = prod
            r = 15.0 * unit - mm(prod, 7.0 * unit - prod, TOP)
            rs_ref[step] = r
            q = 13.0 * unit - mm(prod, r, TOP)
            qs_ref[step] = q
            z = 0.25 * mm(z, q, TOP)
        zs_ref[NEWTON] = z
        land[me] = f_ref[me]
        for s in range(n):

            @pl.when(me != s)
            def _(s=s):
                to_seq(f_ref.at[0], land.at[s], s1.at[0], r1.at[s], s).wait_recv()

        top = land[0][DH : DH + 1]
        for s in range(1, n):
            top = jnp.maximum(top, land[s][DH : DH + 1])
        total = jnp.zeros_like(top)
        mixed = jnp.zeros((DH, LANES), f32)
        for s in range(n):
            part = land[s]
            factor = jnp.exp(part[DH : DH + 1] - top)
            total = total + part[DH + 1 : DH + 2] * factor
            mixed = mixed + part[:DH] * factor
        mixed = mixed / total
        mx_ref[...] = mixed
        b_ref[me, 0:DH, :] = mm_t(mixed, z, TOP)
        pad = jnp.zeros((MSG - DH - 2, LANES), f32)
        b_ref[me, DH:MSG, :] = jnp.concatenate([top, total, pad], axis=0)
        for t in range(n):

            @pl.when(me != t)
            def _(t=t):
                to_seq(b_ref.at[me], b_ref.at[me], s2.at[t], r2.at[me], t).start()

    for p in range(PAIRS):

        @pl.when(me != p)
        def _(p=p):
            to_seq(b_ref.at[p], b_ref.at[p], s2.at[p], r2.at[p], p).wait_recv()
            to_seq(f_ref.at[p], land.at[me], s1.at[p], r1.at[me], p).wait_send()

    @pl.when(me < PAIRS)
    def _():
        for t in range(n):

            @pl.when(me != t)
            def _(t=t):
                to_seq(b_ref.at[me], b_ref.at[me], s2.at[t], r2.at[me], t).wait_send()


def far_exchange(n, parts, ql, kl):
    dma = pltpu.SemaphoreType.DMA
    square = (LANES, LANES)
    return pl.pallas_call(
        partial(far_exchange_kernel, n),
        in_specs=[whole()] * 3,
        out_specs=[whole()] * 7,
        out_shape=[
            shape(PAIRS, MSG, LANES), shape(*square), shape(NEWTON + 1, *square),
            shape(NEWTON, *square), shape(NEWTON, *square), shape(NEWTON, *square),
            shape(DH, LANES),
        ],
        scratch_shapes=[pltpu.VMEM((n, MSG, LANES), f32), dma((PAIRS,)), dma((n,)), dma((n,)), dma((n,))],
        compiler_params=params(collective_id=2, has_side_effects=True),
        name="far_exchange",
    )(parts, ql, kl)


def blend_exchange_kernel(
    n, g_ref, rim_ref, ql_ref, kl_ref, core_ref, zs_ref, ps_ref, rs_ref, qs_ref, mx_ref,
    c_ref, left_ref, right_ref, gl_ref,
    land, s1, r1, s2, r2, rsend, rrecv,
):
    me = greet_all(n)
    for p in range(PAIRS):

        @pl.when(me != p)
        def _(p=p):
            to_seq(g_ref.at[p], land.at[me], s1.at[p], r1.at[me], p).start()

    up, down = rim_copies(n, me, rim_ref, left_ref, right_ref, rsend, rrecv)
    rim_start(n, me, up, down, left_ref, right_ref)

    @pl.when(me >= PAIRS)
    def _():
        gl_ref[...] = jnp.zeros_like(gl_ref)

    @pl.when(me < PAIRS)
    def _():
        mask = head_mask(LANES)
        land[me] = g_ref[me]
        for s in range(n):

            @pl.when(me != s)
            def _(s=s):
                to_seq(g_ref.at[0], land.at[s], s1.at[0], r1.at[s], s).wait_recv()

        gblend = land[0]
        for s in range(1, n):
            gblend = gblend + land[s]
        mixed = mx_ref[...]
        gmixed = mm(gblend, zs_ref[NEWTON], TOP)
        c_ref[me, 0:DH, :] = gmixed
        dots = jnp.sum(gmixed * mixed, axis=0, keepdims=True)
        pad = jnp.zeros((MSG - DH - 1, LANES), f32)
        c_ref[me, DH:MSG, :] = jnp.concatenate([dots, pad], axis=0)
        for t in range(n):

            @pl.when(me != t)
            def _(t=t):
                to_seq(c_ref.at[me], c_ref.at[me], s2.at[t], r2.at[me], t).start()

        core = core_ref[...]
        core_t = core.T
        unit = eye(LANES)
        g = jnp.where(mask, t_mm(gblend, mixed, TOP), 0.0)
        gcore = jnp.zeros((LANES, LANES), f32)
        for step in reversed(range(NEWTON)):
            z = zs_ref[step]
            prod_t = ps_ref[step].T
            gq = 0.25 * mm(z.T, g, TOP)
            gr = -mm(prod_t, gq, TOP)
            gs = -mm(prod_t, gr, TOP)
            gp = -mm_t(gq, rs_ref[step], TOP) - mm_t(gr, 7.0 * unit - ps_ref[step], TOP) - gs
            gcore = gcore + mm_t(gp, z, TOP)
            g = 0.25 * mm_t(g, qs_ref[step], TOP) + mm(core_t, gp, TOP)
        colsum = jnp.sum(core, axis=0, keepdims=True)
        square = pair_sums(colsum * colsum)
        sigma = jnp.sqrt(square)
        dot = pair_sums(jnp.sum(g * zs_ref[0], axis=0, keepdims=True))
        gcore = gcore + g.T / sigma - jnp.where(mask, dot / square * colsum, 0.0)
        gscore = core * (gcore - jnp.sum(core * gcore, axis=1, keepdims=True)) * SCALE
        lanes = pl.ds(pl.multiple_of(me * LANES, LANES), LANES)
        query = spread(ql_ref[:, lanes], mask)
        key = spread(kl_ref[:, lanes], mask)
        gl_ref[...] = jnp.zeros_like(gl_ref)
        gl_ref[0, :, lanes] = fold(mm(gscore, key, TOP), mask)
        gl_ref[1, :, lanes] = fold(t_mm(gscore, query, TOP), mask)

    for p in range(PAIRS):

        @pl.when(me != p)
        def _(p=p):
            to_seq(c_ref.at[p], c_ref.at[p], s2.at[p], r2.at[p], p).wait_recv()
            to_seq(g_ref.at[p], land.at[me], s1.at[p], r1.at[me], p).wait_send()

    rim_wait(n, me, up, down)

    @pl.when(me < PAIRS)
    def _():
        for t in range(n):

            @pl.when(me != t)
            def _(t=t):
                to_seq(c_ref.at[me], c_ref.at[me], s2.at[t], r2.at[me], t).wait_send()


def blend_exchange(n, gblend, rim, ql, kl, saved):
    dma = pltpu.SemaphoreType.DMA
    width = rim.shape[1]
    return pl.pallas_call(
        partial(blend_exchange_kernel, n),
        in_specs=[whole()] * 10,
        out_specs=[whole()] * 4,
        out_shape=[shape(PAIRS, MSG, LANES), shape(RIM, width), shape(RIM, width), shape(2, DH, width)],
        scratch_shapes=[
            pltpu.VMEM((n, DH, LANES), f32),
            dma((PAIRS,)), dma((n,)), dma((n,)), dma((n,)), dma((2,)), dma((2,)),
        ],
        compiler_params=params(collective_id=3, has_side_effects=True),
        name="blend_exchange",
    )(gblend, rim, ql, kl, *saved)


def land_return_kernel(n, x_ref, own_ref, land, send, recv):
    me = greet_all(n)
    copies = []
    for d in range(1, n):
        target = lax.rem(me + d, n)
        copy = to_seq(x_ref.at[target], land.at[me], send.at[d], recv.at[me], target)
        copy.start()
        copies.append(copy)
    land[me] = x_ref[me]
    for d in range(1, n):
        source = lax.rem(me + d, n)
        to_seq(x_ref.at[0], land.at[source], send.at[d], recv.at[source], source).wait_recv()
    total = land[0]
    for s in range(1, n):
        total = total + land[s]
    own_ref[...] = total
    for copy in copies:
        copy.wait_send()


def land_return(n, parts):
    dma = pltpu.SemaphoreType.DMA
    return pl.pallas_call(
        partial(land_return_kernel, n),
        in_specs=[whole()],
        out_specs=whole(),
        out_shape=shape(*parts.shape[1:]),
        scratch_shapes=[pltpu.VMEM(parts.shape, f32), dma((n,)), dma((n,))],
        compiler_params=params(collective_id=4, has_side_effects=True),
        name="land_return",
    )(parts)


def far_kernel(lens_ref, k_ref, v_ref, ql_ref, f_ref, p_ref, m_ref):
    slots = k_ref.shape[0]
    count = seg_ends(lens_ref, lens_ref.shape[1])[-1]
    valid = valid_rows(count, slots)
    mask = head_mask(QUAD)
    for g in range(HEADS * DH // QUAD):
        cols = slice(g * QUAD, (g + 1) * QUAD)
        scores = mm_t(k_ref[:, cols], spread(ql_ref[:, cols], mask)) * SCALE
        scores = jnp.where(valid, scores, MASKED)
        top = jnp.max(scores, axis=0, keepdims=True)
        raised = jnp.where(valid, jnp.exp(scores - top), 0.0)
        p_ref[:, cols] = raised
        m_ref[:, cols] = top
        total = jnp.sum(raised, axis=0, keepdims=True)
        weighted = fold(t_mm(v_ref[:, cols], raised), mask)
        tail = jnp.concatenate([top, total, jnp.zeros((MSG - DH - 2, QUAD), f32)], axis=0)
        for j in range(QUAD // LANES):
            part = slice(j * LANES, (j + 1) * LANES)
            f_ref[g * 2 + j, 0:DH, :] = weighted[:, part]
            f_ref[g * 2 + j, DH:MSG, :] = tail[:, part]


def far_local(lens, k, v, ql):
    slots, width = k.shape
    return pl.pallas_call(
        far_kernel,
        in_specs=[smem()] + [whole()] * 3,
        out_specs=[whole()] * 3,
        out_shape=[shape(PAIRS, MSG, LANES), shape(slots, width), shape(1, width)],
        compiler_params=params(),
        name="far_local",
    )(lens, k, v, ql)


def norm_stats(r):
    centered = r - jnp.mean(r, axis=1, keepdims=True)
    spread_ = jnp.mean(centered * centered, axis=1, keepdims=True)
    inv = lax.rsqrt(spread_ + EPS)
    return centered * inv, inv


def norm_back(unit, inv, gain, grad):
    ge = grad * gain
    return (
        ge
        - jnp.mean(ge, axis=1, keepdims=True)
        - unit * jnp.mean(ge * unit, axis=1, keepdims=True)
    ) * inv


def pair_rows(ref, g, rows):
    return jnp.concatenate([ref[2 * g, rows, :], ref[2 * g + 1, rows, :]], axis=1)


def attend_kernel(
    lens_ref, q_ref, v_ref, kl_ref, b_ref, left_ref, right_ref, taps_ref, x_ref, wo_ref, bo_ref, g1_ref, b1_ref,
    near_ref, ctx_ref, h1_ref, u1_ref, inv1_ref,
    ext_ref,
):
    slots = q_ref.shape[0]
    count = seg_ends(lens_ref, lens_ref.shape[1])[-1]
    fill_extended(ext_ref, v_ref[...], left_ref[...], right_ref[...], count)
    conv_into(ctx_ref, ext_ref, taps_ref, slots, False, False)
    mask = head_mask(QUAD)
    ones = jnp.where(mask, 1.0, 0.0)
    head = lax.broadcasted_iota(jnp.int32, (slots, QUAD), 1) >> 6
    for g in range(HEADS * DH // QUAD):
        cols = slice(g * QUAD, (g + 1) * QUAD)
        scores = mm_t(q_ref[:, cols], spread(kl_ref[:, cols], mask)) * SCALE
        tops = [jnp.max(scores[:, h * DH : (h + 1) * DH], axis=1, keepdims=True) for h in range(4)]
        top = jnp.where(head < 2, jnp.where(head < 1, tops[0], tops[1]), jnp.where(head < 3, tops[2], tops[3]))
        raised = jnp.exp(scores - top)
        near = raised / mm(raised, ones)
        near_ref[:, cols] = near
        blend = spread(pair_rows(b_ref, g, slice(0, DH)), mask)
        ctx_ref[:, cols] += mm_t(near, blend)
    summed = x_ref[...] + (mm(ctx_ref[...], wo_ref[...]) + bo_ref[...][None, :])
    unit, inv = norm_stats(summed)
    u1_ref[...] = unit
    inv1_ref[...] = inv
    h1_ref[...] = unit * g1_ref[...][None, :] + b1_ref[...][None, :]


def attend(lens, q, v, kl, b, left, right, taps, x, wo, bo, g1, b1):
    slots, width = q.shape
    return pl.pallas_call(
        attend_kernel,
        in_specs=[smem()] + [whole()] * 12,
        out_specs=[whole()] * 5,
        out_shape=[shape(slots, width)] * 4 + [shape(slots, 1)],
        scratch_shapes=[pltpu.VMEM((slots + 40, width), f32)],
        compiler_params=params(),
        name="attend",
    )(lens, q, v, kl, b, left, right, taps, x, wo, bo, g1, b1)


def forward_kernel(
    lens_ref, h1_ref, wi_ref, bi_ref, wo_ref, bo_ref, cot_ref, g2_ref, b2_ref,
    pre_ref, out_ref, gs2_ref, small_ref,
    acc_ref,
):
    step = pl.program_id(0)
    pre = mm(h1_ref[...], wi_ref[...]) + bi_ref[...]
    pre_ref[...] = pre
    act = 0.5 * pre * (1.0 + lax.erf(pre * ROOT_HALF))
    part = mm(act, wo_ref[...])

    @pl.when(step == 0)
    def _():
        acc_ref[...] = part

    @pl.when(step > 0)
    def _():
        acc_ref[...] += part

    @pl.when(step == pl.num_programs(0) - 1)
    def _():
        slots = h1_ref.shape[0]
        valid = valid_rows(seg_ends(lens_ref, lens_ref.shape[1])[-1], slots)
        summed = h1_ref[...] + (acc_ref[...] + bo_ref[...][None, :])
        unit, inv = norm_stats(summed)
        out_ref[...] = jnp.where(valid, unit * g2_ref[...][None, :] + b2_ref[...][None, :], 0.0)
        e = jnp.where(valid, cot_ref[...], 0.0)
        grad = norm_back(unit, inv, g2_ref[...][None, :], e)
        gs2_ref[...] = grad
        small_ref[...] = jnp.concatenate(
            [
                jnp.sum(e * unit, axis=0, keepdims=True),
                jnp.sum(e, axis=0, keepdims=True),
                jnp.sum(grad, axis=0, keepdims=True),
                jnp.zeros((5, e.shape[1]), f32),
            ],
            axis=0,
        )


def ffn_forward(lens, h1, wi, bi, wo, bo, cot, g2, b2):
    slots, width = h1.shape
    inner = wi.shape[1]
    const = lambda *dims: pl.BlockSpec(dims, lambda j: (0,) * len(dims))
    return pl.pallas_call(
        forward_kernel,
        grid=(inner // width,),
        in_specs=[
            smem(), const(slots, width),
            pl.BlockSpec((width, width), lambda j: (0, j)), pl.BlockSpec((1, width), lambda j: (0, j)),
            pl.BlockSpec((width, width), lambda j: (j, 0)), const(width),
            const(slots, width), const(width), const(width),
        ],
        out_specs=[
            pl.BlockSpec((slots, width), lambda j: (0, j)),
            const(slots, width), const(slots, width), const(8, width),
        ],
        out_shape=[shape(slots, inner), shape(slots, width), shape(slots, width), shape(8, width)],
        scratch_shapes=[pltpu.VMEM((slots, width), f32)],
        compiler_params=params(),
        name="ffn_forward",
    )(lens, h1, wi, bi, wo, bo, cot, g2, b2)


def put_strips(ref, block):
    for s in range(block.shape[1] // LANES):
        ref[s] = block[:, s * LANES : (s + 1) * LANES]


def backward_kernel(
    h1_ref, gs2_ref, pre_ref, wi_ref, wo_ref, u1_ref, inv1_ref, g1_ref,
    dwo_ref, dwi_ref, gs1_ref, dbi_ref, small_ref,
    acc_ref,
):
    step = pl.program_id(0)
    gs2 = gs2_ref[...]
    pre = pre_ref[...]
    phi_big = 0.5 * (1.0 + lax.erf(pre * ROOT_HALF))
    act = pre * phi_big
    slope = phi_big + pre * (INV_ROOT_TAU * jnp.exp(-0.5 * pre * pre))
    gpre = mm_t(gs2, wo_ref[...]) * slope
    put_strips(dwo_ref, t_mm(act, gs2))
    put_strips(dwi_ref, t_mm(h1_ref[...], gpre))
    dbi_ref[...] = jnp.sum(gpre, axis=0, keepdims=True)
    part = mm_t(gpre, wi_ref[...])

    @pl.when(step == 0)
    def _():
        acc_ref[...] = gs2 + part

    @pl.when(step > 0)
    def _():
        acc_ref[...] += part

    @pl.when(step == pl.num_programs(0) - 1)
    def _():
        e = acc_ref[...]
        unit = u1_ref[...]
        grad = norm_back(unit, inv1_ref[...], g1_ref[...][None, :], e)
        gs1_ref[...] = grad
        small_ref[...] = jnp.concatenate(
            [
                jnp.sum(e * unit, axis=0, keepdims=True),
                jnp.sum(e, axis=0, keepdims=True),
                jnp.sum(grad, axis=0, keepdims=True),
                jnp.zeros((5, e.shape[1]), f32),
            ],
            axis=0,
        )


def ffn_backward(h1, gs2, pre, wi, wo, u1, inv1, g1):
    slots, width = h1.shape
    inner = wi.shape[1]
    strips = width // LANES
    const = lambda *dims: pl.BlockSpec(dims, lambda j: (0,) * len(dims))
    return pl.pallas_call(
        backward_kernel,
        grid=(inner // width,),
        in_specs=[
            const(slots, width), const(slots, width),
            pl.BlockSpec((slots, width), lambda j: (0, j)),
            pl.BlockSpec((width, width), lambda j: (0, j)),
            pl.BlockSpec((width, width), lambda j: (j, 0)),
            const(slots, width), const(slots, 1), const(width),
        ],
        out_specs=[
            pl.BlockSpec((strips, width, LANES), lambda j: (j, 0, 0)),
            pl.BlockSpec((strips, width, LANES), lambda j: (j, 0, 0)),
            const(slots, width),
            pl.BlockSpec((1, width), lambda j: (0, j)),
            const(8, width),
        ],
        out_shape=[
            shape(inner // LANES, width, LANES), shape(inner // LANES, width, LANES),
            shape(slots, width), shape(1, inner), shape(8, width),
        ],
        scratch_shapes=[pltpu.VMEM((slots, width), f32)],
        compiler_params=params(),
        name="ffn_backward",
    )(h1, gs2, pre, wi, wo, u1, inv1, g1)


def near_back_kernel(
    lens_ref, gs1_ref, wo_ref, near_ref, q_ref, kl_ref, b_ref,
    gctx_ref, gq_ref, gb_ref, gkl_ref, rim_ref,
):
    count = seg_ends(lens_ref, lens_ref.shape[1])[-1]
    gctx_ref[...] = mm_t(gs1_ref[...], wo_ref[...])
    rim_ref[...] = rims_of(gctx_ref[...], count)
    mask = head_mask(QUAD)
    ones = jnp.where(mask, 1.0, 0.0)
    for g in range(HEADS * DH // QUAD):
        cols = slice(g * QUAD, (g + 1) * QUAD)
        gctx = gctx_ref[:, cols]
        near = near_ref[:, cols]
        gblend = fold(t_mm(gctx, near), mask)
        gb_ref[2 * g] = gblend[:, :LANES]
        gb_ref[2 * g + 1] = gblend[:, LANES:]
        gnear = mm(gctx, spread(pair_rows(b_ref, g, slice(0, DH)), mask))
        gscore = near * (gnear - mm(near * gnear, ones)) * SCALE
        gq_ref[:, cols] = mm(gscore, spread(kl_ref[:, cols], mask))
        gkl_ref[:, cols] = fold(t_mm(gscore, q_ref[:, cols]), mask)


def near_back(lens, gs1, wo, near, q, kl, b):
    slots, width = gs1.shape
    return pl.pallas_call(
        near_back_kernel,
        in_specs=[smem()] + [whole()] * 6,
        out_specs=[whole()] * 5,
        out_shape=[
            shape(slots, width), shape(slots, width), shape(PAIRS, DH, LANES),
            shape(DH, width), shape(2 * RIM, width),
        ],
        compiler_params=params(),
        name="near_back",
    )(lens, gs1, wo, near, q, kl, b)


def far_back_kernel(
    lens_ref, k_ref, v_ref, p_ref, m_ref, b_ref, c_ref, ql_ref, gkl_ref, gl_ref,
    gk_ref, gv_ref, ret_ref,
):
    mask = head_mask(QUAD)
    n, _, segs, _ = ret_ref.shape
    for g in range(HEADS * DH // QUAD):
        cols = slice(g * QUAD, (g + 1) * QUAD)
        top = pair_rows(b_ref, g, slice(DH, DH + 1))
        total = pair_rows(b_ref, g, slice(DH + 1, DH + 2))
        prob = p_ref[:, cols] * (jnp.exp(m_ref[:, cols] - top) / total)
        gmixed = spread(pair_rows(c_ref, g, slice(0, DH)), mask)
        dots = pair_rows(c_ref, g, slice(DH, DH + 1))
        gscore = prob * (mm(v_ref[:, cols], gmixed) - dots) * SCALE
        gk_ref[:, cols] = mm(gscore, spread(ql_ref[:, cols], mask))
        gv_ref[:, cols] = mm_t(prob, gmixed)
        gql = fold(t_mm(gscore, k_ref[:, cols]), mask) + gl_ref[0, :, cols]
        gkl = gkl_ref[:, cols] + gl_ref[1, :, cols]
        for s in range(n):
            rows = slice(s * segs, (s + 1) * segs)
            ret_ref[s, 0, :, cols] = gql[rows]
            ret_ref[s, 1, :, cols] = gkl[rows]


def far_back(n, lens, k, v, p, m, b, c, ql, gkl, gl):
    slots, width = k.shape
    segs = lens.shape[1]
    return pl.pallas_call(
        far_back_kernel,
        in_specs=[smem()] + [whole()] * 9,
        out_specs=[whole()] * 3,
        out_shape=[shape(slots, width), shape(slots, width), shape(n, 2, segs, width)],
        compiler_params=params(),
        name="far_back",
    )(lens, k, v, p, m, b, c, ql, gkl, gl)


def conv_back_kernel(
    lens_ref, v_ref, left_ref, right_ref, gctx_ref, gleft_ref, gright_ref, taps_ref, ctx_ref, gs1_ref,
    gv_ref, gtaps_ref, dwo_ref,
    ext_ref, scr_ref,
):
    slots = v_ref.shape[0]
    count = seg_ends(lens_ref, lens_ref.shape[1])[-1]
    put_strips(dwo_ref, t_mm(ctx_ref[...], gs1_ref[...]))
    fill_extended(ext_ref, gctx_ref[...], gleft_ref[...], gright_ref[...], count)
    conv_into(gv_ref, ext_ref, taps_ref, slots, True, False)
    fill_extended(ext_ref, v_ref[...], left_ref[...], right_ref[...], count)
    taps_grad_into(scr_ref, gctx_ref, ext_ref, slots)
    rows = jnp.concatenate(
        [jnp.sum(scr_ref[c], axis=0, keepdims=True) for c in range(CONV)] + [jnp.zeros((7, v_ref.shape[1]), f32)],
        axis=0,
    )
    row = lax.broadcasted_iota(jnp.int32, (v_ref.shape[1], LANES), 0) >> 6
    col = lax.broadcasted_iota(jnp.int32, (v_ref.shape[1], LANES), 1)
    gtaps_ref[...] = mm(rows, jnp.where(row == col, 1.0, 0.0), TOP)


def conv_back(lens, v, left, right, gctx, gleft, gright, taps, ctx, gs1):
    slots, width = v.shape
    return pl.pallas_call(
        conv_back_kernel,
        in_specs=[smem()] + [whole()] * 9,
        out_specs=[whole()] * 3,
        out_shape=[shape(slots, width), shape(40, LANES), shape(width // LANES, width, LANES)],
        scratch_shapes=[pltpu.VMEM((slots + 40, width), f32), pltpu.VMEM((CONV, 8, width), f32)],
        compiler_params=params(),
        name="conv_back",
    )(lens, v, left, right, gctx, gleft, gright, taps, ctx, gs1)


def project_back_kernel(
    lens_ref, x_ref, gs1_ref, gqn_ref, gkf_ref, gvc_ref, gvf_ref, own_ref, wq_ref, wk_ref, wv_ref,
    ig_ref, dq_ref, dk_ref, dv_ref, small_ref,
    gq_ref, gk_ref, gv_ref,
):
    @pl.when(pl.program_id(0) == 0)
    def _():
        slots = gqn_ref.shape[0]
        segs = own_ref.shape[1]
        ends = seg_ends(lens_ref, segs)
        member = member_rows(ends, slots)
        inv = inverse_lens(lens_ref, segs)
        gq = gqn_ref[...] + t_mm(member, own_ref[0] * inv)
        gk = gkf_ref[...] + t_mm(member, own_ref[1] * inv)
        gv = jnp.where(valid_rows(ends[-1], slots), gvc_ref[...] + gvf_ref[...], 0.0)
        gq_ref[...] = gq
        gk_ref[...] = gk
        gv_ref[...] = gv
        small_ref[...] = jnp.concatenate(
            [
                jnp.sum(gq, axis=0, keepdims=True),
                jnp.sum(gv, axis=0, keepdims=True),
                jnp.zeros((6, gq.shape[1]), f32),
            ],
            axis=0,
        )

    x = x_ref[...]
    put_strips(dq_ref, t_mm(x, gq_ref[...]))
    put_strips(dk_ref, t_mm(x, gk_ref[...]))
    put_strips(dv_ref, t_mm(x, gv_ref[...]))
    ig_ref[...] = (
        gs1_ref[...]
        + mm_t(gq_ref[...], wq_ref[...])
        + mm_t(gk_ref[...], wk_ref[...])
        + mm_t(gv_ref[...], wv_ref[...])
    )


def project_back(lens, x, gs1, gqn, gkf, gvc, gvf, own, wq, wk, wv):
    slots, width = x.shape
    col = 256
    strips = width // LANES
    const = lambda *dims: pl.BlockSpec(dims, lambda i: (0,) * len(dims))
    part = pl.BlockSpec((slots, col), lambda i: (0, i))
    wspec = pl.BlockSpec((col, width), lambda i: (i, 0))
    dspec = pl.BlockSpec((strips, col, LANES), lambda i: (0, i, 0))
    return pl.pallas_call(
        project_back_kernel,
        grid=(width // col,),
        in_specs=[smem(), part, part] + [const(slots, width)] * 4 + [const(*own.shape), wspec, wspec, wspec],
        out_specs=[part, dspec, dspec, dspec, const(8, width)],
        out_shape=[shape(slots, width)] + [shape(strips, width, LANES)] * 3 + [shape(8, width)],
        scratch_shapes=[pltpu.VMEM((slots, width), f32)] * 3,
        compiler_params=params(),
        name="project_back",
    )(lens, x, gs1, gqn, gkf, gvc, gvf, own, wq, wk, wv)


def sum_plain(parts):
    sizes = [part.size for part in parts]
    shapes = [part.shape for part in parts]
    devices = lax.axis_size(("seq", "dp"))
    flat = jnp.concatenate([part.reshape(-1) for part in parts])
    flat = jnp.pad(flat, (0, -flat.shape[0] % devices))
    own = lax.psum_scatter(flat, ("seq", "dp"), scatter_dimension=0, tiled=True)
    flat = lax.all_gather(own, ("seq", "dp"), axis=0, tiled=True)
    out = []
    at = 0
    for size, dims in zip(sizes, shapes):
        out.append(flat[at : at + size].reshape(dims))
        at += size
    return out


STRIP = 768
HALF = STRIP // 2
PART = HALF // 2
Z_ROWS = PART // 4
OWN = Z_ROWS // 2
STAGES = 13
SMALL_STEPS = 5


def pack_small(sb_ref, small0, small1, small2, inner_bias, taps):
    at = 0
    for ref, count in ((small0, 2), (small1, 3), (small2, 3), (inner_bias, 1)):
        for r in range(count):
            for j in range(ref.shape[1] // LANES):
                sb_ref[0, at : at + 1, :] = ref[r : r + 1, j * LANES : (j + 1) * LANES]
                at += 1
    sb_ref[0, at : at + 40, :] = taps[...]


SMALL_ROWS = 8 * 6 + 24 + 40


def unpack_small(s_ref, outs):
    at = 0
    for ref in outs[:-1]:
        for j in range(ref.shape[0] // LANES):
            ref[pl.ds(j * LANES, LANES)] = s_ref[at, :]
            at += 1
    outs[-1][...] = s_ref[at : at + CONV, :HEADS]


def reduce_kernel(spans, lag, *refs):
    count = len(spans)
    grads = refs[:count]
    smalls = refs[count : count + 5]
    o_ref, so_ref, acc, lc, l1, lz, l3, sb, sl = refs[count + 5 : count + 14]
    (
        local, out_local, cs, cr, s1, r1, zs, zr, s3, r3, s4, r4, gs, gr, s5, r5, es, er, ss, sr,
    ) = refs[count + 14 :]
    chunks = spans[-1][1]
    seq = lax.axis_index("seq")
    dp = lax.axis_index("dp")
    z = seq // 2
    c = lax.rem(seq, 2)
    y = dp // 2
    x = lax.rem(dp, 2)
    zb = 3 - z
    place = lambda z_, c_, y_, x_: (z_ * 2 + c_, y_ * 2 + x_)
    by_core = place(z, 1 - c, y, x)
    by_x = place(z, c, y, 1 - x)
    by_y = place(z, c, 1 - y, x)
    right = place(lax.rem(z + 1, 4), c, y, x)
    left = place(lax.rem(z + 3, 4), c, y, x)
    opposite = place(lax.rem(z + 2, 4), c, y, x)
    near_z = place(z + 1 - 2 * lax.rem(z, 2), c, y, x)
    barrier = pltpu.get_barrier_semaphore()
    for target in (by_core, by_x, by_y, right, left, opposite):
        pl.semaphore_signal(barrier, inc=1, device_id=target, device_id_type=MESH)
    pl.semaphore_wait(barrier, 6)

    def remote(src, dst, send, recv, target):
        return pltpu.make_async_remote_copy(src, dst, send, recv, device_id=target, device_id_type=MESH)

    aligned = lambda at: pl.multiple_of(at, 8)
    a1 = x * PART
    b1 = HALF + y * PART
    firsts = ((0, a1, (1 - x) * PART, by_x), (1, b1, HALF + (1 - y) * PART, by_y))
    starts = (a1, b1)
    az = a1 + z * Z_ROWS
    bz = b1 + z * Z_ROWS
    thirds = (
        (0, az + y * OWN, az + (1 - y) * OWN, by_y),
        (1, bz + x * OWN, bz + (1 - x) * OWN, by_x),
    )

    def rows(ref, k, at, size):
        return ref.at[k, pl.ds(aligned(at), size)]

    def core_out(k):
        for g, (lo, hi) in zip(grads, spans):
            half = hi - lo

            @pl.when((k >= lo) & (k < hi))
            def _(g=g, lo=lo, half=half):
                pltpu.make_async_copy(g.at[c * half + (k - lo)], acc.at[k], local.at[k]).start()
                remote(g.at[(1 - c) * half + (k - lo)], lc.at[k], cs.at[k], cr.at[k], by_core).start()

    def first(k, j):
        _, _, other, target = firsts[j]
        return remote(rows(acc, k, other, PART), l1.at[k, j], s1.at[k, j], r1.at[k, j], target)

    def first_out(k):
        pltpu.make_async_copy(grads[0].at[0], acc.at[k], local.at[k]).wait()
        remote(grads[0].at[0], lc.at[k], cs.at[k], cr.at[k], by_core).wait_recv()
        acc[k] += lc[k]
        for j in range(2):
            first(k, j).start()

    def z_copy(k, j, way, step, block):
        target = right if way == 0 else left
        return remote(
            rows(acc, k, starts[j] + block * Z_ROWS, Z_ROWS), lz.at[k, way, j, step],
            zs.at[k, way, step, j], zr.at[k, way, step, j], target,
        )

    def z_out(k, step):
        if step == 0:
            for j, mine, _, _ in firsts:
                first(k, j).wait_recv()
                acc[k, pl.ds(aligned(mine), PART)] += l1[k, j]
        for way, at in ((0, z), (1, zb)):
            block = 3 - step + z if way == 0 else step - zb
            if step > 0:

                @pl.when((at > 0) & (at <= step))
                def _(way=way, block=block):
                    for j in range(2):
                        z_copy(k, j, way, step - 1, 0).wait_recv()
                    for j in range(2):
                        acc[k, pl.ds(aligned(starts[j] + block * Z_ROWS), Z_ROWS)] += lz[k, way, j, step - 1]

            if step < 3:

                @pl.when((at <= step) & (at < 3))
                def _(way=way, block=block):
                    for j in range(2):
                        z_copy(k, j, way, step, block).start()

    def third(k, j):
        _, _, other, target = thirds[j]
        return remote(rows(acc, k, other, OWN), l3.at[k, j], s3.at[k, j], r3.at[k, j], target)

    def third_out(k):
        z_out(k, 3)
        for j in range(2):
            third(k, j).start()

    def back_third(k, j):
        _, mine, _, target = thirds[j]
        return remote(rows(acc, k, mine, OWN), rows(o_ref.at[c], k, mine, OWN), s4.at[k, j], r4.at[k, j], target)

    def keep(k, j):
        mine = thirds[j][1]
        return pltpu.make_async_copy(rows(acc, k, mine, OWN), rows(o_ref.at[c], k, mine, OWN), out_local.at[k, j])

    def back_third_out(k):
        for j, mine, _, _ in thirds:
            third(k, j).wait_recv()
            acc[k, pl.ds(aligned(mine), OWN)] += l3[k, j]
        for j in range(2):
            back_third(k, j).start()
            keep(k, j).start()

    def back_z(k, j, way, step, block):
        target = right if way == 0 else left
        part = rows(o_ref.at[c], k, starts[j] + block * Z_ROWS, Z_ROWS)
        return remote(part, part, gs.at[k, way, step, j], gr.at[k, way, step, j], target)

    def back_z_out(k, step):
        if step == 0:
            for j in range(2):
                keep(k, j).wait()
                back_third(k, j).wait_recv()
        for way, at in ((0, z), (1, zb)):
            block = z - step if way == 0 else z + step
            if step > 0:

                @pl.when(at >= step)
                def _(way=way):
                    for j in range(2):
                        back_z(k, j, way, step - 1, 0).wait_recv()

            if step < 3:

                @pl.when((at >= step) & (at < 3))
                def _(way=way, block=block):
                    for j in range(2):
                        back_z(k, j, way, step, block).start()

    def back_first(k, j):
        _, mine, _, target = firsts[j]
        part = rows(o_ref.at[c], k, mine, PART)
        return remote(part, part, s5.at[k, j], r5.at[k, j], target)

    def back_first_out(k):
        back_z_out(k, 3)
        for j in range(2):
            back_first(k, j).start()

    def back_core(k):
        part = o_ref.at[c, k]
        return remote(part, part, es.at[k], er.at[k], by_core)

    def back_core_out(k):
        for j in range(2):
            back_first(k, j).wait_recv()
        back_core(k).start()

    def finish(k):
        back_core(k).wait()
        remote(grads[0].at[0], lc.at[k], cs.at[k], cr.at[k], by_core).wait_send()
        for j in range(2):
            first(k, j).wait_send()
            third(k, j).wait_send()
            back_third(k, j).wait_send()
            back_first(k, j).wait_send()
        for step in range(3):
            for way, at in ((0, z), (1, zb)):

                @pl.when((at <= step) & (at < 3))
                def _(way=way, step=step):
                    for j in range(2):
                        z_copy(k, j, way, step, 0).wait_send()

                @pl.when((at >= step) & (at < 3))
                def _(way=way, step=step):
                    for j in range(2):
                        back_z(k, j, way, step, 0).wait_send()

    stages = [
        core_out, first_out, partial(z_out, step=0), partial(z_out, step=1), partial(z_out, step=2), third_out,
        back_third_out, partial(back_z_out, step=0), partial(back_z_out, step=1), partial(back_z_out, step=2),
        back_first_out, back_core_out, finish,
    ]

    partners = (by_core, by_x, by_y, near_z, opposite)

    def small(i):
        return remote(sb.at[i], sl.at[i], ss.at[i], sr.at[i], partners[i])

    pack_small(sb, *smalls)
    small(0).start()

    def tick(t, carry):
        for i in range(1, SMALL_STEPS + 1):

            @pl.when(t == 2 * i)
            def _(i=i):
                small(i - 1).wait_recv()
                sb[i] = sb[i - 1] + sl[i - 1]
                if i < SMALL_STEPS:
                    small(i).start()

        for stage, run in reversed(list(enumerate(stages))):
            k = t - lag[stage]

            @pl.when((k >= 0) & (k < chunks))
            def _(run=run, k=k):
                run(k)

        return carry

    lax.fori_loop(0, chunks + lag[-1], tick, 0)
    for i in range(SMALL_STEPS):
        small(i).wait_send()
    so_ref[...] = sb[SMALL_STEPS]


LAG = tuple(range(0, 2 * STAGES, 2))


def reduce_grads(grads, smalls):
    spans = []
    at = 0
    for g in grads:
        spans.append((at, at + g.shape[0] // 2))
        at += g.shape[0] // 2
    dma = pltpu.SemaphoreType.DMA
    vm = lambda *dims: pltpu.VMEM(dims, f32)
    return pl.pallas_call(
        partial(reduce_kernel, tuple(spans), LAG),
        in_specs=[pl.BlockSpec(memory_space=pl.ANY)] * len(grads) + [whole()] * 5,
        out_specs=[pl.BlockSpec(memory_space=pl.ANY), whole()],
        out_shape=[shape(2, at, STRIP, LANES), shape(SMALL_ROWS, LANES)],
        scratch_shapes=[
            vm(at, STRIP, LANES), vm(at, STRIP, LANES), vm(at, 2, PART, LANES), vm(at, 2, 2, 3, Z_ROWS, LANES),
            vm(at, 2, OWN, LANES), vm(SMALL_STEPS + 1, SMALL_ROWS, LANES), vm(SMALL_STEPS, SMALL_ROWS, LANES),
            dma((at,)), dma((at, 2)), dma((at,)), dma((at,)), dma((at, 2)), dma((at, 2)),
            dma((at, 2, 3, 2)), dma((at, 2, 3, 2)), dma((at, 2)), dma((at, 2)), dma((at, 2)), dma((at, 2)),
            dma((at, 2, 3, 2)), dma((at, 2, 3, 2)), dma((at, 2)), dma((at, 2)), dma((at,)), dma((at,)),
            dma((SMALL_STEPS,)), dma((SMALL_STEPS,)),
        ],
        compiler_params=params(collective_id=5, has_side_effects=True),
        name="reduce_grads",
    )(*grads, *smalls)


def sum_on_block(grads, smalls, shapes):
    summed, packed = reduce_grads(grads, smalls)
    spans = []
    at = 0
    for g in grads:
        spans.append((at, at + g.shape[0] // 2))
        at += g.shape[0] // 2
    return place_strips(summed, packed, spans, shapes)


def unstrip(strips):
    count, rows, _ = strips.shape
    return strips.transpose(1, 0, 2).reshape(rows, count * LANES)


def unstrip_tall(strips, across):
    count, rows, _ = strips.shape
    down = count // across
    return strips.reshape(down, across, rows, LANES).transpose(0, 2, 1, 3).reshape(down * rows, across * LANES)


PLACE_SLOTS = 24


def place_strips_kernel(spans, s_ref, small_ref, *refs):
    outs = refs[: len(spans)]
    smalls = refs[len(spans) : -3]
    buf, in_sem, out_sem = refs[-3:]
    moves = []
    for out, (lo, hi) in zip(outs, spans):
        across = out.shape[1] // LANES
        for c in range(2):
            for k in range(lo, hi):
                at = c * (hi - lo) + k - lo
                rows = pl.ds(at // across * STRIP, STRIP)
                cols = pl.ds(at % across * LANES, LANES)
                slot = len(moves) % PLACE_SLOTS
                moves.append((
                    pltpu.make_async_copy(s_ref.at[c, k], buf.at[slot], in_sem.at[slot]),
                    pltpu.make_async_copy(buf.at[slot], out.at[rows, cols], out_sem.at[slot]),
                ))
    ahead = PLACE_SLOTS // 2
    for i in range(len(moves) + ahead):
        if i < len(moves):
            if i >= PLACE_SLOTS:
                moves[i - PLACE_SLOTS][1].wait()
            moves[i][0].start()
        if i >= ahead:
            moves[i - ahead][0].wait()
            moves[i - ahead][1].start()
    unpack_small(small_ref, smalls)
    for _, out in moves[-PLACE_SLOTS:]:
        out.wait()


def place_strips(summed, packed, spans, shapes):
    anywhere = pl.BlockSpec(memory_space=pl.ANY)
    dma = pltpu.SemaphoreType.DMA
    width = shapes[0][1]
    return pl.pallas_call(
        partial(place_strips_kernel, spans),
        in_specs=[anywhere, whole()],
        out_specs=[anywhere] * len(shapes) + [whole()] * 10,
        out_shape=[shape(*dims) for dims in shapes] + [shape(width)] * 8 + [shape(shapes[0][0]), shape(CONV, HEADS)],
        scratch_shapes=[pltpu.VMEM((PLACE_SLOTS, STRIP, LANES), f32), dma((PLACE_SLOTS,)), dma((PLACE_SLOTS,))],
        compiler_params=params(),
        name="place_strips",
    )(summed, packed)


def per_device(
    tokens, segment_lens, query_weight, query_bias, key_weight, value_weight, value_bias, conv_taps,
    output_weight, output_bias, first_gain, first_bias, inner_weight, inner_bias, outer_weight, outer_bias,
    second_gain, second_bias, cotangent,
):
    n = lax.axis_size("seq")
    _, slots, width = tokens.shape
    x = tokens.reshape(slots, width)
    cot = cotangent.reshape(slots, width)
    lens = segment_lens
    taps = jnp.repeat(conv_taps, DH, axis=1)

    q, k, v, land, rim = project(lens, x, query_weight, key_weight, value_weight, query_bias, value_bias)
    lands, left, right = land_exchange(n, land, rim)
    ql = lands[:, 0].reshape(DH, width)
    kl = lands[:, 1].reshape(DH, width)
    parts, raised, tops = far_local(lens, k, v, ql)
    b, *saved = far_exchange(n, parts, ql, kl)
    near, ctx, h1, u1, inv1 = attend(
        lens, q, v, kl, b, left, right, taps, x, output_weight, output_bias, first_gain, first_bias
    )
    pre, layer_out, gs2, small2 = ffn_forward(
        lens, h1, inner_weight, inner_bias.reshape(1, -1), outer_weight, outer_bias, cot, second_gain, second_bias
    )
    d_outer, d_inner, gs1, d_inner_bias, small1 = ffn_backward(
        h1, gs2, pre, inner_weight, outer_weight, u1, inv1, first_gain
    )
    gctx, gqn, gblend, gkl, grim = near_back(lens, gs1, output_weight, near, q, kl, b)
    c, gleft, gright, gl = blend_exchange(n, gblend, grim, ql, kl, saved)
    gkf, gvf, back = far_back(n, lens, k, v, raised, tops, b, c, ql, gkl, gl)
    own = land_return(n, back)
    gvc, gtaps, d_output = conv_back(lens, v, left, right, gctx, gleft, gright, taps, ctx, gs1)
    input_grad, d_query, d_key, d_value, small0 = project_back(
        lens, x, gs1, gqn, gkf, gvc, gvf, own, query_weight, key_weight, value_weight
    )
    grads = [d_outer, d_inner, d_output, d_query, d_key, d_value]
    smalls = [small0, small1, small2, d_inner_bias, gtaps]
    weights = [outer_weight, inner_weight, output_weight, query_weight, key_weight, value_weight]
    if n == 8 and lax.axis_size("dp") == 4:
        sums = sum_on_block(grads, smalls, [w.shape for w in weights])
    else:
        sums = sum_plain(grads + smalls)
        small = sums[6:]
        sums = (
            [unstrip_tall(sums[0], width // LANES)] + [unstrip(s) for s in sums[1:6]]
            + [small[0][0], small[0][1], *small[1][:3], *small[2][:3], small[3][0], small[4][:CONV, :HEADS]]
        )
    d_outer, d_inner, d_output, d_query, d_key, d_value, *vectors = sums
    d_query_bias, d_value_bias, d_first_gain, d_first_bias, d_output_bias = vectors[:5]
    d_second_gain, d_second_bias, d_outer_bias, d_inner_bias, d_taps = vectors[5:]
    return (
        layer_out.reshape(tokens.shape), input_grad.reshape(tokens.shape),
        d_query, d_query_bias, d_key, d_value, d_value_bias, d_taps,
        d_output, d_output_bias, d_first_gain, d_first_bias,
        d_inner, d_inner_bias, d_outer, d_outer_bias, d_second_gain, d_second_bias,
    )


def solution(mesh):
    block = P("dp", "seq", None)
    return jax.shard_map(
        per_device,
        mesh=mesh,
        in_specs=(block, P("dp", "seq")) + (P(),) * 16 + (block,),
        out_specs=(block, block) + (P(),) * 16,
        check_vma=False,
    )
```

```python
from functools import partial
import math

import jax
import jax.numpy as jnp
from jax import lax
from jax.experimental import pallas as pl
from jax.experimental.pallas import tpu as pltpu
from jax.sharding import PartitionSpec as P

HEADS = 12
DH = 64
CONV = 33
NEWTON = 6
RIM = (CONV - 1) // 2
LANES = 128
PAIRS = HEADS * DH // LANES
QUAD = 256
QUADS = HEADS * DH // QUAD
SCALE = DH ** (-0.5)
EPS = 1e-05
ROOT_HALF = 0.7071067811865476
INV_ROOT_TAU = 0.3989422804014327
MASKED = -1e30
f32 = jnp.float32
HI = lax.Precision.HIGH
TOP = lax.Precision.HIGHEST
MESH = pl.DeviceIdType.MESH
VMEM_CAP = 60 << 20


def _dg(a, b, ca, cb, prec):
    return lax.dot_general(
        a, b, (((ca,), (cb,)), ((), ())), precision=prec, preferred_element_type=f32
    )


def mm(a, b, prec=HI):
    return _dg(a, b, 1, 0, prec)


def mm_t(a, b, prec=HI):
    return _dg(a, b, 1, 1, prec)


def t_mm(a, b, prec=HI):
    return _dg(a, b, 0, 0, prec)


def head_mask(size):
    row = lax.broadcasted_iota(jnp.int32, (size, size), 0) >> 6
    col = lax.broadcasted_iota(jnp.int32, (size, size), 1) >> 6
    return row == col


def spread(rows, mask):
    return jnp.where(mask, jnp.concatenate([rows] * (mask.shape[0] // DH), axis=0), 0.0)


def fold(square, mask):
    kept = jnp.where(mask, square, 0.0)
    total = kept[:DH]
    for at in range(DH, mask.shape[0], DH):
        total = total + kept[at : at + DH]
    return total


def seg_ends(lens_ref, count):
    ends = []
    total = 0
    for j in range(count):
        total = total + lens_ref[0, j]
        ends.append(total)
    return ends


def member_rows(ends, slots):
    shape = (len(ends), slots)
    row = lax.broadcasted_iota(jnp.int32, shape, 0)
    col = lax.broadcasted_iota(jnp.int32, shape, 1)
    low = jnp.zeros(shape, jnp.int32)
    high = jnp.zeros(shape, jnp.int32)
    before = 0
    for j, end in enumerate(ends):
        low = jnp.where(row == j, before, low)
        high = jnp.where(row == j, end, high)
        before = end
    return jnp.where((col >= low) & (col < high), 1.0, 0.0)


def inverse_lens(lens_ref, count):
    row = lax.broadcasted_iota(jnp.int32, (count, 1), 0)
    out = jnp.zeros((count, 1), f32)
    for j in range(count):
        out = jnp.where(row == j, lens_ref[0, j].astype(f32), out)
    return 1.0 / out


def valid_rows(count, slots):
    return lax.broadcasted_iota(jnp.int32, (slots, 1), 0) < count


def rims_of(matrix, count):
    slots = matrix.shape[0]
    row = lax.broadcasted_iota(jnp.int32, (2 * RIM, slots), 0)
    col = lax.broadcasted_iota(jnp.int32, (2 * RIM, slots), 1)
    want = jnp.where(row < RIM, row, row - 2 * RIM + count)
    return mm(jnp.where(col == want, 1.0, 0.0), matrix)


def fill_extended(ext_ref, middle, left, right, count):
    slots = middle.shape[0]
    ext_ref[0:RIM, :] = left
    ext_ref[RIM : RIM + slots, :] = middle
    tail = ext_ref.shape[0] - RIM - slots
    ext_ref[RIM + slots :, :] = jnp.zeros((tail, middle.shape[1]), f32)
    rows = slots + RIM
    row = lax.broadcasted_iota(jnp.int32, (rows, RIM), 0)
    col = lax.broadcasted_iota(jnp.int32, (rows, RIM), 1)
    put = jnp.where(row == col + count, 1.0, 0.0)
    ext_ref[RIM : RIM + rows, :] += mm(put, right)


CONV_ROWS = 64


def shifted(ext_ref, r0, l0):
    slab = ext_ref[pl.ds(r0, CONV_ROWS + 40), pl.ds(l0, LANES)]
    for b in range(8):
        moved = slab[b : b + CONV_ROWS + 32]
        for a in range(5):
            if 8 * a + b < CONV:
                yield 8 * a + b, moved[8 * a : 8 * a + CONV_ROWS]


def conv_into(out_ref, ext_ref, taps_ref, slots, flip, add, low=0):
    def block(i, carry):
        r0 = pl.multiple_of((i // PAIRS) * CONV_ROWS, CONV_ROWS)
        l0 = pl.multiple_of((i % PAIRS) * LANES, LANES)
        acc = jnp.zeros((CONV_ROWS, LANES), f32)
        for c, part in shifted(ext_ref, r0, l0):
            at = CONV - 1 - c if flip else c
            acc = acc + taps_ref[at : at + 1, pl.ds(l0, LANES)] * part
        here = (pl.ds(r0, CONV_ROWS), pl.ds(l0, LANES))
        if add:
            out_ref[here] += acc
        else:
            out_ref[here] = acc
        return carry

    lax.fori_loop((low // CONV_ROWS) * PAIRS, (slots // CONV_ROWS) * PAIRS, block, 0)


def taps_grad_into(scr_ref, grad_ref, ext_ref, slots, low=0, clear=True):
    if clear:
        scr_ref[...] = jnp.zeros_like(scr_ref)

    def block(i, carry):
        r0 = pl.multiple_of((i // PAIRS) * CONV_ROWS, CONV_ROWS)
        l0 = pl.multiple_of((i % PAIRS) * LANES, LANES)
        grad = grad_ref[pl.ds(r0, CONV_ROWS), pl.ds(l0, LANES)]
        for c, part in shifted(ext_ref, r0, l0):
            prod = grad * part
            total = prod[0:8]
            for at in range(8, CONV_ROWS, 8):
                total = total + prod[at : at + 8]
            scr_ref[c, :, pl.ds(l0, LANES)] += total
        return carry

    lax.fori_loop((low // CONV_ROWS) * PAIRS, (slots // CONV_ROWS) * PAIRS, block, 0)


def whole(shape=None):
    return pl.BlockSpec(memory_space=pltpu.VMEM)


def smem():
    return pl.BlockSpec(memory_space=pltpu.SMEM)


def params(**more):
    return pltpu.CompilerParams(vmem_limit_bytes=VMEM_CAP, **more)


def shape(*dims):
    return jax.ShapeDtypeStruct(dims, f32)


def project_kernel(
    lens_ref, x_ref, wq_hbm, wk_hbm, wv_hbm, bq_ref, bv_ref,
    q_ref, k_ref, v_ref, land_ref, rim_ref,
    w_ref, bias_ref, out_ref, load,
):
    slots, width = x_ref.shape
    segs = land_ref.shape[1]
    loads = [
        pltpu.make_async_copy(hbm.at[:, pl.ds(g * QUAD, QUAD)], w_ref.at[i * QUADS + g], load.at[i * QUADS + g])
        for i, hbm in enumerate((wq_hbm, wk_hbm, wv_hbm))
        for g in range(QUADS)
    ]
    for copy in loads:
        copy.start()
    ends = seg_ends(lens_ref, segs)
    member = member_rows(ends, slots)
    inv = inverse_lens(lens_ref, segs)
    for g in range(QUADS):
        bias_ref[g] = jnp.broadcast_to(bq_ref[pl.ds(g * QUAD, QUAD)][None, :], (8, QUAD))
        bias_ref[QUADS + g] = jnp.zeros((8, QUAD), f32)
        bias_ref[2 * QUADS + g] = jnp.broadcast_to(bv_ref[pl.ds(g * QUAD, QUAD)][None, :], (8, QUAD))

    def one(i, carry):
        pltpu.make_async_copy(wq_hbm.at[:, pl.ds(0, QUAD)], w_ref.at[i], load.at[i]).wait()
        out_ref[i] = mm(x_ref[...], w_ref[i]) + bias_ref[i, 0:1, :]
        return carry

    lax.fori_loop(0, 3 * QUADS, one, 0)
    valid = valid_rows(ends[-1], slots)
    for g in range(QUADS):
        cols = slice(g * QUAD, (g + 1) * QUAD)
        q_ref[:, cols] = out_ref[g]
        k_ref[:, cols] = out_ref[QUADS + g]
        v_ref[:, cols] = jnp.where(valid, out_ref[2 * QUADS + g], 0.0)
    land_ref[0] = mm(member, q_ref[...]) * inv
    land_ref[1] = mm(member, k_ref[...]) * inv
    rim_ref[...] = rims_of(v_ref[...], ends[-1])


def project(lens, x, wq, wk, wv, bq, bv):
    slots, width = x.shape
    segs = lens.shape[1]
    anywhere = pl.BlockSpec(memory_space=pl.ANY)
    count = 3 * QUADS
    return pl.pallas_call(
        project_kernel,
        in_specs=[smem(), whole()] + [anywhere] * 3 + [whole()] * 2,
        out_specs=[whole()] * 5,
        out_shape=[
            shape(slots, width), shape(slots, width), shape(slots, width),
            shape(2, segs, width), shape(2 * RIM, width),
        ],
        scratch_shapes=[
            pltpu.VMEM((count, width, QUAD), f32), pltpu.VMEM((count, 8, QUAD), f32),
            pltpu.VMEM((count, slots, QUAD), f32), pltpu.SemaphoreType.DMA((count,)),
        ],
        compiler_params=params(),
        name="project",
    )(lens, x, wq, wk, wv, bq, bv)


def greet_all(n):
    me = lax.axis_index("seq")
    barrier = pltpu.get_barrier_semaphore()
    for d in range(1, n):
        pl.semaphore_signal(
            barrier, inc=1, device_id={"seq": lax.rem(me + d, n)}, device_id_type=MESH
        )
    pl.semaphore_wait(barrier, n - 1)
    return me


def to_seq(src, dst, send, recv, target):
    return pltpu.make_async_remote_copy(
        src, dst, send, recv, device_id={"seq": target}, device_id_type=MESH
    )


def rim_copies(n, me, rim_ref, left_ref, right_ref, rsend, rrecv):
    up = to_seq(rim_ref.at[pl.ds(RIM, RIM)], left_ref, rsend.at[0], rrecv.at[0], lax.rem(me + 1, n))
    down = to_seq(rim_ref.at[pl.ds(0, RIM)], right_ref, rsend.at[1], rrecv.at[1], lax.rem(me + n - 1, n))
    return up, down


def rim_start(n, me, up, down, left_ref, right_ref):
    @pl.when(me < n - 1)
    def _():
        up.start()

    @pl.when(me > 0)
    def _():
        down.start()

    @pl.when(me == 0)
    def _():
        left_ref[...] = jnp.zeros_like(left_ref)

    @pl.when(me == n - 1)
    def _():
        right_ref[...] = jnp.zeros_like(right_ref)


def rim_wait(n, me, up, down):
    @pl.when(me > 0)
    def _():
        up.wait_recv()
        down.wait_send()

    @pl.when(me < n - 1)
    def _():
        down.wait_recv()
        up.wait_send()


def land_exchange_kernel(
    n, mine_ref, rim_ref, all_ref, left_ref, right_ref, send, recv, rsend, rrecv
):
    me = greet_all(n)
    up, down = rim_copies(n, me, rim_ref, left_ref, right_ref, rsend, rrecv)
    copies = []
    for d in range(1, n):
        copy = to_seq(
            mine_ref, all_ref.at[me], send.at[d], recv.at[me], lax.rem(me + d, n)
        )
        copy.start()
        copies.append(copy)
    rim_start(n, me, up, down, left_ref, right_ref)
    all_ref[me] = mine_ref[...]
    for d in range(1, n):
        source = lax.rem(me + d, n)
        to_seq(mine_ref, all_ref.at[source], send.at[d], recv.at[source], source).wait_recv()
    rim_wait(n, me, up, down)
    for copy in copies:
        copy.wait_send()


def land_exchange(n, mine, rim):
    _, segs, width = mine.shape
    dma = pltpu.SemaphoreType.DMA
    return pl.pallas_call(
        partial(land_exchange_kernel, n),
        in_specs=[whole()] * 2,
        out_specs=[whole()] * 3,
        out_shape=[shape(n, 2, segs, width), shape(RIM, width), shape(RIM, width)],
        scratch_shapes=[dma((n,)), dma((n,)), dma((2,)), dma((2,))],
        compiler_params=params(collective_id=1, has_side_effects=True),
        name="land_exchange",
    )(mine, rim)


MSG = DH + 8


def eye(size):
    row = lax.broadcasted_iota(jnp.int32, (size, size), 0)
    col = lax.broadcasted_iota(jnp.int32, (size, size), 1)
    return jnp.where(row == col, 1.0, 0.0)


def pair_sums(row):
    lane = lax.broadcasted_iota(jnp.int32, row.shape, 1)
    first = jnp.sum(jnp.where(lane < DH, row, 0.0), axis=1, keepdims=True)
    second = jnp.sum(jnp.where(lane < DH, 0.0, row), axis=1, keepdims=True)
    return jnp.where(lane < DH, first, second)


def core_of(query, key, mask):
    scores = jnp.where(mask, mm_t(query, key, TOP) * SCALE, MASKED)
    raised = jnp.exp(scores - jnp.max(scores, axis=1, keepdims=True))
    return raised / jnp.sum(raised, axis=1, keepdims=True)


def far_exchange_kernel(
    n, f_ref, ql_ref, kl_ref, b_ref, core_ref, zs_ref, ps_ref, rs_ref, qs_ref, mx_ref,
    land, s1, r1, s2, r2,
):
    me = greet_all(n)
    for p in range(PAIRS):

        @pl.when(me != p)
        def _(p=p):
            to_seq(f_ref.at[p], land.at[me], s1.at[p], r1.at[me], p).start()

    @pl.when(me < PAIRS)
    def _():
        mask = head_mask(LANES)
        lanes = pl.ds(pl.multiple_of(me * LANES, LANES), LANES)
        query = spread(ql_ref[:, lanes], mask)
        key = spread(kl_ref[:, lanes], mask)
        core = core_of(query, key, mask)
        core_ref[...] = core
        colsum = jnp.sum(core, axis=0, keepdims=True)
        sigma = jnp.sqrt(pair_sums(colsum * colsum))
        z = core.T / sigma
        unit = eye(LANES)
        zs_ref[0] = z

        def newton(step, carry):
            z = zs_ref[step]
            prod = mm(core_ref[...], z, TOP)
            ps_ref[step] = prod
            r = 15.0 * unit - mm(prod, 7.0 * unit - prod, TOP)
            rs_ref[step] = r
            q = 13.0 * unit - mm(prod, r, TOP)
            qs_ref[step] = q
            zs_ref[step + 1] = 0.25 * mm(z, q, TOP)
            return carry

        lax.fori_loop(0, NEWTON, newton, 0)
        z = zs_ref[NEWTON]
        land[me] = f_ref[me]
        for s in range(n):

            @pl.when(me != s)
            def _(s=s):
                to_seq(f_ref.at[0], land.at[s], s1.at[0], r1.at[s], s).wait_recv()

        top = land[0][DH : DH + 1]
        for s in range(1, n):
            top = jnp.maximum(top, land[s][DH : DH + 1])
        total = jnp.zeros_like(top)
        mixed = jnp.zeros((DH, LANES), f32)
        for s in range(n):
            part = land[s]
            factor = jnp.exp(part[DH : DH + 1] - top)
            total = total + part[DH + 1 : DH + 2] * factor
            mixed = mixed + part[:DH] * factor
        mixed = mixed / total
        mx_ref[...] = mixed
        b_ref[me, 0:DH, :] = mm_t(mixed, z, TOP)
        pad = jnp.zeros((MSG - DH - 2, LANES), f32)
        b_ref[me, DH:MSG, :] = jnp.concatenate([top, total, pad], axis=0)
        for t in range(n):

            @pl.when(me != t)
            def _(t=t):
                to_seq(b_ref.at[me], b_ref.at[me], s2.at[t], r2.at[me], t).start()

    for p in range(PAIRS):

        @pl.when(me != p)
        def _(p=p):
            to_seq(b_ref.at[p], b_ref.at[p], s2.at[p], r2.at[p], p).wait_recv()
            to_seq(f_ref.at[p], land.at[me], s1.at[p], r1.at[me], p).wait_send()

    @pl.when(me < PAIRS)
    def _():
        for t in range(n):

            @pl.when(me != t)
            def _(t=t):
                to_seq(b_ref.at[me], b_ref.at[me], s2.at[t], r2.at[me], t).wait_send()


def far_exchange(n, parts, ql, kl):
    dma = pltpu.SemaphoreType.DMA
    square = (LANES, LANES)
    return pl.pallas_call(
        partial(far_exchange_kernel, n),
        in_specs=[whole()] * 3,
        out_specs=[whole()] * 7,
        out_shape=[
            shape(PAIRS, MSG, LANES), shape(*square), shape(NEWTON + 1, *square),
            shape(NEWTON, *square), shape(NEWTON, *square), shape(NEWTON, *square),
            shape(DH, LANES),
        ],
        scratch_shapes=[pltpu.VMEM((n, MSG, LANES), f32), dma((PAIRS,)), dma((n,)), dma((n,)), dma((n,))],
        compiler_params=params(collective_id=2, has_side_effects=True),
        name="far_exchange",
    )(parts, ql, kl)


def inverse_grad(gblend, mixed):
    return jnp.where(head_mask(LANES), t_mm(gblend, mixed, TOP), 0.0)


def newton_back(g, gcore, core, z, prod, r, q):
    prod_t = prod.T
    gq = 0.25 * mm(z.T, g, TOP)
    gr = -mm(prod_t, gq, TOP)
    gs = -mm(prod_t, gr, TOP)
    gp = -mm_t(gq, r, TOP) - mm_t(gr, 7.0 * eye(LANES) - prod, TOP) - gs
    return 0.25 * mm_t(g, q, TOP) + mm(core.T, gp, TOP), gcore + mm_t(gp, z, TOP)


def core_back(g, gcore, core, first, ql_ref, kl_ref, gl_ref, me):
    mask = head_mask(LANES)
    colsum = jnp.sum(core, axis=0, keepdims=True)
    square = pair_sums(colsum * colsum)
    sigma = jnp.sqrt(square)
    dot = pair_sums(jnp.sum(g * first, axis=0, keepdims=True))
    gcore = gcore + g.T / sigma - jnp.where(mask, dot / square * colsum, 0.0)
    gscore = core * (gcore - jnp.sum(core * gcore, axis=1, keepdims=True)) * SCALE
    lanes = pl.ds(pl.multiple_of(me * LANES, LANES), LANES)
    query = spread(ql_ref[:, lanes], mask)
    key = spread(kl_ref[:, lanes], mask)
    gl_ref[...] = jnp.zeros_like(gl_ref)
    gl_ref[0, :, lanes] = fold(mm(gscore, key, TOP), mask)
    gl_ref[1, :, lanes] = fold(t_mm(gscore, query, TOP), mask)


def blend_exchange_kernel(
    n, g_ref, rim_ref, ql_ref, kl_ref, core_ref, zs_ref, ps_ref, rs_ref, qs_ref, mx_ref,
    c_ref, left_ref, right_ref, gl_ref,
    land, s1, r1, s2, r2, rsend, rrecv,
):
    me = greet_all(n)
    for p in range(PAIRS):

        @pl.when(me != p)
        def _(p=p):
            to_seq(g_ref.at[p], land.at[me], s1.at[p], r1.at[me], p).start()

    up, down = rim_copies(n, me, rim_ref, left_ref, right_ref, rsend, rrecv)
    rim_start(n, me, up, down, left_ref, right_ref)

    @pl.when(me >= PAIRS)
    def _():
        gl_ref[...] = jnp.zeros_like(gl_ref)

    @pl.when(me < PAIRS)
    def _():
        mask = head_mask(LANES)
        land[me] = g_ref[me]
        for s in range(n):

            @pl.when(me != s)
            def _(s=s):
                to_seq(g_ref.at[0], land.at[s], s1.at[0], r1.at[s], s).wait_recv()

        gblend = land[0]
        for s in range(1, n):
            gblend = gblend + land[s]
        mixed = mx_ref[...]
        gmixed = mm(gblend, zs_ref[NEWTON], TOP)
        c_ref[me, 0:DH, :] = gmixed
        dots = jnp.sum(gmixed * mixed, axis=0, keepdims=True)
        pad = jnp.zeros((MSG - DH - 1, LANES), f32)
        c_ref[me, DH:MSG, :] = jnp.concatenate([dots, pad], axis=0)
        for t in range(n):

            @pl.when(me != t)
            def _(t=t):
                to_seq(c_ref.at[me], c_ref.at[me], s2.at[t], r2.at[me], t).start()

        gcore = jnp.zeros((LANES, LANES), f32)
        g = inverse_grad(gblend, mixed)
        for step in reversed(range(NEWTON)):
            g, gcore = newton_back(g, gcore, core_ref[...], zs_ref[step], ps_ref[step], rs_ref[step], qs_ref[step])
        core_back(g, gcore, core_ref[...], zs_ref[0], ql_ref, kl_ref, gl_ref, me)

    for p in range(PAIRS):

        @pl.when(me != p)
        def _(p=p):
            to_seq(c_ref.at[p], c_ref.at[p], s2.at[p], r2.at[p], p).wait_recv()
            to_seq(g_ref.at[p], land.at[me], s1.at[p], r1.at[me], p).wait_send()

    rim_wait(n, me, up, down)

    @pl.when(me < PAIRS)
    def _():
        for t in range(n):

            @pl.when(me != t)
            def _(t=t):
                to_seq(c_ref.at[me], c_ref.at[me], s2.at[t], r2.at[me], t).wait_send()


def blend_exchange(n, gblend, rim, ql, kl, saved):
    dma = pltpu.SemaphoreType.DMA
    width = rim.shape[1]
    return pl.pallas_call(
        partial(blend_exchange_kernel, n),
        in_specs=[whole()] * 10,
        out_specs=[whole()] * 4,
        out_shape=[shape(PAIRS, MSG, LANES), shape(RIM, width), shape(RIM, width), shape(2, DH, width)],
        scratch_shapes=[
            pltpu.VMEM((n, DH, LANES), f32),
            dma((PAIRS,)), dma((n,)), dma((n,)), dma((n,)), dma((2,)), dma((2,)),
        ],
        compiler_params=params(collective_id=3, has_side_effects=True),
        name="blend_exchange",
    )(gblend, rim, ql, kl, *saved)


def land_return_kernel(n, x_ref, own_ref, land, send, recv):
    me = greet_all(n)
    copies = []
    for d in range(1, n):
        target = lax.rem(me + d, n)
        copy = to_seq(x_ref.at[target], land.at[me], send.at[d], recv.at[me], target)
        copy.start()
        copies.append(copy)
    land[me] = x_ref[me]
    for d in range(1, n):
        source = lax.rem(me + d, n)
        to_seq(x_ref.at[0], land.at[source], send.at[d], recv.at[source], source).wait_recv()
    total = land[0]
    for s in range(1, n):
        total = total + land[s]
    own_ref[...] = total
    for copy in copies:
        copy.wait_send()


def land_return(n, parts):
    dma = pltpu.SemaphoreType.DMA
    return pl.pallas_call(
        partial(land_return_kernel, n),
        in_specs=[whole()],
        out_specs=whole(),
        out_shape=shape(*parts.shape[1:]),
        scratch_shapes=[pltpu.VMEM(parts.shape, f32), dma((n,)), dma((n,))],
        compiler_params=params(collective_id=4, has_side_effects=True),
        name="land_return",
    )(parts)


def far_kernel(lens_ref, k_ref, v_ref, ql_ref, f_ref, p_ref, m_ref):
    slots = k_ref.shape[0]
    count = seg_ends(lens_ref, lens_ref.shape[1])[-1]
    valid = valid_rows(count, slots)
    mask = head_mask(QUAD)

    def one(g, carry):
        cols = quad(g)
        scores = mm_t(k_ref[:, cols], spread(ql_ref[:, cols], mask)) * SCALE
        scores = jnp.where(valid, scores, MASKED)
        top = jnp.max(scores, axis=0, keepdims=True)
        raised = jnp.where(valid, jnp.exp(scores - top), 0.0)
        p_ref[:, cols] = raised
        m_ref[:, cols] = top
        total = jnp.sum(raised, axis=0, keepdims=True)
        weighted = fold(t_mm(v_ref[:, cols], raised), mask)
        tail = jnp.concatenate([top, total, jnp.zeros((MSG - DH - 2, QUAD), f32)], axis=0)
        for j in range(QUAD // LANES):
            part = slice(j * LANES, (j + 1) * LANES)
            f_ref[g * 2 + j, 0:DH, :] = weighted[:, part]
            f_ref[g * 2 + j, DH:MSG, :] = tail[:, part]
        return carry

    lax.fori_loop(0, QUADS, one, 0)


def far_local(lens, k, v, ql):
    slots, width = k.shape
    return pl.pallas_call(
        far_kernel,
        in_specs=[smem()] + [whole()] * 3,
        out_specs=[whole()] * 3,
        out_shape=[shape(PAIRS, MSG, LANES), shape(slots, width), shape(1, width)],
        compiler_params=params(),
        name="far_local",
    )(lens, k, v, ql)


def norm_stats(r):
    centered = r - jnp.mean(r, axis=1, keepdims=True)
    spread_ = jnp.mean(centered * centered, axis=1, keepdims=True)
    inv = lax.rsqrt(spread_ + EPS)
    return centered * inv, inv


def norm_back(unit, inv, gain, grad):
    ge = grad * gain
    return (
        ge
        - jnp.mean(ge, axis=1, keepdims=True)
        - unit * jnp.mean(ge * unit, axis=1, keepdims=True)
    ) * inv


def quad(g):
    return pl.ds(pl.multiple_of(g * QUAD, QUAD), QUAD)


def pair_rows(ref, g, rows):
    return jnp.concatenate([ref[2 * g, rows, :], ref[2 * g + 1, rows, :]], axis=1)


def attend_kernel(
    lens_ref, q_ref, v_ref, kl_ref, b_ref, left_ref, right_ref, taps_ref, x_ref, wo_ref, bo_ref, g1_ref, b1_ref,
    near_ref, ctx_ref, h1_ref, u1_ref, inv1_ref, ext_ref,
):
    slots = q_ref.shape[0]
    count = seg_ends(lens_ref, lens_ref.shape[1])[-1]
    fill_extended(ext_ref, v_ref[...], left_ref[...], right_ref[...], count)
    conv_into(ctx_ref, ext_ref, taps_ref, slots, False, False)
    mask = head_mask(QUAD)
    ones = jnp.where(mask, 1.0, 0.0)
    head = lax.broadcasted_iota(jnp.int32, (slots, QUAD), 1) >> 6

    def one(g, carry):
        cols = quad(g)
        scores = mm_t(q_ref[:, cols], spread(kl_ref[:, cols], mask)) * SCALE
        tops = [jnp.max(scores[:, h * DH : (h + 1) * DH], axis=1, keepdims=True) for h in range(4)]
        top = jnp.where(head < 2, jnp.where(head < 1, tops[0], tops[1]), jnp.where(head < 3, tops[2], tops[3]))
        raised = jnp.exp(scores - top)
        near = raised / mm(raised, ones)
        near_ref[:, cols] = near
        blend = spread(pair_rows(b_ref, g, slice(0, DH)), mask)
        ctx_ref[:, cols] += mm_t(near, blend)
        return carry

    lax.fori_loop(0, QUADS, one, 0)

    def two(g, carry):
        cols = quad(g)
        u1_ref[:, cols] = mm(ctx_ref[...], wo_ref[:, cols])
        return carry

    lax.fori_loop(0, QUADS, two, 0)
    summed = x_ref[...] + (u1_ref[...] + bo_ref[...][None, :])
    unit, inv = norm_stats(summed)
    u1_ref[...] = unit
    inv1_ref[...] = inv
    h1_ref[...] = unit * g1_ref[...][None, :] + b1_ref[...][None, :]


def attend(lens, q, v, kl, b, left, right, taps, x, wo, bo, g1, b1):
    slots, width = q.shape
    return pl.pallas_call(
        attend_kernel,
        in_specs=[smem()] + [whole()] * 12,
        out_specs=[whole()] * 6,
        out_shape=[shape(slots, width)] * 4 + [shape(slots, 1), shape(slots + 40, width)],
        compiler_params=params(),
        name="attend",
    )(lens, q, v, kl, b, left, right, taps, x, wo, bo, g1, b1)


def forward_kernel(
    lens_ref, h1_ref, wi_ref, bi_ref, wo_ref, bo_ref, cot_ref, g2_ref, b2_ref,
    pre_ref, out_ref, gs2_ref, small_ref,
    acc_ref, act_ref,
):
    step = pl.program_id(0)

    @pl.when(step == 0)
    def _():
        acc_ref[...] = jnp.zeros_like(acc_ref)

    def one(g, carry):
        cols = quad(g)
        pre = mm(h1_ref[...], wi_ref[:, cols]) + bi_ref[:, cols]
        pre_ref[:, cols] = pre
        act_ref[:, cols] = 0.5 * pre * (1.0 + lax.erf(pre * ROOT_HALF))
        return carry

    lax.fori_loop(0, QUADS, one, 0)

    def two(g, carry):
        cols = quad(g)
        acc_ref[:, cols] += mm(act_ref[...], wo_ref[:, cols])
        return carry

    lax.fori_loop(0, QUADS, two, 0)

    @pl.when(step == pl.num_programs(0) - 1)
    def _():
        slots = h1_ref.shape[0]
        valid = valid_rows(seg_ends(lens_ref, lens_ref.shape[1])[-1], slots)
        summed = h1_ref[...] + (acc_ref[...] + bo_ref[...][None, :])
        unit, inv = norm_stats(summed)
        out_ref[...] = jnp.where(valid, unit * g2_ref[...][None, :] + b2_ref[...][None, :], 0.0)
        e = jnp.where(valid, cot_ref[...], 0.0)
        grad = norm_back(unit, inv, g2_ref[...][None, :], e)
        gs2_ref[...] = grad
        small_ref[...] = jnp.concatenate(
            [
                jnp.sum(e * unit, axis=0, keepdims=True),
                jnp.sum(e, axis=0, keepdims=True),
                jnp.sum(grad, axis=0, keepdims=True),
                jnp.zeros((5, e.shape[1]), f32),
            ],
            axis=0,
        )


def ffn_forward(lens, h1, wi, bi, wo, bo, cot, g2, b2):
    slots, width = h1.shape
    inner = wi.shape[1]
    const = lambda *dims: pl.BlockSpec(dims, lambda j: (0,) * len(dims))
    return pl.pallas_call(
        forward_kernel,
        grid=(inner // width,),
        in_specs=[
            smem(), const(slots, width),
            pl.BlockSpec((width, width), lambda j: (0, j)), pl.BlockSpec((1, width), lambda j: (0, j)),
            pl.BlockSpec((width, width), lambda j: (j, 0)), const(width),
            const(slots, width), const(width), const(width),
        ],
        out_specs=[
            pl.BlockSpec((slots, width), lambda j: (0, j)),
            const(slots, width), const(slots, width), const(8, width),
        ],
        out_shape=[shape(slots, inner), shape(slots, width), shape(slots, width), shape(8, width)],
        scratch_shapes=[pltpu.VMEM((slots, width), f32)] * 2,
        compiler_params=params(),
        name="ffn_forward",
    )(lens, h1, wi, bi, wo, bo, cot, g2, b2)


def put_strips(ref, block, rows=slice(None), first=0):
    for s in range(block.shape[1] // LANES):
        ref[first + s, rows, :] = block[:, s * LANES : (s + 1) * LANES]


def backward_kernel(
    h1_ref, gs2_ref, pre_ref, wi_ref, wo_ref, u1_ref, inv1_ref, g1_ref,
    dwo_ref, dwi_ref, gs1_ref, dbi_ref, small_ref,
    acc_ref, gpre_ref,
):
    step = pl.program_id(0)

    @pl.when(step == 0)
    def _():
        acc_ref[...] = gs2_ref[...]

    def one(g, carry):
        cols = quad(g)
        pre = pre_ref[:, cols]
        phi_big = 0.5 * (1.0 + lax.erf(pre * ROOT_HALF))
        slope = phi_big + pre * (INV_ROOT_TAU * jnp.exp(-0.5 * pre * pre))
        gpre = mm_t(gs2_ref[...], wo_ref[cols, :]) * slope
        gpre_ref[:, cols] = gpre
        dbi_ref[:, cols] = jnp.sum(gpre, axis=0, keepdims=True)
        put_strips(dwo_ref, t_mm(pre * phi_big, gs2_ref[...]), cols)
        return carry

    lax.fori_loop(0, QUADS, one, 0)

    def two(g, carry):
        cols = quad(g)
        put_strips(dwi_ref, t_mm(h1_ref[:, cols], gpre_ref[...]), cols)
        acc_ref[:, cols] += mm_t(gpre_ref[...], wi_ref[cols, :])
        return carry

    lax.fori_loop(0, QUADS, two, 0)

    @pl.when(step == pl.num_programs(0) - 1)
    def _():
        e = acc_ref[...]
        unit = u1_ref[...]
        grad = norm_back(unit, inv1_ref[...], g1_ref[...][None, :], e)
        gs1_ref[...] = grad
        small_ref[...] = jnp.concatenate(
            [
                jnp.sum(e * unit, axis=0, keepdims=True),
                jnp.sum(e, axis=0, keepdims=True),
                jnp.sum(grad, axis=0, keepdims=True),
                jnp.zeros((5, e.shape[1]), f32),
            ],
            axis=0,
        )


def ffn_backward(h1, gs2, pre, wi, wo, u1, inv1, g1):
    slots, width = h1.shape
    inner = wi.shape[1]
    strips = width // LANES
    const = lambda *dims: pl.BlockSpec(dims, lambda j: (0,) * len(dims))
    return pl.pallas_call(
        backward_kernel,
        grid=(inner // width,),
        in_specs=[
            const(slots, width), const(slots, width),
            pl.BlockSpec((slots, width), lambda j: (0, j)),
            pl.BlockSpec((width, width), lambda j: (0, j)),
            pl.BlockSpec((width, width), lambda j: (j, 0)),
            const(slots, width), const(slots, 1), const(width),
        ],
        out_specs=[
            pl.BlockSpec((strips, width, LANES), lambda j: (j, 0, 0)),
            pl.BlockSpec((strips, width, LANES), lambda j: (j, 0, 0)),
            const(slots, width),
            pl.BlockSpec((1, width), lambda j: (0, j)),
            const(8, width),
        ],
        out_shape=[
            shape(inner // LANES, width, LANES), shape(inner // LANES, width, LANES),
            shape(slots, width), shape(1, inner), shape(8, width),
        ],
        scratch_shapes=[pltpu.VMEM((slots, width), f32)] * 2,
        compiler_params=params(),
        name="ffn_backward",
    )(h1, gs2, pre, wi, wo, u1, inv1, g1)


def near_back_quad(g, gctx_ref, near_ref, q_ref, kl_ref, b_ref, gq_ref, gb_ref, gkl_ref):
    mask = head_mask(QUAD)
    ones = jnp.where(mask, 1.0, 0.0)
    cols = quad(g)
    gctx = gctx_ref[:, cols]
    near = near_ref[:, cols]
    gblend = fold(t_mm(gctx, near), mask)
    gb_ref[2 * g] = gblend[:, :LANES]
    gb_ref[2 * g + 1] = gblend[:, LANES:]
    gnear = mm(gctx, spread(pair_rows(b_ref, g, slice(0, DH)), mask))
    gscore = near * (gnear - mm(near * gnear, ones)) * SCALE
    gq_ref[:, cols] = mm(gscore, spread(kl_ref[:, cols], mask))
    gkl_ref[:, cols] = fold(t_mm(gscore, q_ref[:, cols]), mask)


def near_back_kernel(
    lens_ref, gs1_ref, wo_ref, near_ref, q_ref, kl_ref, b_ref,
    gctx_ref, gq_ref, gb_ref, gkl_ref, rim_ref,
):
    count = seg_ends(lens_ref, lens_ref.shape[1])[-1]
    gctx_ref[...] = mm_t(gs1_ref[...], wo_ref[...])
    rim_ref[...] = rims_of(gctx_ref[...], count)
    def one(g, carry):
        near_back_quad(g, gctx_ref, near_ref, q_ref, kl_ref, b_ref, gq_ref, gb_ref, gkl_ref)
        return carry

    lax.fori_loop(0, QUADS, one, 0)


def near_back(lens, gs1, wo, near, q, kl, b):
    slots, width = gs1.shape
    return pl.pallas_call(
        near_back_kernel,
        in_specs=[smem()] + [whole()] * 6,
        out_specs=[whole()] * 5,
        out_shape=[
            shape(slots, width), shape(slots, width), shape(PAIRS, DH, LANES),
            shape(DH, width), shape(2 * RIM, width),
        ],
        compiler_params=params(),
        name="near_back",
    )(lens, gs1, wo, near, q, kl, b)


def far_back_quad(g, k_ref, v_ref, p_ref, m_ref, b_ref, c_ref, ql_ref, gk_ref, gv_ref, gql_ref, add):
    mask = head_mask(QUAD)
    cols = quad(g)
    top = pair_rows(b_ref, g, slice(DH, DH + 1))
    total = pair_rows(b_ref, g, slice(DH + 1, DH + 2))
    prob = p_ref[:, cols] * (jnp.exp(m_ref[:, cols] - top) / total)
    gmixed = spread(pair_rows(c_ref, g, slice(0, DH)), mask)
    dots = pair_rows(c_ref, g, slice(DH, DH + 1))
    gscore = prob * (mm(v_ref[:, cols], gmixed) - dots) * SCALE
    gk_ref[:, cols] = mm(gscore, spread(ql_ref[:, cols], mask))
    gval = mm_t(prob, gmixed)
    if add:
        gv_ref[:, cols] += gval
    else:
        gv_ref[:, cols] = gval
    gql_ref[:, cols] = fold(t_mm(gscore, k_ref[:, cols]), mask)


def land_parts(ret_ref, gql, gkl):
    n, _, segs, _ = ret_ref.shape
    for s in range(n):
        rows = slice(s * segs, (s + 1) * segs)
        ret_ref[s, 0] = gql[rows]
        ret_ref[s, 1] = gkl[rows]


def far_back_kernel(
    k_ref, v_ref, p_ref, m_ref, b_ref, c_ref, ql_ref, gkl_ref, gl_ref,
    gk_ref, gv_ref, ret_ref, gql_ref,
):
    def one(g, carry):
        far_back_quad(g, k_ref, v_ref, p_ref, m_ref, b_ref, c_ref, ql_ref, gk_ref, gv_ref, gql_ref, False)
        return carry

    lax.fori_loop(0, QUADS, one, 0)
    land_parts(ret_ref, gql_ref[...] + gl_ref[0], gkl_ref[...] + gl_ref[1])


def far_back(n, lens, k, v, p, m, b, c, ql, gkl, gl):
    slots, width = k.shape
    segs = lens.shape[1]
    return pl.pallas_call(
        far_back_kernel,
        in_specs=[whole()] * 9,
        out_specs=[whole()] * 3,
        out_shape=[shape(slots, width), shape(slots, width), shape(n, 2, segs, width)],
        scratch_shapes=[pltpu.VMEM((DH, width), f32)],
        compiler_params=params(),
        name="far_back",
    )(k, v, p, m, b, c, ql, gkl, gl)


def taps_sums(scr_ref):
    width = scr_ref.shape[2]
    rows = jnp.concatenate(
        [jnp.sum(scr_ref[c], axis=0, keepdims=True) for c in range(CONV)] + [jnp.zeros((7, width), f32)], axis=0
    )
    row = lax.broadcasted_iota(jnp.int32, (width, LANES), 0) >> 6
    col = lax.broadcasted_iota(jnp.int32, (width, LANES), 1)
    return mm(rows, jnp.where(row == col, 1.0, 0.0), TOP)


def conv_back_kernel(
    lens_ref, v_ref, left_ref, right_ref, gctx_ref, gleft_ref, gright_ref, taps_ref, ctx_ref, gs1_ref,
    gv_ref, gtaps_ref, dwo_ref,
    ext_ref, scr_ref,
):
    slots = v_ref.shape[0]
    count = seg_ends(lens_ref, lens_ref.shape[1])[-1]
    put_strips(dwo_ref, t_mm(ctx_ref[...], gs1_ref[...]))
    fill_extended(ext_ref, gctx_ref[...], gleft_ref[...], gright_ref[...], count)
    conv_into(gv_ref, ext_ref, taps_ref, slots, True, False)
    fill_extended(ext_ref, v_ref[...], left_ref[...], right_ref[...], count)
    taps_grad_into(scr_ref, gctx_ref, ext_ref, slots)
    gtaps_ref[...] = taps_sums(scr_ref)


def conv_back(lens, v, left, right, gctx, gleft, gright, taps, ctx, gs1):
    slots, width = v.shape
    return pl.pallas_call(
        conv_back_kernel,
        in_specs=[smem()] + [whole()] * 9,
        out_specs=[whole()] * 3,
        out_shape=[shape(slots, width), shape(40, LANES), shape(width // LANES, width, LANES)],
        scratch_shapes=[pltpu.VMEM((slots + 40, width), f32), pltpu.VMEM((CONV, 8, width), f32)],
        compiler_params=params(),
        name="conv_back",
    )(lens, v, left, right, gctx, gleft, gright, taps, ctx, gs1)


def project_back_kernel(
    lens_ref, x_ref, gs1_ref, gqn_ref, gkf_ref, gvc_ref, gvf_ref, own_ref, wq_ref, wk_ref, wv_ref,
    ig_ref, dq_ref, dk_ref, dv_ref, small_ref,
    gq_ref, gk_ref, gv_ref,
):
    @pl.when(pl.program_id(0) == 0)
    def _():
        slots = gqn_ref.shape[0]
        segs = own_ref.shape[1]
        ends = seg_ends(lens_ref, segs)
        member = member_rows(ends, slots)
        inv = inverse_lens(lens_ref, segs)
        gq = gqn_ref[...] + t_mm(member, own_ref[0] * inv)
        gk = gkf_ref[...] + t_mm(member, own_ref[1] * inv)
        gv = jnp.where(valid_rows(ends[-1], slots), gvc_ref[...] + gvf_ref[...], 0.0)
        gq_ref[...] = gq
        gk_ref[...] = gk
        gv_ref[...] = gv
        small_ref[...] = jnp.concatenate(
            [
                jnp.sum(gq, axis=0, keepdims=True),
                jnp.sum(gv, axis=0, keepdims=True),
                jnp.zeros((6, gq.shape[1]), f32),
            ],
            axis=0,
        )

    x = x_ref[...]
    put_strips(dq_ref, t_mm(x, gq_ref[...]))
    put_strips(dk_ref, t_mm(x, gk_ref[...]))
    put_strips(dv_ref, t_mm(x, gv_ref[...]))
    ig_ref[...] = (
        gs1_ref[...]
        + mm_t(gq_ref[...], wq_ref[...])
        + mm_t(gk_ref[...], wk_ref[...])
        + mm_t(gv_ref[...], wv_ref[...])
    )


def project_back(lens, x, gs1, gqn, gkf, gvc, gvf, own, wq, wk, wv):
    slots, width = x.shape
    col = 256
    strips = width // LANES
    const = lambda *dims: pl.BlockSpec(dims, lambda i: (0,) * len(dims))
    part = pl.BlockSpec((slots, col), lambda i: (0, i))
    wspec = pl.BlockSpec((col, width), lambda i: (i, 0))
    dspec = pl.BlockSpec((strips, col, LANES), lambda i: (0, i, 0))
    return pl.pallas_call(
        project_back_kernel,
        grid=(width // col,),
        in_specs=[smem(), part, part] + [const(slots, width)] * 4 + [const(*own.shape), wspec, wspec, wspec],
        out_specs=[part, dspec, dspec, dspec, const(8, width)],
        out_shape=[shape(slots, width)] + [shape(strips, width, LANES)] * 3 + [shape(8, width)],
        scratch_shapes=[pltpu.VMEM((slots, width), f32)] * 3,
        compiler_params=params(),
        name="project_back",
    )(lens, x, gs1, gqn, gkf, gvc, gvf, own, wq, wk, wv)


def sum_plain(parts):
    sizes = [part.size for part in parts]
    shapes = [part.shape for part in parts]
    devices = lax.axis_size(("seq", "dp"))
    flat = jnp.concatenate([part.reshape(-1) for part in parts])
    flat = jnp.pad(flat, (0, -flat.shape[0] % devices))
    own = lax.psum_scatter(flat, ("seq", "dp"), scatter_dimension=0, tiled=True)
    flat = lax.all_gather(own, ("seq", "dp"), axis=0, tiled=True)
    out = []
    at = 0
    for size, dims in zip(sizes, shapes):
        out.append(flat[at : at + size].reshape(dims))
        at += size
    return out


STRIP = 768
HALF = STRIP // 2
PART = HALF // 2
Z_ROWS = PART // 4
OWN = Z_ROWS // 2
STAGES = 13
SMALL_STEPS = 5


def pack_small(sb_ref, small0, small1, small2, inner_bias, taps):
    at = 0
    for ref, count in ((small0, 2), (small1, 3), (small2, 3), (inner_bias, 1)):
        for r in range(count):
            for j in range(ref.shape[1] // LANES):
                sb_ref[0, at : at + 1, :] = ref[r : r + 1, j * LANES : (j + 1) * LANES]
                at += 1
    sb_ref[0, at : at + 40, :] = taps[...]


SMALL_ROWS = 8 * 6 + 24 + 40


def unpack_small(s_ref, outs):
    at = 0
    for ref in outs[:-1]:
        for j in range(ref.shape[0] // LANES):
            ref[pl.ds(j * LANES, LANES)] = s_ref[at, :]
            at += 1
    outs[-1][...] = s_ref[at : at + CONV, :HEADS]


def reduce_stages(spans, grads, o_ref, bufs, sems):
    acc, lc, l1, lz, l3 = bufs
    local, out_local, cs, cr, s1, r1, zs, zr, s3, r3, s4, r4, gs, gr, s5, r5, es, er = sems
    seq = lax.axis_index("seq")
    dp = lax.axis_index("dp")
    z = seq // 2
    c = lax.rem(seq, 2)
    y = dp // 2
    x = lax.rem(dp, 2)
    zb = 3 - z
    place = lambda z_, c_, y_, x_: (z_ * 2 + c_, y_ * 2 + x_)
    by_core = place(z, 1 - c, y, x)
    by_x = place(z, c, y, 1 - x)
    by_y = place(z, c, 1 - y, x)
    right = place(lax.rem(z + 1, 4), c, y, x)
    left = place(lax.rem(z + 3, 4), c, y, x)
    opposite = place(lax.rem(z + 2, 4), c, y, x)
    near_z = place(z + 1 - 2 * lax.rem(z, 2), c, y, x)

    def remote(src, dst, send, recv, target):
        return pltpu.make_async_remote_copy(src, dst, send, recv, device_id=target, device_id_type=MESH)

    aligned = lambda at: pl.multiple_of(at, 8)
    slot = lambda ref, k: lax.rem(k, ref.shape[0])
    a1 = x * PART
    b1 = HALF + y * PART
    firsts = ((0, a1, (1 - x) * PART, by_x), (1, b1, HALF + (1 - y) * PART, by_y))
    starts = (a1, b1)
    az = a1 + z * Z_ROWS
    bz = b1 + z * Z_ROWS
    thirds = (
        (0, az + y * OWN, az + (1 - y) * OWN, by_y),
        (1, bz + x * OWN, bz + (1 - x) * OWN, by_x),
    )

    def rows(ref, k, at, size):
        return ref.at[k, pl.ds(aligned(at), size)]

    def acc_rows(k, at, size):
        return rows(acc, slot(acc, k), at, size)

    def core_copies(k, g, lo):
        mine = pltpu.make_async_copy(g.at[2 * (k - lo) + c], acc.at[slot(acc, k)], local.at[k])
        other = remote(g.at[2 * (k - lo) + 1 - c], lc.at[slot(lc, k)], cs.at[k], cr.at[k], by_core)
        return mine, other

    def core_out(k):
        for g, (lo, hi) in zip(grads, spans):

            @pl.when((k >= lo) & (k < hi))
            def _(g=g, lo=lo):
                for copy in core_copies(k, g, lo):
                    copy.start()

    def first(k, j):
        _, _, other, target = firsts[j]
        return remote(acc_rows(k, other, PART), l1.at[slot(l1, k), j], s1.at[k, j], r1.at[k, j], target)

    def first_out(k):
        mine, other = core_copies(k, grads[0], k)
        mine.wait()
        other.wait_recv()
        acc[slot(acc, k)] += lc[slot(lc, k)]
        for j in range(2):
            first(k, j).start()

    def z_copy(k, j, way, step, block):
        target = right if way == 0 else left
        return remote(
            acc_rows(k, starts[j] + block * Z_ROWS, Z_ROWS), lz.at[slot(lz, k), way, j, step],
            zs.at[k, way, step, j], zr.at[k, way, step, j], target,
        )

    def z_out(k, step):
        if step == 0:
            for j, mine, _, _ in firsts:
                first(k, j).wait_recv()
                acc[slot(acc, k), pl.ds(aligned(mine), PART)] += l1[slot(l1, k), j]
        for way, at in ((0, z), (1, zb)):
            block = 3 - step + z if way == 0 else step - zb
            if step > 0:

                @pl.when((at > 0) & (at <= step))
                def _(way=way, block=block):
                    for j in range(2):
                        z_copy(k, j, way, step - 1, 0).wait_recv()
                        here = (slot(acc, k), pl.ds(aligned(starts[j] + block * Z_ROWS), Z_ROWS))
                        acc[here] += lz[slot(lz, k), way, j, step - 1]

            if step < 3:

                @pl.when((at <= step) & (at < 3))
                def _(way=way, block=block):
                    for j in range(2):
                        z_copy(k, j, way, step, block).start()

    def third(k, j):
        _, _, other, target = thirds[j]
        return remote(acc_rows(k, other, OWN), l3.at[slot(l3, k), j], s3.at[k, j], r3.at[k, j], target)

    def third_out(k):
        z_out(k, 3)
        for j in range(2):
            third(k, j).start()

    def back_third(k, j):
        _, mine, _, target = thirds[j]
        return remote(acc_rows(k, mine, OWN), rows(o_ref.at[c], k, mine, OWN), s4.at[k, j], r4.at[k, j], target)

    def keep(k, j):
        mine = thirds[j][1]
        return pltpu.make_async_copy(acc_rows(k, mine, OWN), rows(o_ref.at[c], k, mine, OWN), out_local.at[k, j])

    def back_third_out(k):
        for j, mine, _, _ in thirds:
            third(k, j).wait_recv()
            acc[slot(acc, k), pl.ds(aligned(mine), OWN)] += l3[slot(l3, k), j]
        for j in range(2):
            back_third(k, j).start()
            keep(k, j).start()

    def back_z(k, j, way, step, block):
        target = right if way == 0 else left
        part = rows(o_ref.at[c], k, starts[j] + block * Z_ROWS, Z_ROWS)
        return remote(part, part, gs.at[k, way, step, j], gr.at[k, way, step, j], target)

    def back_z_out(k, step):
        if step == 0:
            core_copies(k, grads[0], k)[1].wait_send()
            for j in range(2):
                keep(k, j).wait()
                first(k, j).wait_send()
                third(k, j).wait_send()
                back_third(k, j).wait()
            for s in range(3):
                for way, at in ((0, z), (1, zb)):

                    @pl.when((at <= s) & (at < 3))
                    def _(way=way, s=s):
                        for j in range(2):
                            z_copy(k, j, way, s, 0).wait_send()

        for way, at in ((0, z), (1, zb)):
            block = z - step if way == 0 else z + step
            if step > 0:

                @pl.when(at >= step)
                def _(way=way):
                    for j in range(2):
                        back_z(k, j, way, step - 1, 0).wait_recv()

            if step < 3:

                @pl.when((at >= step) & (at < 3))
                def _(way=way, block=block):
                    for j in range(2):
                        back_z(k, j, way, step, block).start()

    def back_first(k, j):
        _, mine, _, target = firsts[j]
        part = rows(o_ref.at[c], k, mine, PART)
        return remote(part, part, s5.at[k, j], r5.at[k, j], target)

    def back_first_out(k):
        back_z_out(k, 3)
        for j in range(2):
            back_first(k, j).start()

    def back_core(k):
        part = o_ref.at[c, k]
        return remote(part, part, es.at[k], er.at[k], by_core)

    def back_core_out(k):
        for j in range(2):
            back_first(k, j).wait_recv()
        back_core(k).start()

    def finish(k):
        back_core(k).wait()
        for j in range(2):
            back_first(k, j).wait_send()
        for step in range(3):
            for way, at in ((0, z), (1, zb)):

                @pl.when((at >= step) & (at < 3))
                def _(way=way, step=step):
                    for j in range(2):
                        back_z(k, j, way, step, 0).wait_send()

    stages = [
        core_out, first_out, partial(z_out, step=0), partial(z_out, step=1), partial(z_out, step=2), third_out,
        back_third_out, partial(back_z_out, step=0), partial(back_z_out, step=1), partial(back_z_out, step=2),
        back_first_out, back_core_out, finish,
    ]
    return stages, (by_core, by_x, by_y, near_z, opposite), remote


LAG = tuple(range(0, 2 * STAGES, 2))
RING_ACC = 16
RING_LC = 4
RING_Z = 6
SEQ_DEVICES = 8
SMALL_AT = 24


def greet_block():
    seq = lax.axis_index("seq")
    dp = lax.axis_index("dp")
    y = dp // 2
    x = lax.rem(dp, 2)
    barrier = pltpu.get_barrier_semaphore()
    for d in range(1, SEQ_DEVICES):
        pl.semaphore_signal(
            barrier, inc=1, device_id=(lax.rem(seq + d, SEQ_DEVICES), dp), device_id_type=MESH
        )
    for other in (y * 2 + 1 - x, (1 - y) * 2 + x):
        pl.semaphore_signal(barrier, inc=1, device_id=(seq, other), device_id_type=MESH)
    pl.semaphore_wait(barrier, SEQ_DEVICES + 1)
    return seq


def tail_kernel(
    spans,
    lens_ref, dout_ref, din_ref, gs1_hbm, wo_hbm, near_hbm, q_hbm, ctx_hbm, ext_hbm, k_hbm, v_hbm, p_hbm, x_hbm,
    wq_hbm, wk_hbm, wv_hbm,
    m_ref, b_ref, ql_ref, kl_ref, core_ref, zs_ref, ps_ref, rs_ref, qs_ref, mx_ref, taps_ref,
    small1_ref, small2_ref, dbi_ref,
    o_ref, so_ref, ig_hbm,
    acc, lc, l1, lz, l3, sb, sl, gw,
    stack, w, ext, k, v, gext, tap_scr, gtaps, small0,
    gb, rim, gkl, gql, gl, land, cmsg, gleft, gright, ng, ncore, ret, rland, own,
    loads, ig_sem, b1s, b1r, b2s, b2r, ms, mr, rets, retr, ss, sr,
    *sems,
):
    n = SEQ_DEVICES
    chunks = spans[-1][1]
    slots = k.shape[0]
    segs = own.shape[1]
    gs1, near, p, gv, ctx, q, gctx, ig = [stack.at[i] for i in range(8)]

    def load(i, src, dst):
        return pltpu.make_async_copy(src, dst, loads.at[i])

    early = [
        load(0, gs1_hbm, gs1), load(1, wo_hbm, w.at[0]), load(2, near_hbm, near), load(3, q_hbm, q), load(4, ctx_hbm, ctx),
        load(5, ext_hbm, ext), load(6, v_hbm, v), load(7, p_hbm, p), load(8, k_hbm, k),
    ]
    late = [load(9, x_hbm, q), load(10, wq_hbm, w.at[1]), load(11, wk_hbm, w.at[2]), load(12, wv_hbm, w.at[3])]
    for copy in early:
        copy.start()
    me = greet_block()
    owner = me < PAIRS
    stages, partners, remote = reduce_stages(spans, (dout_ref, din_ref, gw), o_ref, (acc, lc, l1, lz, l3), sems)
    ends = seg_ends(lens_ref, segs)
    count = ends[-1]

    def weight_event(i):
        left = jnp.where(i == 0, 4, 5)

        def one(g, carry):
            block = t_mm(stack[left, :, quad(g)], stack[i])
            put_strips(gw, block, quad(g), i * PAIRS)
            return carry

        lax.fori_loop(0, QUADS, one, 0)

    def through_event(i):
        at = jnp.where(i == 0, 6, 7)

        def one(g, carry):
            stack[at, :, quad(g)] += mm_t(stack[i], w[i, quad(g), :])
            return carry

        lax.fori_loop(0, QUADS, one, 0)

    def ev_start():
        gctx[...] = jnp.zeros_like(gctx)
        early[0].wait()
        early[1].wait()
        ig[...] = gs1[...]

    def ev_near(g):
        near_back_quad(g, gctx, near, q, kl_ref, b_ref, near, gb, gkl)

    def blend_copy(pair):
        return to_seq(gb.at[pair], land.at[me], b1s.at[pair], b1r.at[me], pair)

    up, down = rim_copies(n, me, rim, gleft, gright, ms, mr)

    def ev_blend():
        for pair in range(PAIRS):

            @pl.when(me != pair)
            def _(pair=pair):
                blend_copy(pair).start()

        rim_start(n, me, up, down, gleft, gright)
        for copy in late[:2]:
            copy.start()

    def mixed_copy(target):
        return to_seq(cmsg.at[me], cmsg.at[me], b2s.at[target], b2r.at[me], target)

    def ev_owner():
        @pl.when(owner)
        def _():
            land[me] = gb[me]
            for s in range(n):

                @pl.when(me != s)
                def _(s=s):
                    to_seq(gb.at[0], land.at[s], b1s.at[0], b1r.at[s], s).wait_recv()

            gblend = land[0]
            for s in range(1, n):
                gblend = gblend + land[s]
            mixed = mx_ref[...]
            gmixed = mm(gblend, zs_ref[NEWTON], TOP)
            cmsg[me, 0:DH, :] = gmixed
            dots = jnp.sum(gmixed * mixed, axis=0, keepdims=True)
            cmsg[me, DH:MSG, :] = jnp.concatenate([dots, jnp.zeros((MSG - DH - 1, LANES), f32)], axis=0)
            for t in range(n):

                @pl.when(me != t)
                def _(t=t):
                    mixed_copy(t).start()

            ng[...] = inverse_grad(gblend, mixed)
            ncore[...] = jnp.zeros_like(ncore)

        gl[...] = jnp.zeros_like(gl)

    def ev_newton(step):
        @pl.when(owner)
        def _():
            ng[...], ncore[...] = newton_back(
                ng[...], ncore[...], core_ref[...], zs_ref[step], ps_ref[step], rs_ref[step], qs_ref[step]
            )

    def ev_core():
        @pl.when(owner)
        def _():
            core_back(ng[...], ncore[...], core_ref[...], zs_ref[0], ql_ref, kl_ref, gl, me)

    quarter = slots // 4

    def ev_taps(part):
        @pl.when(part == 0)
        def _():
            early[5].wait()
            tap_scr[...] = jnp.zeros_like(tap_scr)

        taps_grad_into(tap_scr, gctx, ext, quarter * (part + 1), quarter * part, False)

        @pl.when(part == 3)
        def _():
            gtaps[...] = taps_sums(tap_scr)

    def ev_conv(part):
        @pl.when(part == 0)
        def _():
            rim_wait(n, me, up, down)
            fill_extended(gext, gctx[...], gleft[...], gright[...], count)

        conv_into(gv, gext, taps_ref, quarter * (part + 1), True, False, quarter * part)

    def ev_mixed():
        for pair in range(PAIRS):

            @pl.when(me != pair)
            def _(pair=pair):
                to_seq(cmsg.at[pair], cmsg.at[pair], b2s.at[pair], b2r.at[pair], pair).wait_recv()

        for copy in early[6:]:
            copy.wait()

    def ev_far(g):
        far_back_quad(g, k, v, p, m_ref, b_ref, cmsg, ql_ref, p, gv, gql, True)

    def ev_return():
        land_parts(ret, gql[...] + gl[0], gkl[...] + gl[1])
        for d in range(1, n):
            target = lax.rem(me + d, n)
            to_seq(ret.at[target], rland.at[me], rets.at[d], retr.at[me], target).start()
        for copy in late[2:]:
            copy.start()

    def ev_own():
        rland[me] = ret[me]
        for d in range(1, n):
            source = lax.rem(me + d, n)
            to_seq(ret.at[0], rland.at[source], rets.at[d], retr.at[source], source).wait_recv()
        total = rland[0]
        for s in range(1, n):
            total = total + rland[s]
        own[...] = total
        inv = inverse_lens(lens_ref, segs)
        member = member_rows(ends, slots)
        near[...] += t_mm(member, own[0] * inv)
        p[...] += t_mm(member, own[1] * inv)
        gv[...] = jnp.where(valid_rows(count, slots), gv[...], 0.0)
        small0[0:1, :] = jnp.sum(near[...], axis=0, keepdims=True)
        small0[1:2, :] = jnp.sum(gv[...], axis=0, keepdims=True)

    def small(i):
        return remote(sb.at[i], sl.at[i], ss.at[i], sr.at[i], partners[i])

    def ev_small(i):
        if i == 0:
            pack_small(sb, small0, small1_ref, small2_ref, dbi_ref, gtaps)
        else:
            small(i - 1).wait_recv()
            sb[i] = sb[i - 1] + sl[i - 1]
        if i < SMALL_STEPS:
            small(i).start()

    def at_tick(t, when, event):
        @pl.when(t == when)
        def _():
            event()

    def at_ticks(t, start, every, count, event):
        after = t - start

        @pl.when((after >= 0) & (after < every * count) & (lax.rem(after + every, every) == 0))
        def _():
            event(after // every)

    def tick(t, carry):
        for stage, run in reversed(list(enumerate(stages))):
            at = t - LAG[stage]

            @pl.when((at >= 0) & (at < chunks))
            def _(run=run, at=at):
                run(at)

        at_tick(t, 0, ev_start)
        at_tick(t, 21, lambda: early[4].wait())
        at_tick(t, 24, lambda: [copy.wait() for copy in late])
        turn = jnp.where(t == 0, 0, (t - 23) // 3)

        @pl.when((t == 0) | (t == 26) | (t == 29) | (t == 32))
        def _():
            through_event(turn)

        @pl.when(t == 0)
        def _():
            rim[...] = rims_of(gctx[...], count)
            early[2].wait()
            early[3].wait()

        at_ticks(t, 1, 1, QUADS, ev_near)
        at_tick(t, 3, ev_blend)
        at_ticks(t, 4, 1, 4, ev_taps)
        at_tick(t, 7, ev_owner)
        at_ticks(t, 8, 1, NEWTON, lambda i: ev_newton(NEWTON - 1 - i))
        at_ticks(t, 9, 2, 4, ev_conv)
        at_tick(t, 16, ev_core)
        at_tick(t, 16, ev_mixed)
        at_ticks(t, 16, 1, QUADS, ev_far)
        at_tick(t, 19, ev_return)
        at_tick(t, 23, ev_own)
        filled = jnp.where(t == 21, 0, (t - 22) // 3)

        @pl.when((t == 21) | (t == 25) | (t == 28) | (t == 31))
        def _():
            weight_event(filled)

        at_tick(t, 33, lambda: pltpu.make_async_copy(ig, ig_hbm, ig_sem.at[0]).start())
        for i in range(SMALL_STEPS + 1):
            at_tick(t, SMALL_AT + 3 * i, partial(ev_small, i))
        return carry

    lax.fori_loop(0, chunks + LAG[-1], tick, 0)
    for i in range(SMALL_STEPS):
        small(i).wait_send()
    so_ref[...] = sb[SMALL_STEPS]
    pltpu.make_async_copy(ig, ig_hbm, ig_sem.at[0]).wait()
    for pair in range(PAIRS):

        @pl.when(me != pair)
        def _(pair=pair):
            blend_copy(pair).wait_send()

    @pl.when(owner)
    def _():
        for t in range(n):

            @pl.when(me != t)
            def _(t=t):
                mixed_copy(t).wait_send()

    for d in range(1, n):
        target = lax.rem(me + d, n)
        to_seq(ret.at[target], rland.at[me], rets.at[d], retr.at[me], target).wait_send()


def tail(lens, d_outer, d_inner, big, little, small1, small2, d_inner_bias):
    slots, width = big[0].shape
    segs = lens.shape[1]
    spans = ((0, 12), (12, 24), (24, 36))
    at = spans[-1][1]
    n = SEQ_DEVICES
    dma = pltpu.SemaphoreType.DMA
    vm = lambda *dims: pltpu.VMEM(dims, f32)
    rows = vm(slots, width)
    anywhere = pl.BlockSpec(memory_space=pl.ANY)
    two = dma((at, 2))
    zsem = dma((at, 2, 3, 2))
    one = dma((at,))
    return pl.pallas_call(
        partial(tail_kernel, spans),
        in_specs=[smem()] + [anywhere] * (2 + len(big)) + [whole()] * (len(little) + 3),
        out_specs=[anywhere, whole(), anywhere],
        out_shape=[shape(2, at, STRIP, LANES), shape(SMALL_ROWS, LANES), shape(slots, width)],
        scratch_shapes=[
            vm(RING_ACC, STRIP, LANES), vm(RING_LC, STRIP, LANES), vm(RING_LC, 2, PART, LANES),
            vm(RING_Z, 2, 2, 3, Z_ROWS, LANES), vm(RING_LC, 2, OWN, LANES),
            vm(SMALL_STEPS + 1, SMALL_ROWS, LANES), vm(SMALL_STEPS, SMALL_ROWS, LANES), vm(24, STRIP, LANES),
            vm(8, slots, width), vm(4, width, width), vm(slots + 40, width), rows, rows,
            vm(slots + 40, width), vm(CONV, 8, width), vm(40, LANES), vm(8, width),
            vm(PAIRS, DH, LANES), vm(2 * RIM, width), vm(DH, width), vm(DH, width), vm(2, DH, width),
            vm(n, DH, LANES), vm(PAIRS, MSG, LANES), vm(RIM, width), vm(RIM, width), vm(LANES, LANES), vm(LANES, LANES),
            vm(n, 2, segs, width), vm(n, 2, segs, width), vm(2, segs, width),
            dma((13,)), dma((1,)), dma((PAIRS,)), dma((n,)), dma((n,)), dma((n,)), dma((2,)), dma((2,)),
            dma((n,)), dma((n,)), dma((SMALL_STEPS,)), dma((SMALL_STEPS,)),
            one, two, one, one, two, two, zsem, zsem, two, two, two, two, zsem, zsem, two, two, one, one,
        ],
        compiler_params=params(collective_id=5, has_side_effects=True),
        name="tail",
    )(lens, d_outer, d_inner, *big, *little, small1, small2, d_inner_bias)


def unstrip(strips):
    count, rows, _ = strips.shape
    return strips.transpose(1, 0, 2).reshape(rows, count * LANES)


def unstrip_tall(strips, across):
    count, rows, _ = strips.shape
    down = count // across
    return strips.reshape(down, across, rows, LANES).transpose(0, 2, 1, 3).reshape(down * rows, across * LANES)


PLACE_SLOTS = 24


def place_strips_kernel(spans, s_ref, small_ref, *refs):
    outs = refs[: len(spans)]
    smalls = refs[len(spans) : -3]
    buf, in_sem, out_sem = refs[-3:]
    moves = []
    for out, (lo, hi) in zip(outs, spans):
        across = out.shape[1] // LANES
        for c in range(2):
            for k in range(lo, hi):
                at = 2 * (k - lo) + c
                rows = pl.ds(at // across * STRIP, STRIP)
                cols = pl.ds(at % across * LANES, LANES)
                slot = len(moves) % PLACE_SLOTS
                moves.append((
                    pltpu.make_async_copy(s_ref.at[c, k], buf.at[slot], in_sem.at[slot]),
                    pltpu.make_async_copy(buf.at[slot], out.at[rows, cols], out_sem.at[slot]),
                ))
    ahead = PLACE_SLOTS // 2
    for i in range(len(moves) + ahead):
        if i < len(moves):
            if i >= PLACE_SLOTS:
                moves[i - PLACE_SLOTS][1].wait()
            moves[i][0].start()
        if i >= ahead:
            moves[i - ahead][0].wait()
            moves[i - ahead][1].start()
    unpack_small(small_ref, smalls)
    for _, out in moves[-PLACE_SLOTS:]:
        out.wait()


def place_strips(summed, packed, spans, shapes):
    anywhere = pl.BlockSpec(memory_space=pl.ANY)
    dma = pltpu.SemaphoreType.DMA
    width = shapes[0][1]
    return pl.pallas_call(
        partial(place_strips_kernel, spans),
        in_specs=[anywhere, whole()],
        out_specs=[anywhere] * len(shapes) + [whole()] * 10,
        out_shape=[shape(*dims) for dims in shapes] + [shape(width)] * 8 + [shape(shapes[0][0]), shape(CONV, HEADS)],
        scratch_shapes=[pltpu.VMEM((PLACE_SLOTS, STRIP, LANES), f32), dma((PLACE_SLOTS,)), dma((PLACE_SLOTS,))],
        compiler_params=params(),
        name="place_strips",
    )(summed, packed)


def per_device(
    tokens, segment_lens, query_weight, query_bias, key_weight, value_weight, value_bias, conv_taps,
    output_weight, output_bias, first_gain, first_bias, inner_weight, inner_bias, outer_weight, outer_bias,
    second_gain, second_bias, cotangent,
):
    n = lax.axis_size("seq")
    _, slots, width = tokens.shape
    x = tokens.reshape(slots, width)
    cot = cotangent.reshape(slots, width)
    lens = segment_lens
    taps = jnp.repeat(conv_taps, DH, axis=1)

    q, k, v, land, rim = project(lens, x, query_weight, key_weight, value_weight, query_bias, value_bias)
    lands, left, right = land_exchange(n, land, rim)
    ql = lands[:, 0].reshape(DH, width)
    kl = lands[:, 1].reshape(DH, width)
    parts, raised, tops = far_local(lens, k, v, ql)
    b, *saved = far_exchange(n, parts, ql, kl)
    near, ctx, h1, u1, inv1, ext = attend(
        lens, q, v, kl, b, left, right, taps, x, output_weight, output_bias, first_gain, first_bias
    )
    pre, layer_out, gs2, small2 = ffn_forward(
        lens, h1, inner_weight, inner_bias.reshape(1, -1), outer_weight, outer_bias, cot, second_gain, second_bias
    )
    d_outer, d_inner, gs1, d_inner_bias, small1 = ffn_backward(
        h1, gs2, pre, inner_weight, outer_weight, u1, inv1, first_gain
    )
    weights = [outer_weight, inner_weight, output_weight, query_weight, key_weight, value_weight]
    if n == SEQ_DEVICES and lax.axis_size("dp") == 4:
        big = [gs1, output_weight, near, q, ctx, ext, k, v, raised, x, query_weight, key_weight, value_weight]
        little = [tops, b, ql, kl, *saved, taps]
        summed, packed, input_grad = tail(lens, d_outer, d_inner, big, little, small1, small2, d_inner_bias)
        spans = ((0, 12), (12, 24), (24, 27), (27, 30), (30, 33), (33, 36))
        sums = place_strips(summed, packed, spans, [w.shape for w in weights])
    else:
        gctx, gqn, gblend, gkl, grim = near_back(lens, gs1, output_weight, near, q, kl, b)
        c, gleft, gright, gl = blend_exchange(n, gblend, grim, ql, kl, saved)
        gkf, gvf, back = far_back(n, lens, k, v, raised, tops, b, c, ql, gkl, gl)
        own = land_return(n, back)
        gvc, gtaps, d_output = conv_back(lens, v, left, right, gctx, gleft, gright, taps, ctx, gs1)
        input_grad, d_query, d_key, d_value, small0 = project_back(
            lens, x, gs1, gqn, gkf, gvc, gvf, own, query_weight, key_weight, value_weight
        )
        grads = [d_outer, d_inner, d_output, d_query, d_key, d_value]
        sums = sum_plain(grads + [small0, small1, small2, d_inner_bias, gtaps])
        small = sums[6:]
        sums = (
            [unstrip_tall(sums[0], width // LANES)] + [unstrip(s) for s in sums[1:6]]
            + [small[0][0], small[0][1], *small[1][:3], *small[2][:3], small[3][0], small[4][:CONV, :HEADS]]
        )
    d_outer, d_inner, d_output, d_query, d_key, d_value, *vectors = sums
    d_query_bias, d_value_bias, d_first_gain, d_first_bias, d_output_bias = vectors[:5]
    d_second_gain, d_second_bias, d_outer_bias, d_inner_bias, d_taps = vectors[5:]
    return (
        layer_out.reshape(tokens.shape), input_grad.reshape(tokens.shape),
        d_query, d_query_bias, d_key, d_value, d_value_bias, d_taps,
        d_output, d_output_bias, d_first_gain, d_first_bias,
        d_inner, d_inner_bias, d_outer, d_outer_bias, d_second_gain, d_second_bias,
    )


def solution(mesh):
    block = P("dp", "seq", None)
    return jax.shard_map(
        per_device,
        mesh=mesh,
        in_specs=(block, P("dp", "seq")) + (P(),) * 16 + (block,),
        out_specs=(block, block) + (P(),) * 16,
        check_vma=False,
    )
```

```python
from functools import partial
import math

import jax
import jax.numpy as jnp
from jax import lax
from jax.experimental import pallas as pl
from jax.experimental.pallas import tpu as pltpu
from jax.sharding import PartitionSpec as P

HEADS = 12
DH = 64
CONV = 33
NEWTON = 6
RIM = (CONV - 1) // 2
LANES = 128
PAIRS = HEADS * DH // LANES
QUAD = 256
QUADS = HEADS * DH // QUAD
SCALE = DH ** (-0.5)
EPS = 1e-05
ROOT_HALF = 0.7071067811865476
INV_ROOT_TAU = 0.3989422804014327
MASKED = -1e30
f32 = jnp.float32
HI = lax.Precision.HIGH
TOP = lax.Precision.HIGHEST
MESH = pl.DeviceIdType.MESH
VMEM_CAP = 60 << 20


def _dg(a, b, ca, cb, prec):
    return lax.dot_general(
        a, b, (((ca,), (cb,)), ((), ())), precision=prec, preferred_element_type=f32
    )


def mm(a, b, prec=HI):
    return _dg(a, b, 1, 0, prec)


def mm_t(a, b, prec=HI):
    return _dg(a, b, 1, 1, prec)


def t_mm(a, b, prec=HI):
    return _dg(a, b, 0, 0, prec)


def head_mask(size):
    row = lax.broadcasted_iota(jnp.int32, (size, size), 0) >> 6
    col = lax.broadcasted_iota(jnp.int32, (size, size), 1) >> 6
    return row == col


def spread(rows, mask):
    return jnp.where(mask, jnp.concatenate([rows] * (mask.shape[0] // DH), axis=0), 0.0)


def fold(square, mask):
    kept = jnp.where(mask, square, 0.0)
    total = kept[:DH]
    for at in range(DH, mask.shape[0], DH):
        total = total + kept[at : at + DH]
    return total


def seg_ends(lens_ref, count):
    ends = []
    total = 0
    for j in range(count):
        total = total + lens_ref[0, j]
        ends.append(total)
    return ends


def member_rows(ends, slots):
    shape = (len(ends), slots)
    row = lax.broadcasted_iota(jnp.int32, shape, 0)
    col = lax.broadcasted_iota(jnp.int32, shape, 1)
    low = jnp.zeros(shape, jnp.int32)
    high = jnp.zeros(shape, jnp.int32)
    before = 0
    for j, end in enumerate(ends):
        low = jnp.where(row == j, before, low)
        high = jnp.where(row == j, end, high)
        before = end
    return jnp.where((col >= low) & (col < high), 1.0, 0.0)


def inverse_lens(lens_ref, count):
    row = lax.broadcasted_iota(jnp.int32, (count, 1), 0)
    out = jnp.zeros((count, 1), f32)
    for j in range(count):
        out = jnp.where(row == j, lens_ref[0, j].astype(f32), out)
    return 1.0 / out


def valid_rows(count, slots):
    return lax.broadcasted_iota(jnp.int32, (slots, 1), 0) < count


def rims_of(matrix, count):
    slots = matrix.shape[0]
    row = lax.broadcasted_iota(jnp.int32, (2 * RIM, slots), 0)
    col = lax.broadcasted_iota(jnp.int32, (2 * RIM, slots), 1)
    want = jnp.where(row < RIM, row, row - 2 * RIM + count)
    return mm(jnp.where(col == want, 1.0, 0.0), matrix)


def fill_extended(ext_ref, middle, left, right, count):
    slots = middle.shape[0]
    ext_ref[0:RIM, :] = left
    ext_ref[RIM : RIM + slots, :] = middle
    tail = ext_ref.shape[0] - RIM - slots
    ext_ref[RIM + slots :, :] = jnp.zeros((tail, middle.shape[1]), f32)
    rows = slots + RIM
    row = lax.broadcasted_iota(jnp.int32, (rows, RIM), 0)
    col = lax.broadcasted_iota(jnp.int32, (rows, RIM), 1)
    put = jnp.where(row == col + count, 1.0, 0.0)
    ext_ref[RIM : RIM + rows, :] += mm(put, right)


CONV_ROWS = 64


def shifted(ext_ref, r0, l0):
    slab = ext_ref[pl.ds(r0, CONV_ROWS + 40), pl.ds(l0, LANES)]
    for b in range(8):
        moved = slab[b : b + CONV_ROWS + 32]
        for a in range(5):
            if 8 * a + b < CONV:
                yield 8 * a + b, moved[8 * a : 8 * a + CONV_ROWS]


def conv_into(out_ref, ext_ref, taps_ref, slots, flip, add, low=0):
    def block(i, carry):
        r0 = pl.multiple_of((i // PAIRS) * CONV_ROWS, CONV_ROWS)
        l0 = pl.multiple_of((i % PAIRS) * LANES, LANES)
        acc = jnp.zeros((CONV_ROWS, LANES), f32)
        for c, part in shifted(ext_ref, r0, l0):
            at = CONV - 1 - c if flip else c
            acc = acc + taps_ref[at : at + 1, pl.ds(l0, LANES)] * part
        here = (pl.ds(r0, CONV_ROWS), pl.ds(l0, LANES))
        if add:
            out_ref[here] += acc
        else:
            out_ref[here] = acc
        return carry

    lax.fori_loop((low // CONV_ROWS) * PAIRS, (slots // CONV_ROWS) * PAIRS, block, 0)


def taps_grad_into(scr_ref, grad_ref, ext_ref, slots, low=0, clear=True):
    if clear:
        scr_ref[...] = jnp.zeros_like(scr_ref)

    def block(i, carry):
        r0 = pl.multiple_of((i // PAIRS) * CONV_ROWS, CONV_ROWS)
        l0 = pl.multiple_of((i % PAIRS) * LANES, LANES)
        grad = grad_ref[pl.ds(r0, CONV_ROWS), pl.ds(l0, LANES)]
        for c, part in shifted(ext_ref, r0, l0):
            prod = grad * part
            total = prod[0:8]
            for at in range(8, CONV_ROWS, 8):
                total = total + prod[at : at + 8]
            scr_ref[c, :, pl.ds(l0, LANES)] += total
        return carry

    lax.fori_loop((low // CONV_ROWS) * PAIRS, (slots // CONV_ROWS) * PAIRS, block, 0)


def whole(shape=None):
    return pl.BlockSpec(memory_space=pltpu.VMEM)


def smem():
    return pl.BlockSpec(memory_space=pltpu.SMEM)


def params(**more):
    return pltpu.CompilerParams(vmem_limit_bytes=VMEM_CAP, **more)


def shape(*dims):
    return jax.ShapeDtypeStruct(dims, f32)


def project_kernel(
    lens_ref, x_ref, wq_hbm, wk_hbm, wv_hbm, bq_ref, bv_ref,
    q_ref, k_ref, v_ref, land_ref, rim_ref,
    w_ref, bias_ref, out_ref, load,
):
    slots, width = x_ref.shape
    segs = land_ref.shape[1]
    loads = [
        pltpu.make_async_copy(hbm.at[:, pl.ds(g * QUAD, QUAD)], w_ref.at[i * QUADS + g], load.at[i * QUADS + g])
        for i, hbm in enumerate((wq_hbm, wk_hbm, wv_hbm))
        for g in range(QUADS)
    ]
    for copy in loads:
        copy.start()
    ends = seg_ends(lens_ref, segs)
    member = member_rows(ends, slots)
    inv = inverse_lens(lens_ref, segs)
    for g in range(QUADS):
        bias_ref[g] = jnp.broadcast_to(bq_ref[pl.ds(g * QUAD, QUAD)][None, :], (8, QUAD))
        bias_ref[QUADS + g] = jnp.zeros((8, QUAD), f32)
        bias_ref[2 * QUADS + g] = jnp.broadcast_to(bv_ref[pl.ds(g * QUAD, QUAD)][None, :], (8, QUAD))

    def one(i, carry):
        pltpu.make_async_copy(wq_hbm.at[:, pl.ds(0, QUAD)], w_ref.at[i], load.at[i]).wait()
        out_ref[i] = mm(x_ref[...], w_ref[i]) + bias_ref[i, 0:1, :]
        return carry

    lax.fori_loop(0, 3 * QUADS, one, 0)
    valid = valid_rows(ends[-1], slots)
    for g in range(QUADS):
        cols = slice(g * QUAD, (g + 1) * QUAD)
        q_ref[:, cols] = out_ref[g]
        k_ref[:, cols] = out_ref[QUADS + g]
        v_ref[:, cols] = jnp.where(valid, out_ref[2 * QUADS + g], 0.0)
    land_ref[0] = mm(member, q_ref[...]) * inv
    land_ref[1] = mm(member, k_ref[...]) * inv
    rim_ref[...] = rims_of(v_ref[...], ends[-1])


def project(lens, x, wq, wk, wv, bq, bv):
    slots, width = x.shape
    segs = lens.shape[1]
    anywhere = pl.BlockSpec(memory_space=pl.ANY)
    count = 3 * QUADS
    return pl.pallas_call(
        project_kernel,
        in_specs=[smem(), whole()] + [anywhere] * 3 + [whole()] * 2,
        out_specs=[whole()] * 5,
        out_shape=[
            shape(slots, width), shape(slots, width), shape(slots, width),
            shape(2, segs, width), shape(2 * RIM, width),
        ],
        scratch_shapes=[
            pltpu.VMEM((count, width, QUAD), f32), pltpu.VMEM((count, 8, QUAD), f32),
            pltpu.VMEM((count, slots, QUAD), f32), pltpu.SemaphoreType.DMA((count,)),
        ],
        compiler_params=params(),
        name="project",
    )(lens, x, wq, wk, wv, bq, bv)


def greet_all(n):
    me = lax.axis_index("seq")
    barrier = pltpu.get_barrier_semaphore()
    for d in range(1, n):
        pl.semaphore_signal(
            barrier, inc=1, device_id={"seq": lax.rem(me + d, n)}, device_id_type=MESH
        )
    pl.semaphore_wait(barrier, n - 1)
    return me


def to_seq(src, dst, send, recv, target):
    return pltpu.make_async_remote_copy(
        src, dst, send, recv, device_id={"seq": target}, device_id_type=MESH
    )


def rim_copies(n, me, rim_ref, left_ref, right_ref, rsend, rrecv):
    up = to_seq(rim_ref.at[pl.ds(RIM, RIM)], left_ref, rsend.at[0], rrecv.at[0], lax.rem(me + 1, n))
    down = to_seq(rim_ref.at[pl.ds(0, RIM)], right_ref, rsend.at[1], rrecv.at[1], lax.rem(me + n - 1, n))
    return up, down


def rim_start(n, me, up, down, left_ref, right_ref):
    @pl.when(me < n - 1)
    def _():
        up.start()

    @pl.when(me > 0)
    def _():
        down.start()

    @pl.when(me == 0)
    def _():
        left_ref[...] = jnp.zeros_like(left_ref)

    @pl.when(me == n - 1)
    def _():
        right_ref[...] = jnp.zeros_like(right_ref)


def rim_wait(n, me, up, down):
    @pl.when(me > 0)
    def _():
        up.wait_recv()
        down.wait_send()

    @pl.when(me < n - 1)
    def _():
        down.wait_recv()
        up.wait_send()


def land_exchange_kernel(
    n, mine_ref, rim_ref, all_ref, left_ref, right_ref, send, recv, rsend, rrecv
):
    me = greet_all(n)
    up, down = rim_copies(n, me, rim_ref, left_ref, right_ref, rsend, rrecv)
    copies = []
    for d in range(1, n):
        copy = to_seq(
            mine_ref, all_ref.at[me], send.at[d], recv.at[me], lax.rem(me + d, n)
        )
        copy.start()
        copies.append(copy)
    rim_start(n, me, up, down, left_ref, right_ref)
    all_ref[me] = mine_ref[...]
    for d in range(1, n):
        source = lax.rem(me + d, n)
        to_seq(mine_ref, all_ref.at[source], send.at[d], recv.at[source], source).wait_recv()
    rim_wait(n, me, up, down)
    for copy in copies:
        copy.wait_send()


def land_exchange(n, mine, rim):
    _, segs, width = mine.shape
    dma = pltpu.SemaphoreType.DMA
    return pl.pallas_call(
        partial(land_exchange_kernel, n),
        in_specs=[whole()] * 2,
        out_specs=[whole()] * 3,
        out_shape=[shape(n, 2, segs, width), shape(RIM, width), shape(RIM, width)],
        scratch_shapes=[dma((n,)), dma((n,)), dma((2,)), dma((2,))],
        compiler_params=params(collective_id=1, has_side_effects=True),
        name="land_exchange",
    )(mine, rim)


MSG = DH + 8


def eye(size):
    row = lax.broadcasted_iota(jnp.int32, (size, size), 0)
    col = lax.broadcasted_iota(jnp.int32, (size, size), 1)
    return jnp.where(row == col, 1.0, 0.0)


def pair_sums(row):
    lane = lax.broadcasted_iota(jnp.int32, row.shape, 1)
    first = jnp.sum(jnp.where(lane < DH, row, 0.0), axis=1, keepdims=True)
    second = jnp.sum(jnp.where(lane < DH, 0.0, row), axis=1, keepdims=True)
    return jnp.where(lane < DH, first, second)


def core_of(query, key, mask):
    scores = jnp.where(mask, mm_t(query, key, TOP) * SCALE, MASKED)
    raised = jnp.exp(scores - jnp.max(scores, axis=1, keepdims=True))
    return raised / jnp.sum(raised, axis=1, keepdims=True)


def far_exchange_kernel(
    n, f_ref, ql_ref, kl_ref, b_ref, core_ref, zs_ref, ps_ref, rs_ref, qs_ref, mx_ref,
    land, s1, r1, s2, r2,
):
    me = greet_all(n)
    for p in range(PAIRS):

        @pl.when(me != p)
        def _(p=p):
            to_seq(f_ref.at[p], land.at[me], s1.at[p], r1.at[me], p).start()

    @pl.when(me < PAIRS)
    def _():
        mask = head_mask(LANES)
        lanes = pl.ds(pl.multiple_of(me * LANES, LANES), LANES)
        query = spread(ql_ref[:, lanes], mask)
        key = spread(kl_ref[:, lanes], mask)
        core = core_of(query, key, mask)
        core_ref[...] = core
        colsum = jnp.sum(core, axis=0, keepdims=True)
        sigma = jnp.sqrt(pair_sums(colsum * colsum))
        z = core.T / sigma
        unit = eye(LANES)
        zs_ref[0] = z

        def newton(step, carry):
            z = zs_ref[step]
            prod = mm(core_ref[...], z, TOP)
            ps_ref[step] = prod
            r = 15.0 * unit - mm(prod, 7.0 * unit - prod, TOP)
            rs_ref[step] = r
            q = 13.0 * unit - mm(prod, r, TOP)
            qs_ref[step] = q
            zs_ref[step + 1] = 0.25 * mm(z, q, TOP)
            return carry

        lax.fori_loop(0, NEWTON, newton, 0)
        z = zs_ref[NEWTON]
        land[me] = f_ref[me]
        for s in range(n):

            @pl.when(me != s)
            def _(s=s):
                to_seq(f_ref.at[0], land.at[s], s1.at[0], r1.at[s], s).wait_recv()

        top = land[0][DH : DH + 1]
        for s in range(1, n):
            top = jnp.maximum(top, land[s][DH : DH + 1])
        total = jnp.zeros_like(top)
        mixed = jnp.zeros((DH, LANES), f32)
        for s in range(n):
            part = land[s]
            factor = jnp.exp(part[DH : DH + 1] - top)
            total = total + part[DH + 1 : DH + 2] * factor
            mixed = mixed + part[:DH] * factor
        mixed = mixed / total
        mx_ref[...] = mixed
        b_ref[me, 0:DH, :] = mm_t(mixed, z, TOP)
        pad = jnp.zeros((MSG - DH - 2, LANES), f32)
        b_ref[me, DH:MSG, :] = jnp.concatenate([top, total, pad], axis=0)
        for t in range(n):

            @pl.when(me != t)
            def _(t=t):
                to_seq(b_ref.at[me], b_ref.at[me], s2.at[t], r2.at[me], t).start()

    for p in range(PAIRS):

        @pl.when(me != p)
        def _(p=p):
            to_seq(b_ref.at[p], b_ref.at[p], s2.at[p], r2.at[p], p).wait_recv()
            to_seq(f_ref.at[p], land.at[me], s1.at[p], r1.at[me], p).wait_send()

    @pl.when(me < PAIRS)
    def _():
        for t in range(n):

            @pl.when(me != t)
            def _(t=t):
                to_seq(b_ref.at[me], b_ref.at[me], s2.at[t], r2.at[me], t).wait_send()


def far_exchange(n, parts, ql, kl):
    dma = pltpu.SemaphoreType.DMA
    square = (LANES, LANES)
    return pl.pallas_call(
        partial(far_exchange_kernel, n),
        in_specs=[whole()] * 3,
        out_specs=[whole()] * 7,
        out_shape=[
            shape(PAIRS, MSG, LANES), shape(*square), shape(NEWTON + 1, *square),
            shape(NEWTON, *square), shape(NEWTON, *square), shape(NEWTON, *square),
            shape(DH, LANES),
        ],
        scratch_shapes=[pltpu.VMEM((n, MSG, LANES), f32), dma((PAIRS,)), dma((n,)), dma((n,)), dma((n,))],
        compiler_params=params(collective_id=2, has_side_effects=True),
        name="far_exchange",
    )(parts, ql, kl)


def inverse_grad(gblend, mixed):
    return jnp.where(head_mask(LANES), t_mm(gblend, mixed, TOP), 0.0)


def newton_back(g, gcore, core, z, prod, r, q):
    prod_t = prod.T
    gq = 0.25 * mm(z.T, g, TOP)
    gr = -mm(prod_t, gq, TOP)
    gs = -mm(prod_t, gr, TOP)
    gp = -mm_t(gq, r, TOP) - mm_t(gr, 7.0 * eye(LANES) - prod, TOP) - gs
    return 0.25 * mm_t(g, q, TOP) + mm(core.T, gp, TOP), gcore + mm_t(gp, z, TOP)


def core_back(g, gcore, core, first, ql_ref, kl_ref, gl_ref, me):
    mask = head_mask(LANES)
    colsum = jnp.sum(core, axis=0, keepdims=True)
    square = pair_sums(colsum * colsum)
    sigma = jnp.sqrt(square)
    dot = pair_sums(jnp.sum(g * first, axis=0, keepdims=True))
    gcore = gcore + g.T / sigma - jnp.where(mask, dot / square * colsum, 0.0)
    gscore = core * (gcore - jnp.sum(core * gcore, axis=1, keepdims=True)) * SCALE
    lanes = pl.ds(pl.multiple_of(me * LANES, LANES), LANES)
    query = spread(ql_ref[:, lanes], mask)
    key = spread(kl_ref[:, lanes], mask)
    gl_ref[...] = jnp.zeros_like(gl_ref)
    gl_ref[0, :, lanes] = fold(mm(gscore, key, TOP), mask)
    gl_ref[1, :, lanes] = fold(t_mm(gscore, query, TOP), mask)


def blend_exchange_kernel(
    n, g_ref, rim_ref, ql_ref, kl_ref, core_ref, zs_ref, ps_ref, rs_ref, qs_ref, mx_ref,
    c_ref, left_ref, right_ref, gl_ref,
    land, s1, r1, s2, r2, rsend, rrecv,
):
    me = greet_all(n)
    for p in range(PAIRS):

        @pl.when(me != p)
        def _(p=p):
            to_seq(g_ref.at[p], land.at[me], s1.at[p], r1.at[me], p).start()

    up, down = rim_copies(n, me, rim_ref, left_ref, right_ref, rsend, rrecv)
    rim_start(n, me, up, down, left_ref, right_ref)

    @pl.when(me >= PAIRS)
    def _():
        gl_ref[...] = jnp.zeros_like(gl_ref)

    @pl.when(me < PAIRS)
    def _():
        mask = head_mask(LANES)
        land[me] = g_ref[me]
        for s in range(n):

            @pl.when(me != s)
            def _(s=s):
                to_seq(g_ref.at[0], land.at[s], s1.at[0], r1.at[s], s).wait_recv()

        gblend = land[0]
        for s in range(1, n):
            gblend = gblend + land[s]
        mixed = mx_ref[...]
        gmixed = mm(gblend, zs_ref[NEWTON], TOP)
        c_ref[me, 0:DH, :] = gmixed
        dots = jnp.sum(gmixed * mixed, axis=0, keepdims=True)
        pad = jnp.zeros((MSG - DH - 1, LANES), f32)
        c_ref[me, DH:MSG, :] = jnp.concatenate([dots, pad], axis=0)
        for t in range(n):

            @pl.when(me != t)
            def _(t=t):
                to_seq(c_ref.at[me], c_ref.at[me], s2.at[t], r2.at[me], t).start()

        gcore = jnp.zeros((LANES, LANES), f32)
        g = inverse_grad(gblend, mixed)
        for step in reversed(range(NEWTON)):
            g, gcore = newton_back(g, gcore, core_ref[...], zs_ref[step], ps_ref[step], rs_ref[step], qs_ref[step])
        core_back(g, gcore, core_ref[...], zs_ref[0], ql_ref, kl_ref, gl_ref, me)

    for p in range(PAIRS):

        @pl.when(me != p)
        def _(p=p):
            to_seq(c_ref.at[p], c_ref.at[p], s2.at[p], r2.at[p], p).wait_recv()
            to_seq(g_ref.at[p], land.at[me], s1.at[p], r1.at[me], p).wait_send()

    rim_wait(n, me, up, down)

    @pl.when(me < PAIRS)
    def _():
        for t in range(n):

            @pl.when(me != t)
            def _(t=t):
                to_seq(c_ref.at[me], c_ref.at[me], s2.at[t], r2.at[me], t).wait_send()


def blend_exchange(n, gblend, rim, ql, kl, saved):
    dma = pltpu.SemaphoreType.DMA
    width = rim.shape[1]
    return pl.pallas_call(
        partial(blend_exchange_kernel, n),
        in_specs=[whole()] * 10,
        out_specs=[whole()] * 4,
        out_shape=[shape(PAIRS, MSG, LANES), shape(RIM, width), shape(RIM, width), shape(2, DH, width)],
        scratch_shapes=[
            pltpu.VMEM((n, DH, LANES), f32),
            dma((PAIRS,)), dma((n,)), dma((n,)), dma((n,)), dma((2,)), dma((2,)),
        ],
        compiler_params=params(collective_id=3, has_side_effects=True),
        name="blend_exchange",
    )(gblend, rim, ql, kl, *saved)


def land_return_kernel(n, x_ref, own_ref, land, send, recv):
    me = greet_all(n)
    copies = []
    for d in range(1, n):
        target = lax.rem(me + d, n)
        copy = to_seq(x_ref.at[target], land.at[me], send.at[d], recv.at[me], target)
        copy.start()
        copies.append(copy)
    land[me] = x_ref[me]
    for d in range(1, n):
        source = lax.rem(me + d, n)
        to_seq(x_ref.at[0], land.at[source], send.at[d], recv.at[source], source).wait_recv()
    total = land[0]
    for s in range(1, n):
        total = total + land[s]
    own_ref[...] = total
    for copy in copies:
        copy.wait_send()


def land_return(n, parts):
    dma = pltpu.SemaphoreType.DMA
    return pl.pallas_call(
        partial(land_return_kernel, n),
        in_specs=[whole()],
        out_specs=whole(),
        out_shape=shape(*parts.shape[1:]),
        scratch_shapes=[pltpu.VMEM(parts.shape, f32), dma((n,)), dma((n,))],
        compiler_params=params(collective_id=4, has_side_effects=True),
        name="land_return",
    )(parts)


def far_kernel(lens_ref, k_ref, v_ref, ql_ref, f_ref, p_ref, m_ref):
    slots = k_ref.shape[0]
    count = seg_ends(lens_ref, lens_ref.shape[1])[-1]
    valid = valid_rows(count, slots)
    mask = head_mask(QUAD)

    def one(g, carry):
        cols = quad(g)
        scores = mm_t(k_ref[:, cols], spread(ql_ref[:, cols], mask)) * SCALE
        scores = jnp.where(valid, scores, MASKED)
        top = jnp.max(scores, axis=0, keepdims=True)
        raised = jnp.where(valid, jnp.exp(scores - top), 0.0)
        p_ref[:, cols] = raised
        m_ref[:, cols] = top
        total = jnp.sum(raised, axis=0, keepdims=True)
        weighted = fold(t_mm(v_ref[:, cols], raised), mask)
        tail = jnp.concatenate([top, total, jnp.zeros((MSG - DH - 2, QUAD), f32)], axis=0)
        for j in range(QUAD // LANES):
            part = slice(j * LANES, (j + 1) * LANES)
            f_ref[g * 2 + j, 0:DH, :] = weighted[:, part]
            f_ref[g * 2 + j, DH:MSG, :] = tail[:, part]
        return carry

    lax.fori_loop(0, QUADS, one, 0)


def far_local(lens, k, v, ql):
    slots, width = k.shape
    return pl.pallas_call(
        far_kernel,
        in_specs=[smem()] + [whole()] * 3,
        out_specs=[whole()] * 3,
        out_shape=[shape(PAIRS, MSG, LANES), shape(slots, width), shape(1, width)],
        compiler_params=params(),
        name="far_local",
    )(lens, k, v, ql)


def norm_stats(r):
    centered = r - jnp.mean(r, axis=1, keepdims=True)
    spread_ = jnp.mean(centered * centered, axis=1, keepdims=True)
    inv = lax.rsqrt(spread_ + EPS)
    return centered * inv, inv


def norm_back(unit, inv, gain, grad):
    ge = grad * gain
    return (
        ge
        - jnp.mean(ge, axis=1, keepdims=True)
        - unit * jnp.mean(ge * unit, axis=1, keepdims=True)
    ) * inv


def quad(g):
    return pl.ds(pl.multiple_of(g * QUAD, QUAD), QUAD)


def pair_rows(ref, g, rows):
    return jnp.concatenate([ref[2 * g, rows, :], ref[2 * g + 1, rows, :]], axis=1)


def attend_kernel(
    lens_ref, q_ref, v_ref, kl_ref, b_ref, left_ref, right_ref, taps_ref, x_ref, wo_ref, bo_ref, g1_ref, b1_ref,
    near_ref, ctx_ref, h1_ref, u1_ref, inv1_ref, ext_ref,
):
    slots = q_ref.shape[0]
    count = seg_ends(lens_ref, lens_ref.shape[1])[-1]
    fill_extended(ext_ref, v_ref[...], left_ref[...], right_ref[...], count)
    conv_into(ctx_ref, ext_ref, taps_ref, slots, False, False)
    mask = head_mask(QUAD)
    ones = jnp.where(mask, 1.0, 0.0)
    head = lax.broadcasted_iota(jnp.int32, (slots, QUAD), 1) >> 6

    def one(g, carry):
        cols = quad(g)
        scores = mm_t(q_ref[:, cols], spread(kl_ref[:, cols], mask)) * SCALE
        tops = [jnp.max(scores[:, h * DH : (h + 1) * DH], axis=1, keepdims=True) for h in range(4)]
        top = jnp.where(head < 2, jnp.where(head < 1, tops[0], tops[1]), jnp.where(head < 3, tops[2], tops[3]))
        raised = jnp.exp(scores - top)
        near = raised / mm(raised, ones)
        near_ref[:, cols] = near
        blend = spread(pair_rows(b_ref, g, slice(0, DH)), mask)
        ctx_ref[:, cols] += mm_t(near, blend)
        return carry

    lax.fori_loop(0, QUADS, one, 0)

    def two(g, carry):
        cols = quad(g)
        u1_ref[:, cols] = mm(ctx_ref[...], wo_ref[:, cols])
        return carry

    lax.fori_loop(0, QUADS, two, 0)
    summed = x_ref[...] + (u1_ref[...] + bo_ref[...][None, :])
    unit, inv = norm_stats(summed)
    u1_ref[...] = unit
    inv1_ref[...] = inv
    h1_ref[...] = unit * g1_ref[...][None, :] + b1_ref[...][None, :]


def attend(lens, q, v, kl, b, left, right, taps, x, wo, bo, g1, b1):
    slots, width = q.shape
    return pl.pallas_call(
        attend_kernel,
        in_specs=[smem()] + [whole()] * 12,
        out_specs=[whole()] * 6,
        out_shape=[shape(slots, width)] * 4 + [shape(slots, 1), shape(slots + 40, width)],
        compiler_params=params(),
        name="attend",
    )(lens, q, v, kl, b, left, right, taps, x, wo, bo, g1, b1)


def forward_kernel(
    lens_ref, h1_ref, wi_ref, bi_ref, wo_ref, bo_ref, cot_ref, g2_ref, b2_ref,
    pre_ref, out_ref, gs2_ref, small_ref,
    acc_ref, act_ref,
):
    step = pl.program_id(0)

    @pl.when(step == 0)
    def _():
        acc_ref[...] = jnp.zeros_like(acc_ref)

    def one(g, carry):
        cols = quad(g)
        pre = mm(h1_ref[...], wi_ref[:, cols]) + bi_ref[:, cols]
        pre_ref[:, cols] = pre
        act_ref[:, cols] = 0.5 * pre * (1.0 + lax.erf(pre * ROOT_HALF))
        return carry

    lax.fori_loop(0, QUADS, one, 0)

    def two(g, carry):
        cols = quad(g)
        acc_ref[:, cols] += mm(act_ref[...], wo_ref[:, cols])
        return carry

    lax.fori_loop(0, QUADS, two, 0)

    @pl.when(step == pl.num_programs(0) - 1)
    def _():
        slots = h1_ref.shape[0]
        valid = valid_rows(seg_ends(lens_ref, lens_ref.shape[1])[-1], slots)
        summed = h1_ref[...] + (acc_ref[...] + bo_ref[...][None, :])
        unit, inv = norm_stats(summed)
        out_ref[...] = jnp.where(valid, unit * g2_ref[...][None, :] + b2_ref[...][None, :], 0.0)
        e = jnp.where(valid, cot_ref[...], 0.0)
        grad = norm_back(unit, inv, g2_ref[...][None, :], e)
        gs2_ref[...] = grad
        small_ref[...] = jnp.concatenate(
            [
                jnp.sum(e * unit, axis=0, keepdims=True),
                jnp.sum(e, axis=0, keepdims=True),
                jnp.sum(grad, axis=0, keepdims=True),
                jnp.zeros((5, e.shape[1]), f32),
            ],
            axis=0,
        )


def ffn_forward(lens, h1, wi, bi, wo, bo, cot, g2, b2):
    slots, width = h1.shape
    inner = wi.shape[1]
    const = lambda *dims: pl.BlockSpec(dims, lambda j: (0,) * len(dims))
    return pl.pallas_call(
        forward_kernel,
        grid=(inner // width,),
        in_specs=[
            smem(), const(slots, width),
            pl.BlockSpec((width, width), lambda j: (0, j)), pl.BlockSpec((1, width), lambda j: (0, j)),
            pl.BlockSpec((width, width), lambda j: (j, 0)), const(width),
            const(slots, width), const(width), const(width),
        ],
        out_specs=[
            pl.BlockSpec((slots, width), lambda j: (0, j)),
            const(slots, width), const(slots, width), const(8, width),
        ],
        out_shape=[shape(slots, inner), shape(slots, width), shape(slots, width), shape(8, width)],
        scratch_shapes=[pltpu.VMEM((slots, width), f32)] * 2,
        compiler_params=params(),
        name="ffn_forward",
    )(lens, h1, wi, bi, wo, bo, cot, g2, b2)


def put_strips(ref, block, rows=slice(None), first=0):
    for s in range(block.shape[1] // LANES):
        ref[first + s, rows, :] = block[:, s * LANES : (s + 1) * LANES]


def backward_kernel(
    h1_ref, gs2_ref, pre_ref, wi_ref, wo_ref, u1_ref, inv1_ref, g1_ref,
    dwo_ref, dwi_ref, gs1_ref, dbi_ref, small_ref,
    acc_ref, gpre_ref,
):
    step = pl.program_id(0)

    @pl.when(step == 0)
    def _():
        acc_ref[...] = gs2_ref[...]

    def one(g, carry):
        cols = quad(g)
        pre = pre_ref[:, cols]
        phi_big = 0.5 * (1.0 + lax.erf(pre * ROOT_HALF))
        slope = phi_big + pre * (INV_ROOT_TAU * jnp.exp(-0.5 * pre * pre))
        gpre = mm_t(gs2_ref[...], wo_ref[cols, :]) * slope
        gpre_ref[:, cols] = gpre
        dbi_ref[:, cols] = jnp.sum(gpre, axis=0, keepdims=True)
        put_strips(dwo_ref, t_mm(pre * phi_big, gs2_ref[...]), cols)
        return carry

    lax.fori_loop(0, QUADS, one, 0)

    def two(g, carry):
        cols = quad(g)
        put_strips(dwi_ref, t_mm(h1_ref[:, cols], gpre_ref[...]), cols)
        acc_ref[:, cols] += mm_t(gpre_ref[...], wi_ref[cols, :])
        return carry

    lax.fori_loop(0, QUADS, two, 0)

    @pl.when(step == pl.num_programs(0) - 1)
    def _():
        e = acc_ref[...]
        unit = u1_ref[...]
        grad = norm_back(unit, inv1_ref[...], g1_ref[...][None, :], e)
        gs1_ref[...] = grad
        small_ref[...] = jnp.concatenate(
            [
                jnp.sum(e * unit, axis=0, keepdims=True),
                jnp.sum(e, axis=0, keepdims=True),
                jnp.sum(grad, axis=0, keepdims=True),
                jnp.zeros((5, e.shape[1]), f32),
            ],
            axis=0,
        )


def ffn_backward(h1, gs2, pre, wi, wo, u1, inv1, g1):
    slots, width = h1.shape
    inner = wi.shape[1]
    strips = width // LANES
    const = lambda *dims: pl.BlockSpec(dims, lambda j: (0,) * len(dims))
    return pl.pallas_call(
        backward_kernel,
        grid=(inner // width,),
        in_specs=[
            const(slots, width), const(slots, width),
            pl.BlockSpec((slots, width), lambda j: (0, j)),
            pl.BlockSpec((width, width), lambda j: (0, j)),
            pl.BlockSpec((width, width), lambda j: (j, 0)),
            const(slots, width), const(slots, 1), const(width),
        ],
        out_specs=[
            pl.BlockSpec((strips, width, LANES), lambda j: (j, 0, 0)),
            pl.BlockSpec((strips, width, LANES), lambda j: (j, 0, 0)),
            const(slots, width),
            pl.BlockSpec((1, width), lambda j: (0, j)),
            const(8, width),
        ],
        out_shape=[
            shape(inner // LANES, width, LANES), shape(inner // LANES, width, LANES),
            shape(slots, width), shape(1, inner), shape(8, width),
        ],
        scratch_shapes=[pltpu.VMEM((slots, width), f32)] * 2,
        compiler_params=params(),
        name="ffn_backward",
    )(h1, gs2, pre, wi, wo, u1, inv1, g1)


def near_back_quad(g, gctx_ref, near_ref, q_ref, kl_ref, b_ref, gq_ref, gb_ref, gkl_ref):
    mask = head_mask(QUAD)
    ones = jnp.where(mask, 1.0, 0.0)
    cols = quad(g)
    gctx = gctx_ref[:, cols]
    near = near_ref[:, cols]
    gblend = fold(t_mm(gctx, near), mask)
    gb_ref[2 * g] = gblend[:, :LANES]
    gb_ref[2 * g + 1] = gblend[:, LANES:]
    gnear = mm(gctx, spread(pair_rows(b_ref, g, slice(0, DH)), mask))
    gscore = near * (gnear - mm(near * gnear, ones)) * SCALE
    gq_ref[:, cols] = mm(gscore, spread(kl_ref[:, cols], mask))
    gkl_ref[:, cols] = fold(t_mm(gscore, q_ref[:, cols]), mask)


def near_back_kernel(
    lens_ref, gs1_ref, wo_ref, near_ref, q_ref, kl_ref, b_ref,
    gctx_ref, gq_ref, gb_ref, gkl_ref, rim_ref,
):
    count = seg_ends(lens_ref, lens_ref.shape[1])[-1]
    gctx_ref[...] = mm_t(gs1_ref[...], wo_ref[...])
    rim_ref[...] = rims_of(gctx_ref[...], count)
    def one(g, carry):
        near_back_quad(g, gctx_ref, near_ref, q_ref, kl_ref, b_ref, gq_ref, gb_ref, gkl_ref)
        return carry

    lax.fori_loop(0, QUADS, one, 0)


def near_back(lens, gs1, wo, near, q, kl, b):
    slots, width = gs1.shape
    return pl.pallas_call(
        near_back_kernel,
        in_specs=[smem()] + [whole()] * 6,
        out_specs=[whole()] * 5,
        out_shape=[
            shape(slots, width), shape(slots, width), shape(PAIRS, DH, LANES),
            shape(DH, width), shape(2 * RIM, width),
        ],
        compiler_params=params(),
        name="near_back",
    )(lens, gs1, wo, near, q, kl, b)


def far_back_quad(g, k_ref, v_ref, p_ref, m_ref, b_ref, c_ref, ql_ref, gk_ref, gv_ref, gql_ref, add):
    mask = head_mask(QUAD)
    cols = quad(g)
    top = pair_rows(b_ref, g, slice(DH, DH + 1))
    total = pair_rows(b_ref, g, slice(DH + 1, DH + 2))
    prob = p_ref[:, cols] * (jnp.exp(m_ref[:, cols] - top) / total)
    gmixed = spread(pair_rows(c_ref, g, slice(0, DH)), mask)
    dots = pair_rows(c_ref, g, slice(DH, DH + 1))
    gscore = prob * (mm(v_ref[:, cols], gmixed) - dots) * SCALE
    gk_ref[:, cols] = mm(gscore, spread(ql_ref[:, cols], mask))
    gval = mm_t(prob, gmixed)
    if add:
        gv_ref[:, cols] += gval
    else:
        gv_ref[:, cols] = gval
    gql_ref[:, cols] = fold(t_mm(gscore, k_ref[:, cols]), mask)


def land_parts(ret_ref, gql, gkl):
    n, _, segs, _ = ret_ref.shape
    for s in range(n):
        rows = slice(s * segs, (s + 1) * segs)
        ret_ref[s, 0] = gql[rows]
        ret_ref[s, 1] = gkl[rows]


def far_back_kernel(
    k_ref, v_ref, p_ref, m_ref, b_ref, c_ref, ql_ref, gkl_ref, gl_ref,
    gk_ref, gv_ref, ret_ref, gql_ref,
):
    def one(g, carry):
        far_back_quad(g, k_ref, v_ref, p_ref, m_ref, b_ref, c_ref, ql_ref, gk_ref, gv_ref, gql_ref, False)
        return carry

    lax.fori_loop(0, QUADS, one, 0)
    land_parts(ret_ref, gql_ref[...] + gl_ref[0], gkl_ref[...] + gl_ref[1])


def far_back(n, lens, k, v, p, m, b, c, ql, gkl, gl):
    slots, width = k.shape
    segs = lens.shape[1]
    return pl.pallas_call(
        far_back_kernel,
        in_specs=[whole()] * 9,
        out_specs=[whole()] * 3,
        out_shape=[shape(slots, width), shape(slots, width), shape(n, 2, segs, width)],
        scratch_shapes=[pltpu.VMEM((DH, width), f32)],
        compiler_params=params(),
        name="far_back",
    )(k, v, p, m, b, c, ql, gkl, gl)


def taps_sums(scr_ref):
    width = scr_ref.shape[2]
    rows = jnp.concatenate(
        [jnp.sum(scr_ref[c], axis=0, keepdims=True) for c in range(CONV)] + [jnp.zeros((7, width), f32)], axis=0
    )
    row = lax.broadcasted_iota(jnp.int32, (width, LANES), 0) >> 6
    col = lax.broadcasted_iota(jnp.int32, (width, LANES), 1)
    return mm(rows, jnp.where(row == col, 1.0, 0.0), TOP)


def conv_back_kernel(
    lens_ref, v_ref, left_ref, right_ref, gctx_ref, gleft_ref, gright_ref, taps_ref, ctx_ref, gs1_ref,
    gv_ref, gtaps_ref, dwo_ref,
    ext_ref, scr_ref,
):
    slots = v_ref.shape[0]
    count = seg_ends(lens_ref, lens_ref.shape[1])[-1]
    put_strips(dwo_ref, t_mm(ctx_ref[...], gs1_ref[...]))
    fill_extended(ext_ref, gctx_ref[...], gleft_ref[...], gright_ref[...], count)
    conv_into(gv_ref, ext_ref, taps_ref, slots, True, False)
    fill_extended(ext_ref, v_ref[...], left_ref[...], right_ref[...], count)
    taps_grad_into(scr_ref, gctx_ref, ext_ref, slots)
    gtaps_ref[...] = taps_sums(scr_ref)


def conv_back(lens, v, left, right, gctx, gleft, gright, taps, ctx, gs1):
    slots, width = v.shape
    return pl.pallas_call(
        conv_back_kernel,
        in_specs=[smem()] + [whole()] * 9,
        out_specs=[whole()] * 3,
        out_shape=[shape(slots, width), shape(40, LANES), shape(width // LANES, width, LANES)],
        scratch_shapes=[pltpu.VMEM((slots + 40, width), f32), pltpu.VMEM((CONV, 8, width), f32)],
        compiler_params=params(),
        name="conv_back",
    )(lens, v, left, right, gctx, gleft, gright, taps, ctx, gs1)


def project_back_kernel(
    lens_ref, x_ref, gs1_ref, gqn_ref, gkf_ref, gvc_ref, gvf_ref, own_ref, wq_ref, wk_ref, wv_ref,
    ig_ref, dq_ref, dk_ref, dv_ref, small_ref,
    gq_ref, gk_ref, gv_ref,
):
    @pl.when(pl.program_id(0) == 0)
    def _():
        slots = gqn_ref.shape[0]
        segs = own_ref.shape[1]
        ends = seg_ends(lens_ref, segs)
        member = member_rows(ends, slots)
        inv = inverse_lens(lens_ref, segs)
        gq = gqn_ref[...] + t_mm(member, own_ref[0] * inv)
        gk = gkf_ref[...] + t_mm(member, own_ref[1] * inv)
        gv = jnp.where(valid_rows(ends[-1], slots), gvc_ref[...] + gvf_ref[...], 0.0)
        gq_ref[...] = gq
        gk_ref[...] = gk
        gv_ref[...] = gv
        small_ref[...] = jnp.concatenate(
            [
                jnp.sum(gq, axis=0, keepdims=True),
                jnp.sum(gv, axis=0, keepdims=True),
                jnp.zeros((6, gq.shape[1]), f32),
            ],
            axis=0,
        )

    x = x_ref[...]
    put_strips(dq_ref, t_mm(x, gq_ref[...]))
    put_strips(dk_ref, t_mm(x, gk_ref[...]))
    put_strips(dv_ref, t_mm(x, gv_ref[...]))
    ig_ref[...] = (
        gs1_ref[...]
        + mm_t(gq_ref[...], wq_ref[...])
        + mm_t(gk_ref[...], wk_ref[...])
        + mm_t(gv_ref[...], wv_ref[...])
    )


def project_back(lens, x, gs1, gqn, gkf, gvc, gvf, own, wq, wk, wv):
    slots, width = x.shape
    col = 256
    strips = width // LANES
    const = lambda *dims: pl.BlockSpec(dims, lambda i: (0,) * len(dims))
    part = pl.BlockSpec((slots, col), lambda i: (0, i))
    wspec = pl.BlockSpec((col, width), lambda i: (i, 0))
    dspec = pl.BlockSpec((strips, col, LANES), lambda i: (0, i, 0))
    return pl.pallas_call(
        project_back_kernel,
        grid=(width // col,),
        in_specs=[smem(), part, part] + [const(slots, width)] * 4 + [const(*own.shape), wspec, wspec, wspec],
        out_specs=[part, dspec, dspec, dspec, const(8, width)],
        out_shape=[shape(slots, width)] + [shape(strips, width, LANES)] * 3 + [shape(8, width)],
        scratch_shapes=[pltpu.VMEM((slots, width), f32)] * 3,
        compiler_params=params(),
        name="project_back",
    )(lens, x, gs1, gqn, gkf, gvc, gvf, own, wq, wk, wv)


def sum_plain(parts):
    sizes = [part.size for part in parts]
    shapes = [part.shape for part in parts]
    devices = lax.axis_size(("seq", "dp"))
    flat = jnp.concatenate([part.reshape(-1) for part in parts])
    flat = jnp.pad(flat, (0, -flat.shape[0] % devices))
    own = lax.psum_scatter(flat, ("seq", "dp"), scatter_dimension=0, tiled=True)
    flat = lax.all_gather(own, ("seq", "dp"), axis=0, tiled=True)
    out = []
    at = 0
    for size, dims in zip(sizes, shapes):
        out.append(flat[at : at + size].reshape(dims))
        at += size
    return out


STRIP = 768
HALF = STRIP // 2
PART = HALF // 2
Z_ROWS = PART // 4
OWN = Z_ROWS // 2
STAGES = 13
SMALL_STEPS = 5


def pack_small(sb_ref, small0, small1, small2, inner_bias, taps):
    at = 0
    for ref, count in ((small0, 2), (small1, 3), (small2, 3), (inner_bias, 1)):
        for r in range(count):
            for j in range(ref.shape[1] // LANES):
                sb_ref[0, at : at + 1, :] = ref[r : r + 1, j * LANES : (j + 1) * LANES]
                at += 1
    sb_ref[0, at : at + 40, :] = taps[...]


SMALL_ROWS = 8 * 6 + 24 + 40


def unpack_small(s_ref, outs):
    at = 0
    for ref in outs[:-1]:
        for j in range(ref.shape[0] // LANES):
            ref[pl.ds(j * LANES, LANES)] = s_ref[at, :]
            at += 1
    outs[-1][...] = s_ref[at : at + CONV, :HEADS]


def reduce_stages(gw, o_ref, bufs, sems):
    acc, lc, l1, mid, lz, l3, ag = bufs
    cs, cr, s1, r1, ms, zr, r3, r4, gs, gr, r5, keep, es, er = sems
    seq = lax.axis_index("seq")
    dp = lax.axis_index("dp")
    z = seq // 2
    c = lax.rem(seq, 2)
    y = dp // 2
    x = lax.rem(dp, 2)
    zb = 3 - z
    place = lambda z_, c_, y_, x_: (z_ * 2 + c_, y_ * 2 + x_)
    by_core = place(z, 1 - c, y, x)
    by_x = place(z, c, y, 1 - x)
    by_y = place(z, c, 1 - y, x)
    right = place(lax.rem(z + 1, 4), c, y, x)
    left = place(lax.rem(z + 3, 4), c, y, x)
    opposite = place(lax.rem(z + 2, 4), c, y, x)
    near_z = place(z + 1 - 2 * lax.rem(z, 2), c, y, x)

    def remote(src, dst, send, recv, target):
        return pltpu.make_async_remote_copy(src, dst, send, recv, device_id=target, device_id_type=MESH)

    aligned = lambda at: pl.multiple_of(at, 8)
    slot = lambda ref, k: lax.rem(k, ref.shape[0])
    starts = (x * PART, HALF + y * PART)
    others = ((1 - x) * PART, HALF + (1 - y) * PART)
    own_rows = (pl.ds(aligned(y * OWN), OWN), pl.ds(aligned(x * OWN), OWN))
    other_rows = (pl.ds(aligned((1 - y) * OWN), OWN), pl.ds(aligned((1 - x) * OWN), OWN))
    first_to = (by_x, by_y)
    third_to = (by_y, by_x)
    ways = ((0, z, right), (1, zb, left))

    def bytes_of(rows, send, recv, pieces=1):
        part = lc.at[pl.ds(0, pieces), pl.ds(0, rows // pieces)]
        return remote(part, part, send, recv, by_core)

    def strip(k):
        return lax.rem(k // 3, GW_SLOTS) * PAIRS + 2 * lax.rem(k, 3)

    def core_copy(k):
        return remote(gw.at[strip(k) + 1 - c], lc.at[slot(lc, k)], cs.at[k], cr.at[k], by_core)

    def core_out(k):
        core_copy(k).start()

    def first_out(k):
        core_copy(k).wait()
        at = slot(acc, k)
        acc[at] = gw[strip(k) + c] + lc[slot(lc, k)]
        for j in range(2):
            remote(
                acc.at[at, pl.ds(aligned(others[j]), PART)], l1.at[slot(l1, k), j], s1.at[k], r1.at[k], first_to[j]
            ).start()

    def z_copy(k, way, step, block, target):
        return remote(mid.at[slot(mid, k), block], lz.at[slot(lz, k), way, step], ms.at[k], zr.at[k, way, step], target)

    def z_out(k, step):
        if step == 0:
            bytes_of(HALF, s1.at[k], r1.at[k]).wait()
            for j in range(2):
                for block in range(4):
                    here = pl.ds(aligned(starts[j] + block * Z_ROWS), Z_ROWS)
                    there = pl.ds(block * Z_ROWS, Z_ROWS)
                    mid[slot(mid, k), block, j] = acc[slot(acc, k), here] + l1[slot(l1, k), j, there]
        for way, at, target in ways:
            block = 3 - step + z if way == 0 else step - zb
            if step > 0:

                @pl.when((at > 0) & (at <= step))
                def _(way=way, block=block, target=target):
                    z_copy(k, way, step - 1, 0, target).wait_recv()
                    mid[slot(mid, k), block] += lz[slot(lz, k), way, step - 1]

            if step < 3:

                @pl.when((at <= step) & (at < 3))
                def _(way=way, block=block, target=target):
                    z_copy(k, way, step, block, target).start()

    def third_out(k):
        z_out(k, 3)
        for j in range(2):
            remote(
                mid.at[slot(mid, k), z, j, other_rows[j]], l3.at[slot(l3, k), j], ms.at[k], r3.at[k], third_to[j]
            ).start()

    def back_third_out(k):
        bytes_of(2 * OWN, ms.at[k], r3.at[k]).wait_recv()
        for j in range(2):
            ag[slot(ag, k), z, j, own_rows[j]] = mid[slot(mid, k), z, j, own_rows[j]] + l3[slot(l3, k), j]
            part = ag.at[slot(ag, k), z, j, own_rows[j]]
            remote(part, part, gs.at[k], r4.at[k], third_to[j]).start()

    def back_z(k, way, step, block, target):
        part = ag.at[slot(ag, k), block]
        return remote(part, part, gs.at[k], gr.at[k, way, step], target)

    def back_z_out(k, step):
        if step == 0:
            bytes_of(6 * Z_ROWS + 2 * OWN, ms.at[k], r3.at[k]).wait_send()
            bytes_of(2 * OWN, gs.at[k], r4.at[k]).wait_recv()
        for way, at, target in ways:
            block = z - step if way == 0 else z + step
            if step > 0:

                @pl.when(at >= step)
                def _(way=way, target=target):
                    back_z(k, way, step - 1, 0, target).wait_recv()

            if step < 3:

                @pl.when((at >= step) & (at < 3))
                def _(way=way, block=block, target=target):
                    back_z(k, way, step, block, target).start()

    blocks = (pl.ds(x * 4, 4), pl.ds(8 + y * 4, 4))

    def keep_copy(k, j):
        return pltpu.make_async_copy(ag.at[slot(ag, k), :, j], o_ref.at[c, k, blocks[j]], keep.at[k, j])

    def back_first_out(k):
        back_z_out(k, 3)
        for j in range(2):
            remote(ag.at[slot(ag, k), :, j], o_ref.at[c, k, blocks[j]], gs.at[k], r5.at[k], first_to[j]).start()
            keep_copy(k, j).start()

    def back_core(k):
        part = o_ref.at[c, k]
        return remote(part, part, es.at[k], er.at[k], by_core)

    def back_core_out(k):
        bytes_of(HALF, gs.at[k], r5.at[k]).wait_recv()
        for j in range(2):
            keep_copy(k, j).wait()

        @pl.when((z == 0) | (z == 3))
        def _():
            bytes_of(2 * OWN + 2 * Z_ROWS + HALF, gs.at[k], r5.at[k]).wait_send()

        @pl.when((z > 0) & (z < 3))
        def _():
            bytes_of(2 * OWN + 10 * Z_ROWS + HALF, gs.at[k], r5.at[k], 2).wait_send()

        back_core(k).start()

    def finish(k):
        back_core(k).wait()

    stages = [
        core_out, first_out, partial(z_out, step=0), partial(z_out, step=1), partial(z_out, step=2), third_out,
        back_third_out, partial(back_z_out, step=0), partial(back_z_out, step=1), partial(back_z_out, step=2),
        back_first_out, back_core_out, finish,
    ]
    return stages, (by_core, by_x, by_y, near_z, opposite), remote


LAG = tuple(range(0, 2 * STAGES, 2))
CHUNKS = 36
GW_SLOTS = 4
RING_ACC = 6
RING_LC = 4
RING_MID = 12
RING_Z = 6
RING_AG = 16
SEQ_DEVICES = 8
SMALL_AT = 36
ENTER = 2
HELD = 30
GAP = 2
GS1, GS2, H1, ACT, GPRE, PRE, _, U1, GCTX, IG = range(10)
GV, PROB, CTX, KEYS, NEAR, QUERY, VALS = GS2, H1, ACT, GPRE, PRE, PRE + 1, U1
FFN_AT = (0, 4, 8, 13)
GS1_AT = 17
OUTPUT_AT, VALUE_AT, QUERY_AT, KEY_AT = 21, 28, 32, 33
INPUT_AT = (34, 35, 36)


def pick(t, table):
    value = jnp.int32(0)
    hit = t < 0
    for when, what in table.items():
        value = jnp.where(t == when, what, value)
        hit = hit | (t == when)
    return value, hit


def greet_block():
    seq = lax.axis_index("seq")
    dp = lax.axis_index("dp")
    y = dp // 2
    x = lax.rem(dp, 2)
    barrier = pltpu.get_barrier_semaphore()
    for d in range(1, SEQ_DEVICES):
        pl.semaphore_signal(
            barrier, inc=1, device_id=(lax.rem(seq + d, SEQ_DEVICES), dp), device_id_type=MESH
        )
    for other in (y * 2 + 1 - x, (1 - y) * 2 + x):
        pl.semaphore_signal(barrier, inc=1, device_id=(seq, other), device_id_type=MESH)
    pl.semaphore_wait(barrier, SEQ_DEVICES + 1)
    return seq


def tail_kernel(
    lens_ref, gs2_hbm, h1_hbm, u1_hbm, pre_hbm, wout_hbm, win_hbm, wo_hbm, near_hbm, q_hbm, ctx_hbm, ext_hbm,
    k_hbm, v_hbm, p_hbm, x_hbm, wq_hbm, wk_hbm, wv_hbm,
    inv1_ref, g1_ref, m_ref, b_ref, ql_ref, kl_ref, core_ref, zs_ref, ps_ref, rs_ref, qs_ref, mx_ref, taps_ref, small2_ref,
    o_ref, so_ref, ig_hbm,
    acc, lc, l1, mid, lz, l3, ag, sb, sl, gw,
    stack, w, ext, gext, tap_scr, gtaps, small0, small1, dbi,
    gb, rim, gkl, gql, gl, land, cmsg, gleft, gright, ng, ncore, ret, rland, own,
    loads, ig_sem, b1s, b1r, b2s, b2r, ms, mr, rets, retr, ss, sr,
    *sems,
):
    n = SEQ_DEVICES
    _, slots, width = stack.shape
    segs = own.shape[1]
    gs1, gv, p, ctx, k, near, q, v, gctx, ig = [
        stack.at[i] for i in (GS1, GV, PROB, CTX, KEYS, NEAR, QUERY, VALS, GCTX, IG)
    ]
    moves = []

    def load(src, dst):
        moves.append(pltpu.make_async_copy(src, dst, loads.at[len(moves)]))
        return moves[-1]

    load_gs2 = load(gs2_hbm, stack.at[GS2])
    load_w = []
    load_pre = []
    for j in range(4):
        part = pl.ds(j * width, width)
        load_w.append(load(wout_hbm.at[part, :], w.at[2 * j % 4]))
        load_w.append(load(win_hbm.at[:, part], w.at[(2 * j + 1) % 4]))
        load_pre.append(load(pre_hbm.at[:, part], stack.at[PRE + j % 2]))
    for i, hbm in enumerate((wo_hbm, wv_hbm, wq_hbm, wk_hbm)):
        load_w.append(load(hbm, w.at[i]))
    load_h1, load_u1, load_ext = load(h1_hbm, stack.at[H1]), load(u1_hbm, stack.at[U1]), load(ext_hbm, ext)
    load_near, load_q, load_ctx = load(near_hbm, near), load(q_hbm, q), load(ctx_hbm, ctx)
    load_p, load_k, load_v, load_x = load(p_hbm, p), load(k_hbm, k), load(v_hbm, v), load(x_hbm, q)
    a0, a1, a2, a3 = FFN_AT
    starting = [
        (a0 + 1, load_w[4]), (a0 + 1, load_pre[2]), (a0 + 4, load_w[5]), (a1 + 1, load_w[6]), (a1 + 1, load_pre[3]),
        (a1 + 4, load_w[7]), (a2 + 1, load_w[8]), (a2 + 1, load_near), (a2 + 4, load_w[9]), (a3 + 1, load_w[10]),
        (a3 + 1, load_q), (a3 + 2, load_ctx), (a3 + 3, load_p), (a3 + 4, load_w[11]), (a3 + 4, load_k), (a3 + 4, load_v),
        (GS1_AT + 4, load_x),
    ]
    waiting = [
        (a0, load_gs2), (a0 + 2, load_h1), (a3 + 3, load_u1), (GS1_AT, load_w[8]), (GS1_AT + 1, load_near),
        (GS1_AT + 1, load_q), (OUTPUT_AT, load_ctx), (VALUE_AT, load_x),
    ]
    for j in range(4):
        waiting += [(FFN_AT[j], load_w[2 * j]), (FFN_AT[j], load_pre[j]), (FFN_AT[j] + 3, load_w[2 * j + 1])]
    for i in range(3):
        waiting.append((INPUT_AT[i], load_w[9 + i]))
    for copy in (load_gs2, load_w[0], load_pre[0], load_h1, load_w[1], load_pre[1], load_w[2], load_w[3], load_u1, load_ext):
        copy.start()
    me = greet_block()
    owner = me < PAIRS
    stages, partners, remote = reduce_stages(gw, o_ref, (acc, lc, l1, mid, lz, l3, ag), sems)
    ends = seg_ends(lens_ref, segs)
    count = ends[-1]

    def weight_event(e, left, right):
        def one(g, carry):
            block = t_mm(stack[left, :, quad(g)], stack[right])
            put_strips(gw, block, quad(g), lax.rem(e, GW_SLOTS) * PAIRS)
            return carry

        lax.fori_loop(0, QUADS, one, 0)

    def through_event(source, target, weight):
        def one(g, carry):
            stack[target, :, quad(g)] += mm_t(stack[source], w[weight, quad(g), :])
            return carry

        lax.fori_loop(0, QUADS, one, 0)

    def inner_event(j):
        @pl.when(j == 0)
        def _():
            stack[GS1] = stack[GS2]

        at = PRE + lax.rem(j, 2)
        weight = lax.rem(2 * j, 4)

        def one(g, carry):
            cols = quad(g)
            pre = stack[at, :, cols]
            phi_big = 0.5 * (1.0 + lax.erf(pre * ROOT_HALF))
            slope = phi_big + pre * (INV_ROOT_TAU * jnp.exp(-0.5 * pre * pre))
            gpre = mm_t(stack[GS2], w[weight, cols, :]) * slope
            stack[GPRE, :, cols] = gpre
            stack[ACT, :, cols] = pre * phi_big
            dbi[:, pl.ds(pl.multiple_of(j * width + g * QUAD, QUAD), QUAD)] = jnp.sum(gpre, axis=0, keepdims=True)
            return carry

        lax.fori_loop(0, QUADS, one, 0)

    def ev_norm():
        e = gs1[...]
        unit = stack[U1]
        grad = norm_back(unit, inv1_ref[...], g1_ref[...][None, :], e)
        gs1[...] = grad
        ig[...] = grad
        gctx[...] = jnp.zeros_like(grad)
        small1[0:1, :] = jnp.sum(e * unit, axis=0, keepdims=True)
        small1[1:2, :] = jnp.sum(e, axis=0, keepdims=True)
        small1[2:3, :] = jnp.sum(grad, axis=0, keepdims=True)

    def ev_rims():
        rim[...] = rims_of(gctx[...], count)

    def ev_near(g):
        near_back_quad(g, gctx, near, q, kl_ref, b_ref, near, gb, gkl)

    def blend_copy(pair):
        return to_seq(gb.at[pair], land.at[me], b1s.at[pair], b1r.at[me], pair)

    up, down = rim_copies(n, me, rim, gleft, gright, ms, mr)

    def ev_blend():
        for pair in range(PAIRS):

            @pl.when(me != pair)
            def _(pair=pair):
                blend_copy(pair).start()

        rim_start(n, me, up, down, gleft, gright)

    def mixed_copy(target):
        return to_seq(cmsg.at[me], cmsg.at[me], b2s.at[target], b2r.at[me], target)

    def ev_owner():
        @pl.when(owner)
        def _():
            land[me] = gb[me]
            for s in range(n):

                @pl.when(me != s)
                def _(s=s):
                    to_seq(gb.at[0], land.at[s], b1s.at[0], b1r.at[s], s).wait_recv()

            gblend = land[0]
            for s in range(1, n):
                gblend = gblend + land[s]
            mixed = mx_ref[...]
            gmixed = mm(gblend, zs_ref[NEWTON], TOP)
            cmsg[me, 0:DH, :] = gmixed
            dots = jnp.sum(gmixed * mixed, axis=0, keepdims=True)
            cmsg[me, DH:MSG, :] = jnp.concatenate([dots, jnp.zeros((MSG - DH - 1, LANES), f32)], axis=0)
            for t in range(n):

                @pl.when(me != t)
                def _(t=t):
                    mixed_copy(t).start()

            ng[...] = inverse_grad(gblend, mixed)
            ncore[...] = jnp.zeros_like(ncore)

        gl[...] = jnp.zeros_like(gl)

    def ev_newton(step):
        @pl.when(owner)
        def _():
            ng[...], ncore[...] = newton_back(
                ng[...], ncore[...], core_ref[...], zs_ref[step], ps_ref[step], rs_ref[step], qs_ref[step]
            )

    def ev_core():
        @pl.when(owner)
        def _():
            core_back(ng[...], ncore[...], core_ref[...], zs_ref[0], ql_ref, kl_ref, gl, me)

    quarter = slots // 4

    def ev_taps(part):
        @pl.when(part == 0)
        def _():
            load_ext.wait()
            tap_scr[...] = jnp.zeros_like(tap_scr)

        taps_grad_into(tap_scr, gctx, ext, quarter * (part + 1), quarter * part, False)

        @pl.when(part == 3)
        def _():
            gtaps[...] = taps_sums(tap_scr)

    def ev_conv(part):
        @pl.when(part == 0)
        def _():
            rim_wait(n, me, up, down)
            fill_extended(gext, gctx[...], gleft[...], gright[...], count)

        conv_into(gv, gext, taps_ref, quarter * (part + 1), True, False, quarter * part)

    def ev_mixed():
        for pair in range(PAIRS):

            @pl.when(me != pair)
            def _(pair=pair):
                to_seq(cmsg.at[pair], cmsg.at[pair], b2s.at[pair], b2r.at[pair], pair).wait_recv()

        for copy in (load_k, load_v, load_p):
            copy.wait()

    def ev_far(g):
        far_back_quad(g, k, v, p, m_ref, b_ref, cmsg, ql_ref, p, gv, gql, True)

    def ev_return():
        land_parts(ret, gql[...] + gl[0], gkl[...] + gl[1])
        for d in range(1, n):
            target = lax.rem(me + d, n)
            to_seq(ret.at[target], rland.at[me], rets.at[d], retr.at[me], target).start()

    def ev_own():
        rland[me] = ret[me]
        for d in range(1, n):
            source = lax.rem(me + d, n)
            to_seq(ret.at[0], rland.at[source], rets.at[d], retr.at[source], source).wait_recv()
        total = rland[0]
        for s in range(1, n):
            total = total + rland[s]
        own[...] = total
        inv = inverse_lens(lens_ref, segs)
        member = member_rows(ends, slots)
        near[...] += t_mm(member, own[0] * inv)
        p[...] += t_mm(member, own[1] * inv)
        small0[0:1, :] = jnp.sum(near[...], axis=0, keepdims=True)

    def ev_values():
        masked = jnp.where(valid_rows(count, slots), gv[...], 0.0)
        gv[...] = masked
        small0[1:2, :] = jnp.sum(masked, axis=0, keepdims=True)

    def small(i):
        return remote(sb.at[i], sl.at[i], ss.at[i], sr.at[i], partners[i])

    def ev_small(i):
        if i == 0:
            pack_small(sb, small0, small1, small2_ref, dbi, gtaps)
        else:
            small(i - 1).wait_recv()
            sb[i] = sb[i - 1] + sl[i - 1]
        if i < SMALL_STEPS:
            small(i).start()

    def at_tick(t, when, event):
        @pl.when(t == when)
        def _():
            event()

    def at_ticks(t, start, every, count, event):
        after = t - start

        @pl.when((after >= 0) & (after < every * count) & (lax.rem(after + every, every) == 0))
        def _():
            event(after // every)

    weights = {}
    through = {}
    for j, when in enumerate(FFN_AT):
        weights[when + 1] = (2 * j, ACT, GS2)
        weights[when + 2] = (2 * j + 1, H1, GPRE)
        through[when + 3] = (GPRE, GS1, (2 * j + 1) % 4)
    weights[OUTPUT_AT] = (8, CTX, GS1)
    for i, (when, part) in enumerate(((VALUE_AT, GV), (QUERY_AT, NEAR), (KEY_AT, PROB))):
        weights[when] = (9 + i, QUERY, part)
        through[INPUT_AT[i]] = (part, IG, 1 + i)
    through[GS1_AT] = (GS1, GCTX, 0)

    def by_table(t, table, event):
        columns = [pick(t, {when: row[i] for when, row in table.items()}) for i in range(3)]

        @pl.when(columns[0][1])
        def _():
            event(*[value for value, _ in columns])

    def tick(t, carry):
        for stage, run in reversed(list(enumerate(stages))):
            since = t - ENTER - LAG[stage]
            at = jnp.where(since < HELD, since, since - GAP)

            @pl.when((since >= 0) & ((since < HELD) | (since >= HELD + GAP)) & (at < CHUNKS))
            def _(run=run, at=at):
                run(at)

        for when, copy in starting:
            at_tick(t, when, copy.start)
        for when, copy in waiting:
            at_tick(t, when, copy.wait)
        block, hit = pick(t, {when: j for j, when in enumerate(FFN_AT)})

        @pl.when(hit)
        def _():
            inner_event(block)

        by_table(t, through, through_event)
        by_table(t, weights, weight_event)
        at_tick(t, FFN_AT[3] + 3, ev_norm)
        at_tick(t, GS1_AT, ev_rims)
        at_ticks(t, GS1_AT + 1, 1, QUADS, ev_near)
        at_tick(t, GS1_AT + 3, ev_blend)
        at_tick(t, GS1_AT + 5, ev_owner)
        at_ticks(t, GS1_AT + 6, 1, NEWTON, lambda i: ev_newton(NEWTON - 1 - i))
        at_ticks(t, GS1_AT + 5, 1, 4, ev_conv)
        at_tick(t, GS1_AT + 8, ev_mixed)
        at_ticks(t, GS1_AT + 8, 1, QUADS, ev_far)
        at_tick(t, GS1_AT + 10, ev_values)
        at_tick(t, GS1_AT + 12, ev_core)
        at_tick(t, GS1_AT + 12, ev_return)
        at_ticks(t, GS1_AT + 11, 1, 4, ev_taps)
        at_tick(t, GS1_AT + 14, ev_own)
        at_tick(t, INPUT_AT[2], lambda: pltpu.make_async_copy(ig, ig_hbm, ig_sem.at[0]).start())
        for i in range(SMALL_STEPS + 1):
            at_tick(t, SMALL_AT + 2 * i, partial(ev_small, i))
        return carry

    lax.fori_loop(0, CHUNKS + ENTER + GAP + LAG[-1], tick, 0)
    for i in range(SMALL_STEPS):
        small(i).wait_send()
    so_ref[...] = sb[SMALL_STEPS]
    pltpu.make_async_copy(ig, ig_hbm, ig_sem.at[0]).wait()
    for pair in range(PAIRS):

        @pl.when(me != pair)
        def _(pair=pair):
            blend_copy(pair).wait_send()

    @pl.when(owner)
    def _():
        for t in range(n):

            @pl.when(me != t)
            def _(t=t):
                mixed_copy(t).wait_send()

    for d in range(1, n):
        target = lax.rem(me + d, n)
        to_seq(ret.at[target], rland.at[me], rets.at[d], retr.at[me], target).wait_send()


def tail(lens, big, little):
    slots, width = big[0].shape
    segs = lens.shape[1]
    at = CHUNKS
    n = SEQ_DEVICES
    dma = pltpu.SemaphoreType.DMA
    vm = lambda *dims: pltpu.VMEM(dims, f32)
    anywhere = pl.BlockSpec(memory_space=pl.ANY)
    one = dma((at,))
    zsem = dma((at, 2, 3))
    return pl.pallas_call(
        tail_kernel,
        in_specs=[smem()] + [anywhere] * len(big) + [whole()] * len(little),
        out_specs=[anywhere, whole(), anywhere],
        out_shape=[shape(2, at, STRIP // Z_ROWS, Z_ROWS, LANES), shape(SMALL_ROWS, LANES), shape(slots, width)],
        scratch_shapes=[
            vm(RING_ACC, STRIP, LANES), vm(RING_LC, STRIP, LANES), vm(RING_LC, 2, PART, LANES),
            vm(RING_MID, 4, 2, Z_ROWS, LANES), vm(RING_Z, 2, 3, 2, Z_ROWS, LANES), vm(RING_LC, 2, OWN, LANES),
            vm(RING_AG, 4, 2, Z_ROWS, LANES),
            vm(SMALL_STEPS + 1, SMALL_ROWS, LANES), vm(SMALL_STEPS, SMALL_ROWS, LANES), vm(GW_SLOTS * PAIRS, STRIP, LANES),
            vm(10, slots, width), vm(4, width, width), vm(slots + 40, width), vm(slots + 40, width),
            vm(CONV, 8, width), vm(40, LANES), vm(8, width), vm(8, width), vm(1, 4 * width),
            vm(PAIRS, DH, LANES), vm(2 * RIM, width), vm(DH, width), vm(DH, width), vm(2, DH, width),
            vm(n, DH, LANES), vm(PAIRS, MSG, LANES), vm(RIM, width), vm(RIM, width), vm(LANES, LANES), vm(LANES, LANES),
            vm(n, 2, segs, width), vm(n, 2, segs, width), vm(2, segs, width),
            dma((27,)), dma((1,)), dma((PAIRS,)), dma((n,)), dma((n,)), dma((n,)), dma((2,)), dma((2,)),
            dma((n,)), dma((n,)), dma((SMALL_STEPS,)), dma((SMALL_STEPS,)),
            one, one, one, one, one, zsem, one, one, one, zsem, one, dma((at, 2)), one, one,
        ],
        compiler_params=params(collective_id=5, has_side_effects=True),
        name="tail",
    )(lens, *big, *little)


def unstrip(strips):
    count, rows, _ = strips.shape
    return strips.transpose(1, 0, 2).reshape(rows, count * LANES)


def unstrip_tall(strips, across):
    count, rows, _ = strips.shape
    down = count // across
    return strips.reshape(down, across, rows, LANES).transpose(0, 2, 1, 3).reshape(down * rows, across * LANES)


PLACE_SLOTS = 24


def place_strips_kernel(s_ref, small_ref, *refs):
    outs = refs[:6]
    smalls = refs[6:-3]
    buf, in_sem, out_sem = refs[-3:]
    moves = []
    for e in range(CHUNKS // 3):
        if e < 8:
            out, row, col = outs[e % 2], (e // 2) * (1 - e % 2), (e // 2) * (e % 2)
        else:
            out, row, col = outs[e - 6], 0, 0
        for k in range(3):
            for c in range(2):
                rows = pl.ds(row * STRIP, STRIP)
                cols = pl.ds(col * STRIP + (2 * k + c) * LANES, LANES)
                slot = len(moves) % PLACE_SLOTS
                moves.append((
                    pltpu.make_async_copy(s_ref.at[c, 3 * e + k], buf.at[slot], in_sem.at[slot]),
                    pltpu.make_async_copy(buf.at[slot], out.at[rows, cols], out_sem.at[slot]),
                ))
    ahead = PLACE_SLOTS // 2
    for i in range(len(moves) + ahead):
        if i < len(moves):
            if i >= PLACE_SLOTS:
                moves[i - PLACE_SLOTS][1].wait()
            moves[i][0].start()
        if i >= ahead:
            moves[i - ahead][0].wait()
            moves[i - ahead][1].start()
    unpack_small(small_ref, smalls)
    for _, out in moves[-PLACE_SLOTS:]:
        out.wait()


def place_strips(summed, packed, shapes):
    anywhere = pl.BlockSpec(memory_space=pl.ANY)
    dma = pltpu.SemaphoreType.DMA
    width = shapes[0][1]
    return pl.pallas_call(
        place_strips_kernel,
        in_specs=[anywhere, whole()],
        out_specs=[anywhere] * len(shapes) + [whole()] * 10,
        out_shape=[shape(*dims) for dims in shapes] + [shape(width)] * 8 + [shape(shapes[0][0]), shape(CONV, HEADS)],
        scratch_shapes=[pltpu.VMEM((PLACE_SLOTS, STRIP, LANES), f32), dma((PLACE_SLOTS,)), dma((PLACE_SLOTS,))],
        compiler_params=params(),
        name="place_strips",
    )(summed, packed)


def per_device(
    tokens, segment_lens, query_weight, query_bias, key_weight, value_weight, value_bias, conv_taps,
    output_weight, output_bias, first_gain, first_bias, inner_weight, inner_bias, outer_weight, outer_bias,
    second_gain, second_bias, cotangent,
):
    n = lax.axis_size("seq")
    _, slots, width = tokens.shape
    x = tokens.reshape(slots, width)
    cot = cotangent.reshape(slots, width)
    lens = segment_lens
    taps = jnp.repeat(conv_taps, DH, axis=1)

    q, k, v, land, rim = project(lens, x, query_weight, key_weight, value_weight, query_bias, value_bias)
    lands, left, right = land_exchange(n, land, rim)
    ql = lands[:, 0].reshape(DH, width)
    kl = lands[:, 1].reshape(DH, width)
    parts, raised, tops = far_local(lens, k, v, ql)
    b, *saved = far_exchange(n, parts, ql, kl)
    near, ctx, h1, u1, inv1, ext = attend(
        lens, q, v, kl, b, left, right, taps, x, output_weight, output_bias, first_gain, first_bias
    )
    pre, layer_out, gs2, small2 = ffn_forward(
        lens, h1, inner_weight, inner_bias.reshape(1, -1), outer_weight, outer_bias, cot, second_gain, second_bias
    )
    weights = [outer_weight, inner_weight, output_weight, value_weight, query_weight, key_weight]
    if n == SEQ_DEVICES and lax.axis_size("dp") == 4:
        big = [
            gs2, h1, u1, pre, outer_weight, inner_weight, output_weight, near, q, ctx, ext, k, v, raised, x,
            query_weight, key_weight, value_weight,
        ]
        little = [inv1, first_gain, tops, b, ql, kl, *saved, taps, small2]
        summed, packed, input_grad = tail(lens, big, little)
        sums = place_strips(summed.reshape(2, CHUNKS, STRIP, LANES), packed, [w.shape for w in weights])
    else:
        d_outer, d_inner, gs1, d_inner_bias, small1 = ffn_backward(
            h1, gs2, pre, inner_weight, outer_weight, u1, inv1, first_gain
        )
        gctx, gqn, gblend, gkl, grim = near_back(lens, gs1, output_weight, near, q, kl, b)
        c, gleft, gright, gl = blend_exchange(n, gblend, grim, ql, kl, saved)
        gkf, gvf, back = far_back(n, lens, k, v, raised, tops, b, c, ql, gkl, gl)
        own = land_return(n, back)
        gvc, gtaps, d_output = conv_back(lens, v, left, right, gctx, gleft, gright, taps, ctx, gs1)
        input_grad, d_query, d_key, d_value, small0 = project_back(
            lens, x, gs1, gqn, gkf, gvc, gvf, own, query_weight, key_weight, value_weight
        )
        grads = [d_outer, d_inner, d_output, d_value, d_query, d_key]
        sums = sum_plain(grads + [small0, small1, small2, d_inner_bias, gtaps])
        small = sums[6:]
        sums = (
            [unstrip_tall(sums[0], width // LANES)] + [unstrip(s) for s in sums[1:6]]
            + [small[0][0], small[0][1], *small[1][:3], *small[2][:3], small[3][0], small[4][:CONV, :HEADS]]
        )
    d_outer, d_inner, d_output, d_value, d_query, d_key, *vectors = sums
    d_query_bias, d_value_bias, d_first_gain, d_first_bias, d_output_bias = vectors[:5]
    d_second_gain, d_second_bias, d_outer_bias, d_inner_bias, d_taps = vectors[5:]
    return (
        layer_out.reshape(tokens.shape), input_grad.reshape(tokens.shape),
        d_query, d_query_bias, d_key, d_value, d_value_bias, d_taps,
        d_output, d_output_bias, d_first_gain, d_first_bias,
        d_inner, d_inner_bias, d_outer, d_outer_bias, d_second_gain, d_second_bias,
    )


def solution(mesh):
    block = P("dp", "seq", None)
    return jax.shard_map(
        per_device,
        mesh=mesh,
        in_specs=(block, P("dp", "seq")) + (P(),) * 16 + (block,),
        out_specs=(block, block) + (P(),) * 16,
        check_vma=False,
    )
```

```python
from functools import partial
import math

import jax
import jax.numpy as jnp
from jax import lax
from jax.experimental import pallas as pl
from jax.experimental.pallas import tpu as pltpu
from jax.sharding import PartitionSpec as P

HEADS = 12
DH = 64
CONV = 33
NEWTON = 6
RIM = (CONV - 1) // 2
LANES = 128
PAIRS = HEADS * DH // LANES
QUAD = 256
QUADS = HEADS * DH // QUAD
SCALE = DH ** (-0.5)
EPS = 1e-05
ROOT_HALF = 0.7071067811865476
INV_ROOT_TAU = 0.3989422804014327
MASKED = -1e30
f32 = jnp.float32
HI = lax.Precision.HIGH
TOP = lax.Precision.HIGHEST
MESH = pl.DeviceIdType.MESH
VMEM_CAP = 60 << 20


def _dg(a, b, ca, cb, prec):
    return lax.dot_general(
        a, b, (((ca,), (cb,)), ((), ())), precision=prec, preferred_element_type=f32
    )


def mm(a, b, prec=HI):
    return _dg(a, b, 1, 0, prec)


def mm_t(a, b, prec=HI):
    return _dg(a, b, 1, 1, prec)


def t_mm(a, b, prec=HI):
    return _dg(a, b, 0, 0, prec)


def head_mask(size):
    row = lax.broadcasted_iota(jnp.int32, (size, size), 0) >> 6
    col = lax.broadcasted_iota(jnp.int32, (size, size), 1) >> 6
    return row == col


def spread(rows, mask):
    return jnp.where(mask, jnp.concatenate([rows] * (mask.shape[0] // DH), axis=0), 0.0)


def fold(square, mask):
    kept = jnp.where(mask, square, 0.0)
    total = kept[:DH]
    for at in range(DH, mask.shape[0], DH):
        total = total + kept[at : at + DH]
    return total


def seg_ends(lens_ref, count):
    ends = []
    total = 0
    for j in range(count):
        total = total + lens_ref[0, j]
        ends.append(total)
    return ends


def member_rows(ends, slots):
    shape = (len(ends), slots)
    row = lax.broadcasted_iota(jnp.int32, shape, 0)
    col = lax.broadcasted_iota(jnp.int32, shape, 1)
    low = jnp.zeros(shape, jnp.int32)
    high = jnp.zeros(shape, jnp.int32)
    before = 0
    for j, end in enumerate(ends):
        low = jnp.where(row == j, before, low)
        high = jnp.where(row == j, end, high)
        before = end
    return jnp.where((col >= low) & (col < high), 1.0, 0.0)


def inverse_lens(lens_ref, count):
    row = lax.broadcasted_iota(jnp.int32, (count, 1), 0)
    out = jnp.zeros((count, 1), f32)
    for j in range(count):
        out = jnp.where(row == j, lens_ref[0, j].astype(f32), out)
    return 1.0 / out


def valid_rows(count, slots):
    return lax.broadcasted_iota(jnp.int32, (slots, 1), 0) < count


def rims_of(matrix, count):
    slots = matrix.shape[0]
    row = lax.broadcasted_iota(jnp.int32, (2 * RIM, slots), 0)
    col = lax.broadcasted_iota(jnp.int32, (2 * RIM, slots), 1)
    want = jnp.where(row < RIM, row, row - 2 * RIM + count)
    return mm(jnp.where(col == want, 1.0, 0.0), matrix)


def fill_extended(ext_ref, middle, left, right, count):
    slots = middle.shape[0]
    ext_ref[0:RIM, :] = left
    ext_ref[RIM : RIM + slots, :] = middle
    tail = ext_ref.shape[0] - RIM - slots
    ext_ref[RIM + slots :, :] = jnp.zeros((tail, middle.shape[1]), f32)
    rows = slots + RIM
    row = lax.broadcasted_iota(jnp.int32, (rows, RIM), 0)
    col = lax.broadcasted_iota(jnp.int32, (rows, RIM), 1)
    put = jnp.where(row == col + count, 1.0, 0.0)
    ext_ref[RIM : RIM + rows, :] += mm(put, right)


CONV_ROWS = 64


def shifted(ext_ref, r0, l0):
    slab = ext_ref[pl.ds(r0, CONV_ROWS + 40), pl.ds(l0, LANES)]
    for b in range(8):
        moved = slab[b : b + CONV_ROWS + 32]
        for a in range(5):
            if 8 * a + b < CONV:
                yield 8 * a + b, moved[8 * a : 8 * a + CONV_ROWS]


def conv_into(out_ref, ext_ref, taps_ref, slots, flip, add, low=0):
    def block(i, carry):
        r0 = pl.multiple_of((i // PAIRS) * CONV_ROWS, CONV_ROWS)
        l0 = pl.multiple_of((i % PAIRS) * LANES, LANES)
        acc = jnp.zeros((CONV_ROWS, LANES), f32)
        for c, part in shifted(ext_ref, r0, l0):
            at = CONV - 1 - c if flip else c
            acc = acc + taps_ref[at : at + 1, pl.ds(l0, LANES)] * part
        here = (pl.ds(r0, CONV_ROWS), pl.ds(l0, LANES))
        if add:
            out_ref[here] += acc
        else:
            out_ref[here] = acc
        return carry

    lax.fori_loop((low // CONV_ROWS) * PAIRS, (slots // CONV_ROWS) * PAIRS, block, 0)


def taps_grad_into(scr_ref, grad_ref, ext_ref, slots, low=0, clear=True):
    if clear:
        scr_ref[...] = jnp.zeros_like(scr_ref)

    def block(i, carry):
        r0 = pl.multiple_of((i // PAIRS) * CONV_ROWS, CONV_ROWS)
        l0 = pl.multiple_of((i % PAIRS) * LANES, LANES)
        grad = grad_ref[pl.ds(r0, CONV_ROWS), pl.ds(l0, LANES)]
        for c, part in shifted(ext_ref, r0, l0):
            prod = grad * part
            total = prod[0:8]
            for at in range(8, CONV_ROWS, 8):
                total = total + prod[at : at + 8]
            scr_ref[c, :, pl.ds(l0, LANES)] += total
        return carry

    lax.fori_loop((low // CONV_ROWS) * PAIRS, (slots // CONV_ROWS) * PAIRS, block, 0)


def whole(shape=None):
    return pl.BlockSpec(memory_space=pltpu.VMEM)


def smem():
    return pl.BlockSpec(memory_space=pltpu.SMEM)


def params(**more):
    return pltpu.CompilerParams(vmem_limit_bytes=VMEM_CAP, **more)


def shape(*dims):
    return jax.ShapeDtypeStruct(dims, f32)


def greet_signal(n):
    me = lax.axis_index("seq")
    for d in range(1, n):
        pl.semaphore_signal(
            pltpu.get_barrier_semaphore(), inc=1, device_id={"seq": lax.rem(me + d, n)}, device_id_type=MESH
        )
    return me


def greet_all(n):
    me = greet_signal(n)
    pl.semaphore_wait(pltpu.get_barrier_semaphore(), n - 1)
    return me


def to_seq(src, dst, send, recv, target):
    return pltpu.make_async_remote_copy(
        src, dst, send, recv, device_id={"seq": target}, device_id_type=MESH
    )


def rim_copies(n, me, rim_ref, left_ref, right_ref, rsend, rrecv):
    up = to_seq(rim_ref.at[pl.ds(RIM, RIM)], left_ref, rsend.at[0], rrecv.at[0], lax.rem(me + 1, n))
    down = to_seq(rim_ref.at[pl.ds(0, RIM)], right_ref, rsend.at[1], rrecv.at[1], lax.rem(me + n - 1, n))
    return up, down


def rim_start(n, me, up, down, left_ref, right_ref):
    @pl.when(me < n - 1)
    def _():
        up.start()

    @pl.when(me > 0)
    def _():
        down.start()

    @pl.when(me == 0)
    def _():
        left_ref[...] = jnp.zeros_like(left_ref)

    @pl.when(me == n - 1)
    def _():
        right_ref[...] = jnp.zeros_like(right_ref)


def rim_wait(n, me, up, down):
    @pl.when(me > 0)
    def _():
        up.wait_recv()
        down.wait_send()

    @pl.when(me < n - 1)
    def _():
        down.wait_recv()
        up.wait_send()


MSG = DH + 8


def eye(size):
    row = lax.broadcasted_iota(jnp.int32, (size, size), 0)
    col = lax.broadcasted_iota(jnp.int32, (size, size), 1)
    return jnp.where(row == col, 1.0, 0.0)


def pair_sums(row):
    lane = lax.broadcasted_iota(jnp.int32, row.shape, 1)
    first = jnp.sum(jnp.where(lane < DH, row, 0.0), axis=1, keepdims=True)
    second = jnp.sum(jnp.where(lane < DH, 0.0, row), axis=1, keepdims=True)
    return jnp.where(lane < DH, first, second)


def core_of(query, key, mask):
    scores = jnp.where(mask, mm_t(query, key, TOP) * SCALE, MASKED)
    raised = jnp.exp(scores - jnp.max(scores, axis=1, keepdims=True))
    return raised / jnp.sum(raised, axis=1, keepdims=True)


def inverse_grad(gblend, mixed):
    return jnp.where(head_mask(LANES), t_mm(gblend, mixed, TOP), 0.0)


def newton_back(g, gcore, core, z, prod, r, q):
    prod_t = prod.T
    gq = 0.25 * mm(z.T, g, TOP)
    gr = -mm(prod_t, gq, TOP)
    gs = -mm(prod_t, gr, TOP)
    gp = -mm_t(gq, r, TOP) - mm_t(gr, 7.0 * eye(LANES) - prod, TOP) - gs
    return 0.25 * mm_t(g, q, TOP) + mm(core.T, gp, TOP), gcore + mm_t(gp, z, TOP)


def core_back(g, gcore, core, first, ql_ref, kl_ref, gl_ref, me):
    mask = head_mask(LANES)
    colsum = jnp.sum(core, axis=0, keepdims=True)
    square = pair_sums(colsum * colsum)
    sigma = jnp.sqrt(square)
    dot = pair_sums(jnp.sum(g * first, axis=0, keepdims=True))
    gcore = gcore + g.T / sigma - jnp.where(mask, dot / square * colsum, 0.0)
    gscore = core * (gcore - jnp.sum(core * gcore, axis=1, keepdims=True)) * SCALE
    lanes = pl.ds(pl.multiple_of(me * LANES, LANES), LANES)
    query = spread(ql_ref[:, lanes], mask)
    key = spread(kl_ref[:, lanes], mask)
    gl_ref[...] = jnp.zeros_like(gl_ref)
    gl_ref[0, :, lanes] = fold(mm(gscore, key, TOP), mask)
    gl_ref[1, :, lanes] = fold(t_mm(gscore, query, TOP), mask)


def blend_exchange_kernel(
    n, g_ref, rim_ref, ql_ref, kl_ref, core_ref, zs_ref, ps_ref, rs_ref, qs_ref, mx_ref,
    c_ref, left_ref, right_ref, gl_ref,
    land, s1, r1, s2, r2, rsend, rrecv,
):
    me = greet_all(n)
    for p in range(PAIRS):

        @pl.when(me != p)
        def _(p=p):
            to_seq(g_ref.at[p], land.at[me], s1.at[p], r1.at[me], p).start()

    up, down = rim_copies(n, me, rim_ref, left_ref, right_ref, rsend, rrecv)
    rim_start(n, me, up, down, left_ref, right_ref)

    @pl.when(me >= PAIRS)
    def _():
        gl_ref[...] = jnp.zeros_like(gl_ref)

    @pl.when(me < PAIRS)
    def _():
        mask = head_mask(LANES)
        land[me] = g_ref[me]
        for s in range(n):

            @pl.when(me != s)
            def _(s=s):
                to_seq(g_ref.at[0], land.at[s], s1.at[0], r1.at[s], s).wait_recv()

        gblend = land[0]
        for s in range(1, n):
            gblend = gblend + land[s]
        mixed = mx_ref[...]
        gmixed = mm(gblend, zs_ref[NEWTON], TOP)
        c_ref[me, 0:DH, :] = gmixed
        dots = jnp.sum(gmixed * mixed, axis=0, keepdims=True)
        pad = jnp.zeros((MSG - DH - 1, LANES), f32)
        c_ref[me, DH:MSG, :] = jnp.concatenate([dots, pad], axis=0)
        for t in range(n):

            @pl.when(me != t)
            def _(t=t):
                to_seq(c_ref.at[me], c_ref.at[me], s2.at[t], r2.at[me], t).start()

        gcore = jnp.zeros((LANES, LANES), f32)
        g = inverse_grad(gblend, mixed)
        for step in reversed(range(NEWTON)):
            g, gcore = newton_back(g, gcore, core_ref[...], zs_ref[step], ps_ref[step], rs_ref[step], qs_ref[step])
        core_back(g, gcore, core_ref[...], zs_ref[0], ql_ref, kl_ref, gl_ref, me)

    for p in range(PAIRS):

        @pl.when(me != p)
        def _(p=p):
            to_seq(c_ref.at[p], c_ref.at[p], s2.at[p], r2.at[p], p).wait_recv()
            to_seq(g_ref.at[p], land.at[me], s1.at[p], r1.at[me], p).wait_send()

    rim_wait(n, me, up, down)

    @pl.when(me < PAIRS)
    def _():
        for t in range(n):

            @pl.when(me != t)
            def _(t=t):
                to_seq(c_ref.at[me], c_ref.at[me], s2.at[t], r2.at[me], t).wait_send()


def blend_exchange(n, gblend, rim, ql, kl, saved):
    dma = pltpu.SemaphoreType.DMA
    width = rim.shape[1]
    return pl.pallas_call(
        partial(blend_exchange_kernel, n),
        in_specs=[whole()] * 10,
        out_specs=[whole()] * 4,
        out_shape=[shape(PAIRS, MSG, LANES), shape(RIM, width), shape(RIM, width), shape(2, DH, width)],
        scratch_shapes=[
            pltpu.VMEM((n, DH, LANES), f32),
            dma((PAIRS,)), dma((n,)), dma((n,)), dma((n,)), dma((2,)), dma((2,)),
        ],
        compiler_params=params(collective_id=3, has_side_effects=True),
        name="blend_exchange",
    )(gblend, rim, ql, kl, *saved)


def land_return_kernel(n, x_ref, own_ref, land, send, recv):
    me = greet_all(n)
    copies = []
    for d in range(1, n):
        target = lax.rem(me + d, n)
        copy = to_seq(x_ref.at[target], land.at[me], send.at[d], recv.at[me], target)
        copy.start()
        copies.append(copy)
    land[me] = x_ref[me]
    for d in range(1, n):
        source = lax.rem(me + d, n)
        to_seq(x_ref.at[0], land.at[source], send.at[d], recv.at[source], source).wait_recv()
    total = land[0]
    for s in range(1, n):
        total = total + land[s]
    own_ref[...] = total
    for copy in copies:
        copy.wait_send()


def land_return(n, parts):
    dma = pltpu.SemaphoreType.DMA
    return pl.pallas_call(
        partial(land_return_kernel, n),
        in_specs=[whole()],
        out_specs=whole(),
        out_shape=shape(*parts.shape[1:]),
        scratch_shapes=[pltpu.VMEM(parts.shape, f32), dma((n,)), dma((n,))],
        compiler_params=params(collective_id=4, has_side_effects=True),
        name="land_return",
    )(parts)


def norm_stats(r):
    centered = r - jnp.mean(r, axis=1, keepdims=True)
    spread_ = jnp.mean(centered * centered, axis=1, keepdims=True)
    inv = lax.rsqrt(spread_ + EPS)
    return centered * inv, inv


def norm_back(unit, inv, gain, grad):
    ge = grad * gain
    return (
        ge
        - jnp.mean(ge, axis=1, keepdims=True)
        - unit * jnp.mean(ge * unit, axis=1, keepdims=True)
    ) * inv


def quad(g):
    return pl.ds(pl.multiple_of(g * QUAD, QUAD), QUAD)


def pair_rows(ref, g, rows):
    return jnp.concatenate([ref[2 * g, rows, :], ref[2 * g + 1, rows, :]], axis=1)


def front_kernel(
    n, lens_ref, x_ref, taps_in, bq_ref, bv_ref, bo_ref, g1_ref, b1_ref, wq_hbm, wk_hbm, wv_hbm, wo_hbm,
    q_out, k_out, v_out, p_out, near_out, ctx_out, ext_out, h1_out, u1_out,
    m_ref, b_ref, ql_ref, kl_ref, core_ref, zs_ref, ps_ref, rs_ref, qs_ref, mx_ref, taps_ref, inv1_ref,
    w, wo, bias, stack, ext, f_ref, mine, lands, rim, left, right, land,
    load, out, ms, mr, ls, lr, s1, r1, s2, r2,
):
    _, slots, width = stack.shape
    segs = mine.shape[1]
    v, q, k, p, near, ctx, h1, u1 = [stack.at[i] for i in range(8)]
    loads = [
        pltpu.make_async_copy(hbm.at[:, pl.ds(g * QUAD, QUAD)], w.at[i * QUADS + g], load.at[i * QUADS + g])
        for i, hbm in enumerate((wv_hbm, wq_hbm, wk_hbm))
        for g in range(QUADS)
    ]
    loads.append(pltpu.make_async_copy(wo_hbm, wo, load.at[3 * QUADS]))
    for copy in loads:
        copy.start()
    leaving = []

    def leave(src, dst):
        leaving.append(pltpu.make_async_copy(src, dst, out.at[len(leaving)]))
        leaving[-1].start()

    me = greet_signal(n)
    ends = seg_ends(lens_ref, segs)
    count = ends[-1]
    valid = valid_rows(count, slots)
    member = member_rows(ends, slots)
    inv = inverse_lens(lens_ref, segs)
    for g in range(QUADS):
        cols = pl.ds(g * QUAD, QUAD)
        bias[g] = jnp.broadcast_to(bv_ref[cols][None, :], (8, QUAD))
        bias[QUADS + g] = jnp.broadcast_to(bq_ref[cols][None, :], (8, QUAD))
        bias[2 * QUADS + g] = jnp.zeros((8, QUAD), f32)

    def one(i, carry):
        pltpu.make_async_copy(wv_hbm.at[:, pl.ds(0, QUAD)], w.at[i], load.at[i]).wait()
        stack[i // QUADS, :, quad(lax.rem(i, QUADS))] = mm(x_ref[...], w[i]) + bias[i, 0:1, :]

        @pl.when(i == QUADS - 1)
        def _():
            v[...] = jnp.where(valid, v[...], 0.0)
            rim[...] = rims_of(v[...], count)
            pl.semaphore_wait(pltpu.get_barrier_semaphore(), n - 1)
            rim_start(n, me, up, down, left, right)

        return carry

    up, down = rim_copies(n, me, rim, left, right, ms, mr)
    lax.fori_loop(0, 3 * QUADS, one, 0)
    mine[0] = mm(member, q[...]) * inv
    mine[1] = mm(member, k[...]) * inv
    for d in range(1, n):
        to_seq(mine, lands.at[me], ls.at[d], lr.at[me], lax.rem(me + d, n)).start()
    lands[me] = mine[...]
    leave(q, q_out)
    leave(k, k_out)
    leave(v, v_out)
    row = lax.broadcasted_iota(jnp.int32, (HEADS, width), 0)
    col = lax.broadcasted_iota(jnp.int32, (HEADS, width), 1) >> 6
    taps_ref[...] = mm(taps_in[...], jnp.where(row == col, 1.0, 0.0), TOP)
    rim_wait(n, me, up, down)
    fill_extended(ext, v[...], left[...], right[...], count)
    leave(ext, ext_out)
    conv_into(ctx, ext, taps_ref, slots, False, False)

    for d in range(1, n):
        source = lax.rem(me + d, n)
        to_seq(mine, lands.at[source], ls.at[d], lr.at[source], source).wait_recv()
    for s in range(n):
        rows = slice(s * segs, (s + 1) * segs)
        ql_ref[rows, :] = lands[s, 0]
        kl_ref[rows, :] = lands[s, 1]

    def far(g, carry):
        cols = quad(g)
        mask = head_mask(QUAD)
        scores = mm_t(k[:, cols], spread(ql_ref[:, cols], mask)) * SCALE
        scores = jnp.where(valid, scores, MASKED)
        top = jnp.max(scores, axis=0, keepdims=True)
        raised = jnp.where(valid, jnp.exp(scores - top), 0.0)
        p[:, cols] = raised
        m_ref[:, cols] = top
        total = jnp.sum(raised, axis=0, keepdims=True)
        weighted = fold(t_mm(v[:, cols], raised), mask)
        rest = jnp.concatenate([top, total, jnp.zeros((MSG - DH - 2, QUAD), f32)], axis=0)
        for j in range(QUAD // LANES):
            part = slice(j * LANES, (j + 1) * LANES)
            f_ref[g * 2 + j, 0:DH, :] = weighted[:, part]
            f_ref[g * 2 + j, DH:MSG, :] = rest[:, part]
        return carry

    lax.fori_loop(0, QUADS, far, 0)
    for pair in range(PAIRS):

        @pl.when(me != pair)
        def _(pair=pair):
            to_seq(f_ref.at[pair], land.at[me], s1.at[pair], r1.at[me], pair).start()

    leave(p, p_out)

    @pl.when(me < PAIRS)
    def _():
        mask = head_mask(LANES)
        lanes = pl.ds(pl.multiple_of(me * LANES, LANES), LANES)
        core = core_of(spread(ql_ref[:, lanes], mask), spread(kl_ref[:, lanes], mask), mask)
        core_ref[...] = core
        colsum = jnp.sum(core, axis=0, keepdims=True)
        zs_ref[0] = core.T / jnp.sqrt(pair_sums(colsum * colsum))
        unit = eye(LANES)

        def newton(step, carry):
            z = zs_ref[step]
            prod = mm(core_ref[...], z, TOP)
            ps_ref[step] = prod
            r = 15.0 * unit - mm(prod, 7.0 * unit - prod, TOP)
            rs_ref[step] = r
            q_ = 13.0 * unit - mm(prod, r, TOP)
            qs_ref[step] = q_
            zs_ref[step + 1] = 0.25 * mm(z, q_, TOP)
            return carry

        lax.fori_loop(0, NEWTON, newton, 0)
        land[me] = f_ref[me]
        for s in range(n):

            @pl.when(me != s)
            def _(s=s):
                to_seq(f_ref.at[0], land.at[s], s1.at[0], r1.at[s], s).wait_recv()

        top = land[0][DH : DH + 1]
        for s in range(1, n):
            top = jnp.maximum(top, land[s][DH : DH + 1])
        total = jnp.zeros_like(top)
        mixed = jnp.zeros((DH, LANES), f32)
        for s in range(n):
            part = land[s]
            factor = jnp.exp(part[DH : DH + 1] - top)
            total = total + part[DH + 1 : DH + 2] * factor
            mixed = mixed + part[:DH] * factor
        mixed = mixed / total
        mx_ref[...] = mixed
        b_ref[me, 0:DH, :] = mm_t(mixed, zs_ref[NEWTON], TOP)
        pad = jnp.zeros((MSG - DH - 2, LANES), f32)
        b_ref[me, DH:MSG, :] = jnp.concatenate([top, total, pad], axis=0)
        for t in range(n):

            @pl.when(me != t)
            def _(t=t):
                to_seq(b_ref.at[me], b_ref.at[me], s2.at[t], r2.at[me], t).start()

    def soft(g, carry):
        cols = quad(g)
        mask = head_mask(QUAD)
        head = lax.broadcasted_iota(jnp.int32, (slots, QUAD), 1) >> 6
        scores = mm_t(q[:, cols], spread(kl_ref[:, cols], mask)) * SCALE
        tops = [jnp.max(scores[:, h * DH : (h + 1) * DH], axis=1, keepdims=True) for h in range(4)]
        top = jnp.where(head < 2, jnp.where(head < 1, tops[0], tops[1]), jnp.where(head < 3, tops[2], tops[3]))
        raised = jnp.exp(scores - top)
        near[:, cols] = raised / mm(raised, jnp.where(mask, 1.0, 0.0))
        return carry

    lax.fori_loop(0, QUADS, soft, 0)
    leave(near, near_out)
    for pair in range(PAIRS):

        @pl.when(me != pair)
        def _(pair=pair):
            to_seq(b_ref.at[pair], b_ref.at[pair], s2.at[pair], r2.at[pair], pair).wait_recv()

    def blend(g, carry):
        cols = quad(g)
        ctx[:, cols] += mm_t(near[:, cols], spread(pair_rows(b_ref, g, slice(0, DH)), head_mask(QUAD)))
        return carry

    lax.fori_loop(0, QUADS, blend, 0)
    leave(ctx, ctx_out)
    loads[-1].wait()

    def project(g, carry):
        cols = quad(g)
        u1[:, cols] = mm(ctx[...], wo[:, cols])
        return carry

    lax.fori_loop(0, QUADS, project, 0)
    unit, scale = norm_stats(x_ref[...] + (u1[...] + bo_ref[...][None, :]))
    h1[...] = unit * g1_ref[...][None, :] + b1_ref[...][None, :]
    leave(h1, h1_out)
    u1[...] = unit
    leave(u1, u1_out)
    inv1_ref[...] = scale
    for d in range(1, n):
        to_seq(mine, lands.at[me], ls.at[d], lr.at[me], lax.rem(me + d, n)).wait_send()
    for pair in range(PAIRS):

        @pl.when(me != pair)
        def _(pair=pair):
            to_seq(f_ref.at[pair], land.at[me], s1.at[pair], r1.at[me], pair).wait_send()

    @pl.when(me < PAIRS)
    def _():
        for t in range(n):

            @pl.when(me != t)
            def _(t=t):
                to_seq(b_ref.at[me], b_ref.at[me], s2.at[t], r2.at[me], t).wait_send()

    for copy in leaving:
        copy.wait()


def front(n, lens, x, taps, bq, bv, bo, g1, b1, wq, wk, wv, wo):
    slots, width = x.shape
    segs = lens.shape[1]
    dma = pltpu.SemaphoreType.DMA
    vm = lambda *dims: pltpu.VMEM(dims, f32)
    anywhere = pl.BlockSpec(memory_space=pl.ANY)
    square = (LANES, LANES)
    rows = shape(slots, width)
    count = 3 * QUADS
    return pl.pallas_call(
        partial(front_kernel, n),
        in_specs=[smem()] + [whole()] * 7 + [anywhere] * 4,
        out_specs=[anywhere] * 9 + [whole()] * 12,
        out_shape=[rows] * 6 + [shape(slots + 40, width), rows, rows]
        + [
            shape(1, width), shape(PAIRS, MSG, LANES), shape(DH, width), shape(DH, width), shape(*square),
            shape(NEWTON + 1, *square), shape(NEWTON, *square), shape(NEWTON, *square), shape(NEWTON, *square),
            shape(DH, LANES), shape(CONV, width), shape(slots, 1),
        ],
        scratch_shapes=[
            vm(count, width, QUAD), vm(width, width), vm(count, 8, QUAD), vm(8, slots, width), vm(slots + 40, width),
            vm(PAIRS, MSG, LANES), vm(2, segs, width), vm(n, 2, segs, width), vm(2 * RIM, width), vm(RIM, width),
            vm(RIM, width), vm(n, MSG, LANES),
            dma((count + 1,)), dma((9,)), dma((2,)), dma((2,)), dma((n,)), dma((n,)), dma((PAIRS,)), dma((n,)),
            dma((n,)), dma((n,)),
        ],
        compiler_params=params(collective_id=1, has_side_effects=True),
        name="front",
    )(lens, x, taps, bq, bv, bo, g1, b1, wq, wk, wv, wo)


def forward_kernel(
    lens_ref, h1_ref, wi_ref, bi_ref, wo_ref, bo_ref, cot_ref, g2_ref, b2_ref,
    pre_ref, out_ref, gs2_ref, small_ref,
    acc_ref, act_ref,
):
    step = pl.program_id(0)

    @pl.when(step == 0)
    def _():
        acc_ref[...] = jnp.zeros_like(acc_ref)

    def one(g, carry):
        cols = quad(g)
        pre = mm(h1_ref[...], wi_ref[:, cols]) + bi_ref[:, cols]
        pre_ref[:, cols] = pre
        act_ref[:, cols] = 0.5 * pre * (1.0 + lax.erf(pre * ROOT_HALF))
        return carry

    lax.fori_loop(0, QUADS, one, 0)

    def two(g, carry):
        cols = quad(g)
        acc_ref[:, cols] += mm(act_ref[...], wo_ref[:, cols])
        return carry

    lax.fori_loop(0, QUADS, two, 0)

    @pl.when(step == pl.num_programs(0) - 1)
    def _():
        slots = h1_ref.shape[0]
        valid = valid_rows(seg_ends(lens_ref, lens_ref.shape[1])[-1], slots)
        summed = h1_ref[...] + (acc_ref[...] + bo_ref[...][None, :])
        unit, inv = norm_stats(summed)
        out_ref[...] = jnp.where(valid, unit * g2_ref[...][None, :] + b2_ref[...][None, :], 0.0)
        e = jnp.where(valid, cot_ref[...], 0.0)
        grad = norm_back(unit, inv, g2_ref[...][None, :], e)
        gs2_ref[...] = grad
        small_ref[...] = jnp.concatenate(
            [
                jnp.sum(e * unit, axis=0, keepdims=True),
                jnp.sum(e, axis=0, keepdims=True),
                jnp.sum(grad, axis=0, keepdims=True),
                jnp.zeros((5, e.shape[1]), f32),
            ],
            axis=0,
        )


def ffn_forward(lens, h1, wi, bi, wo, bo, cot, g2, b2):
    slots, width = h1.shape
    inner = wi.shape[1]
    const = lambda *dims: pl.BlockSpec(dims, lambda j: (0,) * len(dims))
    return pl.pallas_call(
        forward_kernel,
        grid=(inner // width,),
        in_specs=[
            smem(), const(slots, width),
            pl.BlockSpec((width, width), lambda j: (0, j)), pl.BlockSpec((1, width), lambda j: (0, j)),
            pl.BlockSpec((width, width), lambda j: (j, 0)), const(width),
            const(slots, width), const(width), const(width),
        ],
        out_specs=[
            pl.BlockSpec((slots, width), lambda j: (0, j)),
            const(slots, width), const(slots, width), const(8, width),
        ],
        out_shape=[shape(slots, inner), shape(slots, width), shape(slots, width), shape(8, width)],
        scratch_shapes=[pltpu.VMEM((slots, width), f32)] * 2,
        compiler_params=params(),
        name="ffn_forward",
    )(lens, h1, wi, bi, wo, bo, cot, g2, b2)


def put_strips(ref, block, rows=slice(None), first=0):
    for s in range(block.shape[1] // LANES):
        ref[first + s, rows, :] = block[:, s * LANES : (s + 1) * LANES]


def backward_kernel(
    h1_ref, gs2_ref, pre_ref, wi_ref, wo_ref, u1_ref, inv1_ref, g1_ref,
    dwo_ref, dwi_ref, gs1_ref, dbi_ref, small_ref,
    acc_ref, gpre_ref,
):
    step = pl.program_id(0)

    @pl.when(step == 0)
    def _():
        acc_ref[...] = gs2_ref[...]

    def one(g, carry):
        cols = quad(g)
        pre = pre_ref[:, cols]
        phi_big = 0.5 * (1.0 + lax.erf(pre * ROOT_HALF))
        slope = phi_big + pre * (INV_ROOT_TAU * jnp.exp(-0.5 * pre * pre))
        gpre = mm_t(gs2_ref[...], wo_ref[cols, :]) * slope
        gpre_ref[:, cols] = gpre
        dbi_ref[:, cols] = jnp.sum(gpre, axis=0, keepdims=True)
        put_strips(dwo_ref, t_mm(pre * phi_big, gs2_ref[...]), cols)
        return carry

    lax.fori_loop(0, QUADS, one, 0)

    def two(g, carry):
        cols = quad(g)
        put_strips(dwi_ref, t_mm(h1_ref[:, cols], gpre_ref[...]), cols)
        acc_ref[:, cols] += mm_t(gpre_ref[...], wi_ref[cols, :])
        return carry

    lax.fori_loop(0, QUADS, two, 0)

    @pl.when(step == pl.num_programs(0) - 1)
    def _():
        e = acc_ref[...]
        unit = u1_ref[...]
        grad = norm_back(unit, inv1_ref[...], g1_ref[...][None, :], e)
        gs1_ref[...] = grad
        small_ref[...] = jnp.concatenate(
            [
                jnp.sum(e * unit, axis=0, keepdims=True),
                jnp.sum(e, axis=0, keepdims=True),
                jnp.sum(grad, axis=0, keepdims=True),
                jnp.zeros((5, e.shape[1]), f32),
            ],
            axis=0,
        )


def ffn_backward(h1, gs2, pre, wi, wo, u1, inv1, g1):
    slots, width = h1.shape
    inner = wi.shape[1]
    strips = width // LANES
    const = lambda *dims: pl.BlockSpec(dims, lambda j: (0,) * len(dims))
    return pl.pallas_call(
        backward_kernel,
        grid=(inner // width,),
        in_specs=[
            const(slots, width), const(slots, width),
            pl.BlockSpec((slots, width), lambda j: (0, j)),
            pl.BlockSpec((width, width), lambda j: (0, j)),
            pl.BlockSpec((width, width), lambda j: (j, 0)),
            const(slots, width), const(slots, 1), const(width),
        ],
        out_specs=[
            pl.BlockSpec((strips, width, LANES), lambda j: (j, 0, 0)),
            pl.BlockSpec((strips, width, LANES), lambda j: (j, 0, 0)),
            const(slots, width),
            pl.BlockSpec((1, width), lambda j: (0, j)),
            const(8, width),
        ],
        out_shape=[
            shape(inner // LANES, width, LANES), shape(inner // LANES, width, LANES),
            shape(slots, width), shape(1, inner), shape(8, width),
        ],
        scratch_shapes=[pltpu.VMEM((slots, width), f32)] * 2,
        compiler_params=params(),
        name="ffn_backward",
    )(h1, gs2, pre, wi, wo, u1, inv1, g1)


def near_back_quad(g, gctx_ref, near_ref, q_ref, kl_ref, b_ref, gq_ref, gb_ref, gkl_ref):
    mask = head_mask(QUAD)
    ones = jnp.where(mask, 1.0, 0.0)
    cols = quad(g)
    gctx = gctx_ref[:, cols]
    near = near_ref[:, cols]
    gblend = fold(t_mm(gctx, near), mask)
    gb_ref[2 * g] = gblend[:, :LANES]
    gb_ref[2 * g + 1] = gblend[:, LANES:]
    gnear = mm(gctx, spread(pair_rows(b_ref, g, slice(0, DH)), mask))
    gscore = near * (gnear - mm(near * gnear, ones)) * SCALE
    gq_ref[:, cols] = mm(gscore, spread(kl_ref[:, cols], mask))
    gkl_ref[:, cols] = fold(t_mm(gscore, q_ref[:, cols]), mask)


def near_back_kernel(
    lens_ref, gs1_ref, wo_ref, near_ref, q_ref, kl_ref, b_ref,
    gctx_ref, gq_ref, gb_ref, gkl_ref, rim_ref,
):
    count = seg_ends(lens_ref, lens_ref.shape[1])[-1]
    gctx_ref[...] = mm_t(gs1_ref[...], wo_ref[...])
    rim_ref[...] = rims_of(gctx_ref[...], count)
    def one(g, carry):
        near_back_quad(g, gctx_ref, near_ref, q_ref, kl_ref, b_ref, gq_ref, gb_ref, gkl_ref)
        return carry

    lax.fori_loop(0, QUADS, one, 0)


def near_back(lens, gs1, wo, near, q, kl, b):
    slots, width = gs1.shape
    return pl.pallas_call(
        near_back_kernel,
        in_specs=[smem()] + [whole()] * 6,
        out_specs=[whole()] * 5,
        out_shape=[
            shape(slots, width), shape(slots, width), shape(PAIRS, DH, LANES),
            shape(DH, width), shape(2 * RIM, width),
        ],
        compiler_params=params(),
        name="near_back",
    )(lens, gs1, wo, near, q, kl, b)


def far_back_quad(g, k_ref, v_ref, p_ref, m_ref, b_ref, c_ref, ql_ref, gk_ref, gv_ref, gql_ref, add):
    mask = head_mask(QUAD)
    cols = quad(g)
    top = pair_rows(b_ref, g, slice(DH, DH + 1))
    total = pair_rows(b_ref, g, slice(DH + 1, DH + 2))
    prob = p_ref[:, cols] * (jnp.exp(m_ref[:, cols] - top) / total)
    gmixed = spread(pair_rows(c_ref, g, slice(0, DH)), mask)
    dots = pair_rows(c_ref, g, slice(DH, DH + 1))
    gscore = prob * (mm(v_ref[:, cols], gmixed) - dots) * SCALE
    gk_ref[:, cols] = mm(gscore, spread(ql_ref[:, cols], mask))
    gval = mm_t(prob, gmixed)
    if add:
        gv_ref[:, cols] += gval
    else:
        gv_ref[:, cols] = gval
    gql_ref[:, cols] = fold(t_mm(gscore, k_ref[:, cols]), mask)


def land_parts(ret_ref, gql, gkl):
    n, _, segs, _ = ret_ref.shape
    for s in range(n):
        rows = slice(s * segs, (s + 1) * segs)
        ret_ref[s, 0] = gql[rows]
        ret_ref[s, 1] = gkl[rows]


def far_back_kernel(
    k_ref, v_ref, p_ref, m_ref, b_ref, c_ref, ql_ref, gkl_ref, gl_ref,
    gk_ref, gv_ref, ret_ref, gql_ref,
):
    def one(g, carry):
        far_back_quad(g, k_ref, v_ref, p_ref, m_ref, b_ref, c_ref, ql_ref, gk_ref, gv_ref, gql_ref, False)
        return carry

    lax.fori_loop(0, QUADS, one, 0)
    land_parts(ret_ref, gql_ref[...] + gl_ref[0], gkl_ref[...] + gl_ref[1])


def far_back(n, lens, k, v, p, m, b, c, ql, gkl, gl):
    slots, width = k.shape
    segs = lens.shape[1]
    return pl.pallas_call(
        far_back_kernel,
        in_specs=[whole()] * 9,
        out_specs=[whole()] * 3,
        out_shape=[shape(slots, width), shape(slots, width), shape(n, 2, segs, width)],
        scratch_shapes=[pltpu.VMEM((DH, width), f32)],
        compiler_params=params(),
        name="far_back",
    )(k, v, p, m, b, c, ql, gkl, gl)


def taps_sums(scr_ref):
    width = scr_ref.shape[2]
    rows = jnp.concatenate(
        [jnp.sum(scr_ref[c], axis=0, keepdims=True) for c in range(CONV)] + [jnp.zeros((7, width), f32)], axis=0
    )
    row = lax.broadcasted_iota(jnp.int32, (width, LANES), 0) >> 6
    col = lax.broadcasted_iota(jnp.int32, (width, LANES), 1)
    return mm(rows, jnp.where(row == col, 1.0, 0.0), TOP)


def conv_back_kernel(
    lens_ref, values_ref, gctx_ref, gleft_ref, gright_ref, taps_ref, ctx_ref, gs1_ref,
    gv_ref, gtaps_ref, dwo_ref,
    ext_ref, scr_ref,
):
    slots = gctx_ref.shape[0]
    count = seg_ends(lens_ref, lens_ref.shape[1])[-1]
    put_strips(dwo_ref, t_mm(ctx_ref[...], gs1_ref[...]))
    fill_extended(ext_ref, gctx_ref[...], gleft_ref[...], gright_ref[...], count)
    conv_into(gv_ref, ext_ref, taps_ref, slots, True, False)
    taps_grad_into(scr_ref, gctx_ref, values_ref, slots)
    gtaps_ref[...] = taps_sums(scr_ref)


def conv_back(lens, ext, gctx, gleft, gright, taps, ctx, gs1):
    slots, width = gctx.shape
    return pl.pallas_call(
        conv_back_kernel,
        in_specs=[smem()] + [whole()] * 7,
        out_specs=[whole()] * 3,
        out_shape=[shape(slots, width), shape(40, LANES), shape(width // LANES, width, LANES)],
        scratch_shapes=[pltpu.VMEM((slots + 40, width), f32), pltpu.VMEM((CONV, 8, width), f32)],
        compiler_params=params(),
        name="conv_back",
    )(lens, ext, gctx, gleft, gright, taps, ctx, gs1)


def project_back_kernel(
    lens_ref, x_ref, gs1_ref, gqn_ref, gkf_ref, gvc_ref, gvf_ref, own_ref, wq_ref, wk_ref, wv_ref,
    ig_ref, dq_ref, dk_ref, dv_ref, small_ref,
    gq_ref, gk_ref, gv_ref,
):
    @pl.when(pl.program_id(0) == 0)
    def _():
        slots = gqn_ref.shape[0]
        segs = own_ref.shape[1]
        ends = seg_ends(lens_ref, segs)
        member = member_rows(ends, slots)
        inv = inverse_lens(lens_ref, segs)
        gq = gqn_ref[...] + t_mm(member, own_ref[0] * inv)
        gk = gkf_ref[...] + t_mm(member, own_ref[1] * inv)
        gv = jnp.where(valid_rows(ends[-1], slots), gvc_ref[...] + gvf_ref[...], 0.0)
        gq_ref[...] = gq
        gk_ref[...] = gk
        gv_ref[...] = gv
        small_ref[...] = jnp.concatenate(
            [
                jnp.sum(gq, axis=0, keepdims=True),
                jnp.sum(gv, axis=0, keepdims=True),
                jnp.zeros((6, gq.shape[1]), f32),
            ],
            axis=0,
        )

    x = x_ref[...]
    put_strips(dq_ref, t_mm(x, gq_ref[...]))
    put_strips(dk_ref, t_mm(x, gk_ref[...]))
    put_strips(dv_ref, t_mm(x, gv_ref[...]))
    ig_ref[...] = (
        gs1_ref[...]
        + mm_t(gq_ref[...], wq_ref[...])
        + mm_t(gk_ref[...], wk_ref[...])
        + mm_t(gv_ref[...], wv_ref[...])
    )


def project_back(lens, x, gs1, gqn, gkf, gvc, gvf, own, wq, wk, wv):
    slots, width = x.shape
    col = 256
    strips = width // LANES
    const = lambda *dims: pl.BlockSpec(dims, lambda i: (0,) * len(dims))
    part = pl.BlockSpec((slots, col), lambda i: (0, i))
    wspec = pl.BlockSpec((col, width), lambda i: (i, 0))
    dspec = pl.BlockSpec((strips, col, LANES), lambda i: (0, i, 0))
    return pl.pallas_call(
        project_back_kernel,
        grid=(width // col,),
        in_specs=[smem(), part, part] + [const(slots, width)] * 4 + [const(*own.shape), wspec, wspec, wspec],
        out_specs=[part, dspec, dspec, dspec, const(8, width)],
        out_shape=[shape(slots, width)] + [shape(strips, width, LANES)] * 3 + [shape(8, width)],
        scratch_shapes=[pltpu.VMEM((slots, width), f32)] * 3,
        compiler_params=params(),
        name="project_back",
    )(lens, x, gs1, gqn, gkf, gvc, gvf, own, wq, wk, wv)


def sum_plain(parts):
    sizes = [part.size for part in parts]
    shapes = [part.shape for part in parts]
    devices = lax.axis_size(("seq", "dp"))
    flat = jnp.concatenate([part.reshape(-1) for part in parts])
    flat = jnp.pad(flat, (0, -flat.shape[0] % devices))
    own = lax.psum_scatter(flat, ("seq", "dp"), scatter_dimension=0, tiled=True)
    flat = lax.all_gather(own, ("seq", "dp"), axis=0, tiled=True)
    out = []
    at = 0
    for size, dims in zip(sizes, shapes):
        out.append(flat[at : at + size].reshape(dims))
        at += size
    return out


STRIP = 768
HALF = STRIP // 2
PART = HALF // 2
Z_ROWS = PART // 4
OWN = Z_ROWS // 2
STAGES = 13
SMALL_STEPS = 5


def pack_small(sb_ref, small0, small1, small2, inner_bias, taps):
    at = 0
    for ref, count in ((small0, 2), (small1, 3), (small2, 3), (inner_bias, 1)):
        for r in range(count):
            for j in range(ref.shape[1] // LANES):
                sb_ref[0, at : at + 1, :] = ref[r : r + 1, j * LANES : (j + 1) * LANES]
                at += 1
    sb_ref[0, at : at + 40, :] = taps[...]


SMALL_ROWS = 8 * 6 + 24 + 40


def unpack_small(s_ref, outs):
    at = 0
    for ref in outs[:-1]:
        for j in range(ref.shape[0] // LANES):
            ref[pl.ds(j * LANES, LANES)] = s_ref[at, :]
            at += 1
    outs[-1][...] = s_ref[at : at + CONV, :HEADS]


def reduce_stages(gw, o_ref, bufs, sems):
    acc, lc, l1, mid, lz, l3, ag = bufs
    cs, cr, s1, r1, ms, zr, r3, r4, gs, gr, r5, keep, es, er = sems
    seq = lax.axis_index("seq")
    dp = lax.axis_index("dp")
    z = seq // 2
    c = lax.rem(seq, 2)
    y = dp // 2
    x = lax.rem(dp, 2)
    zb = 3 - z
    place = lambda z_, c_, y_, x_: (z_ * 2 + c_, y_ * 2 + x_)
    by_core = place(z, 1 - c, y, x)
    by_x = place(z, c, y, 1 - x)
    by_y = place(z, c, 1 - y, x)
    right = place(lax.rem(z + 1, 4), c, y, x)
    left = place(lax.rem(z + 3, 4), c, y, x)
    opposite = place(lax.rem(z + 2, 4), c, y, x)
    near_z = place(z + 1 - 2 * lax.rem(z, 2), c, y, x)

    def remote(src, dst, send, recv, target):
        return pltpu.make_async_remote_copy(src, dst, send, recv, device_id=target, device_id_type=MESH)

    aligned = lambda at: pl.multiple_of(at, 8)
    slot = lambda ref, k: lax.rem(k, ref.shape[0])
    starts = (x * PART, HALF + y * PART)
    others = ((1 - x) * PART, HALF + (1 - y) * PART)
    own_rows = (pl.ds(aligned(y * OWN), OWN), pl.ds(aligned(x * OWN), OWN))
    other_rows = (pl.ds(aligned((1 - y) * OWN), OWN), pl.ds(aligned((1 - x) * OWN), OWN))
    first_to = (by_x, by_y)
    third_to = (by_y, by_x)
    ways = ((0, z, right), (1, zb, left))

    def bytes_of(rows, send, recv, pieces=1):
        part = lc.at[pl.ds(0, pieces), pl.ds(0, rows // pieces)]
        return remote(part, part, send, recv, by_core)

    def strip(k):
        return lax.rem(k // 3, GW_SLOTS) * PAIRS + 2 * lax.rem(k, 3)

    def core_copy(k):
        return remote(gw.at[strip(k) + 1 - c], lc.at[slot(lc, k)], cs.at[k], cr.at[k], by_core)

    def core_out(k):
        core_copy(k).start()

    def first_out(k):
        core_copy(k).wait()
        at = slot(acc, k)
        acc[at] = gw[strip(k) + c] + lc[slot(lc, k)]
        for j in range(2):
            remote(
                acc.at[at, pl.ds(aligned(others[j]), PART)], l1.at[slot(l1, k), j], s1.at[k], r1.at[k], first_to[j]
            ).start()

    def z_copy(k, way, step, block, target):
        return remote(mid.at[slot(mid, k), block], lz.at[slot(lz, k), way, step], ms.at[k], zr.at[k, way, step], target)

    def z_out(k, step):
        if step == 0:
            bytes_of(HALF, s1.at[k], r1.at[k]).wait()
            for j in range(2):
                for block in range(4):
                    here = pl.ds(aligned(starts[j] + block * Z_ROWS), Z_ROWS)
                    there = pl.ds(block * Z_ROWS, Z_ROWS)
                    mid[slot(mid, k), block, j] = acc[slot(acc, k), here] + l1[slot(l1, k), j, there]
        for way, at, target in ways:
            block = 3 - step + z if way == 0 else step - zb
            if step > 0:

                @pl.when((at > 0) & (at <= step))
                def _(way=way, block=block, target=target):
                    z_copy(k, way, step - 1, 0, target).wait_recv()
                    mid[slot(mid, k), block] += lz[slot(lz, k), way, step - 1]

            if step < 3:

                @pl.when((at <= step) & (at < 3))
                def _(way=way, block=block, target=target):
                    z_copy(k, way, step, block, target).start()

    def third_out(k):
        z_out(k, 3)
        for j in range(2):
            remote(
                mid.at[slot(mid, k), z, j, other_rows[j]], l3.at[slot(l3, k), j], ms.at[k], r3.at[k], third_to[j]
            ).start()

    def back_third_out(k):
        bytes_of(2 * OWN, ms.at[k], r3.at[k]).wait_recv()
        for j in range(2):
            ag[slot(ag, k), z, j, own_rows[j]] = mid[slot(mid, k), z, j, own_rows[j]] + l3[slot(l3, k), j]
            part = ag.at[slot(ag, k), z, j, own_rows[j]]
            remote(part, part, gs.at[k], r4.at[k], third_to[j]).start()

    def back_z(k, way, step, block, target):
        part = ag.at[slot(ag, k), block]
        return remote(part, part, gs.at[k], gr.at[k, way, step], target)

    def back_z_out(k, step):
        if step == 0:
            bytes_of(6 * Z_ROWS + 2 * OWN, ms.at[k], r3.at[k]).wait_send()
            bytes_of(2 * OWN, gs.at[k], r4.at[k]).wait_recv()
        for way, at, target in ways:
            block = z - step if way == 0 else z + step
            if step > 0:

                @pl.when(at >= step)
                def _(way=way, target=target):
                    back_z(k, way, step - 1, 0, target).wait_recv()

            if step < 3:

                @pl.when((at >= step) & (at < 3))
                def _(way=way, block=block, target=target):
                    back_z(k, way, step, block, target).start()

    blocks = (pl.ds(x * 4, 4), pl.ds(8 + y * 4, 4))

    def keep_copy(k, j):
        return pltpu.make_async_copy(ag.at[slot(ag, k), :, j], o_ref.at[c, k, blocks[j]], keep.at[k, j])

    def back_first_out(k):
        back_z_out(k, 3)
        for j in range(2):
            remote(ag.at[slot(ag, k), :, j], o_ref.at[c, k, blocks[j]], gs.at[k], r5.at[k], first_to[j]).start()
            keep_copy(k, j).start()

    def back_core(k):
        part = o_ref.at[c, k]
        return remote(part, part, es.at[k], er.at[k], by_core)

    def back_core_out(k):
        bytes_of(HALF, gs.at[k], r5.at[k]).wait_recv()
        for j in range(2):
            keep_copy(k, j).wait()

        @pl.when((z == 0) | (z == 3))
        def _():
            bytes_of(2 * OWN + 2 * Z_ROWS + HALF, gs.at[k], r5.at[k]).wait_send()

        @pl.when((z > 0) & (z < 3))
        def _():
            bytes_of(2 * OWN + 10 * Z_ROWS + HALF, gs.at[k], r5.at[k], 2).wait_send()

        back_core(k).start()

    def finish(k):
        back_core(k).wait()

    stages = [
        core_out, first_out, partial(z_out, step=0), partial(z_out, step=1), partial(z_out, step=2), third_out,
        back_third_out, partial(back_z_out, step=0), partial(back_z_out, step=1), partial(back_z_out, step=2),
        back_first_out, back_core_out, finish,
    ]
    return stages, (by_core, by_x, by_y, near_z, opposite), remote


LAG = tuple(range(0, 2 * STAGES, 2))
CHUNKS = 36
GW_SLOTS = 4
RING_ACC = 6
RING_LC = 4
RING_MID = 12
RING_Z = 6
RING_AG = 16
SEQ_DEVICES = 8
SMALL_AT = 36
ENTER = 2
HELD = 30
GAP = 2
GS1, GS2, H1, ACT, GPRE, PRE, _, U1, GCTX, IG = range(10)
GV, PROB, CTX, KEYS, NEAR, QUERY, VALS = GS2, H1, ACT, GPRE, PRE, PRE + 1, U1
FFN_AT = (0, 4, 8, 13)
GS1_AT = 17
OUTPUT_AT, VALUE_AT, QUERY_AT, KEY_AT = 21, 28, 32, 33
INPUT_AT = (34, 35, 36)


def pick(t, table):
    value = jnp.int32(0)
    hit = t < 0
    for when, what in table.items():
        value = jnp.where(t == when, what, value)
        hit = hit | (t == when)
    return value, hit


def greet_block():
    seq = lax.axis_index("seq")
    dp = lax.axis_index("dp")
    y = dp // 2
    x = lax.rem(dp, 2)
    barrier = pltpu.get_barrier_semaphore()
    for d in range(1, SEQ_DEVICES):
        pl.semaphore_signal(
            barrier, inc=1, device_id=(lax.rem(seq + d, SEQ_DEVICES), dp), device_id_type=MESH
        )
    for other in (y * 2 + 1 - x, (1 - y) * 2 + x):
        pl.semaphore_signal(barrier, inc=1, device_id=(seq, other), device_id_type=MESH)
    pl.semaphore_wait(barrier, SEQ_DEVICES + 1)
    return seq


def tail_kernel(
    lens_ref, gs2_hbm, h1_hbm, u1_hbm, pre_hbm, wout_hbm, win_hbm, wo_hbm, near_hbm, q_hbm, ctx_hbm, ext_hbm,
    k_hbm, v_hbm, p_hbm, x_hbm, wq_hbm, wk_hbm, wv_hbm,
    inv1_ref, g1_ref, m_ref, b_ref, ql_ref, kl_ref, core_ref, zs_ref, ps_ref, rs_ref, qs_ref, mx_ref, taps_ref, small2_ref,
    o_ref, so_ref, ig_hbm,
    acc, lc, l1, mid, lz, l3, ag, sb, sl, gw,
    stack, w, ext, gext, tap_scr, gtaps, small0, small1, dbi,
    gb, rim, gkl, gql, gl, land, cmsg, gleft, gright, ng, ncore, ret, rland, own,
    loads, ig_sem, b1s, b1r, b2s, b2r, ms, mr, rets, retr, ss, sr,
    *sems,
):
    n = SEQ_DEVICES
    _, slots, width = stack.shape
    segs = own.shape[1]
    gs1, gv, p, ctx, k, near, q, v, gctx, ig = [
        stack.at[i] for i in (GS1, GV, PROB, CTX, KEYS, NEAR, QUERY, VALS, GCTX, IG)
    ]
    moves = []

    def load(src, dst):
        moves.append(pltpu.make_async_copy(src, dst, loads.at[len(moves)]))
        return moves[-1]

    load_gs2 = load(gs2_hbm, stack.at[GS2])
    load_w = []
    load_pre = []
    for j in range(4):
        part = pl.ds(j * width, width)
        load_w.append(load(wout_hbm.at[part, :], w.at[2 * j % 4]))
        load_w.append(load(win_hbm.at[:, part], w.at[(2 * j + 1) % 4]))
        load_pre.append(load(pre_hbm.at[:, part], stack.at[PRE + j % 2]))
    for i, hbm in enumerate((wo_hbm, wv_hbm, wq_hbm, wk_hbm)):
        load_w.append(load(hbm, w.at[i]))
    load_h1, load_u1, load_ext = load(h1_hbm, stack.at[H1]), load(u1_hbm, stack.at[U1]), load(ext_hbm, ext)
    load_near, load_q, load_ctx = load(near_hbm, near), load(q_hbm, q), load(ctx_hbm, ctx)
    load_p, load_k, load_v, load_x = load(p_hbm, p), load(k_hbm, k), load(v_hbm, v), load(x_hbm, q)
    a0, a1, a2, a3 = FFN_AT
    starting = [
        (a0 + 1, load_w[4]), (a0 + 1, load_pre[2]), (a0 + 4, load_w[5]), (a1 + 1, load_w[6]), (a1 + 1, load_pre[3]),
        (a1 + 4, load_w[7]), (a2 + 1, load_w[8]), (a2 + 1, load_near), (a2 + 4, load_w[9]), (a3 + 1, load_w[10]),
        (a3 + 1, load_q), (a3 + 2, load_ctx), (a3 + 3, load_p), (a3 + 4, load_w[11]), (a3 + 4, load_k), (a3 + 4, load_v),
        (GS1_AT + 4, load_x),
    ]
    waiting = [
        (a0, load_gs2), (a0 + 2, load_h1), (a3 + 3, load_u1), (GS1_AT, load_w[8]), (GS1_AT + 1, load_near),
        (GS1_AT + 1, load_q), (OUTPUT_AT, load_ctx), (VALUE_AT, load_x),
    ]
    for j in range(4):
        waiting += [(FFN_AT[j], load_w[2 * j]), (FFN_AT[j], load_pre[j]), (FFN_AT[j] + 3, load_w[2 * j + 1])]
    for i in range(3):
        waiting.append((INPUT_AT[i], load_w[9 + i]))
    for copy in (load_gs2, load_w[0], load_pre[0], load_h1, load_w[1], load_pre[1], load_w[2], load_w[3], load_u1, load_ext):
        copy.start()
    me = greet_block()
    owner = me < PAIRS
    stages, partners, remote = reduce_stages(gw, o_ref, (acc, lc, l1, mid, lz, l3, ag), sems)
    ends = seg_ends(lens_ref, segs)
    count = ends[-1]

    def weight_event(e, left, right):
        def one(g, carry):
            block = t_mm(stack[left, :, quad(g)], stack[right])
            put_strips(gw, block, quad(g), lax.rem(e, GW_SLOTS) * PAIRS)
            return carry

        lax.fori_loop(0, QUADS, one, 0)

    def through_event(source, target, weight):
        def one(g, carry):
            stack[target, :, quad(g)] += mm_t(stack[source], w[weight, quad(g), :])
            return carry

        lax.fori_loop(0, QUADS, one, 0)

    def inner_event(j):
        @pl.when(j == 0)
        def _():
            stack[GS1] = stack[GS2]

        at = PRE + lax.rem(j, 2)
        weight = lax.rem(2 * j, 4)

        def one(g, carry):
            cols = quad(g)
            pre = stack[at, :, cols]
            phi_big = 0.5 * (1.0 + lax.erf(pre * ROOT_HALF))
            slope = phi_big + pre * (INV_ROOT_TAU * jnp.exp(-0.5 * pre * pre))
            gpre = mm_t(stack[GS2], w[weight, cols, :]) * slope
            stack[GPRE, :, cols] = gpre
            stack[ACT, :, cols] = pre * phi_big
            dbi[:, pl.ds(pl.multiple_of(j * width + g * QUAD, QUAD), QUAD)] = jnp.sum(gpre, axis=0, keepdims=True)
            return carry

        lax.fori_loop(0, QUADS, one, 0)

    def ev_norm():
        e = gs1[...]
        unit = stack[U1]
        grad = norm_back(unit, inv1_ref[...], g1_ref[...][None, :], e)
        gs1[...] = grad
        ig[...] = grad
        gctx[...] = jnp.zeros_like(grad)
        small1[0:1, :] = jnp.sum(e * unit, axis=0, keepdims=True)
        small1[1:2, :] = jnp.sum(e, axis=0, keepdims=True)
        small1[2:3, :] = jnp.sum(grad, axis=0, keepdims=True)

    def ev_rims():
        rim[...] = rims_of(gctx[...], count)

    def ev_near(g):
        near_back_quad(g, gctx, near, q, kl_ref, b_ref, near, gb, gkl)

    def blend_copy(pair):
        return to_seq(gb.at[pair], land.at[me], b1s.at[pair], b1r.at[me], pair)

    up, down = rim_copies(n, me, rim, gleft, gright, ms, mr)

    def ev_blend():
        for pair in range(PAIRS):

            @pl.when(me != pair)
            def _(pair=pair):
                blend_copy(pair).start()

        rim_start(n, me, up, down, gleft, gright)

    def mixed_copy(target):
        return to_seq(cmsg.at[me], cmsg.at[me], b2s.at[target], b2r.at[me], target)

    def ev_owner():
        @pl.when(owner)
        def _():
            land[me] = gb[me]
            for s in range(n):

                @pl.when(me != s)
                def _(s=s):
                    to_seq(gb.at[0], land.at[s], b1s.at[0], b1r.at[s], s).wait_recv()

            gblend = land[0]
            for s in range(1, n):
                gblend = gblend + land[s]
            mixed = mx_ref[...]
            gmixed = mm(gblend, zs_ref[NEWTON], TOP)
            cmsg[me, 0:DH, :] = gmixed
            dots = jnp.sum(gmixed * mixed, axis=0, keepdims=True)
            cmsg[me, DH:MSG, :] = jnp.concatenate([dots, jnp.zeros((MSG - DH - 1, LANES), f32)], axis=0)
            for t in range(n):

                @pl.when(me != t)
                def _(t=t):
                    mixed_copy(t).start()

            ng[...] = inverse_grad(gblend, mixed)
            ncore[...] = jnp.zeros_like(ncore)

        gl[...] = jnp.zeros_like(gl)

    def ev_newton(step):
        @pl.when(owner)
        def _():
            ng[...], ncore[...] = newton_back(
                ng[...], ncore[...], core_ref[...], zs_ref[step], ps_ref[step], rs_ref[step], qs_ref[step]
            )

    def ev_core():
        @pl.when(owner)
        def _():
            core_back(ng[...], ncore[...], core_ref[...], zs_ref[0], ql_ref, kl_ref, gl, me)

    quarter = slots // 4

    def ev_taps(part):
        @pl.when(part == 0)
        def _():
            load_ext.wait()
            tap_scr[...] = jnp.zeros_like(tap_scr)

        taps_grad_into(tap_scr, gctx, ext, quarter * (part + 1), quarter * part, False)

        @pl.when(part == 3)
        def _():
            gtaps[...] = taps_sums(tap_scr)

    def ev_conv(part):
        @pl.when(part == 0)
        def _():
            rim_wait(n, me, up, down)
            fill_extended(gext, gctx[...], gleft[...], gright[...], count)

        conv_into(gv, gext, taps_ref, quarter * (part + 1), True, False, quarter * part)

    def ev_mixed():
        for pair in range(PAIRS):

            @pl.when(me != pair)
            def _(pair=pair):
                to_seq(cmsg.at[pair], cmsg.at[pair], b2s.at[pair], b2r.at[pair], pair).wait_recv()

        for copy in (load_k, load_v, load_p):
            copy.wait()

    def ev_far(g):
        far_back_quad(g, k, v, p, m_ref, b_ref, cmsg, ql_ref, p, gv, gql, True)

    def ev_return():
        land_parts(ret, gql[...] + gl[0], gkl[...] + gl[1])
        for d in range(1, n):
            target = lax.rem(me + d, n)
            to_seq(ret.at[target], rland.at[me], rets.at[d], retr.at[me], target).start()

    def ev_own():
        rland[me] = ret[me]
        for d in range(1, n):
            source = lax.rem(me + d, n)
            to_seq(ret.at[0], rland.at[source], rets.at[d], retr.at[source], source).wait_recv()
        total = rland[0]
        for s in range(1, n):
            total = total + rland[s]
        own[...] = total
        inv = inverse_lens(lens_ref, segs)
        member = member_rows(ends, slots)
        near[...] += t_mm(member, own[0] * inv)
        p[...] += t_mm(member, own[1] * inv)
        small0[0:1, :] = jnp.sum(near[...], axis=0, keepdims=True)

    def ev_values():
        masked = jnp.where(valid_rows(count, slots), gv[...], 0.0)
        gv[...] = masked
        small0[1:2, :] = jnp.sum(masked, axis=0, keepdims=True)

    def small(i):
        return remote(sb.at[i], sl.at[i], ss.at[i], sr.at[i], partners[i])

    def ev_small(i):
        if i == 0:
            pack_small(sb, small0, small1, small2_ref, dbi, gtaps)
        else:
            small(i - 1).wait_recv()
            sb[i] = sb[i - 1] + sl[i - 1]
        if i < SMALL_STEPS:
            small(i).start()

    def at_tick(t, when, event):
        @pl.when(t == when)
        def _():
            event()

    def at_ticks(t, start, every, count, event):
        after = t - start

        @pl.when((after >= 0) & (after < every * count) & (lax.rem(after + every, every) == 0))
        def _():
            event(after // every)

    weights = {}
    through = {}
    for j, when in enumerate(FFN_AT):
        weights[when + 1] = (2 * j, ACT, GS2)
        weights[when + 2] = (2 * j + 1, H1, GPRE)
        through[when + 3] = (GPRE, GS1, (2 * j + 1) % 4)
    weights[OUTPUT_AT] = (8, CTX, GS1)
    for i, (when, part) in enumerate(((VALUE_AT, GV), (QUERY_AT, NEAR), (KEY_AT, PROB))):
        weights[when] = (9 + i, QUERY, part)
        through[INPUT_AT[i]] = (part, IG, 1 + i)
    through[GS1_AT] = (GS1, GCTX, 0)

    def by_table(t, table, event):
        columns = [pick(t, {when: row[i] for when, row in table.items()}) for i in range(3)]

        @pl.when(columns[0][1])
        def _():
            event(*[value for value, _ in columns])

    def tick(t, carry):
        for stage, run in reversed(list(enumerate(stages))):
            since = t - ENTER - LAG[stage]
            at = jnp.where(since < HELD, since, since - GAP)

            @pl.when((since >= 0) & ((since < HELD) | (since >= HELD + GAP)) & (at < CHUNKS))
            def _(run=run, at=at):
                run(at)

        for when, copy in starting:
            at_tick(t, when, copy.start)
        for when, copy in waiting:
            at_tick(t, when, copy.wait)
        block, hit = pick(t, {when: j for j, when in enumerate(FFN_AT)})

        @pl.when(hit)
        def _():
            inner_event(block)

        by_table(t, through, through_event)
        by_table(t, weights, weight_event)
        at_tick(t, FFN_AT[3] + 3, ev_norm)
        at_tick(t, GS1_AT, ev_rims)
        at_ticks(t, GS1_AT + 1, 1, QUADS, ev_near)
        at_tick(t, GS1_AT + 3, ev_blend)
        at_tick(t, GS1_AT + 5, ev_owner)
        at_ticks(t, GS1_AT + 6, 1, NEWTON, lambda i: ev_newton(NEWTON - 1 - i))
        at_ticks(t, GS1_AT + 5, 1, 4, ev_conv)
        at_tick(t, GS1_AT + 8, ev_mixed)
        at_ticks(t, GS1_AT + 8, 1, QUADS, ev_far)
        at_tick(t, GS1_AT + 10, ev_values)
        at_tick(t, GS1_AT + 12, ev_core)
        at_tick(t, GS1_AT + 12, ev_return)
        at_ticks(t, GS1_AT + 11, 1, 4, ev_taps)
        at_tick(t, GS1_AT + 14, ev_own)
        at_tick(t, INPUT_AT[2], lambda: pltpu.make_async_copy(ig, ig_hbm, ig_sem.at[0]).start())
        for i in range(SMALL_STEPS + 1):
            at_tick(t, SMALL_AT + 2 * i, partial(ev_small, i))
        return carry

    lax.fori_loop(0, CHUNKS + ENTER + GAP + LAG[-1], tick, 0)
    for i in range(SMALL_STEPS):
        small(i).wait_send()
    so_ref[...] = sb[SMALL_STEPS]
    pltpu.make_async_copy(ig, ig_hbm, ig_sem.at[0]).wait()
    for pair in range(PAIRS):

        @pl.when(me != pair)
        def _(pair=pair):
            blend_copy(pair).wait_send()

    @pl.when(owner)
    def _():
        for t in range(n):

            @pl.when(me != t)
            def _(t=t):
                mixed_copy(t).wait_send()

    for d in range(1, n):
        target = lax.rem(me + d, n)
        to_seq(ret.at[target], rland.at[me], rets.at[d], retr.at[me], target).wait_send()


def tail(lens, big, little):
    slots, width = big[0].shape
    segs = lens.shape[1]
    at = CHUNKS
    n = SEQ_DEVICES
    dma = pltpu.SemaphoreType.DMA
    vm = lambda *dims: pltpu.VMEM(dims, f32)
    anywhere = pl.BlockSpec(memory_space=pl.ANY)
    one = dma((at,))
    zsem = dma((at, 2, 3))
    return pl.pallas_call(
        tail_kernel,
        in_specs=[smem()] + [anywhere] * len(big) + [whole()] * len(little),
        out_specs=[anywhere, whole(), anywhere],
        out_shape=[shape(2, at, STRIP // Z_ROWS, Z_ROWS, LANES), shape(SMALL_ROWS, LANES), shape(slots, width)],
        scratch_shapes=[
            vm(RING_ACC, STRIP, LANES), vm(RING_LC, STRIP, LANES), vm(RING_LC, 2, PART, LANES),
            vm(RING_MID, 4, 2, Z_ROWS, LANES), vm(RING_Z, 2, 3, 2, Z_ROWS, LANES), vm(RING_LC, 2, OWN, LANES),
            vm(RING_AG, 4, 2, Z_ROWS, LANES),
            vm(SMALL_STEPS + 1, SMALL_ROWS, LANES), vm(SMALL_STEPS, SMALL_ROWS, LANES), vm(GW_SLOTS * PAIRS, STRIP, LANES),
            vm(10, slots, width), vm(4, width, width), vm(slots + 40, width), vm(slots + 40, width),
            vm(CONV, 8, width), vm(40, LANES), vm(8, width), vm(8, width), vm(1, 4 * width),
            vm(PAIRS, DH, LANES), vm(2 * RIM, width), vm(DH, width), vm(DH, width), vm(2, DH, width),
            vm(n, DH, LANES), vm(PAIRS, MSG, LANES), vm(RIM, width), vm(RIM, width), vm(LANES, LANES), vm(LANES, LANES),
            vm(n, 2, segs, width), vm(n, 2, segs, width), vm(2, segs, width),
            dma((27,)), dma((1,)), dma((PAIRS,)), dma((n,)), dma((n,)), dma((n,)), dma((2,)), dma((2,)),
            dma((n,)), dma((n,)), dma((SMALL_STEPS,)), dma((SMALL_STEPS,)),
            one, one, one, one, one, zsem, one, one, one, zsem, one, dma((at, 2)), one, one,
        ],
        compiler_params=params(collective_id=5, has_side_effects=True),
        name="tail",
    )(lens, *big, *little)


def unstrip(strips):
    count, rows, _ = strips.shape
    return strips.transpose(1, 0, 2).reshape(rows, count * LANES)


def unstrip_tall(strips, across):
    count, rows, _ = strips.shape
    down = count // across
    return strips.reshape(down, across, rows, LANES).transpose(0, 2, 1, 3).reshape(down * rows, across * LANES)


PLACE_SLOTS = 24


def place_strips_kernel(s_ref, small_ref, *refs):
    outs = refs[:6]
    smalls = refs[6:-3]
    buf, in_sem, out_sem = refs[-3:]
    moves = []
    for e in range(CHUNKS // 3):
        if e < 8:
            out, row, col = outs[e % 2], (e // 2) * (1 - e % 2), (e // 2) * (e % 2)
        else:
            out, row, col = outs[e - 6], 0, 0
        for k in range(3):
            for c in range(2):
                rows = pl.ds(row * STRIP, STRIP)
                cols = pl.ds(col * STRIP + (2 * k + c) * LANES, LANES)
                slot = len(moves) % PLACE_SLOTS
                moves.append((
                    pltpu.make_async_copy(s_ref.at[c, 3 * e + k], buf.at[slot], in_sem.at[slot]),
                    pltpu.make_async_copy(buf.at[slot], out.at[rows, cols], out_sem.at[slot]),
                ))
    ahead = PLACE_SLOTS // 2
    for i in range(len(moves) + ahead):
        if i < len(moves):
            if i >= PLACE_SLOTS:
                moves[i - PLACE_SLOTS][1].wait()
            moves[i][0].start()
        if i >= ahead:
            moves[i - ahead][0].wait()
            moves[i - ahead][1].start()
    unpack_small(small_ref, smalls)
    for _, out in moves[-PLACE_SLOTS:]:
        out.wait()


def place_strips(summed, packed, shapes):
    anywhere = pl.BlockSpec(memory_space=pl.ANY)
    dma = pltpu.SemaphoreType.DMA
    width = shapes[0][1]
    return pl.pallas_call(
        place_strips_kernel,
        in_specs=[anywhere, whole()],
        out_specs=[anywhere] * len(shapes) + [whole()] * 10,
        out_shape=[shape(*dims) for dims in shapes] + [shape(width)] * 8 + [shape(shapes[0][0]), shape(CONV, HEADS)],
        scratch_shapes=[pltpu.VMEM((PLACE_SLOTS, STRIP, LANES), f32), dma((PLACE_SLOTS,)), dma((PLACE_SLOTS,))],
        compiler_params=params(),
        name="place_strips",
    )(summed, packed)


def per_device(
    tokens, segment_lens, query_weight, query_bias, key_weight, value_weight, value_bias, conv_taps,
    output_weight, output_bias, first_gain, first_bias, inner_weight, inner_bias, outer_weight, outer_bias,
    second_gain, second_bias, cotangent,
):
    n = lax.axis_size("seq")
    _, slots, width = tokens.shape
    x = tokens.reshape(slots, width)
    cot = cotangent.reshape(slots, width)
    lens = segment_lens

    q, k, v, raised, near, ctx, ext, h1, u1, tops, b, ql, kl, *saved, taps, inv1 = front(
        n, lens, x, conv_taps, query_bias, value_bias, output_bias, first_gain, first_bias,
        query_weight, key_weight, value_weight, output_weight,
    )
    pre, layer_out, gs2, small2 = ffn_forward(
        lens, h1, inner_weight, inner_bias.reshape(1, -1), outer_weight, outer_bias, cot, second_gain, second_bias
    )
    weights = [outer_weight, inner_weight, output_weight, value_weight, query_weight, key_weight]
    if n == SEQ_DEVICES and lax.axis_size("dp") == 4:
        big = [
            gs2, h1, u1, pre, outer_weight, inner_weight, output_weight, near, q, ctx, ext, k, v, raised, x,
            query_weight, key_weight, value_weight,
        ]
        little = [inv1, first_gain, tops, b, ql, kl, *saved, taps, small2]
        summed, packed, input_grad = tail(lens, big, little)
        sums = place_strips(summed.reshape(2, CHUNKS, STRIP, LANES), packed, [w.shape for w in weights])
    else:
        d_outer, d_inner, gs1, d_inner_bias, small1 = ffn_backward(
            h1, gs2, pre, inner_weight, outer_weight, u1, inv1, first_gain
        )
        gctx, gqn, gblend, gkl, grim = near_back(lens, gs1, output_weight, near, q, kl, b)
        c, gleft, gright, gl = blend_exchange(n, gblend, grim, ql, kl, saved)
        gkf, gvf, back = far_back(n, lens, k, v, raised, tops, b, c, ql, gkl, gl)
        own = land_return(n, back)
        gvc, gtaps, d_output = conv_back(lens, ext, gctx, gleft, gright, taps, ctx, gs1)
        input_grad, d_query, d_key, d_value, small0 = project_back(
            lens, x, gs1, gqn, gkf, gvc, gvf, own, query_weight, key_weight, value_weight
        )
        grads = [d_outer, d_inner, d_output, d_value, d_query, d_key]
        sums = sum_plain(grads + [small0, small1, small2, d_inner_bias, gtaps])
        small = sums[6:]
        sums = (
            [unstrip_tall(sums[0], width // LANES)] + [unstrip(s) for s in sums[1:6]]
            + [small[0][0], small[0][1], *small[1][:3], *small[2][:3], small[3][0], small[4][:CONV, :HEADS]]
        )
    d_outer, d_inner, d_output, d_value, d_query, d_key, *vectors = sums
    d_query_bias, d_value_bias, d_first_gain, d_first_bias, d_output_bias = vectors[:5]
    d_second_gain, d_second_bias, d_outer_bias, d_inner_bias, d_taps = vectors[5:]
    return (
        layer_out.reshape(tokens.shape), input_grad.reshape(tokens.shape),
        d_query, d_query_bias, d_key, d_value, d_value_bias, d_taps,
        d_output, d_output_bias, d_first_gain, d_first_bias,
        d_inner, d_inner_bias, d_outer, d_outer_bias, d_second_gain, d_second_bias,
    )


def solution(mesh):
    block = P("dp", "seq", None)
    return jax.shard_map(
        per_device,
        mesh=mesh,
        in_specs=(block, P("dp", "seq")) + (P(),) * 16 + (block,),
        out_specs=(block, block) + (P(),) * 16,
        check_vma=False,
    )
```

```python
from functools import partial
import math

import jax
import jax.numpy as jnp
from jax import lax
from jax.experimental import pallas as pl
from jax.experimental.pallas import tpu as pltpu
from jax.sharding import PartitionSpec as P

HEADS = 12
DH = 64
CONV = 33
NEWTON = 6
RIM = (CONV - 1) // 2
LANES = 128
PAIRS = HEADS * DH // LANES
QUAD = 256
QUADS = HEADS * DH // QUAD
SCALE = DH ** (-0.5)
EPS = 1e-05
ROOT_HALF = 0.7071067811865476
INV_ROOT_TAU = 0.3989422804014327
MASKED = -1e30
f32 = jnp.float32
HI = lax.Precision.HIGH
TOP = lax.Precision.HIGHEST
MESH = pl.DeviceIdType.MESH
VMEM_CAP = 60 << 20


def _dg(a, b, ca, cb, prec):
    return lax.dot_general(
        a, b, (((ca,), (cb,)), ((), ())), precision=prec, preferred_element_type=f32
    )


def mm(a, b, prec=HI):
    return _dg(a, b, 1, 0, prec)


def mm_t(a, b, prec=HI):
    return _dg(a, b, 1, 1, prec)


def t_mm(a, b, prec=HI):
    return _dg(a, b, 0, 0, prec)


def head_mask(size):
    row = lax.broadcasted_iota(jnp.int32, (size, size), 0) >> 6
    col = lax.broadcasted_iota(jnp.int32, (size, size), 1) >> 6
    return row == col


def spread(rows, mask):
    return jnp.where(mask, jnp.concatenate([rows] * (mask.shape[0] // DH), axis=0), 0.0)


def fold(square, mask):
    kept = jnp.where(mask, square, 0.0)
    total = kept[:DH]
    for at in range(DH, mask.shape[0], DH):
        total = total + kept[at : at + DH]
    return total


def seg_ends(lens_ref, count):
    ends = []
    total = 0
    for j in range(count):
        total = total + lens_ref[0, j]
        ends.append(total)
    return ends


def member_rows(ends, slots):
    shape = (len(ends), slots)
    row = lax.broadcasted_iota(jnp.int32, shape, 0)
    col = lax.broadcasted_iota(jnp.int32, shape, 1)
    low = jnp.zeros(shape, jnp.int32)
    high = jnp.zeros(shape, jnp.int32)
    before = 0
    for j, end in enumerate(ends):
        low = jnp.where(row == j, before, low)
        high = jnp.where(row == j, end, high)
        before = end
    return jnp.where((col >= low) & (col < high), 1.0, 0.0)


def inverse_lens(lens_ref, count):
    row = lax.broadcasted_iota(jnp.int32, (count, 1), 0)
    out = jnp.zeros((count, 1), f32)
    for j in range(count):
        out = jnp.where(row == j, lens_ref[0, j].astype(f32), out)
    return 1.0 / out


def valid_rows(count, slots):
    return lax.broadcasted_iota(jnp.int32, (slots, 1), 0) < count


def rims_of(matrix, count):
    slots = matrix.shape[0]
    row = lax.broadcasted_iota(jnp.int32, (2 * RIM, slots), 0)
    col = lax.broadcasted_iota(jnp.int32, (2 * RIM, slots), 1)
    want = jnp.where(row < RIM, row, row - 2 * RIM + count)
    return mm(jnp.where(col == want, 1.0, 0.0), matrix)


def fill_extended(ext_ref, middle, left, right, count):
    slots = middle.shape[0]
    ext_ref[0:RIM, :] = left
    ext_ref[RIM : RIM + slots, :] = middle
    tail = ext_ref.shape[0] - RIM - slots
    ext_ref[RIM + slots :, :] = jnp.zeros((tail, middle.shape[1]), f32)
    rows = slots + RIM
    row = lax.broadcasted_iota(jnp.int32, (rows, RIM), 0)
    col = lax.broadcasted_iota(jnp.int32, (rows, RIM), 1)
    put = jnp.where(row == col + count, 1.0, 0.0)
    ext_ref[RIM : RIM + rows, :] += mm(put, right)


CONV_ROWS = 64


def shifted(ext_ref, r0, l0):
    slab = ext_ref[pl.ds(r0, CONV_ROWS + 40), pl.ds(l0, LANES)]
    for b in range(8):
        moved = slab[b : b + CONV_ROWS + 32]
        for a in range(5):
            if 8 * a + b < CONV:
                yield 8 * a + b, moved[8 * a : 8 * a + CONV_ROWS]


def conv_into(out_ref, ext_ref, taps_ref, slots, flip, add, low=0):
    def block(i, carry):
        r0 = pl.multiple_of((i // PAIRS) * CONV_ROWS, CONV_ROWS)
        l0 = pl.multiple_of((i % PAIRS) * LANES, LANES)
        acc = jnp.zeros((CONV_ROWS, LANES), f32)
        for c, part in shifted(ext_ref, r0, l0):
            at = CONV - 1 - c if flip else c
            acc = acc + taps_ref[at : at + 1, pl.ds(l0, LANES)] * part
        here = (pl.ds(r0, CONV_ROWS), pl.ds(l0, LANES))
        if add:
            out_ref[here] += acc
        else:
            out_ref[here] = acc
        return carry

    lax.fori_loop((low // CONV_ROWS) * PAIRS, (slots // CONV_ROWS) * PAIRS, block, 0)


def taps_grad_into(scr_ref, grad_ref, ext_ref, slots, low=0, clear=True):
    if clear:
        scr_ref[...] = jnp.zeros_like(scr_ref)

    def block(i, carry):
        r0 = pl.multiple_of((i // PAIRS) * CONV_ROWS, CONV_ROWS)
        l0 = pl.multiple_of((i % PAIRS) * LANES, LANES)
        grad = grad_ref[pl.ds(r0, CONV_ROWS), pl.ds(l0, LANES)]
        for c, part in shifted(ext_ref, r0, l0):
            prod = grad * part
            total = prod[0:8]
            for at in range(8, CONV_ROWS, 8):
                total = total + prod[at : at + 8]
            scr_ref[c, :, pl.ds(l0, LANES)] += total
        return carry

    lax.fori_loop((low // CONV_ROWS) * PAIRS, (slots // CONV_ROWS) * PAIRS, block, 0)


def whole(shape=None):
    return pl.BlockSpec(memory_space=pltpu.VMEM)


def smem():
    return pl.BlockSpec(memory_space=pltpu.SMEM)


def params(**more):
    return pltpu.CompilerParams(vmem_limit_bytes=VMEM_CAP, **more)


def shape(*dims):
    return jax.ShapeDtypeStruct(dims, f32)


def greet_signal(n):
    me = lax.axis_index("seq")
    for d in range(1, n):
        pl.semaphore_signal(
            pltpu.get_barrier_semaphore(), inc=1, device_id={"seq": lax.rem(me + d, n)}, device_id_type=MESH
        )
    return me


def greet_all(n):
    me = greet_signal(n)
    pl.semaphore_wait(pltpu.get_barrier_semaphore(), n - 1)
    return me


def to_seq(src, dst, send, recv, target):
    return pltpu.make_async_remote_copy(
        src, dst, send, recv, device_id={"seq": target}, device_id_type=MESH
    )


def rim_copies(n, me, rim_ref, left_ref, right_ref, rsend, rrecv):
    up = to_seq(rim_ref.at[pl.ds(RIM, RIM)], left_ref, rsend.at[0], rrecv.at[0], lax.rem(me + 1, n))
    down = to_seq(rim_ref.at[pl.ds(0, RIM)], right_ref, rsend.at[1], rrecv.at[1], lax.rem(me + n - 1, n))
    return up, down


def rim_start(n, me, up, down, left_ref, right_ref):
    @pl.when(me < n - 1)
    def _():
        up.start()

    @pl.when(me > 0)
    def _():
        down.start()

    @pl.when(me == 0)
    def _():
        left_ref[...] = jnp.zeros_like(left_ref)

    @pl.when(me == n - 1)
    def _():
        right_ref[...] = jnp.zeros_like(right_ref)


def rim_wait(n, me, up, down):
    @pl.when(me > 0)
    def _():
        up.wait_recv()
        down.wait_send()

    @pl.when(me < n - 1)
    def _():
        down.wait_recv()
        up.wait_send()


MSG = DH + 8


def eye(size):
    row = lax.broadcasted_iota(jnp.int32, (size, size), 0)
    col = lax.broadcasted_iota(jnp.int32, (size, size), 1)
    return jnp.where(row == col, 1.0, 0.0)


def pair_sums(row):
    lane = lax.broadcasted_iota(jnp.int32, row.shape, 1)
    first = jnp.sum(jnp.where(lane < DH, row, 0.0), axis=1, keepdims=True)
    second = jnp.sum(jnp.where(lane < DH, 0.0, row), axis=1, keepdims=True)
    return jnp.where(lane < DH, first, second)


def core_of(query, key, mask):
    scores = jnp.where(mask, mm_t(query, key, TOP) * SCALE, MASKED)
    raised = jnp.exp(scores - jnp.max(scores, axis=1, keepdims=True))
    return raised / jnp.sum(raised, axis=1, keepdims=True)


def inverse_grad(gblend, mixed):
    return jnp.where(head_mask(LANES), t_mm(gblend, mixed, TOP), 0.0)


def newton_back(g, gcore, core, z, prod, r, q):
    prod_t = prod.T
    gq = 0.25 * mm(z.T, g, TOP)
    gr = -mm(prod_t, gq, TOP)
    gs = -mm(prod_t, gr, TOP)
    gp = -mm_t(gq, r, TOP) - mm_t(gr, 7.0 * eye(LANES) - prod, TOP) - gs
    return 0.25 * mm_t(g, q, TOP) + mm(core.T, gp, TOP), gcore + mm_t(gp, z, TOP)


def newton_lead(z, prod):
    zp = mm(z, prod, TOP)
    zpp = mm(zp, prod, TOP)
    return jnp.concatenate([0.25 * z.T, -0.25 * zp.T, 0.25 * zpp.T], axis=0)


def newton_short(g, gcore, lead, core, z, prod, r, q):
    gqrs = mm(lead, g, TOP)
    gq, gr, gs = [gqrs[at : at + LANES] for at in range(0, 3 * LANES, LANES)]
    left = jnp.concatenate([gq, gr], axis=1)
    right = jnp.concatenate([r, 7.0 * eye(LANES) - prod], axis=1)
    gp = -mm_t(left, right, TOP) - gs
    through = mm(jnp.concatenate([g, core.T], axis=1), jnp.concatenate([0.25 * q.T, gp], axis=0), TOP)
    return through, gcore + mm_t(gp, z, TOP)


def core_back(g, gcore, core, first, ql_ref, kl_ref, gl_ref, me):
    mask = head_mask(LANES)
    colsum = jnp.sum(core, axis=0, keepdims=True)
    square = pair_sums(colsum * colsum)
    sigma = jnp.sqrt(square)
    dot = pair_sums(jnp.sum(g * first, axis=0, keepdims=True))
    gcore = gcore + g.T / sigma - jnp.where(mask, dot / square * colsum, 0.0)
    gscore = core * (gcore - jnp.sum(core * gcore, axis=1, keepdims=True)) * SCALE
    lanes = pl.ds(pl.multiple_of(me * LANES, LANES), LANES)
    query = spread(ql_ref[:, lanes], mask)
    key = spread(kl_ref[:, lanes], mask)
    gl_ref[...] = jnp.zeros_like(gl_ref)
    gl_ref[0, :, lanes] = fold(mm(gscore, key, TOP), mask)
    gl_ref[1, :, lanes] = fold(t_mm(gscore, query, TOP), mask)


def blend_exchange_kernel(
    n, g_ref, rim_ref, ql_ref, kl_ref, core_ref, zs_ref, ps_ref, rs_ref, qs_ref, mx_ref,
    c_ref, left_ref, right_ref, gl_ref,
    land, s1, r1, s2, r2, rsend, rrecv,
):
    me = greet_all(n)
    for p in range(PAIRS):

        @pl.when(me != p)
        def _(p=p):
            to_seq(g_ref.at[p], land.at[me], s1.at[p], r1.at[me], p).start()

    up, down = rim_copies(n, me, rim_ref, left_ref, right_ref, rsend, rrecv)
    rim_start(n, me, up, down, left_ref, right_ref)

    @pl.when(me >= PAIRS)
    def _():
        gl_ref[...] = jnp.zeros_like(gl_ref)

    @pl.when(me < PAIRS)
    def _():
        mask = head_mask(LANES)
        land[me] = g_ref[me]
        for s in range(n):

            @pl.when(me != s)
            def _(s=s):
                to_seq(g_ref.at[0], land.at[s], s1.at[0], r1.at[s], s).wait_recv()

        gblend = land[0]
        for s in range(1, n):
            gblend = gblend + land[s]
        mixed = mx_ref[...]
        gmixed = mm(gblend, zs_ref[NEWTON], TOP)
        c_ref[me, 0:DH, :] = gmixed
        dots = jnp.sum(gmixed * mixed, axis=0, keepdims=True)
        pad = jnp.zeros((MSG - DH - 1, LANES), f32)
        c_ref[me, DH:MSG, :] = jnp.concatenate([dots, pad], axis=0)
        for t in range(n):

            @pl.when(me != t)
            def _(t=t):
                to_seq(c_ref.at[me], c_ref.at[me], s2.at[t], r2.at[me], t).start()

        gcore = jnp.zeros((LANES, LANES), f32)
        g = inverse_grad(gblend, mixed)
        for step in reversed(range(NEWTON)):
            g, gcore = newton_back(g, gcore, core_ref[...], zs_ref[step], ps_ref[step], rs_ref[step], qs_ref[step])
        core_back(g, gcore, core_ref[...], zs_ref[0], ql_ref, kl_ref, gl_ref, me)

    for p in range(PAIRS):

        @pl.when(me != p)
        def _(p=p):
            to_seq(c_ref.at[p], c_ref.at[p], s2.at[p], r2.at[p], p).wait_recv()
            to_seq(g_ref.at[p], land.at[me], s1.at[p], r1.at[me], p).wait_send()

    rim_wait(n, me, up, down)

    @pl.when(me < PAIRS)
    def _():
        for t in range(n):

            @pl.when(me != t)
            def _(t=t):
                to_seq(c_ref.at[me], c_ref.at[me], s2.at[t], r2.at[me], t).wait_send()


def blend_exchange(n, gblend, rim, ql, kl, saved):
    dma = pltpu.SemaphoreType.DMA
    width = rim.shape[1]
    return pl.pallas_call(
        partial(blend_exchange_kernel, n),
        in_specs=[whole()] * 10,
        out_specs=[whole()] * 4,
        out_shape=[shape(PAIRS, MSG, LANES), shape(RIM, width), shape(RIM, width), shape(2, DH, width)],
        scratch_shapes=[
            pltpu.VMEM((n, DH, LANES), f32),
            dma((PAIRS,)), dma((n,)), dma((n,)), dma((n,)), dma((2,)), dma((2,)),
        ],
        compiler_params=params(collective_id=3, has_side_effects=True),
        name="blend_exchange",
    )(gblend, rim, ql, kl, *saved)


def land_return_kernel(n, x_ref, own_ref, land, send, recv):
    me = greet_all(n)
    copies = []
    for d in range(1, n):
        target = lax.rem(me + d, n)
        copy = to_seq(x_ref.at[target], land.at[me], send.at[d], recv.at[me], target)
        copy.start()
        copies.append(copy)
    land[me] = x_ref[me]
    for d in range(1, n):
        source = lax.rem(me + d, n)
        to_seq(x_ref.at[0], land.at[source], send.at[d], recv.at[source], source).wait_recv()
    total = land[0]
    for s in range(1, n):
        total = total + land[s]
    own_ref[...] = total
    for copy in copies:
        copy.wait_send()


def land_return(n, parts):
    dma = pltpu.SemaphoreType.DMA
    return pl.pallas_call(
        partial(land_return_kernel, n),
        in_specs=[whole()],
        out_specs=whole(),
        out_shape=shape(*parts.shape[1:]),
        scratch_shapes=[pltpu.VMEM(parts.shape, f32), dma((n,)), dma((n,))],
        compiler_params=params(collective_id=4, has_side_effects=True),
        name="land_return",
    )(parts)


def norm_stats(r):
    centered = r - jnp.mean(r, axis=1, keepdims=True)
    spread_ = jnp.mean(centered * centered, axis=1, keepdims=True)
    inv = lax.rsqrt(spread_ + EPS)
    return centered * inv, inv


def norm_back(unit, inv, gain, grad):
    ge = grad * gain
    return (
        ge
        - jnp.mean(ge, axis=1, keepdims=True)
        - unit * jnp.mean(ge * unit, axis=1, keepdims=True)
    ) * inv


def quad(g):
    return pl.ds(pl.multiple_of(g * QUAD, QUAD), QUAD)


def pair_rows(ref, g, rows):
    return jnp.concatenate([ref[2 * g, rows, :], ref[2 * g + 1, rows, :]], axis=1)


def front_kernel(
    n, lens_ref, x_ref, taps_in, bq_ref, bv_ref, bo_ref, g1_ref, b1_ref, wq_hbm, wk_hbm, wv_hbm, wo_hbm,
    q_out, k_out, v_out, p_out, near_out, ctx_out, ext_out, h1_out, u1_out,
    m_ref, b_ref, ql_ref, kl_ref, core_ref, zs_ref, ps_ref, rs_ref, qs_ref, mx_ref, taps_ref, inv1_ref,
    w, bias, stack, ext, f_ref, mine, lands, rim, left, right, land,
    load, out, ms, mr, ls, lr, s1, r1, s2, r2,
):
    _, slots, width = stack.shape
    segs = mine.shape[1]
    v, q, k, p, near, ctx, h1, u1 = [stack.at[i] for i in range(8)]
    loads = [pltpu.make_async_copy(hbm, w.at[i], load.at[i]) for i, hbm in enumerate((wv_hbm, wq_hbm, wk_hbm, wo_hbm))]
    for copy in loads:
        copy.start()
    leaving = []

    def leave(src, dst):
        leaving.append(pltpu.make_async_copy(src, dst, out.at[len(leaving)]))
        leaving[-1].start()

    me = greet_signal(n)
    ends = seg_ends(lens_ref, segs)
    count = ends[-1]
    valid = valid_rows(count, slots)
    member = member_rows(ends, slots)
    inv = inverse_lens(lens_ref, segs)
    bias[0:1, :] = bv_ref[...][None, :]
    bias[1:2, :] = bq_ref[...][None, :]
    bias[2:3, :] = jnp.zeros((1, width), f32)

    def one(i, carry):
        pltpu.make_async_copy(wv_hbm, w.at[i], load.at[i]).wait()
        stack[i] = mm(x_ref[...], w[i]) + bias[pl.ds(i, 1), :]

        @pl.when(i == 0)
        def _():
            v[...] = jnp.where(valid, v[...], 0.0)
            rim[...] = rims_of(v[...], count)
            pl.semaphore_wait(pltpu.get_barrier_semaphore(), n - 1)
            rim_start(n, me, up, down, left, right)

        return carry

    up, down = rim_copies(n, me, rim, left, right, ms, mr)
    lax.fori_loop(0, 3, one, 0)
    mine[0] = mm(member, q[...]) * inv
    mine[1] = mm(member, k[...]) * inv
    for d in range(1, n):
        to_seq(mine, lands.at[me], ls.at[d], lr.at[me], lax.rem(me + d, n)).start()
    lands[me] = mine[...]
    leave(q, q_out)
    leave(k, k_out)
    leave(v, v_out)
    row = lax.broadcasted_iota(jnp.int32, (HEADS, width), 0)
    col = lax.broadcasted_iota(jnp.int32, (HEADS, width), 1) >> 6
    taps_ref[...] = t_mm(taps_in[...], jnp.where(row == col, 1.0, 0.0), TOP)
    rim_wait(n, me, up, down)
    fill_extended(ext, v[...], left[...], right[...], count)
    leave(ext, ext_out)
    conv_into(ctx, ext, taps_ref, slots, False, False)

    for d in range(1, n):
        source = lax.rem(me + d, n)
        to_seq(mine, lands.at[source], ls.at[d], lr.at[source], source).wait_recv()
    for s in range(n):
        rows = slice(s * segs, (s + 1) * segs)
        ql_ref[rows, :] = lands[s, 0]
        kl_ref[rows, :] = lands[s, 1]

    def far(g, carry):
        cols = quad(g)
        mask = head_mask(QUAD)
        scores = mm_t(k[:, cols], spread(ql_ref[:, cols], mask)) * SCALE
        scores = jnp.where(valid, scores, MASKED)
        top = jnp.max(scores, axis=0, keepdims=True)
        raised = jnp.where(valid, jnp.exp(scores - top), 0.0)
        p[:, cols] = raised
        m_ref[:, cols] = top
        total = jnp.sum(raised, axis=0, keepdims=True)
        weighted = fold(t_mm(v[:, cols], raised), mask)
        rest = jnp.concatenate([top, total, jnp.zeros((MSG - DH - 2, QUAD), f32)], axis=0)
        for j in range(QUAD // LANES):
            part = slice(j * LANES, (j + 1) * LANES)
            f_ref[g * 2 + j, 0:DH, :] = weighted[:, part]
            f_ref[g * 2 + j, DH:MSG, :] = rest[:, part]
        return carry

    lax.fori_loop(0, QUADS, far, 0)
    for pair in range(PAIRS):

        @pl.when(me != pair)
        def _(pair=pair):
            to_seq(f_ref.at[pair], land.at[me], s1.at[pair], r1.at[me], pair).start()

    leave(p, p_out)

    @pl.when(me < PAIRS)
    def _():
        mask = head_mask(LANES)
        lanes = pl.ds(pl.multiple_of(me * LANES, LANES), LANES)
        core = core_of(spread(ql_ref[:, lanes], mask), spread(kl_ref[:, lanes], mask), mask)
        core_ref[...] = core
        colsum = jnp.sum(core, axis=0, keepdims=True)
        zs_ref[0] = core.T / jnp.sqrt(pair_sums(colsum * colsum))
        unit = eye(LANES)

        def newton(step, carry):
            z = zs_ref[step]
            prod = mm(core_ref[...], z, TOP)
            ps_ref[step] = prod
            r = 15.0 * unit - mm(prod, 7.0 * unit - prod, TOP)
            rs_ref[step] = r
            q_ = 13.0 * unit - mm(prod, r, TOP)
            qs_ref[step] = q_
            zs_ref[step + 1] = 0.25 * mm(z, q_, TOP)
            return carry

        lax.fori_loop(0, NEWTON, newton, 0)
        land[me] = f_ref[me]
        for s in range(n):

            @pl.when(me != s)
            def _(s=s):
                to_seq(f_ref.at[0], land.at[s], s1.at[0], r1.at[s], s).wait_recv()

        top = land[0][DH : DH + 1]
        for s in range(1, n):
            top = jnp.maximum(top, land[s][DH : DH + 1])
        total = jnp.zeros_like(top)
        mixed = jnp.zeros((DH, LANES), f32)
        for s in range(n):
            part = land[s]
            factor = jnp.exp(part[DH : DH + 1] - top)
            total = total + part[DH + 1 : DH + 2] * factor
            mixed = mixed + part[:DH] * factor
        mixed = mixed / total
        mx_ref[...] = mixed
        b_ref[me, 0:DH, :] = mm_t(mixed, zs_ref[NEWTON], TOP)
        pad = jnp.zeros((MSG - DH - 2, LANES), f32)
        b_ref[me, DH:MSG, :] = jnp.concatenate([top, total, pad], axis=0)
        for t in range(n):

            @pl.when(me != t)
            def _(t=t):
                to_seq(b_ref.at[me], b_ref.at[me], s2.at[t], r2.at[me], t).start()

    def soft(g, carry):
        cols = quad(g)
        mask = head_mask(QUAD)
        head = lax.broadcasted_iota(jnp.int32, (slots, QUAD), 1) >> 6
        scores = mm_t(q[:, cols], spread(kl_ref[:, cols], mask)) * SCALE
        tops = [jnp.max(scores[:, h * DH : (h + 1) * DH], axis=1, keepdims=True) for h in range(4)]
        top = jnp.where(head < 2, jnp.where(head < 1, tops[0], tops[1]), jnp.where(head < 3, tops[2], tops[3]))
        raised = jnp.exp(scores - top)
        near[:, cols] = raised / mm(raised, jnp.where(mask, 1.0, 0.0))
        return carry

    lax.fori_loop(0, QUADS, soft, 0)
    leave(near, near_out)
    for pair in range(PAIRS):

        @pl.when(me != pair)
        def _(pair=pair):
            to_seq(b_ref.at[pair], b_ref.at[pair], s2.at[pair], r2.at[pair], pair).wait_recv()

    def blend(g, carry):
        cols = quad(g)
        ctx[:, cols] += mm_t(near[:, cols], spread(pair_rows(b_ref, g, slice(0, DH)), head_mask(QUAD)))
        return carry

    lax.fori_loop(0, QUADS, blend, 0)
    leave(ctx, ctx_out)
    loads[-1].wait()

    unit, scale = norm_stats(x_ref[...] + (mm(ctx[...], w[3]) + bo_ref[...][None, :]))
    h1[...] = unit * g1_ref[...][None, :] + b1_ref[...][None, :]
    leave(h1, h1_out)
    u1[...] = unit
    leave(u1, u1_out)
    inv1_ref[...] = scale
    for d in range(1, n):
        to_seq(mine, lands.at[me], ls.at[d], lr.at[me], lax.rem(me + d, n)).wait_send()
    for pair in range(PAIRS):

        @pl.when(me != pair)
        def _(pair=pair):
            to_seq(f_ref.at[pair], land.at[me], s1.at[pair], r1.at[me], pair).wait_send()

    @pl.when(me < PAIRS)
    def _():
        for t in range(n):

            @pl.when(me != t)
            def _(t=t):
                to_seq(b_ref.at[me], b_ref.at[me], s2.at[t], r2.at[me], t).wait_send()

    for copy in leaving:
        copy.wait()


def front(n, lens, x, taps, bq, bv, bo, g1, b1, wq, wk, wv, wo):
    slots, width = x.shape
    segs = lens.shape[1]
    dma = pltpu.SemaphoreType.DMA
    vm = lambda *dims: pltpu.VMEM(dims, f32)
    anywhere = pl.BlockSpec(memory_space=pl.ANY)
    square = (LANES, LANES)
    rows = shape(slots, width)
    return pl.pallas_call(
        partial(front_kernel, n),
        in_specs=[smem()] + [whole()] * 7 + [anywhere] * 4,
        out_specs=[anywhere] * 9 + [whole()] * 12,
        out_shape=[rows] * 6 + [shape(slots + 40, width), rows, rows]
        + [
            shape(1, width), shape(PAIRS, MSG, LANES), shape(DH, width), shape(DH, width), shape(*square),
            shape(NEWTON + 1, *square), shape(NEWTON, *square), shape(NEWTON, *square), shape(NEWTON, *square),
            shape(DH, LANES), shape(CONV, width), shape(slots, 1),
        ],
        scratch_shapes=[
            vm(4, width, width), vm(8, width), vm(8, slots, width), vm(slots + 40, width),
            vm(PAIRS, MSG, LANES), vm(2, segs, width), vm(n, 2, segs, width), vm(2 * RIM, width), vm(RIM, width),
            vm(RIM, width), vm(n, MSG, LANES),
            dma((4,)), dma((9,)), dma((2,)), dma((2,)), dma((n,)), dma((n,)), dma((PAIRS,)), dma((n,)),
            dma((n,)), dma((n,)),
        ],
        compiler_params=params(collective_id=1, has_side_effects=True),
        name="front",
    )(lens, x, taps, bq, bv, bo, g1, b1, wq, wk, wv, wo)


def forward_kernel(
    lens_ref, h1_ref, wi_ref, bi_ref, wo_ref, bo_ref, cot_ref, g2_ref, b2_ref,
    pre_ref, out_ref, gs2_ref, small_ref,
    acc_ref, act_ref,
):
    step = pl.program_id(0)

    @pl.when(step == 0)
    def _():
        acc_ref[...] = jnp.zeros_like(acc_ref)

    def one(g, carry):
        cols = quad(g)
        pre = mm(h1_ref[...], wi_ref[:, cols]) + bi_ref[:, cols]
        pre_ref[:, cols] = pre
        act_ref[:, cols] = 0.5 * pre * (1.0 + lax.erf(pre * ROOT_HALF))
        return carry

    lax.fori_loop(0, QUADS, one, 0)

    def two(g, carry):
        cols = quad(g)
        acc_ref[:, cols] += mm(act_ref[...], wo_ref[:, cols])
        return carry

    lax.fori_loop(0, QUADS, two, 0)

    @pl.when(step == pl.num_programs(0) - 1)
    def _():
        slots = h1_ref.shape[0]
        valid = valid_rows(seg_ends(lens_ref, lens_ref.shape[1])[-1], slots)
        summed = h1_ref[...] + (acc_ref[...] + bo_ref[...][None, :])
        unit, inv = norm_stats(summed)
        out_ref[...] = jnp.where(valid, unit * g2_ref[...][None, :] + b2_ref[...][None, :], 0.0)
        e = jnp.where(valid, cot_ref[...], 0.0)
        grad = norm_back(unit, inv, g2_ref[...][None, :], e)
        gs2_ref[...] = grad
        small_ref[...] = jnp.concatenate(
            [
                jnp.sum(e * unit, axis=0, keepdims=True),
                jnp.sum(e, axis=0, keepdims=True),
                jnp.sum(grad, axis=0, keepdims=True),
                jnp.zeros((5, e.shape[1]), f32),
            ],
            axis=0,
        )


def ffn_forward(lens, h1, wi, bi, wo, bo, cot, g2, b2):
    slots, width = h1.shape
    inner = wi.shape[1]
    const = lambda *dims: pl.BlockSpec(dims, lambda j: (0,) * len(dims))
    return pl.pallas_call(
        forward_kernel,
        grid=(inner // width,),
        in_specs=[
            smem(), const(slots, width),
            pl.BlockSpec((width, width), lambda j: (0, j)), pl.BlockSpec((1, width), lambda j: (0, j)),
            pl.BlockSpec((width, width), lambda j: (j, 0)), const(width),
            const(slots, width), const(width), const(width),
        ],
        out_specs=[
            pl.BlockSpec((slots, width), lambda j: (0, j)),
            const(slots, width), const(slots, width), const(8, width),
        ],
        out_shape=[shape(slots, inner), shape(slots, width), shape(slots, width), shape(8, width)],
        scratch_shapes=[pltpu.VMEM((slots, width), f32)] * 2,
        compiler_params=params(),
        name="ffn_forward",
    )(lens, h1, wi, bi, wo, bo, cot, g2, b2)


def put_strips(ref, block, rows=slice(None), first=0):
    for s in range(block.shape[1] // LANES):
        ref[first + s, rows, :] = block[:, s * LANES : (s + 1) * LANES]


def backward_kernel(
    h1_ref, gs2_ref, pre_ref, wi_ref, wo_ref, u1_ref, inv1_ref, g1_ref,
    dwo_ref, dwi_ref, gs1_ref, dbi_ref, small_ref,
    acc_ref, gpre_ref,
):
    step = pl.program_id(0)

    @pl.when(step == 0)
    def _():
        acc_ref[...] = gs2_ref[...]

    def one(g, carry):
        cols = quad(g)
        pre = pre_ref[:, cols]
        phi_big = 0.5 * (1.0 + lax.erf(pre * ROOT_HALF))
        slope = phi_big + pre * (INV_ROOT_TAU * jnp.exp(-0.5 * pre * pre))
        gpre = mm_t(gs2_ref[...], wo_ref[cols, :]) * slope
        gpre_ref[:, cols] = gpre
        dbi_ref[:, cols] = jnp.sum(gpre, axis=0, keepdims=True)
        put_strips(dwo_ref, t_mm(pre * phi_big, gs2_ref[...]), cols)
        return carry

    lax.fori_loop(0, QUADS, one, 0)

    def two(g, carry):
        cols = quad(g)
        put_strips(dwi_ref, t_mm(h1_ref[:, cols], gpre_ref[...]), cols)
        acc_ref[:, cols] += mm_t(gpre_ref[...], wi_ref[cols, :])
        return carry

    lax.fori_loop(0, QUADS, two, 0)

    @pl.when(step == pl.num_programs(0) - 1)
    def _():
        e = acc_ref[...]
        unit = u1_ref[...]
        grad = norm_back(unit, inv1_ref[...], g1_ref[...][None, :], e)
        gs1_ref[...] = grad
        small_ref[...] = jnp.concatenate(
            [
                jnp.sum(e * unit, axis=0, keepdims=True),
                jnp.sum(e, axis=0, keepdims=True),
                jnp.sum(grad, axis=0, keepdims=True),
                jnp.zeros((5, e.shape[1]), f32),
            ],
            axis=0,
        )


def ffn_backward(h1, gs2, pre, wi, wo, u1, inv1, g1):
    slots, width = h1.shape
    inner = wi.shape[1]
    strips = width // LANES
    const = lambda *dims: pl.BlockSpec(dims, lambda j: (0,) * len(dims))
    return pl.pallas_call(
        backward_kernel,
        grid=(inner // width,),
        in_specs=[
            const(slots, width), const(slots, width),
            pl.BlockSpec((slots, width), lambda j: (0, j)),
            pl.BlockSpec((width, width), lambda j: (0, j)),
            pl.BlockSpec((width, width), lambda j: (j, 0)),
            const(slots, width), const(slots, 1), const(width),
        ],
        out_specs=[
            pl.BlockSpec((strips, width, LANES), lambda j: (j, 0, 0)),
            pl.BlockSpec((strips, width, LANES), lambda j: (j, 0, 0)),
            const(slots, width),
            pl.BlockSpec((1, width), lambda j: (0, j)),
            const(8, width),
        ],
        out_shape=[
            shape(inner // LANES, width, LANES), shape(inner // LANES, width, LANES),
            shape(slots, width), shape(1, inner), shape(8, width),
        ],
        scratch_shapes=[pltpu.VMEM((slots, width), f32)] * 2,
        compiler_params=params(),
        name="ffn_backward",
    )(h1, gs2, pre, wi, wo, u1, inv1, g1)


def near_back_quad(g, gctx_ref, near_ref, q_ref, kl_ref, b_ref, gq_ref, gb_ref, gkl_ref):
    mask = head_mask(QUAD)
    ones = jnp.where(mask, 1.0, 0.0)
    cols = quad(g)
    gctx = gctx_ref[:, cols]
    near = near_ref[:, cols]
    gblend = fold(t_mm(gctx, near), mask)
    gb_ref[2 * g] = gblend[:, :LANES]
    gb_ref[2 * g + 1] = gblend[:, LANES:]
    gnear = mm(gctx, spread(pair_rows(b_ref, g, slice(0, DH)), mask))
    gscore = near * (gnear - mm(near * gnear, ones)) * SCALE
    gq_ref[:, cols] = mm(gscore, spread(kl_ref[:, cols], mask))
    gkl_ref[:, cols] = fold(t_mm(gscore, q_ref[:, cols]), mask)


def near_back_kernel(
    lens_ref, gs1_ref, wo_ref, near_ref, q_ref, kl_ref, b_ref,
    gctx_ref, gq_ref, gb_ref, gkl_ref, rim_ref,
):
    count = seg_ends(lens_ref, lens_ref.shape[1])[-1]
    gctx_ref[...] = mm_t(gs1_ref[...], wo_ref[...])
    rim_ref[...] = rims_of(gctx_ref[...], count)
    def one(g, carry):
        near_back_quad(g, gctx_ref, near_ref, q_ref, kl_ref, b_ref, gq_ref, gb_ref, gkl_ref)
        return carry

    lax.fori_loop(0, QUADS, one, 0)


def near_back(lens, gs1, wo, near, q, kl, b):
    slots, width = gs1.shape
    return pl.pallas_call(
        near_back_kernel,
        in_specs=[smem()] + [whole()] * 6,
        out_specs=[whole()] * 5,
        out_shape=[
            shape(slots, width), shape(slots, width), shape(PAIRS, DH, LANES),
            shape(DH, width), shape(2 * RIM, width),
        ],
        compiler_params=params(),
        name="near_back",
    )(lens, gs1, wo, near, q, kl, b)


def far_back_quad(g, k_ref, v_ref, p_ref, m_ref, b_ref, c_ref, ql_ref, gk_ref, gv_ref, gql_ref, add):
    mask = head_mask(QUAD)
    cols = quad(g)
    top = pair_rows(b_ref, g, slice(DH, DH + 1))
    total = pair_rows(b_ref, g, slice(DH + 1, DH + 2))
    prob = p_ref[:, cols] * (jnp.exp(m_ref[:, cols] - top) / total)
    gmixed = spread(pair_rows(c_ref, g, slice(0, DH)), mask)
    dots = pair_rows(c_ref, g, slice(DH, DH + 1))
    gscore = prob * (mm(v_ref[:, cols], gmixed) - dots) * SCALE
    gk_ref[:, cols] = mm(gscore, spread(ql_ref[:, cols], mask))
    gval = mm_t(prob, gmixed)
    if add:
        gv_ref[:, cols] += gval
    else:
        gv_ref[:, cols] = gval
    gql_ref[:, cols] = fold(t_mm(gscore, k_ref[:, cols]), mask)


def land_parts(ret_ref, gql, gkl):
    n, _, segs, _ = ret_ref.shape
    for s in range(n):
        rows = slice(s * segs, (s + 1) * segs)
        ret_ref[s, 0] = gql[rows]
        ret_ref[s, 1] = gkl[rows]


def far_back_kernel(
    k_ref, v_ref, p_ref, m_ref, b_ref, c_ref, ql_ref, gkl_ref, gl_ref,
    gk_ref, gv_ref, ret_ref, gql_ref,
):
    def one(g, carry):
        far_back_quad(g, k_ref, v_ref, p_ref, m_ref, b_ref, c_ref, ql_ref, gk_ref, gv_ref, gql_ref, False)
        return carry

    lax.fori_loop(0, QUADS, one, 0)
    land_parts(ret_ref, gql_ref[...] + gl_ref[0], gkl_ref[...] + gl_ref[1])


def far_back(n, lens, k, v, p, m, b, c, ql, gkl, gl):
    slots, width = k.shape
    segs = lens.shape[1]
    return pl.pallas_call(
        far_back_kernel,
        in_specs=[whole()] * 9,
        out_specs=[whole()] * 3,
        out_shape=[shape(slots, width), shape(slots, width), shape(n, 2, segs, width)],
        scratch_shapes=[pltpu.VMEM((DH, width), f32)],
        compiler_params=params(),
        name="far_back",
    )(k, v, p, m, b, c, ql, gkl, gl)


def taps_sums(scr_ref):
    width = scr_ref.shape[2]
    rows = jnp.concatenate(
        [jnp.sum(scr_ref[c], axis=0, keepdims=True) for c in range(CONV)] + [jnp.zeros((7, width), f32)], axis=0
    )
    row = lax.broadcasted_iota(jnp.int32, (width, LANES), 0) >> 6
    col = lax.broadcasted_iota(jnp.int32, (width, LANES), 1)
    return mm(rows, jnp.where(row == col, 1.0, 0.0), TOP)


def conv_back_kernel(
    lens_ref, values_ref, gctx_ref, gleft_ref, gright_ref, taps_ref, ctx_ref, gs1_ref,
    gv_ref, gtaps_ref, dwo_ref,
    ext_ref, scr_ref,
):
    slots = gctx_ref.shape[0]
    count = seg_ends(lens_ref, lens_ref.shape[1])[-1]
    put_strips(dwo_ref, t_mm(ctx_ref[...], gs1_ref[...]))
    fill_extended(ext_ref, gctx_ref[...], gleft_ref[...], gright_ref[...], count)
    conv_into(gv_ref, ext_ref, taps_ref, slots, True, False)
    taps_grad_into(scr_ref, gctx_ref, values_ref, slots)
    gtaps_ref[...] = taps_sums(scr_ref)


def conv_back(lens, ext, gctx, gleft, gright, taps, ctx, gs1):
    slots, width = gctx.shape
    return pl.pallas_call(
        conv_back_kernel,
        in_specs=[smem()] + [whole()] * 7,
        out_specs=[whole()] * 3,
        out_shape=[shape(slots, width), shape(40, LANES), shape(width // LANES, width, LANES)],
        scratch_shapes=[pltpu.VMEM((slots + 40, width), f32), pltpu.VMEM((CONV, 8, width), f32)],
        compiler_params=params(),
        name="conv_back",
    )(lens, ext, gctx, gleft, gright, taps, ctx, gs1)


def project_back_kernel(
    lens_ref, x_ref, gs1_ref, gqn_ref, gkf_ref, gvc_ref, gvf_ref, own_ref, wq_ref, wk_ref, wv_ref,
    ig_ref, dq_ref, dk_ref, dv_ref, small_ref,
    gq_ref, gk_ref, gv_ref,
):
    @pl.when(pl.program_id(0) == 0)
    def _():
        slots = gqn_ref.shape[0]
        segs = own_ref.shape[1]
        ends = seg_ends(lens_ref, segs)
        member = member_rows(ends, slots)
        inv = inverse_lens(lens_ref, segs)
        gq = gqn_ref[...] + t_mm(member, own_ref[0] * inv)
        gk = gkf_ref[...] + t_mm(member, own_ref[1] * inv)
        gv = jnp.where(valid_rows(ends[-1], slots), gvc_ref[...] + gvf_ref[...], 0.0)
        gq_ref[...] = gq
        gk_ref[...] = gk
        gv_ref[...] = gv
        small_ref[...] = jnp.concatenate(
            [
                jnp.sum(gq, axis=0, keepdims=True),
                jnp.sum(gv, axis=0, keepdims=True),
                jnp.zeros((6, gq.shape[1]), f32),
            ],
            axis=0,
        )

    x = x_ref[...]
    put_strips(dq_ref, t_mm(x, gq_ref[...]))
    put_strips(dk_ref, t_mm(x, gk_ref[...]))
    put_strips(dv_ref, t_mm(x, gv_ref[...]))
    ig_ref[...] = (
        gs1_ref[...]
        + mm_t(gq_ref[...], wq_ref[...])
        + mm_t(gk_ref[...], wk_ref[...])
        + mm_t(gv_ref[...], wv_ref[...])
    )


def project_back(lens, x, gs1, gqn, gkf, gvc, gvf, own, wq, wk, wv):
    slots, width = x.shape
    col = 256
    strips = width // LANES
    const = lambda *dims: pl.BlockSpec(dims, lambda i: (0,) * len(dims))
    part = pl.BlockSpec((slots, col), lambda i: (0, i))
    wspec = pl.BlockSpec((col, width), lambda i: (i, 0))
    dspec = pl.BlockSpec((strips, col, LANES), lambda i: (0, i, 0))
    return pl.pallas_call(
        project_back_kernel,
        grid=(width // col,),
        in_specs=[smem(), part, part] + [const(slots, width)] * 4 + [const(*own.shape), wspec, wspec, wspec],
        out_specs=[part, dspec, dspec, dspec, const(8, width)],
        out_shape=[shape(slots, width)] + [shape(strips, width, LANES)] * 3 + [shape(8, width)],
        scratch_shapes=[pltpu.VMEM((slots, width), f32)] * 3,
        compiler_params=params(),
        name="project_back",
    )(lens, x, gs1, gqn, gkf, gvc, gvf, own, wq, wk, wv)


def sum_plain(parts):
    sizes = [part.size for part in parts]
    shapes = [part.shape for part in parts]
    devices = lax.axis_size(("seq", "dp"))
    flat = jnp.concatenate([part.reshape(-1) for part in parts])
    flat = jnp.pad(flat, (0, -flat.shape[0] % devices))
    own = lax.psum_scatter(flat, ("seq", "dp"), scatter_dimension=0, tiled=True)
    flat = lax.all_gather(own, ("seq", "dp"), axis=0, tiled=True)
    out = []
    at = 0
    for size, dims in zip(sizes, shapes):
        out.append(flat[at : at + size].reshape(dims))
        at += size
    return out


STRIP = 768
HALF = STRIP // 2
PART = HALF // 2
Z_ROWS = PART // 4
OWN = Z_ROWS // 2
STAGES = 13
SMALL_STEPS = 5


def pack_small(sb_ref, small0, small1, small2, inner_bias, taps):
    at = 0
    for ref, count in ((small0, 2), (small1, 3), (small2, 3), (inner_bias, 1)):
        for r in range(count):
            for j in range(ref.shape[1] // LANES):
                sb_ref[0, at : at + 1, :] = ref[r : r + 1, j * LANES : (j + 1) * LANES]
                at += 1
    sb_ref[0, at : at + 40, :] = taps[...]


SMALL_ROWS = 8 * 6 + 24 + 40


def unpack_small(s_ref, outs):
    at = 0
    for ref in outs[:-1]:
        for j in range(ref.shape[0] // LANES):
            ref[pl.ds(j * LANES, LANES)] = s_ref[at, :]
            at += 1
    outs[-1][...] = s_ref[at : at + 40, :].T[:HEADS, :CONV]


def reduce_stages(gw, o_ref, bufs, sems):
    acc, lc, l1, mid, lz, l3, ag = bufs
    cs, cr, s1, r1, ms, zr, r3, r4, gs, gr, r5, keep, es, er = sems
    seq = lax.axis_index("seq")
    dp = lax.axis_index("dp")
    z = seq // 2
    c = lax.rem(seq, 2)
    y = dp // 2
    x = lax.rem(dp, 2)
    zb = 3 - z
    place = lambda z_, c_, y_, x_: (z_ * 2 + c_, y_ * 2 + x_)
    by_core = place(z, 1 - c, y, x)
    by_x = place(z, c, y, 1 - x)
    by_y = place(z, c, 1 - y, x)
    right = place(lax.rem(z + 1, 4), c, y, x)
    left = place(lax.rem(z + 3, 4), c, y, x)
    opposite = place(lax.rem(z + 2, 4), c, y, x)
    near_z = place(z + 1 - 2 * lax.rem(z, 2), c, y, x)

    def remote(src, dst, send, recv, target):
        return pltpu.make_async_remote_copy(src, dst, send, recv, device_id=target, device_id_type=MESH)

    aligned = lambda at: pl.multiple_of(at, 8)
    slot = lambda ref, k: lax.rem(k, ref.shape[0])
    starts = (x * PART, HALF + y * PART)
    others = ((1 - x) * PART, HALF + (1 - y) * PART)
    own_rows = (pl.ds(aligned(y * OWN), OWN), pl.ds(aligned(x * OWN), OWN))
    other_rows = (pl.ds(aligned((1 - y) * OWN), OWN), pl.ds(aligned((1 - x) * OWN), OWN))
    first_to = (by_x, by_y)
    third_to = (by_y, by_x)
    ways = ((0, z, right), (1, zb, left))

    def bytes_of(rows, send, recv, pieces=1):
        part = lc.at[pl.ds(0, pieces), pl.ds(0, rows // pieces)]
        return remote(part, part, send, recv, by_core)

    def strip(k):
        return lax.rem(k // 3, GW_SLOTS) * PAIRS + 2 * lax.rem(k, 3)

    def core_copy(k):
        return remote(gw.at[strip(k) + 1 - c], lc.at[slot(lc, k)], cs.at[k], cr.at[k], by_core)

    def core_out(k):
        core_copy(k).start()

    def first_out(k):
        core_copy(k).wait()
        at = slot(acc, k)
        acc[at] = gw[strip(k) + c] + lc[slot(lc, k)]
        for j in range(2):
            remote(
                acc.at[at, pl.ds(aligned(others[j]), PART)], l1.at[slot(l1, k), j], s1.at[k], r1.at[k], first_to[j]
            ).start()

    def z_copy(k, way, step, block, target):
        return remote(mid.at[slot(mid, k), block], lz.at[slot(lz, k), way, step], ms.at[k], zr.at[k, way, step], target)

    def z_out(k, step):
        if step == 0:
            bytes_of(HALF, s1.at[k], r1.at[k]).wait()
            for j in range(2):
                for block in range(4):
                    here = pl.ds(aligned(starts[j] + block * Z_ROWS), Z_ROWS)
                    there = pl.ds(block * Z_ROWS, Z_ROWS)
                    mid[slot(mid, k), block, j] = acc[slot(acc, k), here] + l1[slot(l1, k), j, there]
        for way, at, target in ways:
            block = 3 - step + z if way == 0 else step - zb
            if step > 0:

                @pl.when((at > 0) & (at <= step))
                def _(way=way, block=block, target=target):
                    z_copy(k, way, step - 1, 0, target).wait_recv()
                    mid[slot(mid, k), block] += lz[slot(lz, k), way, step - 1]

            if step < 3:

                @pl.when((at <= step) & (at < 3))
                def _(way=way, block=block, target=target):
                    z_copy(k, way, step, block, target).start()

    def third_out(k):
        z_out(k, 3)
        for j in range(2):
            remote(
                mid.at[slot(mid, k), z, j, other_rows[j]], l3.at[slot(l3, k), j], ms.at[k], r3.at[k], third_to[j]
            ).start()

    def back_third_out(k):
        bytes_of(2 * OWN, ms.at[k], r3.at[k]).wait_recv()
        for j in range(2):
            ag[slot(ag, k), z, j, own_rows[j]] = mid[slot(mid, k), z, j, own_rows[j]] + l3[slot(l3, k), j]
            part = ag.at[slot(ag, k), z, j, own_rows[j]]
            remote(part, part, gs.at[k], r4.at[k], third_to[j]).start()

    def back_z(k, way, step, block, target):
        part = ag.at[slot(ag, k), block]
        return remote(part, part, gs.at[k], gr.at[k, way, step], target)

    def back_z_out(k, step):
        if step == 0:
            bytes_of(6 * Z_ROWS + 2 * OWN, ms.at[k], r3.at[k]).wait_send()
            bytes_of(2 * OWN, gs.at[k], r4.at[k]).wait_recv()
        for way, at, target in ways:
            block = z - step if way == 0 else z + step
            if step > 0:

                @pl.when(at >= step)
                def _(way=way, target=target):
                    back_z(k, way, step - 1, 0, target).wait_recv()

            if step < 3:

                @pl.when((at >= step) & (at < 3))
                def _(way=way, block=block, target=target):
                    back_z(k, way, step, block, target).start()

    blocks = (pl.ds(x * 4, 4), pl.ds(8 + y * 4, 4))

    def keep_copy(k, j):
        return pltpu.make_async_copy(ag.at[slot(ag, k), :, j], o_ref.at[c, k, blocks[j]], keep.at[k, j])

    def back_first_out(k):
        back_z_out(k, 3)
        for j in range(2):
            remote(ag.at[slot(ag, k), :, j], o_ref.at[c, k, blocks[j]], gs.at[k], r5.at[k], first_to[j]).start()
            keep_copy(k, j).start()

    def back_core(k):
        part = o_ref.at[c, k]
        return remote(part, part, es.at[k], er.at[k], by_core)

    def back_core_out(k):
        bytes_of(HALF, gs.at[k], r5.at[k]).wait_recv()
        for j in range(2):
            keep_copy(k, j).wait()

        @pl.when((z == 0) | (z == 3))
        def _():
            bytes_of(2 * OWN + 2 * Z_ROWS + HALF, gs.at[k], r5.at[k]).wait_send()

        @pl.when((z > 0) & (z < 3))
        def _():
            bytes_of(2 * OWN + 10 * Z_ROWS + HALF, gs.at[k], r5.at[k], 2).wait_send()

        back_core(k).start()

    def finish(k):
        back_core(k).wait()

    stages = [
        core_out, first_out, partial(z_out, step=0), partial(z_out, step=1), partial(z_out, step=2), third_out,
        back_third_out, partial(back_z_out, step=0), partial(back_z_out, step=1), partial(back_z_out, step=2),
        back_first_out, back_core_out, finish,
    ]
    return stages, (by_core, by_x, by_y, near_z, opposite), remote


LAG = (0, 1, 3, 5, 7, 9, 11, 13, 15, 17, 19, 21, 22)
CHUNKS = 36
GW_SLOTS = 4
RING_ACC = 6
RING_LC = 4
RING_MID = 12
RING_Z = 6
RING_AG = 16
SEQ_DEVICES = 8
SMALL_AT = 44
ENTER = 2
HELD = 30
GAP = 2
GS1, GS2, H1, ACT, GPRE, PRE, _, U1, GCTX, IG = range(10)
GV, PROB, CTX, KEYS, NEAR, QUERY, VALS = GS2, H1, ACT, GPRE, PRE, PRE + 1, U1
FFN_AT = (0, 4, 8, 13)
GS1_AT = 17
OUTPUT_AT, VALUE_AT, QUERY_AT, KEY_AT = 21, 28, 32, 33
INPUT_AT = (41, 42, 43)
TAPS_AT = 36


def pick(t, table):
    value = jnp.int32(0)
    hit = t < 0
    for when, what in table.items():
        value = jnp.where(t == when, what, value)
        hit = hit | (t == when)
    return value, hit


def greet_block():
    seq = lax.axis_index("seq")
    dp = lax.axis_index("dp")
    y = dp // 2
    x = lax.rem(dp, 2)
    barrier = pltpu.get_barrier_semaphore()
    for d in range(1, SEQ_DEVICES):
        pl.semaphore_signal(
            barrier, inc=1, device_id=(lax.rem(seq + d, SEQ_DEVICES), dp), device_id_type=MESH
        )
    for other in (y * 2 + 1 - x, (1 - y) * 2 + x):
        pl.semaphore_signal(barrier, inc=1, device_id=(seq, other), device_id_type=MESH)
    pl.semaphore_wait(barrier, SEQ_DEVICES + 1)
    return seq


def tail_kernel(
    lens_ref, gs2_hbm, h1_hbm, u1_hbm, pre_hbm, wout_hbm, win_hbm, wo_hbm, near_hbm, q_hbm, ctx_hbm, ext_hbm,
    k_hbm, v_hbm, p_hbm, x_hbm, wq_hbm, wk_hbm, wv_hbm,
    inv1_ref, g1_ref, m_ref, b_ref, ql_ref, kl_ref, core_ref, zs_ref, ps_ref, rs_ref, qs_ref, mx_ref, taps_ref, small2_ref,
    o_ref, so_ref, ig_hbm,
    acc, lc, l1, mid, lz, l3, ag, sb, sl, gw,
    stack, w, ext, gext, tap_scr, gtaps, small0, small1, dbi,
    gb, rim, gkl, gql, gl, land, cmsg, gleft, gright, ng, ncore, nlead, ret, rland, own,
    loads, ig_sem, b1s, b1r, b2s, b2r, ms, mr, rets, retr, ss, sr,
    *sems,
):
    n = SEQ_DEVICES
    _, slots, width = stack.shape
    segs = own.shape[1]
    gs1, gv, p, ctx, k, near, q, v, gctx, ig = [
        stack.at[i] for i in (GS1, GV, PROB, CTX, KEYS, NEAR, QUERY, VALS, GCTX, IG)
    ]
    moves = []

    def load(src, dst):
        moves.append(pltpu.make_async_copy(src, dst, loads.at[len(moves)]))
        return moves[-1]

    load_gs2 = load(gs2_hbm, stack.at[GS2])
    load_w = []
    load_pre = []
    for j in range(4):
        part = pl.ds(j * width, width)
        load_w.append(load(wout_hbm.at[part, :], w.at[2 * j % 4]))
        load_w.append(load(win_hbm.at[:, part], w.at[(2 * j + 1) % 4]))
        load_pre.append(load(pre_hbm.at[:, part], stack.at[PRE + j % 2]))
    for i, hbm in enumerate((wo_hbm, wv_hbm, wq_hbm, wk_hbm)):
        load_w.append(load(hbm, w.at[i]))
    load_h1, load_u1, load_ext = load(h1_hbm, stack.at[H1]), load(u1_hbm, stack.at[U1]), load(ext_hbm, ext)
    load_near, load_q, load_ctx = load(near_hbm, near), load(q_hbm, q), load(ctx_hbm, ctx)
    load_p, load_k, load_v, load_x = load(p_hbm, p), load(k_hbm, k), load(v_hbm, v), load(x_hbm, q)
    a0, a1, a2, a3 = FFN_AT
    starting = [
        (a0 + 1, load_w[4]), (a0 + 1, load_pre[2]), (a0 + 4, load_w[5]), (a1 + 1, load_w[6]), (a1 + 1, load_pre[3]),
        (a1 + 4, load_w[7]), (a2 + 1, load_w[8]), (a2 + 1, load_near), (a2 + 4, load_w[9]), (a3 + 1, load_w[10]),
        (a3 + 1, load_q), (a3 + 2, load_ctx), (a3 + 3, load_p), (a3 + 4, load_w[11]), (a3 + 4, load_k), (a3 + 4, load_v),
        (GS1_AT + 4, load_x),
    ]
    waiting = [
        (a0, load_gs2), (a0 + 2, load_h1), (a3 + 3, load_u1), (GS1_AT, load_w[8]), (GS1_AT + 1, load_near),
        (GS1_AT + 1, load_q), (OUTPUT_AT, load_ctx), (VALUE_AT, load_x),
    ]
    for j in range(4):
        waiting += [(FFN_AT[j], load_w[2 * j]), (FFN_AT[j], load_pre[j]), (FFN_AT[j] + 3, load_w[2 * j + 1])]
    for i in range(3):
        waiting.append((INPUT_AT[i], load_w[9 + i]))
    for copy in (load_gs2, load_w[0], load_pre[0], load_h1, load_w[1], load_pre[1], load_w[2], load_w[3], load_u1, load_ext):
        copy.start()
    me = greet_block()
    owner = me < PAIRS
    stages, partners, remote = reduce_stages(gw, o_ref, (acc, lc, l1, mid, lz, l3, ag), sems)
    ends = seg_ends(lens_ref, segs)
    count = ends[-1]

    def weight_event(e, left, right):
        put_strips(gw, t_mm(stack[left], stack[right]), slice(None), lax.rem(e, GW_SLOTS) * PAIRS)

    def through_event(source, target, weight):
        stack[target] += mm_t(stack[source], w[weight])

    def inner_event(j):
        @pl.when(j == 0)
        def _():
            stack[GS1] = stack[GS2]

        at = PRE + lax.rem(j, 2)
        weight = lax.rem(2 * j, 4)

        def one(g, carry):
            cols = quad(g)
            pre = stack[at, :, cols]
            phi_big = 0.5 * (1.0 + lax.erf(pre * ROOT_HALF))
            slope = phi_big + pre * (INV_ROOT_TAU * jnp.exp(-0.5 * pre * pre))
            gpre = mm_t(stack[GS2], w[weight, cols, :]) * slope
            stack[GPRE, :, cols] = gpre
            stack[ACT, :, cols] = pre * phi_big
            dbi[:, pl.ds(pl.multiple_of(j * width + g * QUAD, QUAD), QUAD)] = jnp.sum(gpre, axis=0, keepdims=True)
            return carry

        lax.fori_loop(0, QUADS, one, 0)

    def ev_norm():
        e = gs1[...]
        unit = stack[U1]
        grad = norm_back(unit, inv1_ref[...], g1_ref[...][None, :], e)
        gs1[...] = grad
        ig[...] = grad
        gctx[...] = jnp.zeros_like(grad)
        small1[0:1, :] = jnp.sum(e * unit, axis=0, keepdims=True)
        small1[1:2, :] = jnp.sum(e, axis=0, keepdims=True)
        small1[2:3, :] = jnp.sum(grad, axis=0, keepdims=True)

    def ev_rims():
        rim[...] = rims_of(gctx[...], count)

    def ev_near(g):
        near_back_quad(g, gctx, near, q, kl_ref, b_ref, near, gb, gkl)

    def blend_copy(pair):
        return to_seq(gb.at[pair], land.at[me], b1s.at[pair], b1r.at[me], pair)

    up, down = rim_copies(n, me, rim, gleft, gright, ms, mr)

    def ev_blend():
        for pair in range(PAIRS):

            @pl.when(me != pair)
            def _(pair=pair):
                blend_copy(pair).start()

        rim_start(n, me, up, down, gleft, gright)

    def mixed_copy(target):
        return to_seq(cmsg.at[me], cmsg.at[me], b2s.at[target], b2r.at[me], target)

    def ev_owner():
        @pl.when(owner)
        def _():
            land[me] = gb[me]
            for s in range(n):

                @pl.when(me != s)
                def _(s=s):
                    to_seq(gb.at[0], land.at[s], b1s.at[0], b1r.at[s], s).wait_recv()

            gblend = land[0]
            for s in range(1, n):
                gblend = gblend + land[s]
            mixed = mx_ref[...]
            gmixed = mm(gblend, zs_ref[NEWTON], TOP)
            cmsg[me, 0:DH, :] = gmixed
            dots = jnp.sum(gmixed * mixed, axis=0, keepdims=True)
            cmsg[me, DH:MSG, :] = jnp.concatenate([dots, jnp.zeros((MSG - DH - 1, LANES), f32)], axis=0)
            for t in range(n):

                @pl.when(me != t)
                def _(t=t):
                    mixed_copy(t).start()

            ng[...] = inverse_grad(gblend, mixed)
            ncore[...] = jnp.zeros_like(ncore)
            nlead[...] = newton_lead(zs_ref[NEWTON - 1], ps_ref[NEWTON - 1])

        gl[...] = jnp.zeros_like(gl)

    def ev_newton(step):
        @pl.when(owner)
        def _():
            lead = newton_lead(zs_ref[jnp.maximum(step - 1, 0)], ps_ref[jnp.maximum(step - 1, 0)])
            ng[...], ncore[...] = newton_short(
                ng[...], ncore[...], nlead[...], core_ref[...], zs_ref[step], ps_ref[step], rs_ref[step], qs_ref[step]
            )
            nlead[...] = lead

    def ev_core():
        @pl.when(owner)
        def _():
            core_back(ng[...], ncore[...], core_ref[...], zs_ref[0], ql_ref, kl_ref, gl, me)

    quarter = slots // 4

    def ev_taps(part):
        @pl.when(part == 0)
        def _():
            load_ext.wait()
            tap_scr[...] = jnp.zeros_like(tap_scr)

        taps_grad_into(tap_scr, gctx, ext, quarter * (part + 1), quarter * part, False)

        @pl.when(part == 3)
        def _():
            gtaps[...] = taps_sums(tap_scr)

    def ev_conv(part):
        @pl.when(part == 0)
        def _():
            rim_wait(n, me, up, down)
            fill_extended(gext, gctx[...], gleft[...], gright[...], count)

        conv_into(gv, gext, taps_ref, quarter * (part + 1), True, False, quarter * part)

    def ev_mixed():
        for pair in range(PAIRS):

            @pl.when(me != pair)
            def _(pair=pair):
                to_seq(cmsg.at[pair], cmsg.at[pair], b2s.at[pair], b2r.at[pair], pair).wait_recv()

        for copy in (load_k, load_v, load_p):
            copy.wait()

    def ev_far(g):
        far_back_quad(g, k, v, p, m_ref, b_ref, cmsg, ql_ref, p, gv, gql, True)

    def ev_return():
        land_parts(ret, gql[...] + gl[0], gkl[...] + gl[1])
        for d in range(1, n):
            target = lax.rem(me + d, n)
            to_seq(ret.at[target], rland.at[me], rets.at[d], retr.at[me], target).start()

    def ev_own():
        rland[me] = ret[me]
        for d in range(1, n):
            source = lax.rem(me + d, n)
            to_seq(ret.at[0], rland.at[source], rets.at[d], retr.at[source], source).wait_recv()
        total = rland[0]
        for s in range(1, n):
            total = total + rland[s]
        own[...] = total
        inv = inverse_lens(lens_ref, segs)
        member = member_rows(ends, slots)
        near[...] += t_mm(member, own[0] * inv)
        p[...] += t_mm(member, own[1] * inv)
        small0[0:1, :] = jnp.sum(near[...], axis=0, keepdims=True)

    def ev_values():
        masked = jnp.where(valid_rows(count, slots), gv[...], 0.0)
        gv[...] = masked
        small0[1:2, :] = jnp.sum(masked, axis=0, keepdims=True)

    def small(i):
        return remote(sb.at[i], sl.at[i], ss.at[i], sr.at[i], partners[i])

    def ev_small(i):
        if i == 0:
            pack_small(sb, small0, small1, small2_ref, dbi, gtaps)
        else:
            small(i - 1).wait_recv()
            sb[i] = sb[i - 1] + sl[i - 1]
        if i < SMALL_STEPS:
            small(i).start()

    def at_tick(t, when, event):
        @pl.when(t == when)
        def _():
            event()

    def at_ticks(t, start, every, count, event):
        after = t - start

        @pl.when((after >= 0) & (after < every * count) & (lax.rem(after + every, every) == 0))
        def _():
            event(after // every)

    weights = {}
    through = {}
    for j, when in enumerate(FFN_AT):
        weights[when + 1] = (2 * j, ACT, GS2)
        weights[when + 2] = (2 * j + 1, H1, GPRE)
        through[when + 3] = (GPRE, GS1, (2 * j + 1) % 4)
    weights[OUTPUT_AT] = (8, CTX, GS1)
    for i, (when, part) in enumerate(((VALUE_AT, GV), (QUERY_AT, NEAR), (KEY_AT, PROB))):
        weights[when] = (9 + i, QUERY, part)
        through[INPUT_AT[i]] = (part, IG, 1 + i)
    through[GS1_AT] = (GS1, GCTX, 0)

    def by_table(t, table, event):
        columns = [pick(t, {when: row[i] for when, row in table.items()}) for i in range(3)]

        @pl.when(columns[0][1])
        def _():
            event(*[value for value, _ in columns])

    def by_group(t, table, size=6):
        for low in range(0, max(when for when, _ in table) + 1, size):
            mine = [row for row in table if low <= row[0] < low + size]
            if mine:

                @pl.when((t >= low) & (t < low + size))
                def _(mine=mine):
                    for when, event in mine:
                        at_tick(t, when, event)

    copies = [(when, copy.start) for when, copy in starting] + [(when, copy.wait) for when, copy in waiting]
    others = [(FFN_AT[3] + 3, ev_norm), (GS1_AT, ev_rims)]
    last = [
        (GS1_AT + 12, ev_core), (GS1_AT + 12, ev_return), (GS1_AT + 14, ev_own),
        (INPUT_AT[2], lambda: pltpu.make_async_copy(ig, ig_hbm, ig_sem.at[0]).start()),
    ] + [(SMALL_AT + 2 * i, partial(ev_small, i)) for i in range(SMALL_STEPS + 1)]

    def tick(t, carry):
        for stage, run in reversed(list(enumerate(stages))):
            since = t - ENTER - LAG[stage]
            at = jnp.where(since < HELD, since, since - GAP)

            @pl.when((since >= 0) & ((since < HELD) | (since >= HELD + GAP)) & (at < CHUNKS))
            def _(run=run, at=at):
                run(at)

        by_group(t, copies)
        block, hit = pick(t, {when: j for j, when in enumerate(FFN_AT)})

        @pl.when(hit)
        def _():
            inner_event(block)

        by_table(t, through, through_event)
        by_table(t, weights, weight_event)
        by_group(t, others)

        @pl.when((t > GS1_AT) & (t < GS1_AT + 12))
        def _():
            at_ticks(t, GS1_AT + 1, 1, QUADS, ev_near)
            at_tick(t, GS1_AT + 3, ev_blend)
            at_tick(t, GS1_AT + 5, ev_owner)
            at_ticks(t, GS1_AT + 6, 1, NEWTON, lambda i: ev_newton(NEWTON - 1 - i))
            at_ticks(t, GS1_AT + 5, 1, 4, ev_conv)
            at_tick(t, GS1_AT + 8, ev_mixed)
            at_ticks(t, GS1_AT + 8, 1, QUADS, ev_far)
            at_tick(t, GS1_AT + 10, ev_values)

        @pl.when(t >= GS1_AT + 12)
        def _():
            at_ticks(t, TAPS_AT, 1, 4, ev_taps)
            by_group(t, last)

        return carry

    lax.fori_loop(0, CHUNKS + ENTER + GAP + LAG[-1], tick, 0)
    for i in range(SMALL_STEPS):
        small(i).wait_send()
    so_ref[...] = sb[SMALL_STEPS]
    pltpu.make_async_copy(ig, ig_hbm, ig_sem.at[0]).wait()
    for pair in range(PAIRS):

        @pl.when(me != pair)
        def _(pair=pair):
            blend_copy(pair).wait_send()

    @pl.when(owner)
    def _():
        for t in range(n):

            @pl.when(me != t)
            def _(t=t):
                mixed_copy(t).wait_send()

    for d in range(1, n):
        target = lax.rem(me + d, n)
        to_seq(ret.at[target], rland.at[me], rets.at[d], retr.at[me], target).wait_send()


def tail(lens, big, little):
    slots, width = big[0].shape
    segs = lens.shape[1]
    at = CHUNKS
    n = SEQ_DEVICES
    dma = pltpu.SemaphoreType.DMA
    vm = lambda *dims: pltpu.VMEM(dims, f32)
    anywhere = pl.BlockSpec(memory_space=pl.ANY)
    one = dma((at,))
    zsem = dma((at, 2, 3))
    return pl.pallas_call(
        tail_kernel,
        in_specs=[smem()] + [anywhere] * len(big) + [whole()] * len(little),
        out_specs=[anywhere, whole(), anywhere],
        out_shape=[shape(2, at, STRIP // Z_ROWS, Z_ROWS, LANES), shape(SMALL_ROWS, LANES), shape(slots, width)],
        scratch_shapes=[
            vm(RING_ACC, STRIP, LANES), vm(RING_LC, STRIP, LANES), vm(RING_LC, 2, PART, LANES),
            vm(RING_MID, 4, 2, Z_ROWS, LANES), vm(RING_Z, 2, 3, 2, Z_ROWS, LANES), vm(RING_LC, 2, OWN, LANES),
            vm(RING_AG, 4, 2, Z_ROWS, LANES),
            vm(SMALL_STEPS + 1, SMALL_ROWS, LANES), vm(SMALL_STEPS, SMALL_ROWS, LANES), vm(GW_SLOTS * PAIRS, STRIP, LANES),
            vm(10, slots, width), vm(4, width, width), vm(slots + 40, width), vm(slots + 40, width),
            vm(CONV, 8, width), vm(40, LANES), vm(8, width), vm(8, width), vm(1, 4 * width),
            vm(PAIRS, DH, LANES), vm(2 * RIM, width), vm(DH, width), vm(DH, width), vm(2, DH, width),
            vm(n, DH, LANES), vm(PAIRS, MSG, LANES), vm(RIM, width), vm(RIM, width), vm(LANES, LANES), vm(LANES, LANES),
            vm(3 * LANES, LANES), vm(n, 2, segs, width), vm(n, 2, segs, width), vm(2, segs, width),
            dma((27,)), dma((1,)), dma((PAIRS,)), dma((n,)), dma((n,)), dma((n,)), dma((2,)), dma((2,)),
            dma((n,)), dma((n,)), dma((SMALL_STEPS,)), dma((SMALL_STEPS,)),
            one, one, one, one, one, zsem, one, one, one, zsem, one, dma((at, 2)), one, one,
        ],
        compiler_params=params(collective_id=5, has_side_effects=True),
        name="tail",
    )(lens, *big, *little)


def unstrip(strips):
    count, rows, _ = strips.shape
    return strips.transpose(1, 0, 2).reshape(rows, count * LANES)


def unstrip_tall(strips, across):
    count, rows, _ = strips.shape
    down = count // across
    return strips.reshape(down, across, rows, LANES).transpose(0, 2, 1, 3).reshape(down * rows, across * LANES)


PLACE_SLOTS = 24


def place_strips_kernel(s_ref, small_ref, *refs):
    outs = refs[:6]
    smalls = refs[6:-3]
    buf, in_sem, out_sem = refs[-3:]
    moves = []
    for e in range(CHUNKS // 3):
        if e < 8:
            out, row, col = outs[e % 2], (e // 2) * (1 - e % 2), (e // 2) * (e % 2)
        else:
            out, row, col = outs[e - 6], 0, 0
        for k in range(3):
            for c in range(2):
                rows = pl.ds(row * STRIP, STRIP)
                cols = pl.ds(col * STRIP + (2 * k + c) * LANES, LANES)
                slot = len(moves) % PLACE_SLOTS
                moves.append((
                    pltpu.make_async_copy(s_ref.at[c, 3 * e + k], buf.at[slot], in_sem.at[slot]),
                    pltpu.make_async_copy(buf.at[slot], out.at[rows, cols], out_sem.at[slot]),
                ))
    ahead = PLACE_SLOTS // 2
    for i in range(len(moves) + ahead):
        if i < len(moves):
            if i >= PLACE_SLOTS:
                moves[i - PLACE_SLOTS][1].wait()
            moves[i][0].start()
        if i >= ahead:
            moves[i - ahead][0].wait()
            moves[i - ahead][1].start()
    unpack_small(small_ref, smalls)
    for _, out in moves[-PLACE_SLOTS:]:
        out.wait()


def place_strips(summed, packed, shapes):
    anywhere = pl.BlockSpec(memory_space=pl.ANY)
    dma = pltpu.SemaphoreType.DMA
    width = shapes[0][1]
    return pl.pallas_call(
        place_strips_kernel,
        in_specs=[anywhere, whole()],
        out_specs=[anywhere] * len(shapes) + [whole()] * 10,
        out_shape=[shape(*dims) for dims in shapes] + [shape(width)] * 8 + [shape(shapes[0][0]), shape(HEADS, CONV)],
        scratch_shapes=[pltpu.VMEM((PLACE_SLOTS, STRIP, LANES), f32), dma((PLACE_SLOTS,)), dma((PLACE_SLOTS,))],
        compiler_params=params(),
        name="place_strips",
    )(summed, packed)


def per_device(
    tokens, segment_lens, query_weight, query_bias, key_weight, value_weight, value_bias, conv_taps,
    output_weight, output_bias, first_gain, first_bias, inner_weight, inner_bias, outer_weight, outer_bias,
    second_gain, second_bias, cotangent,
):
    n = lax.axis_size("seq")
    _, slots, width = tokens.shape
    x = tokens.reshape(slots, width)
    cot = cotangent.reshape(slots, width)
    lens = segment_lens

    q, k, v, raised, near, ctx, ext, h1, u1, tops, b, ql, kl, *saved, taps, inv1 = front(
        n, lens, x, conv_taps.T, query_bias, value_bias, output_bias, first_gain, first_bias,
        query_weight, key_weight, value_weight, output_weight,
    )
    pre, layer_out, gs2, small2 = ffn_forward(
        lens, h1, inner_weight, inner_bias.reshape(1, -1), outer_weight, outer_bias, cot, second_gain, second_bias
    )
    weights = [outer_weight, inner_weight, output_weight, value_weight, query_weight, key_weight]
    if n == SEQ_DEVICES and lax.axis_size("dp") == 4:
        big = [
            gs2, h1, u1, pre, outer_weight, inner_weight, output_weight, near, q, ctx, ext, k, v, raised, x,
            query_weight, key_weight, value_weight,
        ]
        little = [inv1, first_gain, tops, b, ql, kl, *saved, taps, small2]
        summed, packed, input_grad = tail(lens, big, little)
        sums = place_strips(summed.reshape(2, CHUNKS, STRIP, LANES), packed, [w.shape for w in weights])
    else:
        d_outer, d_inner, gs1, d_inner_bias, small1 = ffn_backward(
            h1, gs2, pre, inner_weight, outer_weight, u1, inv1, first_gain
        )
        gctx, gqn, gblend, gkl, grim = near_back(lens, gs1, output_weight, near, q, kl, b)
        c, gleft, gright, gl = blend_exchange(n, gblend, grim, ql, kl, saved)
        gkf, gvf, back = far_back(n, lens, k, v, raised, tops, b, c, ql, gkl, gl)
        own = land_return(n, back)
        gvc, gtaps, d_output = conv_back(lens, ext, gctx, gleft, gright, taps, ctx, gs1)
        input_grad, d_query, d_key, d_value, small0 = project_back(
            lens, x, gs1, gqn, gkf, gvc, gvf, own, query_weight, key_weight, value_weight
        )
        grads = [d_outer, d_inner, d_output, d_value, d_query, d_key]
        sums = sum_plain(grads + [small0, small1, small2, d_inner_bias, gtaps])
        small = sums[6:]
        sums = (
            [unstrip_tall(sums[0], width // LANES)] + [unstrip(s) for s in sums[1:6]]
            + [small[0][0], small[0][1], *small[1][:3], *small[2][:3], small[3][0], small[4][:CONV, :HEADS].T]
        )
    d_outer, d_inner, d_output, d_value, d_query, d_key, *vectors = sums
    d_query_bias, d_value_bias, d_first_gain, d_first_bias, d_output_bias = vectors[:5]
    d_second_gain, d_second_bias, d_outer_bias, d_inner_bias, d_taps = vectors[5:]
    return (
        layer_out.reshape(tokens.shape), input_grad.reshape(tokens.shape),
        d_query, d_query_bias, d_key, d_value, d_value_bias, d_taps.T,
        d_output, d_output_bias, d_first_gain, d_first_bias,
        d_inner, d_inner_bias, d_outer, d_outer_bias, d_second_gain, d_second_bias,
    )


def solution(mesh):
    block = P("dp", "seq", None)
    return jax.shard_map(
        per_device,
        mesh=mesh,
        in_specs=(block, P("dp", "seq")) + (P(),) * 16 + (block,),
        out_specs=(block, block) + (P(),) * 16,
        check_vma=False,
    )
```

```python
from functools import partial
import math

import jax
import jax.numpy as jnp
from jax import lax
from jax.experimental import pallas as pl
from jax.experimental.pallas import tpu as pltpu
from jax.sharding import PartitionSpec as P

HEADS = 12
DH = 64
CONV = 33
NEWTON = 6
RIM = (CONV - 1) // 2
LANES = 128
PAIRS = HEADS * DH // LANES
QUAD = 256
QUADS = HEADS * DH // QUAD
SCALE = DH ** (-0.5)
EPS = 1e-05
ROOT_HALF = 0.7071067811865476
INV_ROOT_TAU = 0.3989422804014327
MASKED = -1e30
f32 = jnp.float32
HI = lax.Precision.HIGH
TOP = lax.Precision.HIGHEST
MESH = pl.DeviceIdType.MESH
VMEM_CAP = 60 << 20


def _dg(a, b, ca, cb, prec):
    return lax.dot_general(
        a, b, (((ca,), (cb,)), ((), ())), precision=prec, preferred_element_type=f32
    )


def mm(a, b, prec=HI):
    return _dg(a, b, 1, 0, prec)


def mm_t(a, b, prec=HI):
    return _dg(a, b, 1, 1, prec)


def t_mm(a, b, prec=HI):
    return _dg(a, b, 0, 0, prec)


def head_mask(size):
    row = lax.broadcasted_iota(jnp.int32, (size, size), 0) >> 6
    col = lax.broadcasted_iota(jnp.int32, (size, size), 1) >> 6
    return row == col


def spread(rows, mask):
    return jnp.where(mask, jnp.concatenate([rows] * (mask.shape[0] // DH), axis=0), 0.0)


def fold(square, mask):
    kept = jnp.where(mask, square, 0.0)
    total = kept[:DH]
    for at in range(DH, mask.shape[0], DH):
        total = total + kept[at : at + DH]
    return total


def seg_ends(lens_ref, count):
    ends = []
    total = 0
    for j in range(count):
        total = total + lens_ref[0, j]
        ends.append(total)
    return ends


def member_rows(ends, slots):
    shape = (len(ends), slots)
    row = lax.broadcasted_iota(jnp.int32, shape, 0)
    col = lax.broadcasted_iota(jnp.int32, shape, 1)
    low = jnp.zeros(shape, jnp.int32)
    high = jnp.zeros(shape, jnp.int32)
    before = 0
    for j, end in enumerate(ends):
        low = jnp.where(row == j, before, low)
        high = jnp.where(row == j, end, high)
        before = end
    return jnp.where((col >= low) & (col < high), 1.0, 0.0)


def inverse_lens(lens_ref, count):
    row = lax.broadcasted_iota(jnp.int32, (count, 1), 0)
    out = jnp.zeros((count, 1), f32)
    for j in range(count):
        out = jnp.where(row == j, lens_ref[0, j].astype(f32), out)
    return 1.0 / out


def valid_rows(count, slots):
    return lax.broadcasted_iota(jnp.int32, (slots, 1), 0) < count


def rims_of(matrix, count):
    slots = matrix.shape[0]
    row = lax.broadcasted_iota(jnp.int32, (2 * RIM, slots), 0)
    col = lax.broadcasted_iota(jnp.int32, (2 * RIM, slots), 1)
    want = jnp.where(row < RIM, row, row - 2 * RIM + count)
    return mm(jnp.where(col == want, 1.0, 0.0), matrix)


def fill_extended(ext_ref, middle, left, right, count):
    slots = middle.shape[0]
    ext_ref[0:RIM, :] = left
    ext_ref[RIM : RIM + slots, :] = middle
    tail = ext_ref.shape[0] - RIM - slots
    ext_ref[RIM + slots :, :] = jnp.zeros((tail, middle.shape[1]), f32)
    rows = slots + RIM
    row = lax.broadcasted_iota(jnp.int32, (rows, RIM), 0)
    col = lax.broadcasted_iota(jnp.int32, (rows, RIM), 1)
    put = jnp.where(row == col + count, 1.0, 0.0)
    ext_ref[RIM : RIM + rows, :] += mm(put, right)


CONV_ROWS = 64


def shifted(ext_ref, r0, l0):
    slab = ext_ref[pl.ds(r0, CONV_ROWS + 40), pl.ds(l0, LANES)]
    for b in range(8):
        moved = slab[b : b + CONV_ROWS + 32]
        for a in range(5):
            if 8 * a + b < CONV:
                yield 8 * a + b, moved[8 * a : 8 * a + CONV_ROWS]


def conv_into(out_ref, ext_ref, taps_ref, slots, flip, add, low=0):
    def block(i, carry):
        r0 = pl.multiple_of((i // PAIRS) * CONV_ROWS, CONV_ROWS)
        l0 = pl.multiple_of((i % PAIRS) * LANES, LANES)
        acc = jnp.zeros((CONV_ROWS, LANES), f32)
        for c, part in shifted(ext_ref, r0, l0):
            at = CONV - 1 - c if flip else c
            acc = acc + taps_ref[at : at + 1, pl.ds(l0, LANES)] * part
        here = (pl.ds(r0, CONV_ROWS), pl.ds(l0, LANES))
        if add:
            out_ref[here] += acc
        else:
            out_ref[here] = acc
        return carry

    lax.fori_loop((low // CONV_ROWS) * PAIRS, (slots // CONV_ROWS) * PAIRS, block, 0)


def taps_grad_into(scr_ref, grad_ref, ext_ref, slots, low=0, clear=True):
    if clear:
        scr_ref[...] = jnp.zeros_like(scr_ref)

    def block(i, carry):
        r0 = pl.multiple_of((i // PAIRS) * CONV_ROWS, CONV_ROWS)
        l0 = pl.multiple_of((i % PAIRS) * LANES, LANES)
        grad = grad_ref[pl.ds(r0, CONV_ROWS), pl.ds(l0, LANES)]
        for c, part in shifted(ext_ref, r0, l0):
            prod = grad * part
            total = prod[0:8]
            for at in range(8, CONV_ROWS, 8):
                total = total + prod[at : at + 8]
            scr_ref[c, :, pl.ds(l0, LANES)] += total
        return carry

    lax.fori_loop((low // CONV_ROWS) * PAIRS, (slots // CONV_ROWS) * PAIRS, block, 0)


def whole(shape=None):
    return pl.BlockSpec(memory_space=pltpu.VMEM)


def smem():
    return pl.BlockSpec(memory_space=pltpu.SMEM)


def params(**more):
    return pltpu.CompilerParams(vmem_limit_bytes=VMEM_CAP, **more)


def shape(*dims):
    return jax.ShapeDtypeStruct(dims, f32)


def greet_signal(n):
    me = lax.axis_index("seq")
    for d in range(1, n):
        pl.semaphore_signal(
            pltpu.get_barrier_semaphore(), inc=1, device_id={"seq": lax.rem(me + d, n)}, device_id_type=MESH
        )
    return me


def greet_all(n):
    me = greet_signal(n)
    pl.semaphore_wait(pltpu.get_barrier_semaphore(), n - 1)
    return me


def to_seq(src, dst, send, recv, target):
    return pltpu.make_async_remote_copy(
        src, dst, send, recv, device_id={"seq": target}, device_id_type=MESH
    )


def rim_copies(n, me, rim_ref, left_ref, right_ref, rsend, rrecv):
    up = to_seq(rim_ref.at[pl.ds(RIM, RIM)], left_ref, rsend.at[0], rrecv.at[0], lax.rem(me + 1, n))
    down = to_seq(rim_ref.at[pl.ds(0, RIM)], right_ref, rsend.at[1], rrecv.at[1], lax.rem(me + n - 1, n))
    return up, down


def rim_start(n, me, up, down, left_ref, right_ref):
    @pl.when(me < n - 1)
    def _():
        up.start()

    @pl.when(me > 0)
    def _():
        down.start()

    @pl.when(me == 0)
    def _():
        left_ref[...] = jnp.zeros_like(left_ref)

    @pl.when(me == n - 1)
    def _():
        right_ref[...] = jnp.zeros_like(right_ref)


def rim_wait(n, me, up, down):
    @pl.when(me > 0)
    def _():
        up.wait_recv()
        down.wait_send()

    @pl.when(me < n - 1)
    def _():
        down.wait_recv()
        up.wait_send()


MSG = DH + 8


def owner_of(pair, n):
    return pair if pair < PAIRS // 2 else pair + n // 2 - PAIRS // 2


def pair_at(me, n):
    half = PAIRS // 2
    low = me < half
    owns = low | ((me >= n // 2) & (me < n // 2 + half))
    return owns, jnp.where(low, me, jnp.where(owns, me - n // 2 + half, 0))


def eye(size):
    row = lax.broadcasted_iota(jnp.int32, (size, size), 0)
    col = lax.broadcasted_iota(jnp.int32, (size, size), 1)
    return jnp.where(row == col, 1.0, 0.0)


def pair_sums(row):
    lane = lax.broadcasted_iota(jnp.int32, row.shape, 1)
    first = jnp.sum(jnp.where(lane < DH, row, 0.0), axis=1, keepdims=True)
    second = jnp.sum(jnp.where(lane < DH, 0.0, row), axis=1, keepdims=True)
    return jnp.where(lane < DH, first, second)


def core_of(query, key, mask):
    scores = jnp.where(mask, mm_t(query, key, TOP) * SCALE, MASKED)
    raised = jnp.exp(scores - jnp.max(scores, axis=1, keepdims=True))
    return raised / jnp.sum(raised, axis=1, keepdims=True)


def inverse_grad(gblend, mixed):
    return jnp.where(head_mask(LANES), t_mm(gblend, mixed, TOP), 0.0)


def newton_back(g, gcore, core, z, prod, r, q):
    prod_t = prod.T
    gq = 0.25 * mm(z.T, g, TOP)
    gr = -mm(prod_t, gq, TOP)
    gs = -mm(prod_t, gr, TOP)
    gp = -mm_t(gq, r, TOP) - mm_t(gr, 7.0 * eye(LANES) - prod, TOP) - gs
    return 0.25 * mm_t(g, q, TOP) + mm(core.T, gp, TOP), gcore + mm_t(gp, z, TOP)


def newton_lead(z, prod):
    zp = mm(z, prod, TOP)
    zpp = mm(zp, prod, TOP)
    return jnp.concatenate([0.25 * z.T, -0.25 * zp.T, 0.25 * zpp.T], axis=0)


def newton_short(g, gcore, lead, core, z, prod, r, q):
    gqrs = mm(lead, g, TOP)
    gq, gr, gs = [gqrs[at : at + LANES] for at in range(0, 3 * LANES, LANES)]
    left = jnp.concatenate([gq, gr], axis=1)
    right = jnp.concatenate([r, 7.0 * eye(LANES) - prod], axis=1)
    gp = -mm_t(left, right, TOP) - gs
    through = mm(jnp.concatenate([g, core.T], axis=1), jnp.concatenate([0.25 * q.T, gp], axis=0), TOP)
    return through, gcore + mm_t(gp, z, TOP)


def core_back(g, gcore, core, first, ql_ref, kl_ref, gl_ref, pair):
    mask = head_mask(LANES)
    colsum = jnp.sum(core, axis=0, keepdims=True)
    square = pair_sums(colsum * colsum)
    sigma = jnp.sqrt(square)
    dot = pair_sums(jnp.sum(g * first, axis=0, keepdims=True))
    gcore = gcore + g.T / sigma - jnp.where(mask, dot / square * colsum, 0.0)
    gscore = core * (gcore - jnp.sum(core * gcore, axis=1, keepdims=True)) * SCALE
    lanes = pl.ds(pl.multiple_of(pair * LANES, LANES), LANES)
    query = spread(ql_ref[:, lanes], mask)
    key = spread(kl_ref[:, lanes], mask)
    gl_ref[...] = jnp.zeros_like(gl_ref)
    gl_ref[0, :, lanes] = fold(mm(gscore, key, TOP), mask)
    gl_ref[1, :, lanes] = fold(t_mm(gscore, query, TOP), mask)


def blend_exchange_kernel(
    n, g_ref, rim_ref, ql_ref, kl_ref, core_ref, zs_ref, ps_ref, rs_ref, qs_ref, mx_ref,
    c_ref, left_ref, right_ref, gl_ref,
    land, s1, r1, s2, r2, rsend, rrecv,
):
    me = greet_all(n)
    owns, pair_here = pair_at(me, n)
    for p in range(PAIRS):

        @pl.when(me != owner_of(p, n))
        def _(p=p):
            to_seq(g_ref.at[p], land.at[me], s1.at[p], r1.at[me], owner_of(p, n)).start()

    up, down = rim_copies(n, me, rim_ref, left_ref, right_ref, rsend, rrecv)
    rim_start(n, me, up, down, left_ref, right_ref)

    @pl.when(jnp.logical_not(owns))
    def _():
        gl_ref[...] = jnp.zeros_like(gl_ref)

    @pl.when(owns)
    def _():
        mask = head_mask(LANES)
        land[me] = g_ref[pair_here]
        for s in range(n):

            @pl.when(me != s)
            def _(s=s):
                to_seq(g_ref.at[0], land.at[s], s1.at[0], r1.at[s], s).wait_recv()

        gblend = land[0]
        for s in range(1, n):
            gblend = gblend + land[s]
        mixed = mx_ref[...]
        gmixed = mm(gblend, zs_ref[NEWTON], TOP)
        c_ref[pair_here, 0:DH, :] = gmixed
        dots = jnp.sum(gmixed * mixed, axis=0, keepdims=True)
        pad = jnp.zeros((MSG - DH - 1, LANES), f32)
        c_ref[pair_here, DH:MSG, :] = jnp.concatenate([dots, pad], axis=0)
        for t in range(n):

            @pl.when(me != t)
            def _(t=t):
                to_seq(c_ref.at[pair_here], c_ref.at[pair_here], s2.at[t], r2.at[pair_here], t).start()

        gcore = jnp.zeros((LANES, LANES), f32)
        g = inverse_grad(gblend, mixed)
        for step in reversed(range(NEWTON)):
            g, gcore = newton_back(g, gcore, core_ref[...], zs_ref[step], ps_ref[step], rs_ref[step], qs_ref[step])
        core_back(g, gcore, core_ref[...], zs_ref[0], ql_ref, kl_ref, gl_ref, pair_here)

    for p in range(PAIRS):

        @pl.when(me != owner_of(p, n))
        def _(p=p):
            to_seq(c_ref.at[p], c_ref.at[p], s2.at[p], r2.at[p], owner_of(p, n)).wait_recv()
            to_seq(g_ref.at[p], land.at[me], s1.at[p], r1.at[me], owner_of(p, n)).wait_send()

    rim_wait(n, me, up, down)

    @pl.when(owns)
    def _():
        for t in range(n):

            @pl.when(me != t)
            def _(t=t):
                to_seq(c_ref.at[pair_here], c_ref.at[pair_here], s2.at[t], r2.at[pair_here], t).wait_send()


def blend_exchange(n, gblend, rim, ql, kl, saved):
    dma = pltpu.SemaphoreType.DMA
    width = rim.shape[1]
    return pl.pallas_call(
        partial(blend_exchange_kernel, n),
        in_specs=[whole()] * 10,
        out_specs=[whole()] * 4,
        out_shape=[shape(PAIRS, MSG, LANES), shape(RIM, width), shape(RIM, width), shape(2, DH, width)],
        scratch_shapes=[
            pltpu.VMEM((n, DH, LANES), f32),
            dma((PAIRS,)), dma((n,)), dma((n,)), dma((n,)), dma((2,)), dma((2,)),
        ],
        compiler_params=params(collective_id=3, has_side_effects=True),
        name="blend_exchange",
    )(gblend, rim, ql, kl, *saved)


def land_return_kernel(n, x_ref, own_ref, land, send, recv):
    me = greet_all(n)
    copies = []
    for d in range(1, n):
        target = lax.rem(me + d, n)
        copy = to_seq(x_ref.at[target], land.at[me], send.at[d], recv.at[me], target)
        copy.start()
        copies.append(copy)
    land[me] = x_ref[me]
    for d in range(1, n):
        source = lax.rem(me + d, n)
        to_seq(x_ref.at[0], land.at[source], send.at[d], recv.at[source], source).wait_recv()
    total = land[0]
    for s in range(1, n):
        total = total + land[s]
    own_ref[...] = total
    for copy in copies:
        copy.wait_send()


def land_return(n, parts):
    dma = pltpu.SemaphoreType.DMA
    return pl.pallas_call(
        partial(land_return_kernel, n),
        in_specs=[whole()],
        out_specs=whole(),
        out_shape=shape(*parts.shape[1:]),
        scratch_shapes=[pltpu.VMEM(parts.shape, f32), dma((n,)), dma((n,))],
        compiler_params=params(collective_id=4, has_side_effects=True),
        name="land_return",
    )(parts)


def norm_stats(r):
    centered = r - jnp.mean(r, axis=1, keepdims=True)
    spread_ = jnp.mean(centered * centered, axis=1, keepdims=True)
    inv = lax.rsqrt(spread_ + EPS)
    return centered * inv, inv


def norm_back(unit, inv, gain, grad):
    ge = grad * gain
    return (
        ge
        - jnp.mean(ge, axis=1, keepdims=True)
        - unit * jnp.mean(ge * unit, axis=1, keepdims=True)
    ) * inv


def quad(g):
    return pl.ds(pl.multiple_of(g * QUAD, QUAD), QUAD)


def pair_rows(ref, g, rows):
    return jnp.concatenate([ref[2 * g, rows, :], ref[2 * g + 1, rows, :]], axis=1)


def front_kernel(
    n, lens_ref, x_ref, taps_in, bq_ref, bv_ref, bo_ref, g1_ref, b1_ref, wq_hbm, wk_hbm, wv_hbm, wo_hbm,
    q_out, k_out, v_out, p_out, near_out, ctx_out, ext_out, h1_out, u1_out,
    m_ref, b_ref, ql_ref, kl_ref, core_ref, zs_ref, ps_ref, rs_ref, qs_ref, mx_ref, taps_ref, inv1_ref,
    w, bias, stack, ext, f_ref, mine, lands, rim, left, right, land,
    load, out, ms, mr, ls, lr, s1, r1, s2, r2,
):
    _, slots, width = stack.shape
    segs = mine.shape[1]
    v, q, k, p, near, ctx, h1, u1 = [stack.at[i] for i in range(8)]
    loads = [pltpu.make_async_copy(hbm, w.at[i], load.at[i]) for i, hbm in enumerate((wv_hbm, wq_hbm, wk_hbm, wo_hbm))]
    for copy in loads:
        copy.start()
    leaving = []

    def leave(src, dst):
        leaving.append(pltpu.make_async_copy(src, dst, out.at[len(leaving)]))
        leaving[-1].start()

    me = greet_signal(n)
    owns, pair_here = pair_at(me, n)
    ends = seg_ends(lens_ref, segs)
    count = ends[-1]
    valid = valid_rows(count, slots)
    member = member_rows(ends, slots)
    inv = inverse_lens(lens_ref, segs)
    bias[0:1, :] = bv_ref[...][None, :]
    bias[1:2, :] = bq_ref[...][None, :]
    bias[2:3, :] = jnp.zeros((1, width), f32)

    def one(i, carry):
        pltpu.make_async_copy(wv_hbm, w.at[i], load.at[i]).wait()
        stack[i] = mm(x_ref[...], w[i]) + bias[pl.ds(i, 1), :]

        @pl.when(i == 0)
        def _():
            v[...] = jnp.where(valid, v[...], 0.0)
            rim[...] = rims_of(v[...], count)
            pl.semaphore_wait(pltpu.get_barrier_semaphore(), n - 1)
            rim_start(n, me, up, down, left, right)

        return carry

    def land_copy(kind, source, d, target):
        return to_seq(mine.at[kind], lands.at[source, kind], ls.at[kind, d], lr.at[kind, source], target)

    def land_rows(kind, rows_ref):
        for d in range(1, n):
            source = lax.rem(me + d, n)
            land_copy(kind, source, d, source).wait_recv()
        for s in range(n):
            rows_ref[slice(s * segs, (s + 1) * segs), :] = lands[s, kind]

    up, down = rim_copies(n, me, rim, left, right, ms, mr)
    lax.fori_loop(0, 3, one, 0)
    mine[0] = mm(member, q[...]) * inv
    mine[1] = mm(member, k[...]) * inv
    for kind in range(2):
        for d in range(1, n):
            land_copy(kind, me, d, lax.rem(me + d, n)).start()
    lands[me] = mine[...]
    leave(q, q_out)
    leave(k, k_out)
    leave(v, v_out)
    row = lax.broadcasted_iota(jnp.int32, (HEADS, width), 0)
    col = lax.broadcasted_iota(jnp.int32, (HEADS, width), 1) >> 6
    taps_ref[...] = t_mm(taps_in[...], jnp.where(row == col, 1.0, 0.0), TOP)
    rim_wait(n, me, up, down)
    fill_extended(ext, v[...], left[...], right[...], count)
    leave(ext, ext_out)
    conv_into(ctx, ext, taps_ref, slots, False, False)

    land_rows(0, ql_ref)

    def far(g, carry):
        cols = quad(g)
        mask = head_mask(QUAD)
        scores = mm_t(k[:, cols], spread(ql_ref[:, cols], mask)) * SCALE
        scores = jnp.where(valid, scores, MASKED)
        top = jnp.max(scores, axis=0, keepdims=True)
        raised = jnp.where(valid, jnp.exp(scores - top), 0.0)
        p[:, cols] = raised
        m_ref[:, cols] = top
        total = jnp.sum(raised, axis=0, keepdims=True)
        weighted = fold(t_mm(v[:, cols], raised), mask)
        rest = jnp.concatenate([top, total, jnp.zeros((MSG - DH - 2, QUAD), f32)], axis=0)
        for j in range(QUAD // LANES):
            part = slice(j * LANES, (j + 1) * LANES)
            f_ref[g * 2 + j, 0:DH, :] = weighted[:, part]
            f_ref[g * 2 + j, DH:MSG, :] = rest[:, part]
        return carry

    lax.fori_loop(0, QUADS, far, 0)
    for pair in range(PAIRS):

        @pl.when(me != owner_of(pair, n))
        def _(pair=pair):
            to_seq(f_ref.at[pair], land.at[me], s1.at[pair], r1.at[me], owner_of(pair, n)).start()

    leave(p, p_out)
    land_rows(1, kl_ref)

    @pl.when(owns)
    def _():
        mask = head_mask(LANES)
        lanes = pl.ds(pl.multiple_of(pair_here * LANES, LANES), LANES)
        core = core_of(spread(ql_ref[:, lanes], mask), spread(kl_ref[:, lanes], mask), mask)
        core_ref[...] = core
        colsum = jnp.sum(core, axis=0, keepdims=True)
        zs_ref[0] = core.T / jnp.sqrt(pair_sums(colsum * colsum))
        unit = eye(LANES)

        def newton(step, carry):
            z = zs_ref[step]
            prod = mm(core_ref[...], z, TOP)
            ps_ref[step] = prod
            r = 15.0 * unit - mm(prod, 7.0 * unit - prod, TOP)
            rs_ref[step] = r
            q_ = 13.0 * unit - mm(prod, r, TOP)
            qs_ref[step] = q_
            zs_ref[step + 1] = 0.25 * mm(z, q_, TOP)
            return carry

        lax.fori_loop(0, NEWTON, newton, 0)
        land[me] = f_ref[pair_here]
        for s in range(n):

            @pl.when(me != s)
            def _(s=s):
                to_seq(f_ref.at[0], land.at[s], s1.at[0], r1.at[s], s).wait_recv()

        top = land[0][DH : DH + 1]
        for s in range(1, n):
            top = jnp.maximum(top, land[s][DH : DH + 1])
        total = jnp.zeros_like(top)
        mixed = jnp.zeros((DH, LANES), f32)
        for s in range(n):
            part = land[s]
            factor = jnp.exp(part[DH : DH + 1] - top)
            total = total + part[DH + 1 : DH + 2] * factor
            mixed = mixed + part[:DH] * factor
        mixed = mixed / total
        mx_ref[...] = mixed
        b_ref[pair_here, 0:DH, :] = mm_t(mixed, zs_ref[NEWTON], TOP)
        pad = jnp.zeros((MSG - DH - 2, LANES), f32)
        b_ref[pair_here, DH:MSG, :] = jnp.concatenate([top, total, pad], axis=0)
        for t in range(n):

            @pl.when(me != t)
            def _(t=t):
                to_seq(b_ref.at[pair_here], b_ref.at[pair_here], s2.at[t], r2.at[pair_here], t).start()

    def soft(g, carry):
        cols = quad(g)
        mask = head_mask(QUAD)
        head = lax.broadcasted_iota(jnp.int32, (slots, QUAD), 1) >> 6
        scores = mm_t(q[:, cols], spread(kl_ref[:, cols], mask)) * SCALE
        tops = [jnp.max(scores[:, h * DH : (h + 1) * DH], axis=1, keepdims=True) for h in range(4)]
        top = jnp.where(head < 2, jnp.where(head < 1, tops[0], tops[1]), jnp.where(head < 3, tops[2], tops[3]))
        raised = jnp.exp(scores - top)
        near[:, cols] = raised / mm(raised, jnp.where(mask, 1.0, 0.0))
        return carry

    lax.fori_loop(0, QUADS, soft, 0)
    leave(near, near_out)
    for pair in range(PAIRS):

        @pl.when(me != owner_of(pair, n))
        def _(pair=pair):
            to_seq(b_ref.at[pair], b_ref.at[pair], s2.at[pair], r2.at[pair], owner_of(pair, n)).wait_recv()

    def blend(g, carry):
        cols = quad(g)
        ctx[:, cols] += mm_t(near[:, cols], spread(pair_rows(b_ref, g, slice(0, DH)), head_mask(QUAD)))
        return carry

    lax.fori_loop(0, QUADS, blend, 0)
    leave(ctx, ctx_out)
    loads[-1].wait()

    unit, scale = norm_stats(x_ref[...] + (mm(ctx[...], w[3]) + bo_ref[...][None, :]))
    h1[...] = unit * g1_ref[...][None, :] + b1_ref[...][None, :]
    leave(h1, h1_out)
    u1[...] = unit
    leave(u1, u1_out)
    inv1_ref[...] = scale
    for kind in range(2):
        for d in range(1, n):
            land_copy(kind, me, d, lax.rem(me + d, n)).wait_send()
    for pair in range(PAIRS):

        @pl.when(me != owner_of(pair, n))
        def _(pair=pair):
            to_seq(f_ref.at[pair], land.at[me], s1.at[pair], r1.at[me], owner_of(pair, n)).wait_send()

    @pl.when(owns)
    def _():
        for t in range(n):

            @pl.when(me != t)
            def _(t=t):
                to_seq(b_ref.at[pair_here], b_ref.at[pair_here], s2.at[t], r2.at[pair_here], t).wait_send()

    for copy in leaving:
        copy.wait()


def front(n, lens, x, taps, bq, bv, bo, g1, b1, wq, wk, wv, wo):
    slots, width = x.shape
    segs = lens.shape[1]
    dma = pltpu.SemaphoreType.DMA
    vm = lambda *dims: pltpu.VMEM(dims, f32)
    anywhere = pl.BlockSpec(memory_space=pl.ANY)
    square = (LANES, LANES)
    rows = shape(slots, width)
    return pl.pallas_call(
        partial(front_kernel, n),
        in_specs=[smem()] + [whole()] * 7 + [anywhere] * 4,
        out_specs=[anywhere] * 9 + [whole()] * 12,
        out_shape=[rows] * 6 + [shape(slots + 40, width), rows, rows]
        + [
            shape(1, width), shape(PAIRS, MSG, LANES), shape(DH, width), shape(DH, width), shape(*square),
            shape(NEWTON + 1, *square), shape(NEWTON, *square), shape(NEWTON, *square), shape(NEWTON, *square),
            shape(DH, LANES), shape(CONV, width), shape(slots, 1),
        ],
        scratch_shapes=[
            vm(4, width, width), vm(8, width), vm(8, slots, width), vm(slots + 40, width),
            vm(PAIRS, MSG, LANES), vm(2, segs, width), vm(n, 2, segs, width), vm(2 * RIM, width), vm(RIM, width),
            vm(RIM, width), vm(n, MSG, LANES),
            dma((4,)), dma((9,)), dma((2,)), dma((2,)), dma((2, n)), dma((2, n)), dma((PAIRS,)), dma((n,)),
            dma((n,)), dma((n,)),
        ],
        compiler_params=params(collective_id=1, has_side_effects=True),
        name="front",
    )(lens, x, taps, bq, bv, bo, g1, b1, wq, wk, wv, wo)


def forward_kernel(
    lens_ref, h1_ref, wi_ref, bi_ref, wo_ref, bo_ref, cot_ref, g2_ref, b2_ref,
    pre_ref, out_ref, gs2_ref, small_ref,
    acc_ref, act_ref,
):
    step = pl.program_id(0)

    @pl.when(step == 0)
    def _():
        acc_ref[...] = jnp.zeros_like(acc_ref)

    def one(g, carry):
        cols = quad(g)
        pre = mm(h1_ref[...], wi_ref[:, cols]) + bi_ref[:, cols]
        pre_ref[:, cols] = pre
        act_ref[:, cols] = 0.5 * pre * (1.0 + lax.erf(pre * ROOT_HALF))
        return carry

    lax.fori_loop(0, QUADS, one, 0)

    def two(g, carry):
        cols = quad(g)
        acc_ref[:, cols] += mm(act_ref[...], wo_ref[:, cols])
        return carry

    lax.fori_loop(0, QUADS, two, 0)

    @pl.when(step == pl.num_programs(0) - 1)
    def _():
        slots = h1_ref.shape[0]
        valid = valid_rows(seg_ends(lens_ref, lens_ref.shape[1])[-1], slots)
        summed = h1_ref[...] + (acc_ref[...] + bo_ref[...][None, :])
        unit, inv = norm_stats(summed)
        out_ref[...] = jnp.where(valid, unit * g2_ref[...][None, :] + b2_ref[...][None, :], 0.0)
        e = jnp.where(valid, cot_ref[...], 0.0)
        grad = norm_back(unit, inv, g2_ref[...][None, :], e)
        gs2_ref[...] = grad
        small_ref[...] = jnp.concatenate(
            [
                jnp.sum(e * unit, axis=0, keepdims=True),
                jnp.sum(e, axis=0, keepdims=True),
                jnp.sum(grad, axis=0, keepdims=True),
                jnp.zeros((5, e.shape[1]), f32),
            ],
            axis=0,
        )


def ffn_forward(lens, h1, wi, bi, wo, bo, cot, g2, b2):
    slots, width = h1.shape
    inner = wi.shape[1]
    const = lambda *dims: pl.BlockSpec(dims, lambda j: (0,) * len(dims))
    return pl.pallas_call(
        forward_kernel,
        grid=(inner // width,),
        in_specs=[
            smem(), const(slots, width),
            pl.BlockSpec((width, width), lambda j: (0, j)), pl.BlockSpec((1, width), lambda j: (0, j)),
            pl.BlockSpec((width, width), lambda j: (j, 0)), const(width),
            const(slots, width), const(width), const(width),
        ],
        out_specs=[
            pl.BlockSpec((slots, width), lambda j: (0, j)),
            const(slots, width), const(slots, width), const(8, width),
        ],
        out_shape=[shape(slots, inner), shape(slots, width), shape(slots, width), shape(8, width)],
        scratch_shapes=[pltpu.VMEM((slots, width), f32)] * 2,
        compiler_params=params(),
        name="ffn_forward",
    )(lens, h1, wi, bi, wo, bo, cot, g2, b2)


def put_strips(ref, block, rows=slice(None), first=0):
    for s in range(block.shape[1] // LANES):
        ref[first + s, rows, :] = block[:, s * LANES : (s + 1) * LANES]


def backward_kernel(
    h1_ref, gs2_ref, pre_ref, wi_ref, wo_ref, u1_ref, inv1_ref, g1_ref,
    dwo_ref, dwi_ref, gs1_ref, dbi_ref, small_ref,
    acc_ref, gpre_ref,
):
    step = pl.program_id(0)

    @pl.when(step == 0)
    def _():
        acc_ref[...] = gs2_ref[...]

    def one(g, carry):
        cols = quad(g)
        pre = pre_ref[:, cols]
        phi_big = 0.5 * (1.0 + lax.erf(pre * ROOT_HALF))
        slope = phi_big + pre * (INV_ROOT_TAU * jnp.exp(-0.5 * pre * pre))
        gpre = mm_t(gs2_ref[...], wo_ref[cols, :]) * slope
        gpre_ref[:, cols] = gpre
        dbi_ref[:, cols] = jnp.sum(gpre, axis=0, keepdims=True)
        put_strips(dwo_ref, t_mm(pre * phi_big, gs2_ref[...]), cols)
        return carry

    lax.fori_loop(0, QUADS, one, 0)

    def two(g, carry):
        cols = quad(g)
        put_strips(dwi_ref, t_mm(h1_ref[:, cols], gpre_ref[...]), cols)
        acc_ref[:, cols] += mm_t(gpre_ref[...], wi_ref[cols, :])
        return carry

    lax.fori_loop(0, QUADS, two, 0)

    @pl.when(step == pl.num_programs(0) - 1)
    def _():
        e = acc_ref[...]
        unit = u1_ref[...]
        grad = norm_back(unit, inv1_ref[...], g1_ref[...][None, :], e)
        gs1_ref[...] = grad
        small_ref[...] = jnp.concatenate(
            [
                jnp.sum(e * unit, axis=0, keepdims=True),
                jnp.sum(e, axis=0, keepdims=True),
                jnp.sum(grad, axis=0, keepdims=True),
                jnp.zeros((5, e.shape[1]), f32),
            ],
            axis=0,
        )


def ffn_backward(h1, gs2, pre, wi, wo, u1, inv1, g1):
    slots, width = h1.shape
    inner = wi.shape[1]
    strips = width // LANES
    const = lambda *dims: pl.BlockSpec(dims, lambda j: (0,) * len(dims))
    return pl.pallas_call(
        backward_kernel,
        grid=(inner // width,),
        in_specs=[
            const(slots, width), const(slots, width),
            pl.BlockSpec((slots, width), lambda j: (0, j)),
            pl.BlockSpec((width, width), lambda j: (0, j)),
            pl.BlockSpec((width, width), lambda j: (j, 0)),
            const(slots, width), const(slots, 1), const(width),
        ],
        out_specs=[
            pl.BlockSpec((strips, width, LANES), lambda j: (j, 0, 0)),
            pl.BlockSpec((strips, width, LANES), lambda j: (j, 0, 0)),
            const(slots, width),
            pl.BlockSpec((1, width), lambda j: (0, j)),
            const(8, width),
        ],
        out_shape=[
            shape(inner // LANES, width, LANES), shape(inner // LANES, width, LANES),
            shape(slots, width), shape(1, inner), shape(8, width),
        ],
        scratch_shapes=[pltpu.VMEM((slots, width), f32)] * 2,
        compiler_params=params(),
        name="ffn_backward",
    )(h1, gs2, pre, wi, wo, u1, inv1, g1)


def near_back_quad(g, gctx_ref, near_ref, q_ref, kl_ref, b_ref, gq_ref, gb_ref, gkl_ref):
    mask = head_mask(QUAD)
    ones = jnp.where(mask, 1.0, 0.0)
    cols = quad(g)
    gctx = gctx_ref[:, cols]
    near = near_ref[:, cols]
    gblend = fold(t_mm(gctx, near), mask)
    gb_ref[2 * g] = gblend[:, :LANES]
    gb_ref[2 * g + 1] = gblend[:, LANES:]
    gnear = mm(gctx, spread(pair_rows(b_ref, g, slice(0, DH)), mask))
    gscore = near * (gnear - mm(near * gnear, ones)) * SCALE
    gq_ref[:, cols] = mm(gscore, spread(kl_ref[:, cols], mask))
    gkl_ref[:, cols] = fold(t_mm(gscore, q_ref[:, cols]), mask)


def near_back_kernel(
    lens_ref, gs1_ref, wo_ref, near_ref, q_ref, kl_ref, b_ref,
    gctx_ref, gq_ref, gb_ref, gkl_ref, rim_ref,
):
    count = seg_ends(lens_ref, lens_ref.shape[1])[-1]
    gctx_ref[...] = mm_t(gs1_ref[...], wo_ref[...])
    rim_ref[...] = rims_of(gctx_ref[...], count)
    def one(g, carry):
        near_back_quad(g, gctx_ref, near_ref, q_ref, kl_ref, b_ref, gq_ref, gb_ref, gkl_ref)
        return carry

    lax.fori_loop(0, QUADS, one, 0)


def near_back(lens, gs1, wo, near, q, kl, b):
    slots, width = gs1.shape
    return pl.pallas_call(
        near_back_kernel,
        in_specs=[smem()] + [whole()] * 6,
        out_specs=[whole()] * 5,
        out_shape=[
            shape(slots, width), shape(slots, width), shape(PAIRS, DH, LANES),
            shape(DH, width), shape(2 * RIM, width),
        ],
        compiler_params=params(),
        name="near_back",
    )(lens, gs1, wo, near, q, kl, b)


def far_back_quad(g, k_ref, v_ref, p_ref, m_ref, b_ref, c_ref, ql_ref, gk_ref, gv_ref, gql_ref, add):
    mask = head_mask(QUAD)
    cols = quad(g)
    top = pair_rows(b_ref, g, slice(DH, DH + 1))
    total = pair_rows(b_ref, g, slice(DH + 1, DH + 2))
    prob = p_ref[:, cols] * (jnp.exp(m_ref[:, cols] - top) / total)
    gmixed = spread(pair_rows(c_ref, g, slice(0, DH)), mask)
    dots = pair_rows(c_ref, g, slice(DH, DH + 1))
    gscore = prob * (mm(v_ref[:, cols], gmixed) - dots) * SCALE
    gk_ref[:, cols] = mm(gscore, spread(ql_ref[:, cols], mask))
    gval = mm_t(prob, gmixed)
    if add:
        gv_ref[:, cols] += gval
    else:
        gv_ref[:, cols] = gval
    gql_ref[:, cols] = fold(t_mm(gscore, k_ref[:, cols]), mask)


def land_parts(ret_ref, gql, gkl):
    n, _, segs, _ = ret_ref.shape
    for s in range(n):
        rows = slice(s * segs, (s + 1) * segs)
        ret_ref[s, 0] = gql[rows]
        ret_ref[s, 1] = gkl[rows]


def far_back_kernel(
    k_ref, v_ref, p_ref, m_ref, b_ref, c_ref, ql_ref, gkl_ref, gl_ref,
    gk_ref, gv_ref, ret_ref, gql_ref,
):
    def one(g, carry):
        far_back_quad(g, k_ref, v_ref, p_ref, m_ref, b_ref, c_ref, ql_ref, gk_ref, gv_ref, gql_ref, False)
        return carry

    lax.fori_loop(0, QUADS, one, 0)
    land_parts(ret_ref, gql_ref[...] + gl_ref[0], gkl_ref[...] + gl_ref[1])


def far_back(n, lens, k, v, p, m, b, c, ql, gkl, gl):
    slots, width = k.shape
    segs = lens.shape[1]
    return pl.pallas_call(
        far_back_kernel,
        in_specs=[whole()] * 9,
        out_specs=[whole()] * 3,
        out_shape=[shape(slots, width), shape(slots, width), shape(n, 2, segs, width)],
        scratch_shapes=[pltpu.VMEM((DH, width), f32)],
        compiler_params=params(),
        name="far_back",
    )(k, v, p, m, b, c, ql, gkl, gl)


def taps_sums(scr_ref):
    width = scr_ref.shape[2]
    rows = jnp.concatenate(
        [jnp.sum(scr_ref[c], axis=0, keepdims=True) for c in range(CONV)] + [jnp.zeros((7, width), f32)], axis=0
    )
    row = lax.broadcasted_iota(jnp.int32, (width, LANES), 0) >> 6
    col = lax.broadcasted_iota(jnp.int32, (width, LANES), 1)
    return mm(rows, jnp.where(row == col, 1.0, 0.0), TOP)


def conv_back_kernel(
    lens_ref, values_ref, gctx_ref, gleft_ref, gright_ref, taps_ref, ctx_ref, gs1_ref,
    gv_ref, gtaps_ref, dwo_ref,
    ext_ref, scr_ref,
):
    slots = gctx_ref.shape[0]
    count = seg_ends(lens_ref, lens_ref.shape[1])[-1]
    put_strips(dwo_ref, t_mm(ctx_ref[...], gs1_ref[...]))
    fill_extended(ext_ref, gctx_ref[...], gleft_ref[...], gright_ref[...], count)
    conv_into(gv_ref, ext_ref, taps_ref, slots, True, False)
    taps_grad_into(scr_ref, gctx_ref, values_ref, slots)
    gtaps_ref[...] = taps_sums(scr_ref)


def conv_back(lens, ext, gctx, gleft, gright, taps, ctx, gs1):
    slots, width = gctx.shape
    return pl.pallas_call(
        conv_back_kernel,
        in_specs=[smem()] + [whole()] * 7,
        out_specs=[whole()] * 3,
        out_shape=[shape(slots, width), shape(40, LANES), shape(width // LANES, width, LANES)],
        scratch_shapes=[pltpu.VMEM((slots + 40, width), f32), pltpu.VMEM((CONV, 8, width), f32)],
        compiler_params=params(),
        name="conv_back",
    )(lens, ext, gctx, gleft, gright, taps, ctx, gs1)


def project_back_kernel(
    lens_ref, x_ref, gs1_ref, gqn_ref, gkf_ref, gvc_ref, gvf_ref, own_ref, wq_ref, wk_ref, wv_ref,
    ig_ref, dq_ref, dk_ref, dv_ref, small_ref,
    gq_ref, gk_ref, gv_ref,
):
    @pl.when(pl.program_id(0) == 0)
    def _():
        slots = gqn_ref.shape[0]
        segs = own_ref.shape[1]
        ends = seg_ends(lens_ref, segs)
        member = member_rows(ends, slots)
        inv = inverse_lens(lens_ref, segs)
        gq = gqn_ref[...] + t_mm(member, own_ref[0] * inv)
        gk = gkf_ref[...] + t_mm(member, own_ref[1] * inv)
        gv = jnp.where(valid_rows(ends[-1], slots), gvc_ref[...] + gvf_ref[...], 0.0)
        gq_ref[...] = gq
        gk_ref[...] = gk
        gv_ref[...] = gv
        small_ref[...] = jnp.concatenate(
            [
                jnp.sum(gq, axis=0, keepdims=True),
                jnp.sum(gv, axis=0, keepdims=True),
                jnp.zeros((6, gq.shape[1]), f32),
            ],
            axis=0,
        )

    x = x_ref[...]
    put_strips(dq_ref, t_mm(x, gq_ref[...]))
    put_strips(dk_ref, t_mm(x, gk_ref[...]))
    put_strips(dv_ref, t_mm(x, gv_ref[...]))
    ig_ref[...] = (
        gs1_ref[...]
        + mm_t(gq_ref[...], wq_ref[...])
        + mm_t(gk_ref[...], wk_ref[...])
        + mm_t(gv_ref[...], wv_ref[...])
    )


def project_back(lens, x, gs1, gqn, gkf, gvc, gvf, own, wq, wk, wv):
    slots, width = x.shape
    col = 256
    strips = width // LANES
    const = lambda *dims: pl.BlockSpec(dims, lambda i: (0,) * len(dims))
    part = pl.BlockSpec((slots, col), lambda i: (0, i))
    wspec = pl.BlockSpec((col, width), lambda i: (i, 0))
    dspec = pl.BlockSpec((strips, col, LANES), lambda i: (0, i, 0))
    return pl.pallas_call(
        project_back_kernel,
        grid=(width // col,),
        in_specs=[smem(), part, part] + [const(slots, width)] * 4 + [const(*own.shape), wspec, wspec, wspec],
        out_specs=[part, dspec, dspec, dspec, const(8, width)],
        out_shape=[shape(slots, width)] + [shape(strips, width, LANES)] * 3 + [shape(8, width)],
        scratch_shapes=[pltpu.VMEM((slots, width), f32)] * 3,
        compiler_params=params(),
        name="project_back",
    )(lens, x, gs1, gqn, gkf, gvc, gvf, own, wq, wk, wv)


def sum_plain(parts):
    sizes = [part.size for part in parts]
    shapes = [part.shape for part in parts]
    devices = lax.axis_size(("seq", "dp"))
    flat = jnp.concatenate([part.reshape(-1) for part in parts])
    flat = jnp.pad(flat, (0, -flat.shape[0] % devices))
    own = lax.psum_scatter(flat, ("seq", "dp"), scatter_dimension=0, tiled=True)
    flat = lax.all_gather(own, ("seq", "dp"), axis=0, tiled=True)
    out = []
    at = 0
    for size, dims in zip(sizes, shapes):
        out.append(flat[at : at + size].reshape(dims))
        at += size
    return out


STRIP = 768
HALF = STRIP // 2
PART = HALF // 2
Z_ROWS = PART // 4
OWN = Z_ROWS // 2
STAGES = 13
SMALL_STEPS = 5


def pack_small(sb_ref, small0, small1, small2, inner_bias, taps):
    at = 0
    for ref, count in ((small0, 2), (small1, 3), (small2, 3), (inner_bias, 1)):
        for r in range(count):
            for j in range(ref.shape[1] // LANES):
                sb_ref[0, at : at + 1, :] = ref[r : r + 1, j * LANES : (j + 1) * LANES]
                at += 1
    sb_ref[0, at : at + 40, :] = taps[...]


SMALL_ROWS = 8 * 6 + 24 + 40


def unpack_small(s_ref, outs):
    at = 0
    for ref in outs[:-1]:
        for j in range(ref.shape[0] // LANES):
            ref[pl.ds(j * LANES, LANES)] = s_ref[at, :]
            at += 1
    outs[-1][...] = s_ref[at : at + 40, :].T[:HEADS, :CONV]


def reduce_stages(gw, o_ref, bufs, sems):
    acc, lc, l1, mid, lz, l3, ag = bufs
    cs, cr, s1, r1, ms, zr, r3, r4, gs, gr, r5, keep, es, er = sems
    seq = lax.axis_index("seq")
    dp = lax.axis_index("dp")
    z = seq // 2
    c = lax.rem(seq, 2)
    y = dp // 2
    x = lax.rem(dp, 2)
    zb = 3 - z
    place = lambda z_, c_, y_, x_: (z_ * 2 + c_, y_ * 2 + x_)
    by_core = place(z, 1 - c, y, x)
    by_x = place(z, c, y, 1 - x)
    by_y = place(z, c, 1 - y, x)
    right = place(lax.rem(z + 1, 4), c, y, x)
    left = place(lax.rem(z + 3, 4), c, y, x)
    opposite = place(lax.rem(z + 2, 4), c, y, x)
    near_z = place(z + 1 - 2 * lax.rem(z, 2), c, y, x)

    def remote(src, dst, send, recv, target):
        return pltpu.make_async_remote_copy(src, dst, send, recv, device_id=target, device_id_type=MESH)

    aligned = lambda at: pl.multiple_of(at, 8)
    slot = lambda ref, k: lax.rem(k, ref.shape[0])
    starts = (x * PART, HALF + y * PART)
    others = ((1 - x) * PART, HALF + (1 - y) * PART)
    own_rows = (pl.ds(aligned(y * OWN), OWN), pl.ds(aligned(x * OWN), OWN))
    other_rows = (pl.ds(aligned((1 - y) * OWN), OWN), pl.ds(aligned((1 - x) * OWN), OWN))
    first_to = (by_x, by_y)
    third_to = (by_y, by_x)
    ways = ((0, z, right), (1, zb, left))

    def bytes_of(rows, send, recv, pieces=1):
        part = lc.at[pl.ds(0, pieces), pl.ds(0, rows // pieces)]
        return remote(part, part, send, recv, by_core)

    def strip(k):
        return lax.rem(k // 3, GW_SLOTS) * PAIRS + 2 * lax.rem(k, 3)

    def core_copy(k):
        return remote(gw.at[strip(k) + 1 - c], lc.at[slot(lc, k)], cs.at[k], cr.at[k], by_core)

    def core_out(k):
        core_copy(k).start()

    def first_out(k):
        core_copy(k).wait()
        at = slot(acc, k)
        acc[at] = gw[strip(k) + c] + lc[slot(lc, k)]
        for j in range(2):
            remote(
                acc.at[at, pl.ds(aligned(others[j]), PART)], l1.at[slot(l1, k), j], s1.at[k], r1.at[k], first_to[j]
            ).start()

    def z_copy(k, way, step, block, target):
        return remote(mid.at[slot(mid, k), block], lz.at[slot(lz, k), way, step], ms.at[k], zr.at[k, way, step], target)

    def z_out(k, step):
        if step == 0:
            bytes_of(HALF, s1.at[k], r1.at[k]).wait()
            for j in range(2):
                for block in range(4):
                    here = pl.ds(aligned(starts[j] + block * Z_ROWS), Z_ROWS)
                    there = pl.ds(block * Z_ROWS, Z_ROWS)
                    mid[slot(mid, k), block, j] = acc[slot(acc, k), here] + l1[slot(l1, k), j, there]
        for way, at, target in ways:
            block = 3 - step + z if way == 0 else step - zb
            if step > 0:

                @pl.when((at > 0) & (at <= step))
                def _(way=way, block=block, target=target):
                    z_copy(k, way, step - 1, 0, target).wait_recv()
                    mid[slot(mid, k), block] += lz[slot(lz, k), way, step - 1]

            if step < 3:

                @pl.when((at <= step) & (at < 3))
                def _(way=way, block=block, target=target):
                    z_copy(k, way, step, block, target).start()

    def third_out(k):
        z_out(k, 3)
        for j in range(2):
            remote(
                mid.at[slot(mid, k), z, j, other_rows[j]], l3.at[slot(l3, k), j], ms.at[k], r3.at[k], third_to[j]
            ).start()

    def back_third_out(k):
        bytes_of(2 * OWN, ms.at[k], r3.at[k]).wait_recv()
        for j in range(2):
            ag[slot(ag, k), z, j, own_rows[j]] = mid[slot(mid, k), z, j, own_rows[j]] + l3[slot(l3, k), j]
            part = ag.at[slot(ag, k), z, j, own_rows[j]]
            remote(part, part, gs.at[k], r4.at[k], third_to[j]).start()

    def back_z(k, way, step, block, target):
        part = ag.at[slot(ag, k), block]
        return remote(part, part, gs.at[k], gr.at[k, way, step], target)

    def back_z_out(k, step):
        if step == 0:
            bytes_of(6 * Z_ROWS + 2 * OWN, ms.at[k], r3.at[k]).wait_send()
            bytes_of(2 * OWN, gs.at[k], r4.at[k]).wait_recv()
        for way, at, target in ways:
            block = z - step if way == 0 else z + step
            if step > 0:

                @pl.when(at >= step)
                def _(way=way, target=target):
                    back_z(k, way, step - 1, 0, target).wait_recv()

            if step < 3:

                @pl.when((at >= step) & (at < 3))
                def _(way=way, block=block, target=target):
                    back_z(k, way, step, block, target).start()

    blocks = (pl.ds(x * 4, 4), pl.ds(8 + y * 4, 4))

    def keep_copy(k, j):
        return pltpu.make_async_copy(ag.at[slot(ag, k), :, j], o_ref.at[c, k, blocks[j]], keep.at[k, j])

    def back_first_out(k):
        back_z_out(k, 3)
        for j in range(2):
            remote(ag.at[slot(ag, k), :, j], o_ref.at[c, k, blocks[j]], gs.at[k], r5.at[k], first_to[j]).start()
            keep_copy(k, j).start()

    def back_core(k):
        part = o_ref.at[c, k]
        return remote(part, part, es.at[k], er.at[k], by_core)

    def back_core_out(k):
        bytes_of(HALF, gs.at[k], r5.at[k]).wait_recv()
        for j in range(2):
            keep_copy(k, j).wait()

        @pl.when((z == 0) | (z == 3))
        def _():
            bytes_of(2 * OWN + 2 * Z_ROWS + HALF, gs.at[k], r5.at[k]).wait_send()

        @pl.when((z > 0) & (z < 3))
        def _():
            bytes_of(2 * OWN + 10 * Z_ROWS + HALF, gs.at[k], r5.at[k], 2).wait_send()

        back_core(k).start()

    def finish(k):
        back_core(k).wait()

    stages = [
        core_out, first_out, partial(z_out, step=0), partial(z_out, step=1), partial(z_out, step=2), third_out,
        back_third_out, partial(back_z_out, step=0), partial(back_z_out, step=1), partial(back_z_out, step=2),
        back_first_out, back_core_out, finish,
    ]
    return stages, (by_core, by_x, by_y, near_z, opposite), remote


LAG = (0, 1, 3, 5, 7, 9, 11, 13, 15, 17, 19, 21, 22)
CHUNKS = 36
GW_SLOTS = 4
RING_ACC = 6
RING_LC = 4
RING_MID = 12
RING_Z = 6
RING_AG = 16
SEQ_DEVICES = 8
SMALL_AT = 44
ENTER = 2
HELD = 30
GAP = 2
GS1, GS2, H1, ACT, GPRE, PRE, _, U1, GCTX, IG = range(10)
GV, PROB, CTX, KEYS, NEAR, QUERY, VALS = GS2, H1, ACT, GPRE, PRE, PRE + 1, U1
FFN_AT = (0, 4, 8, 13)
GS1_AT = 17
OUTPUT_AT, VALUE_AT, QUERY_AT, KEY_AT = 21, 28, 32, 33
INPUT_AT = (41, 42, 43)
TAPS_AT = 36


def pick(t, table):
    value = jnp.int32(0)
    hit = t < 0
    for when, what in table.items():
        value = jnp.where(t == when, what, value)
        hit = hit | (t == when)
    return value, hit


def greet_block():
    seq = lax.axis_index("seq")
    dp = lax.axis_index("dp")
    y = dp // 2
    x = lax.rem(dp, 2)
    barrier = pltpu.get_barrier_semaphore()
    for d in range(1, SEQ_DEVICES):
        pl.semaphore_signal(
            barrier, inc=1, device_id=(lax.rem(seq + d, SEQ_DEVICES), dp), device_id_type=MESH
        )
    for other in (y * 2 + 1 - x, (1 - y) * 2 + x):
        pl.semaphore_signal(barrier, inc=1, device_id=(seq, other), device_id_type=MESH)
    pl.semaphore_wait(barrier, SEQ_DEVICES + 1)
    return seq


def tail_kernel(
    lens_ref, gs2_hbm, h1_hbm, u1_hbm, pre_hbm, wout_hbm, win_hbm, wo_hbm, near_hbm, q_hbm, ctx_hbm, ext_hbm,
    k_hbm, v_hbm, p_hbm, x_hbm, wq_hbm, wk_hbm, wv_hbm,
    inv1_ref, g1_ref, m_ref, b_ref, ql_ref, kl_ref, core_ref, zs_ref, ps_ref, rs_ref, qs_ref, mx_ref, taps_ref, small2_ref,
    o_ref, so_ref, ig_hbm,
    acc, lc, l1, mid, lz, l3, ag, sb, sl, gw,
    stack, w, ext, gext, tap_scr, gtaps, small0, small1, dbi,
    gb, rim, gkl, gql, gl, land, cmsg, gleft, gright, ng, ncore, nlead, ret, rland, own,
    loads, ig_sem, b1s, b1r, b2s, b2r, ms, mr, rets, retr, ss, sr,
    *sems,
):
    n = SEQ_DEVICES
    _, slots, width = stack.shape
    segs = own.shape[1]
    gs1, gv, p, ctx, k, near, q, v, gctx, ig = [
        stack.at[i] for i in (GS1, GV, PROB, CTX, KEYS, NEAR, QUERY, VALS, GCTX, IG)
    ]
    moves = []

    def load(src, dst):
        moves.append(pltpu.make_async_copy(src, dst, loads.at[len(moves)]))
        return moves[-1]

    load_gs2 = load(gs2_hbm, stack.at[GS2])
    load_w = []
    load_pre = []
    for j in range(4):
        part = pl.ds(j * width, width)
        load_w.append(load(wout_hbm.at[part, :], w.at[2 * j % 4]))
        load_w.append(load(win_hbm.at[:, part], w.at[(2 * j + 1) % 4]))
        load_pre.append(load(pre_hbm.at[:, part], stack.at[PRE + j % 2]))
    for i, hbm in enumerate((wo_hbm, wv_hbm, wq_hbm, wk_hbm)):
        load_w.append(load(hbm, w.at[i]))
    load_h1, load_u1, load_ext = load(h1_hbm, stack.at[H1]), load(u1_hbm, stack.at[U1]), load(ext_hbm, ext)
    load_near, load_q, load_ctx = load(near_hbm, near), load(q_hbm, q), load(ctx_hbm, ctx)
    load_p, load_k, load_v, load_x = load(p_hbm, p), load(k_hbm, k), load(v_hbm, v), load(x_hbm, q)
    a0, a1, a2, a3 = FFN_AT
    starting = [
        (a0 + 1, load_w[4]), (a0 + 1, load_pre[2]), (a0 + 4, load_w[5]), (a1 + 1, load_w[6]), (a1 + 1, load_pre[3]),
        (a1 + 4, load_w[7]), (a2 + 1, load_w[8]), (a2 + 1, load_near), (a2 + 4, load_w[9]), (a3 + 1, load_w[10]),
        (a3 + 1, load_q), (a3 + 2, load_ctx), (a3 + 3, load_p), (a3 + 4, load_w[11]), (a3 + 4, load_k), (a3 + 4, load_v),
        (GS1_AT + 4, load_x),
    ]
    waiting = [
        (a0, load_gs2), (a0 + 2, load_h1), (a3 + 3, load_u1), (GS1_AT, load_w[8]), (GS1_AT + 1, load_near),
        (GS1_AT + 1, load_q), (OUTPUT_AT, load_ctx), (VALUE_AT, load_x),
    ]
    for j in range(4):
        waiting += [(FFN_AT[j], load_w[2 * j]), (FFN_AT[j], load_pre[j]), (FFN_AT[j] + 3, load_w[2 * j + 1])]
    for i in range(3):
        waiting.append((INPUT_AT[i], load_w[9 + i]))
    for copy in (load_gs2, load_w[0], load_pre[0], load_h1, load_w[1], load_pre[1], load_w[2], load_w[3], load_u1, load_ext):
        copy.start()
    me = greet_block()
    owner, pair_here = pair_at(me, n)
    stages, partners, remote = reduce_stages(gw, o_ref, (acc, lc, l1, mid, lz, l3, ag), sems)
    ends = seg_ends(lens_ref, segs)
    count = ends[-1]

    def weight_event(e, left, right):
        put_strips(gw, t_mm(stack[left], stack[right]), slice(None), lax.rem(e, GW_SLOTS) * PAIRS)

    def through_event(source, target, weight):
        stack[target] += mm_t(stack[source], w[weight])

    def inner_event(j):
        @pl.when(j == 0)
        def _():
            stack[GS1] = stack[GS2]

        at = PRE + lax.rem(j, 2)
        weight = lax.rem(2 * j, 4)

        def one(g, carry):
            cols = quad(g)
            pre = stack[at, :, cols]
            phi_big = 0.5 * (1.0 + lax.erf(pre * ROOT_HALF))
            slope = phi_big + pre * (INV_ROOT_TAU * jnp.exp(-0.5 * pre * pre))
            gpre = mm_t(stack[GS2], w[weight, cols, :]) * slope
            stack[GPRE, :, cols] = gpre
            stack[ACT, :, cols] = pre * phi_big
            dbi[:, pl.ds(pl.multiple_of(j * width + g * QUAD, QUAD), QUAD)] = jnp.sum(gpre, axis=0, keepdims=True)
            return carry

        lax.fori_loop(0, QUADS, one, 0)

    def ev_norm():
        e = gs1[...]
        unit = stack[U1]
        grad = norm_back(unit, inv1_ref[...], g1_ref[...][None, :], e)
        gs1[...] = grad
        ig[...] = grad
        gctx[...] = jnp.zeros_like(grad)
        small1[0:1, :] = jnp.sum(e * unit, axis=0, keepdims=True)
        small1[1:2, :] = jnp.sum(e, axis=0, keepdims=True)
        small1[2:3, :] = jnp.sum(grad, axis=0, keepdims=True)

    def ev_rims():
        rim[...] = rims_of(gctx[...], count)

    def ev_near(g):
        near_back_quad(g, gctx, near, q, kl_ref, b_ref, near, gb, gkl)

    def blend_copy(pair):
        return to_seq(gb.at[pair], land.at[me], b1s.at[pair], b1r.at[me], owner_of(pair, n))

    up, down = rim_copies(n, me, rim, gleft, gright, ms, mr)

    def ev_blend():
        for pair in range(PAIRS):

            @pl.when(me != owner_of(pair, n))
            def _(pair=pair):
                blend_copy(pair).start()

        rim_start(n, me, up, down, gleft, gright)

    def mixed_copy(target):
        return to_seq(cmsg.at[pair_here], cmsg.at[pair_here], b2s.at[target], b2r.at[pair_here], target)

    def ev_owner():
        @pl.when(owner)
        def _():
            land[me] = gb[pair_here]
            for s in range(n):

                @pl.when(me != s)
                def _(s=s):
                    to_seq(gb.at[0], land.at[s], b1s.at[0], b1r.at[s], s).wait_recv()

            gblend = land[0]
            for s in range(1, n):
                gblend = gblend + land[s]
            mixed = mx_ref[...]
            gmixed = mm(gblend, zs_ref[NEWTON], TOP)
            cmsg[pair_here, 0:DH, :] = gmixed
            dots = jnp.sum(gmixed * mixed, axis=0, keepdims=True)
            cmsg[pair_here, DH:MSG, :] = jnp.concatenate([dots, jnp.zeros((MSG - DH - 1, LANES), f32)], axis=0)
            for t in range(n):

                @pl.when(me != t)
                def _(t=t):
                    mixed_copy(t).start()

            ng[...] = inverse_grad(gblend, mixed)
            ncore[...] = jnp.zeros_like(ncore)
            nlead[...] = newton_lead(zs_ref[NEWTON - 1], ps_ref[NEWTON - 1])

        gl[...] = jnp.zeros_like(gl)

    def ev_newton(step):
        @pl.when(owner)
        def _():
            lead = newton_lead(zs_ref[jnp.maximum(step - 1, 0)], ps_ref[jnp.maximum(step - 1, 0)])
            ng[...], ncore[...] = newton_short(
                ng[...], ncore[...], nlead[...], core_ref[...], zs_ref[step], ps_ref[step], rs_ref[step], qs_ref[step]
            )
            nlead[...] = lead

    def ev_core():
        @pl.when(owner)
        def _():
            core_back(ng[...], ncore[...], core_ref[...], zs_ref[0], ql_ref, kl_ref, gl, pair_here)

    quarter = slots // 4

    def ev_taps(part):
        @pl.when(part == 0)
        def _():
            load_ext.wait()
            tap_scr[...] = jnp.zeros_like(tap_scr)

        taps_grad_into(tap_scr, gctx, ext, quarter * (part + 1), quarter * part, False)

        @pl.when(part == 3)
        def _():
            gtaps[...] = taps_sums(tap_scr)

    def ev_conv(part):
        @pl.when(part == 0)
        def _():
            rim_wait(n, me, up, down)
            fill_extended(gext, gctx[...], gleft[...], gright[...], count)

        conv_into(gv, gext, taps_ref, quarter * (part + 1), True, False, quarter * part)

    def ev_mixed():
        for pair in range(PAIRS):

            @pl.when(me != owner_of(pair, n))
            def _(pair=pair):
                to_seq(cmsg.at[pair], cmsg.at[pair], b2s.at[pair], b2r.at[pair], owner_of(pair, n)).wait_recv()

        for copy in (load_k, load_v, load_p):
            copy.wait()

    def ev_far(g):
        far_back_quad(g, k, v, p, m_ref, b_ref, cmsg, ql_ref, p, gv, gql, True)

    def ev_return():
        land_parts(ret, gql[...] + gl[0], gkl[...] + gl[1])
        for d in range(1, n):
            target = lax.rem(me + d, n)
            to_seq(ret.at[target], rland.at[me], rets.at[d], retr.at[me], target).start()

    def ev_own():
        rland[me] = ret[me]
        for d in range(1, n):
            source = lax.rem(me + d, n)
            to_seq(ret.at[0], rland.at[source], rets.at[d], retr.at[source], source).wait_recv()
        total = rland[0]
        for s in range(1, n):
            total = total + rland[s]
        own[...] = total
        inv = inverse_lens(lens_ref, segs)
        member = member_rows(ends, slots)
        near[...] += t_mm(member, own[0] * inv)
        p[...] += t_mm(member, own[1] * inv)
        small0[0:1, :] = jnp.sum(near[...], axis=0, keepdims=True)

    def ev_values():
        masked = jnp.where(valid_rows(count, slots), gv[...], 0.0)
        gv[...] = masked
        small0[1:2, :] = jnp.sum(masked, axis=0, keepdims=True)

    def small(i):
        return remote(sb.at[i], sl.at[i], ss.at[i], sr.at[i], partners[i])

    def ev_small(i):
        if i == 0:
            pack_small(sb, small0, small1, small2_ref, dbi, gtaps)
        else:
            small(i - 1).wait_recv()
            sb[i] = sb[i - 1] + sl[i - 1]
        if i < SMALL_STEPS:
            small(i).start()

    def at_tick(t, when, event):
        @pl.when(t == when)
        def _():
            event()

    def at_ticks(t, start, every, count, event):
        after = t - start

        @pl.when((after >= 0) & (after < every * count) & (lax.rem(after + every, every) == 0))
        def _():
            event(after // every)

    weights = {}
    through = {}
    for j, when in enumerate(FFN_AT):
        weights[when + 1] = (2 * j, ACT, GS2)
        weights[when + 2] = (2 * j + 1, H1, GPRE)
        through[when + 3] = (GPRE, GS1, (2 * j + 1) % 4)
    weights[OUTPUT_AT] = (8, CTX, GS1)
    for i, (when, part) in enumerate(((VALUE_AT, GV), (QUERY_AT, NEAR), (KEY_AT, PROB))):
        weights[when] = (9 + i, QUERY, part)
        through[INPUT_AT[i]] = (part, IG, 1 + i)
    through[GS1_AT] = (GS1, GCTX, 0)

    def by_table(t, table, event):
        columns = [pick(t, {when: row[i] for when, row in table.items()}) for i in range(3)]

        @pl.when(columns[0][1])
        def _():
            event(*[value for value, _ in columns])

    def by_group(t, table, size=6):
        for low in range(0, max(when for when, _ in table) + 1, size):
            mine = [row for row in table if low <= row[0] < low + size]
            if mine:

                @pl.when((t >= low) & (t < low + size))
                def _(mine=mine):
                    for when, event in mine:
                        at_tick(t, when, event)

    copies = [(when, copy.start) for when, copy in starting] + [(when, copy.wait) for when, copy in waiting]
    others = [(FFN_AT[3] + 3, ev_norm), (GS1_AT, ev_rims)]
    last = [
        (GS1_AT + 12, ev_core), (GS1_AT + 12, ev_return), (GS1_AT + 14, ev_own),
        (INPUT_AT[2], lambda: pltpu.make_async_copy(ig, ig_hbm, ig_sem.at[0]).start()),
    ] + [(SMALL_AT + 2 * i, partial(ev_small, i)) for i in range(SMALL_STEPS + 1)]

    def tick(t, carry):
        for stage, run in reversed(list(enumerate(stages))):
            since = t - ENTER - LAG[stage]
            at = jnp.where(since < HELD, since, since - GAP)

            @pl.when((since >= 0) & ((since < HELD) | (since >= HELD + GAP)) & (at < CHUNKS))
            def _(run=run, at=at):
                run(at)

        by_group(t, copies)
        block, hit = pick(t, {when: j for j, when in enumerate(FFN_AT)})

        @pl.when(hit)
        def _():
            inner_event(block)

        by_table(t, through, through_event)
        by_table(t, weights, weight_event)
        by_group(t, others)

        @pl.when((t > GS1_AT) & (t < GS1_AT + 12))
        def _():
            at_ticks(t, GS1_AT + 1, 1, QUADS, ev_near)
            at_tick(t, GS1_AT + 3, ev_blend)
            at_tick(t, GS1_AT + 5, ev_owner)
            at_ticks(t, GS1_AT + 6, 1, NEWTON, lambda i: ev_newton(NEWTON - 1 - i))
            at_ticks(t, GS1_AT + 5, 1, 4, ev_conv)
            at_tick(t, GS1_AT + 8, ev_mixed)
            at_ticks(t, GS1_AT + 8, 1, QUADS, ev_far)
            at_tick(t, GS1_AT + 10, ev_values)

        @pl.when(t >= GS1_AT + 12)
        def _():
            at_ticks(t, TAPS_AT, 1, 4, ev_taps)
            by_group(t, last)

        return carry

    lax.fori_loop(0, CHUNKS + ENTER + GAP + LAG[-1], tick, 0)
    for i in range(SMALL_STEPS):
        small(i).wait_send()
    so_ref[...] = sb[SMALL_STEPS]
    pltpu.make_async_copy(ig, ig_hbm, ig_sem.at[0]).wait()
    for pair in range(PAIRS):

        @pl.when(me != owner_of(pair, n))
        def _(pair=pair):
            blend_copy(pair).wait_send()

    @pl.when(owner)
    def _():
        for t in range(n):

            @pl.when(me != t)
            def _(t=t):
                mixed_copy(t).wait_send()

    for d in range(1, n):
        target = lax.rem(me + d, n)
        to_seq(ret.at[target], rland.at[me], rets.at[d], retr.at[me], target).wait_send()


def tail(lens, big, little):
    slots, width = big[0].shape
    segs = lens.shape[1]
    at = CHUNKS
    n = SEQ_DEVICES
    dma = pltpu.SemaphoreType.DMA
    vm = lambda *dims: pltpu.VMEM(dims, f32)
    anywhere = pl.BlockSpec(memory_space=pl.ANY)
    one = dma((at,))
    zsem = dma((at, 2, 3))
    return pl.pallas_call(
        tail_kernel,
        in_specs=[smem()] + [anywhere] * len(big) + [whole()] * len(little),
        out_specs=[anywhere, whole(), anywhere],
        out_shape=[shape(2, at, STRIP // Z_ROWS, Z_ROWS, LANES), shape(SMALL_ROWS, LANES), shape(slots, width)],
        scratch_shapes=[
            vm(RING_ACC, STRIP, LANES), vm(RING_LC, STRIP, LANES), vm(RING_LC, 2, PART, LANES),
            vm(RING_MID, 4, 2, Z_ROWS, LANES), vm(RING_Z, 2, 3, 2, Z_ROWS, LANES), vm(RING_LC, 2, OWN, LANES),
            vm(RING_AG, 4, 2, Z_ROWS, LANES),
            vm(SMALL_STEPS + 1, SMALL_ROWS, LANES), vm(SMALL_STEPS, SMALL_ROWS, LANES), vm(GW_SLOTS * PAIRS, STRIP, LANES),
            vm(10, slots, width), vm(4, width, width), vm(slots + 40, width), vm(slots + 40, width),
            vm(CONV, 8, width), vm(40, LANES), vm(8, width), vm(8, width), vm(1, 4 * width),
            vm(PAIRS, DH, LANES), vm(2 * RIM, width), vm(DH, width), vm(DH, width), vm(2, DH, width),
            vm(n, DH, LANES), vm(PAIRS, MSG, LANES), vm(RIM, width), vm(RIM, width), vm(LANES, LANES), vm(LANES, LANES),
            vm(3 * LANES, LANES), vm(n, 2, segs, width), vm(n, 2, segs, width), vm(2, segs, width),
            dma((27,)), dma((1,)), dma((PAIRS,)), dma((n,)), dma((n,)), dma((n,)), dma((2,)), dma((2,)),
            dma((n,)), dma((n,)), dma((SMALL_STEPS,)), dma((SMALL_STEPS,)),
            one, one, one, one, one, zsem, one, one, one, zsem, one, dma((at, 2)), one, one,
        ],
        compiler_params=params(collective_id=5, has_side_effects=True),
        name="tail",
    )(lens, *big, *little)


def unstrip(strips):
    count, rows, _ = strips.shape
    return strips.transpose(1, 0, 2).reshape(rows, count * LANES)


def unstrip_tall(strips, across):
    count, rows, _ = strips.shape
    down = count // across
    return strips.reshape(down, across, rows, LANES).transpose(0, 2, 1, 3).reshape(down * rows, across * LANES)


PLACE_SLOTS = 24


def place_strips_kernel(s_ref, small_ref, *refs):
    outs = refs[:6]
    smalls = refs[6:-3]
    buf, in_sem, out_sem = refs[-3:]
    moves = []
    for e in range(CHUNKS // 3):
        if e < 8:
            out, row, col = outs[e % 2], (e // 2) * (1 - e % 2), (e // 2) * (e % 2)
        else:
            out, row, col = outs[e - 6], 0, 0
        for k in range(3):
            for c in range(2):
                rows = pl.ds(row * STRIP, STRIP)
                cols = pl.ds(col * STRIP + (2 * k + c) * LANES, LANES)
                slot = len(moves) % PLACE_SLOTS
                moves.append((
                    pltpu.make_async_copy(s_ref.at[c, 3 * e + k], buf.at[slot], in_sem.at[slot]),
                    pltpu.make_async_copy(buf.at[slot], out.at[rows, cols], out_sem.at[slot]),
                ))
    ahead = PLACE_SLOTS // 2
    for i in range(len(moves) + ahead):
        if i < len(moves):
            if i >= PLACE_SLOTS:
                moves[i - PLACE_SLOTS][1].wait()
            moves[i][0].start()
        if i >= ahead:
            moves[i - ahead][0].wait()
            moves[i - ahead][1].start()
    unpack_small(small_ref, smalls)
    for _, out in moves[-PLACE_SLOTS:]:
        out.wait()


def place_strips(summed, packed, shapes):
    anywhere = pl.BlockSpec(memory_space=pl.ANY)
    dma = pltpu.SemaphoreType.DMA
    width = shapes[0][1]
    return pl.pallas_call(
        place_strips_kernel,
        in_specs=[anywhere, whole()],
        out_specs=[anywhere] * len(shapes) + [whole()] * 10,
        out_shape=[shape(*dims) for dims in shapes] + [shape(width)] * 8 + [shape(shapes[0][0]), shape(HEADS, CONV)],
        scratch_shapes=[pltpu.VMEM((PLACE_SLOTS, STRIP, LANES), f32), dma((PLACE_SLOTS,)), dma((PLACE_SLOTS,))],
        compiler_params=params(),
        name="place_strips",
    )(summed, packed)


def per_device(
    tokens, segment_lens, query_weight, query_bias, key_weight, value_weight, value_bias, conv_taps,
    output_weight, output_bias, first_gain, first_bias, inner_weight, inner_bias, outer_weight, outer_bias,
    second_gain, second_bias, cotangent,
):
    n = lax.axis_size("seq")
    _, slots, width = tokens.shape
    x = tokens.reshape(slots, width)
    cot = cotangent.reshape(slots, width)
    lens = segment_lens

    q, k, v, raised, near, ctx, ext, h1, u1, tops, b, ql, kl, *saved, taps, inv1 = front(
        n, lens, x, conv_taps.T, query_bias, value_bias, output_bias, first_gain, first_bias,
        query_weight, key_weight, value_weight, output_weight,
    )
    pre, layer_out, gs2, small2 = ffn_forward(
        lens, h1, inner_weight, inner_bias.reshape(1, -1), outer_weight, outer_bias, cot, second_gain, second_bias
    )
    weights = [outer_weight, inner_weight, output_weight, value_weight, query_weight, key_weight]
    if n == SEQ_DEVICES and lax.axis_size("dp") == 4:
        big = [
            gs2, h1, u1, pre, outer_weight, inner_weight, output_weight, near, q, ctx, ext, k, v, raised, x,
            query_weight, key_weight, value_weight,
        ]
        little = [inv1, first_gain, tops, b, ql, kl, *saved, taps, small2]
        summed, packed, input_grad = tail(lens, big, little)
        sums = place_strips(summed.reshape(2, CHUNKS, STRIP, LANES), packed, [w.shape for w in weights])
    else:
        d_outer, d_inner, gs1, d_inner_bias, small1 = ffn_backward(
            h1, gs2, pre, inner_weight, outer_weight, u1, inv1, first_gain
        )
        gctx, gqn, gblend, gkl, grim = near_back(lens, gs1, output_weight, near, q, kl, b)
        c, gleft, gright, gl = blend_exchange(n, gblend, grim, ql, kl, saved)
        gkf, gvf, back = far_back(n, lens, k, v, raised, tops, b, c, ql, gkl, gl)
        own = land_return(n, back)
        gvc, gtaps, d_output = conv_back(lens, ext, gctx, gleft, gright, taps, ctx, gs1)
        input_grad, d_query, d_key, d_value, small0 = project_back(
            lens, x, gs1, gqn, gkf, gvc, gvf, own, query_weight, key_weight, value_weight
        )
        grads = [d_outer, d_inner, d_output, d_value, d_query, d_key]
        sums = sum_plain(grads + [small0, small1, small2, d_inner_bias, gtaps])
        small = sums[6:]
        sums = (
            [unstrip_tall(sums[0], width // LANES)] + [unstrip(s) for s in sums[1:6]]
            + [small[0][0], small[0][1], *small[1][:3], *small[2][:3], small[3][0], small[4][:CONV, :HEADS].T]
        )
    d_outer, d_inner, d_output, d_value, d_query, d_key, *vectors = sums
    d_query_bias, d_value_bias, d_first_gain, d_first_bias, d_output_bias = vectors[:5]
    d_second_gain, d_second_bias, d_outer_bias, d_inner_bias, d_taps = vectors[5:]
    return (
        layer_out.reshape(tokens.shape), input_grad.reshape(tokens.shape),
        d_query, d_query_bias, d_key, d_value, d_value_bias, d_taps.T,
        d_output, d_output_bias, d_first_gain, d_first_bias,
        d_inner, d_inner_bias, d_outer, d_outer_bias, d_second_gain, d_second_bias,
    )


def solution(mesh):
    block = P("dp", "seq", None)
    return jax.shard_map(
        per_device,
        mesh=mesh,
        in_specs=(block, P("dp", "seq")) + (P(),) * 16 + (block,),
        out_specs=(block, block) + (P(),) * 16,
        check_vma=False,
    )
```

```python
from functools import partial
import math

import jax
import jax.numpy as jnp
from jax import lax
from jax.experimental import pallas as pl
from jax.experimental.pallas import tpu as pltpu
from jax.sharding import PartitionSpec as P

HEADS = 12
DH = 64
CONV = 33
NEWTON = 6
RIM = (CONV - 1) // 2
LANES = 128
PAIRS = HEADS * DH // LANES
QUAD = 256
QUADS = HEADS * DH // QUAD
SCALE = DH ** (-0.5)
EPS = 1e-05
ROOT_HALF = 0.7071067811865476
INV_ROOT_TAU = 0.3989422804014327
MASKED = -1e30
f32 = jnp.float32
HI = lax.Precision.HIGH
TOP = lax.Precision.HIGHEST
MESH = pl.DeviceIdType.MESH
VMEM_CAP = 60 << 20


def _dg(a, b, ca, cb, prec):
    return lax.dot_general(
        a, b, (((ca,), (cb,)), ((), ())), precision=prec, preferred_element_type=f32
    )


def mm(a, b, prec=HI):
    return _dg(a, b, 1, 0, prec)


def mm_t(a, b, prec=HI):
    return _dg(a, b, 1, 1, prec)


def t_mm(a, b, prec=HI):
    return _dg(a, b, 0, 0, prec)


def head_mask(size):
    row = lax.broadcasted_iota(jnp.int32, (size, size), 0) >> 6
    col = lax.broadcasted_iota(jnp.int32, (size, size), 1) >> 6
    return row == col


def spread(rows, mask):
    return jnp.where(mask, jnp.concatenate([rows] * (mask.shape[0] // DH), axis=0), 0.0)


def fold(square, mask):
    kept = jnp.where(mask, square, 0.0)
    total = kept[:DH]
    for at in range(DH, mask.shape[0], DH):
        total = total + kept[at : at + DH]
    return total


def seg_ends(lens_ref, count):
    ends = []
    total = 0
    for j in range(count):
        total = total + lens_ref[0, j]
        ends.append(total)
    return ends


def member_rows(ends, slots):
    shape = (len(ends), slots)
    row = lax.broadcasted_iota(jnp.int32, shape, 0)
    col = lax.broadcasted_iota(jnp.int32, shape, 1)
    low = jnp.zeros(shape, jnp.int32)
    high = jnp.zeros(shape, jnp.int32)
    before = 0
    for j, end in enumerate(ends):
        low = jnp.where(row == j, before, low)
        high = jnp.where(row == j, end, high)
        before = end
    return jnp.where((col >= low) & (col < high), 1.0, 0.0)


def inverse_lens(lens_ref, count):
    row = lax.broadcasted_iota(jnp.int32, (count, 1), 0)
    out = jnp.zeros((count, 1), f32)
    for j in range(count):
        out = jnp.where(row == j, lens_ref[0, j].astype(f32), out)
    return 1.0 / out


def valid_rows(count, slots):
    return lax.broadcasted_iota(jnp.int32, (slots, 1), 0) < count


def rims_of(matrix, count):
    slots = matrix.shape[0]
    row = lax.broadcasted_iota(jnp.int32, (2 * RIM, slots), 0)
    col = lax.broadcasted_iota(jnp.int32, (2 * RIM, slots), 1)
    want = jnp.where(row < RIM, row, row - 2 * RIM + count)
    return mm(jnp.where(col == want, 1.0, 0.0), matrix)


def fill_extended(ext_ref, middle, left, right, count):
    slots = middle.shape[0]
    ext_ref[0:RIM, :] = left
    ext_ref[RIM : RIM + slots, :] = middle
    tail = ext_ref.shape[0] - RIM - slots
    ext_ref[RIM + slots :, :] = jnp.zeros((tail, middle.shape[1]), f32)
    rows = slots + RIM
    row = lax.broadcasted_iota(jnp.int32, (rows, RIM), 0)
    col = lax.broadcasted_iota(jnp.int32, (rows, RIM), 1)
    put = jnp.where(row == col + count, 1.0, 0.0)
    ext_ref[RIM : RIM + rows, :] += mm(put, right)


CONV_ROWS = 64


def shifted(ext_ref, r0, l0):
    slab = ext_ref[pl.ds(r0, CONV_ROWS + 40), pl.ds(l0, LANES)]
    for b in range(8):
        moved = slab[b : b + CONV_ROWS + 32]
        for a in range(5):
            if 8 * a + b < CONV:
                yield 8 * a + b, moved[8 * a : 8 * a + CONV_ROWS]


def conv_into(out_ref, ext_ref, taps_ref, slots, flip, add, low=0):
    def block(i, carry):
        r0 = pl.multiple_of((i // PAIRS) * CONV_ROWS, CONV_ROWS)
        l0 = pl.multiple_of((i % PAIRS) * LANES, LANES)
        acc = jnp.zeros((CONV_ROWS, LANES), f32)
        for c, part in shifted(ext_ref, r0, l0):
            at = CONV - 1 - c if flip else c
            acc = acc + taps_ref[at : at + 1, pl.ds(l0, LANES)] * part
        here = (pl.ds(r0, CONV_ROWS), pl.ds(l0, LANES))
        if add:
            out_ref[here] += acc
        else:
            out_ref[here] = acc
        return carry

    lax.fori_loop((low // CONV_ROWS) * PAIRS, (slots // CONV_ROWS) * PAIRS, block, 0)


def taps_grad_into(scr_ref, grad_ref, ext_ref, slots, low=0, clear=True):
    if clear:
        scr_ref[...] = jnp.zeros_like(scr_ref)

    def block(i, carry):
        r0 = pl.multiple_of((i // PAIRS) * CONV_ROWS, CONV_ROWS)
        l0 = pl.multiple_of((i % PAIRS) * LANES, LANES)
        grad = grad_ref[pl.ds(r0, CONV_ROWS), pl.ds(l0, LANES)]
        for c, part in shifted(ext_ref, r0, l0):
            prod = grad * part
            total = prod[0:8]
            for at in range(8, CONV_ROWS, 8):
                total = total + prod[at : at + 8]
            scr_ref[c, :, pl.ds(l0, LANES)] += total
        return carry

    lax.fori_loop((low // CONV_ROWS) * PAIRS, (slots // CONV_ROWS) * PAIRS, block, 0)


def whole(shape=None):
    return pl.BlockSpec(memory_space=pltpu.VMEM)


def smem():
    return pl.BlockSpec(memory_space=pltpu.SMEM)


def params(**more):
    return pltpu.CompilerParams(vmem_limit_bytes=VMEM_CAP, **more)


def shape(*dims):
    return jax.ShapeDtypeStruct(dims, f32)


def greet_signal(n):
    me = lax.axis_index("seq")
    for d in range(1, n):
        pl.semaphore_signal(
            pltpu.get_barrier_semaphore(), inc=1, device_id={"seq": lax.rem(me + d, n)}, device_id_type=MESH
        )
    return me


def greet_all(n):
    me = greet_signal(n)
    pl.semaphore_wait(pltpu.get_barrier_semaphore(), n - 1)
    return me


def to_seq(src, dst, send, recv, target):
    return pltpu.make_async_remote_copy(
        src, dst, send, recv, device_id={"seq": target}, device_id_type=MESH
    )


def rim_copies(n, me, rim_ref, left_ref, right_ref, rsend, rrecv):
    up = to_seq(rim_ref.at[pl.ds(RIM, RIM)], left_ref, rsend.at[0], rrecv.at[0], lax.rem(me + 1, n))
    down = to_seq(rim_ref.at[pl.ds(0, RIM)], right_ref, rsend.at[1], rrecv.at[1], lax.rem(me + n - 1, n))
    return up, down


def rim_start(n, me, up, down, left_ref, right_ref):
    @pl.when(me < n - 1)
    def _():
        up.start()

    @pl.when(me > 0)
    def _():
        down.start()

    @pl.when(me == 0)
    def _():
        left_ref[...] = jnp.zeros_like(left_ref)

    @pl.when(me == n - 1)
    def _():
        right_ref[...] = jnp.zeros_like(right_ref)


def rim_wait(n, me, up, down):
    @pl.when(me > 0)
    def _():
        up.wait_recv()
        down.wait_send()

    @pl.when(me < n - 1)
    def _():
        down.wait_recv()
        up.wait_send()


MSG = DH + 8


def owner_of(pair, n):
    return pair if pair < PAIRS // 2 else pair + n // 2 - PAIRS // 2


def pair_at(me, n):
    half = PAIRS // 2
    low = me < half
    owns = low | ((me >= n // 2) & (me < n // 2 + half))
    return owns, jnp.where(low, me, jnp.where(owns, me - n // 2 + half, 0))


def eye(size):
    row = lax.broadcasted_iota(jnp.int32, (size, size), 0)
    col = lax.broadcasted_iota(jnp.int32, (size, size), 1)
    return jnp.where(row == col, 1.0, 0.0)


def pair_sums(row):
    lane = lax.broadcasted_iota(jnp.int32, row.shape, 1)
    first = jnp.sum(jnp.where(lane < DH, row, 0.0), axis=1, keepdims=True)
    second = jnp.sum(jnp.where(lane < DH, 0.0, row), axis=1, keepdims=True)
    return jnp.where(lane < DH, first, second)


def core_of(query, key, mask):
    scores = jnp.where(mask, mm_t(query, key, TOP) * SCALE, MASKED)
    raised = jnp.exp(scores - jnp.max(scores, axis=1, keepdims=True))
    return raised / jnp.sum(raised, axis=1, keepdims=True)


def inverse_grad(gblend, mixed):
    return jnp.where(head_mask(LANES), t_mm(gblend, mixed, TOP), 0.0)


def newton_back(g, gcore, core, z, prod, r, q):
    prod_t = prod.T
    gq = 0.25 * mm(z.T, g, TOP)
    gr = -mm(prod_t, gq, TOP)
    gs = -mm(prod_t, gr, TOP)
    gp = -mm_t(gq, r, TOP) - mm_t(gr, 7.0 * eye(LANES) - prod, TOP) - gs
    return 0.25 * mm_t(g, q, TOP) + mm(core.T, gp, TOP), gcore + mm_t(gp, z, TOP)


def newton_lead(z, prod):
    zp = mm(z, prod, TOP)
    zpp = mm(zp, prod, TOP)
    return jnp.concatenate([0.25 * z.T, -0.25 * zp.T, 0.25 * zpp.T], axis=0)


def newton_short(g, gcore, lead, core, z, prod, r, q):
    gqrs = mm(lead, g, TOP)
    gq, gr, gs = [gqrs[at : at + LANES] for at in range(0, 3 * LANES, LANES)]
    left = jnp.concatenate([gq, gr], axis=1)
    right = jnp.concatenate([r, 7.0 * eye(LANES) - prod], axis=1)
    gp = -mm_t(left, right, TOP) - gs
    through = mm(jnp.concatenate([g, core.T], axis=1), jnp.concatenate([0.25 * q.T, gp], axis=0), TOP)
    return through, gcore + mm_t(gp, z, TOP)


def core_back(g, gcore, core, first, ql_ref, kl_ref, gl_ref, pair):
    mask = head_mask(LANES)
    colsum = jnp.sum(core, axis=0, keepdims=True)
    square = pair_sums(colsum * colsum)
    sigma = jnp.sqrt(square)
    dot = pair_sums(jnp.sum(g * first, axis=0, keepdims=True))
    gcore = gcore + g.T / sigma - jnp.where(mask, dot / square * colsum, 0.0)
    gscore = core * (gcore - jnp.sum(core * gcore, axis=1, keepdims=True)) * SCALE
    lanes = pl.ds(pl.multiple_of(pair * LANES, LANES), LANES)
    query = spread(ql_ref[:, lanes], mask)
    key = spread(kl_ref[:, lanes], mask)
    gl_ref[...] = jnp.zeros_like(gl_ref)
    gl_ref[0, :, lanes] = fold(mm(gscore, key, TOP), mask)
    gl_ref[1, :, lanes] = fold(t_mm(gscore, query, TOP), mask)


def blend_exchange_kernel(
    n, g_ref, rim_ref, ql_ref, kl_ref, core_ref, zs_ref, ps_ref, rs_ref, qs_ref, mx_ref,
    c_ref, left_ref, right_ref, gl_ref,
    land, s1, r1, s2, r2, rsend, rrecv,
):
    me = greet_all(n)
    owns, pair_here = pair_at(me, n)
    for p in range(PAIRS):

        @pl.when(me != owner_of(p, n))
        def _(p=p):
            to_seq(g_ref.at[p], land.at[me], s1.at[p], r1.at[me], owner_of(p, n)).start()

    up, down = rim_copies(n, me, rim_ref, left_ref, right_ref, rsend, rrecv)
    rim_start(n, me, up, down, left_ref, right_ref)

    @pl.when(jnp.logical_not(owns))
    def _():
        gl_ref[...] = jnp.zeros_like(gl_ref)

    @pl.when(owns)
    def _():
        mask = head_mask(LANES)
        land[me] = g_ref[pair_here]
        for s in range(n):

            @pl.when(me != s)
            def _(s=s):
                to_seq(g_ref.at[0], land.at[s], s1.at[0], r1.at[s], s).wait_recv()

        gblend = land[0]
        for s in range(1, n):
            gblend = gblend + land[s]
        mixed = mx_ref[...]
        gmixed = mm(gblend, zs_ref[NEWTON], TOP)
        c_ref[pair_here, 0:DH, :] = gmixed
        dots = jnp.sum(gmixed * mixed, axis=0, keepdims=True)
        pad = jnp.zeros((MSG - DH - 1, LANES), f32)
        c_ref[pair_here, DH:MSG, :] = jnp.concatenate([dots, pad], axis=0)
        for t in range(n):

            @pl.when(me != t)
            def _(t=t):
                to_seq(c_ref.at[pair_here], c_ref.at[pair_here], s2.at[t], r2.at[pair_here], t).start()

        gcore = jnp.zeros((LANES, LANES), f32)
        g = inverse_grad(gblend, mixed)
        for step in reversed(range(NEWTON)):
            g, gcore = newton_back(g, gcore, core_ref[...], zs_ref[step], ps_ref[step], rs_ref[step], qs_ref[step])
        core_back(g, gcore, core_ref[...], zs_ref[0], ql_ref, kl_ref, gl_ref, pair_here)

    for p in range(PAIRS):

        @pl.when(me != owner_of(p, n))
        def _(p=p):
            to_seq(c_ref.at[p], c_ref.at[p], s2.at[p], r2.at[p], owner_of(p, n)).wait_recv()
            to_seq(g_ref.at[p], land.at[me], s1.at[p], r1.at[me], owner_of(p, n)).wait_send()

    rim_wait(n, me, up, down)

    @pl.when(owns)
    def _():
        for t in range(n):

            @pl.when(me != t)
            def _(t=t):
                to_seq(c_ref.at[pair_here], c_ref.at[pair_here], s2.at[t], r2.at[pair_here], t).wait_send()


def blend_exchange(n, gblend, rim, ql, kl, saved):
    dma = pltpu.SemaphoreType.DMA
    width = rim.shape[1]
    return pl.pallas_call(
        partial(blend_exchange_kernel, n),
        in_specs=[whole()] * 10,
        out_specs=[whole()] * 4,
        out_shape=[shape(PAIRS, MSG, LANES), shape(RIM, width), shape(RIM, width), shape(2, DH, width)],
        scratch_shapes=[
            pltpu.VMEM((n, DH, LANES), f32),
            dma((PAIRS,)), dma((n,)), dma((n,)), dma((n,)), dma((2,)), dma((2,)),
        ],
        compiler_params=params(collective_id=3, has_side_effects=True),
        name="blend_exchange",
    )(gblend, rim, ql, kl, *saved)


def land_return_kernel(n, x_ref, own_ref, land, send, recv):
    me = greet_all(n)
    copies = []
    for d in range(1, n):
        target = lax.rem(me + d, n)
        copy = to_seq(x_ref.at[target], land.at[me], send.at[d], recv.at[me], target)
        copy.start()
        copies.append(copy)
    land[me] = x_ref[me]
    for d in range(1, n):
        source = lax.rem(me + d, n)
        to_seq(x_ref.at[0], land.at[source], send.at[d], recv.at[source], source).wait_recv()
    total = land[0]
    for s in range(1, n):
        total = total + land[s]
    own_ref[...] = total
    for copy in copies:
        copy.wait_send()


def land_return(n, parts):
    dma = pltpu.SemaphoreType.DMA
    return pl.pallas_call(
        partial(land_return_kernel, n),
        in_specs=[whole()],
        out_specs=whole(),
        out_shape=shape(*parts.shape[1:]),
        scratch_shapes=[pltpu.VMEM(parts.shape, f32), dma((n,)), dma((n,))],
        compiler_params=params(collective_id=4, has_side_effects=True),
        name="land_return",
    )(parts)


def norm_stats(r):
    centered = r - jnp.mean(r, axis=1, keepdims=True)
    spread_ = jnp.mean(centered * centered, axis=1, keepdims=True)
    inv = lax.rsqrt(spread_ + EPS)
    return centered * inv, inv


def norm_back(unit, inv, gain, grad):
    ge = grad * gain
    return (
        ge
        - jnp.mean(ge, axis=1, keepdims=True)
        - unit * jnp.mean(ge * unit, axis=1, keepdims=True)
    ) * inv


def quad(g):
    return pl.ds(pl.multiple_of(g * QUAD, QUAD), QUAD)


def pair_rows(ref, g, rows):
    return jnp.concatenate([ref[2 * g, rows, :], ref[2 * g + 1, rows, :]], axis=1)


def front_kernel(
    n, lens_ref, x_ref, taps_in, bq_ref, bv_ref, bo_ref, g1_ref, b1_ref, wq_hbm, wk_hbm, wv_hbm, wo_hbm,
    q_out, k_out, v_out, p_out, near_out, ctx_out, ext_out, h1_out, u1_out,
    m_ref, b_ref, ql_ref, kl_ref, core_ref, zs_ref, ps_ref, rs_ref, qs_ref, mx_ref, taps_ref, inv1_ref,
    w, bias, stack, ext, f_ref, mine, lands, rim, left, right, land,
    load, out, ms, mr, ls, lr, s1, r1, s2, r2,
):
    _, slots, width = stack.shape
    segs = mine.shape[1]
    v, q, k, p, near, ctx, h1, u1 = [stack.at[i] for i in range(8)]
    loads = [pltpu.make_async_copy(hbm, w.at[i], load.at[i]) for i, hbm in enumerate((wv_hbm, wq_hbm, wk_hbm, wo_hbm))]
    for copy in loads:
        copy.start()
    leaving = []

    def leave(src, dst):
        leaving.append(pltpu.make_async_copy(src, dst, out.at[len(leaving)]))
        leaving[-1].start()

    me = greet_signal(n)
    owns, pair_here = pair_at(me, n)
    ends = seg_ends(lens_ref, segs)
    count = ends[-1]
    valid = valid_rows(count, slots)
    member = member_rows(ends, slots)
    inv = inverse_lens(lens_ref, segs)
    bias[0:1, :] = bv_ref[...][None, :]
    bias[1:2, :] = bq_ref[...][None, :]
    bias[2:3, :] = jnp.zeros((1, width), f32)

    def one(i, carry):
        pltpu.make_async_copy(wv_hbm, w.at[i], load.at[i]).wait()
        stack[i] = mm(x_ref[...], w[i]) + bias[pl.ds(i, 1), :]

        @pl.when(i == 0)
        def _():
            v[...] = jnp.where(valid, v[...], 0.0)
            rim[...] = rims_of(v[...], count)
            pl.semaphore_wait(pltpu.get_barrier_semaphore(), n - 1)
            rim_start(n, me, up, down, left, right)

        return carry

    def land_copy(kind, source, d, target):
        return to_seq(mine.at[kind], lands.at[source, kind], ls.at[kind, d], lr.at[kind, source], target)

    def land_rows(kind, rows_ref):
        for d in range(1, n):
            source = lax.rem(me + d, n)
            land_copy(kind, source, d, source).wait_recv()
        for s in range(n):
            rows_ref[slice(s * segs, (s + 1) * segs), :] = lands[s, kind]

    up, down = rim_copies(n, me, rim, left, right, ms, mr)
    lax.fori_loop(0, 3, one, 0)
    mine[0] = mm(member, q[...]) * inv
    mine[1] = mm(member, k[...]) * inv
    for kind in range(2):
        for d in range(1, n):
            land_copy(kind, me, d, lax.rem(me + d, n)).start()
    lands[me] = mine[...]
    leave(q, q_out)
    leave(k, k_out)
    leave(v, v_out)
    row = lax.broadcasted_iota(jnp.int32, (HEADS, width), 0)
    col = lax.broadcasted_iota(jnp.int32, (HEADS, width), 1) >> 6
    taps_ref[...] = t_mm(taps_in[...], jnp.where(row == col, 1.0, 0.0), TOP)
    rim_wait(n, me, up, down)
    fill_extended(ext, v[...], left[...], right[...], count)
    leave(ext, ext_out)
    conv_into(ctx, ext, taps_ref, slots, False, False)

    land_rows(0, ql_ref)

    def far(g, carry):
        cols = quad(g)
        mask = head_mask(QUAD)
        scores = mm_t(k[:, cols], spread(ql_ref[:, cols], mask)) * SCALE
        scores = jnp.where(valid, scores, MASKED)
        top = jnp.max(scores, axis=0, keepdims=True)
        raised = jnp.where(valid, jnp.exp(scores - top), 0.0)
        p[:, cols] = raised
        m_ref[:, cols] = top
        total = jnp.sum(raised, axis=0, keepdims=True)
        weighted = fold(t_mm(v[:, cols], raised), mask)
        rest = jnp.concatenate([top, total, jnp.zeros((MSG - DH - 2, QUAD), f32)], axis=0)
        for j in range(QUAD // LANES):
            part = slice(j * LANES, (j + 1) * LANES)
            f_ref[g * 2 + j, 0:DH, :] = weighted[:, part]
            f_ref[g * 2 + j, DH:MSG, :] = rest[:, part]
        return carry

    lax.fori_loop(0, QUADS, far, 0)
    for pair in range(PAIRS):

        @pl.when(me != owner_of(pair, n))
        def _(pair=pair):
            to_seq(f_ref.at[pair], land.at[me], s1.at[pair], r1.at[me], owner_of(pair, n)).start()

    leave(p, p_out)
    land_rows(1, kl_ref)

    @pl.when(owns)
    def _():
        mask = head_mask(LANES)
        lanes = pl.ds(pl.multiple_of(pair_here * LANES, LANES), LANES)
        core = core_of(spread(ql_ref[:, lanes], mask), spread(kl_ref[:, lanes], mask), mask)
        core_ref[...] = core
        colsum = jnp.sum(core, axis=0, keepdims=True)
        zs_ref[0] = core.T / jnp.sqrt(pair_sums(colsum * colsum))
        unit = eye(LANES)

        def newton(step, carry):
            z = zs_ref[step]
            prod = mm(core_ref[...], z, TOP)
            ps_ref[step] = prod
            r = 15.0 * unit - mm(prod, 7.0 * unit - prod, TOP)
            rs_ref[step] = r
            q_ = 13.0 * unit - mm(prod, r, TOP)
            qs_ref[step] = q_
            zs_ref[step + 1] = 0.25 * mm(z, q_, TOP)
            return carry

        lax.fori_loop(0, NEWTON, newton, 0)
        land[me] = f_ref[pair_here]
        for s in range(n):

            @pl.when(me != s)
            def _(s=s):
                to_seq(f_ref.at[0], land.at[s], s1.at[0], r1.at[s], s).wait_recv()

        top = land[0][DH : DH + 1]
        for s in range(1, n):
            top = jnp.maximum(top, land[s][DH : DH + 1])
        total = jnp.zeros_like(top)
        mixed = jnp.zeros((DH, LANES), f32)
        for s in range(n):
            part = land[s]
            factor = jnp.exp(part[DH : DH + 1] - top)
            total = total + part[DH + 1 : DH + 2] * factor
            mixed = mixed + part[:DH] * factor
        mixed = mixed / total
        mx_ref[...] = mixed
        b_ref[pair_here, 0:DH, :] = mm_t(mixed, zs_ref[NEWTON], TOP)
        pad = jnp.zeros((MSG - DH - 2, LANES), f32)
        b_ref[pair_here, DH:MSG, :] = jnp.concatenate([top, total, pad], axis=0)
        for t in range(n):

            @pl.when(me != t)
            def _(t=t):
                to_seq(b_ref.at[pair_here], b_ref.at[pair_here], s2.at[t], r2.at[pair_here], t).start()

    def soft(g, carry):
        cols = quad(g)
        mask = head_mask(QUAD)
        head = lax.broadcasted_iota(jnp.int32, (slots, QUAD), 1) >> 6
        scores = mm_t(q[:, cols], spread(kl_ref[:, cols], mask)) * SCALE
        tops = [jnp.max(scores[:, h * DH : (h + 1) * DH], axis=1, keepdims=True) for h in range(4)]
        top = jnp.where(head < 2, jnp.where(head < 1, tops[0], tops[1]), jnp.where(head < 3, tops[2], tops[3]))
        raised = jnp.exp(scores - top)
        near[:, cols] = raised / mm(raised, jnp.where(mask, 1.0, 0.0))
        return carry

    lax.fori_loop(0, QUADS, soft, 0)
    leave(near, near_out)
    for pair in range(PAIRS):

        @pl.when(me != owner_of(pair, n))
        def _(pair=pair):
            to_seq(b_ref.at[pair], b_ref.at[pair], s2.at[pair], r2.at[pair], owner_of(pair, n)).wait_recv()

    def blend(g, carry):
        cols = quad(g)
        ctx[:, cols] += mm_t(near[:, cols], spread(pair_rows(b_ref, g, slice(0, DH)), head_mask(QUAD)))
        return carry

    lax.fori_loop(0, QUADS, blend, 0)
    leave(ctx, ctx_out)
    loads[-1].wait()

    unit, scale = norm_stats(x_ref[...] + (mm(ctx[...], w[3]) + bo_ref[...][None, :]))
    h1[...] = unit * g1_ref[...][None, :] + b1_ref[...][None, :]
    leave(h1, h1_out)
    u1[...] = unit
    leave(u1, u1_out)
    inv1_ref[...] = scale
    for kind in range(2):
        for d in range(1, n):
            land_copy(kind, me, d, lax.rem(me + d, n)).wait_send()
    for pair in range(PAIRS):

        @pl.when(me != owner_of(pair, n))
        def _(pair=pair):
            to_seq(f_ref.at[pair], land.at[me], s1.at[pair], r1.at[me], owner_of(pair, n)).wait_send()

    @pl.when(owns)
    def _():
        for t in range(n):

            @pl.when(me != t)
            def _(t=t):
                to_seq(b_ref.at[pair_here], b_ref.at[pair_here], s2.at[t], r2.at[pair_here], t).wait_send()

    for copy in leaving:
        copy.wait()


def front(n, lens, x, taps, bq, bv, bo, g1, b1, wq, wk, wv, wo):
    slots, width = x.shape
    segs = lens.shape[1]
    dma = pltpu.SemaphoreType.DMA
    vm = lambda *dims: pltpu.VMEM(dims, f32)
    anywhere = pl.BlockSpec(memory_space=pl.ANY)
    square = (LANES, LANES)
    rows = shape(slots, width)
    return pl.pallas_call(
        partial(front_kernel, n),
        in_specs=[smem()] + [whole()] * 7 + [anywhere] * 4,
        out_specs=[anywhere] * 9 + [whole()] * 12,
        out_shape=[rows] * 6 + [shape(slots + 40, width), rows, rows]
        + [
            shape(1, width), shape(PAIRS, MSG, LANES), shape(DH, width), shape(DH, width), shape(*square),
            shape(NEWTON + 1, *square), shape(NEWTON, *square), shape(NEWTON, *square), shape(NEWTON, *square),
            shape(DH, LANES), shape(CONV, width), shape(slots, 1),
        ],
        scratch_shapes=[
            vm(4, width, width), vm(8, width), vm(8, slots, width), vm(slots + 40, width),
            vm(PAIRS, MSG, LANES), vm(2, segs, width), vm(n, 2, segs, width), vm(2 * RIM, width), vm(RIM, width),
            vm(RIM, width), vm(n, MSG, LANES),
            dma((4,)), dma((9,)), dma((2,)), dma((2,)), dma((2, n)), dma((2, n)), dma((PAIRS,)), dma((n,)),
            dma((n,)), dma((n,)),
        ],
        compiler_params=params(collective_id=1, has_side_effects=True),
        name="front",
    )(lens, x, taps, bq, bv, bo, g1, b1, wq, wk, wv, wo)


def forward_kernel(
    lens_ref, h1_ref, wi_ref, bi_ref, wo_ref, bo_ref, cot_ref, g2_ref, b2_ref,
    pre_ref, out_ref, gs2_ref, small_ref,
    acc_ref, act_ref,
):
    step = pl.program_id(0)

    @pl.when(step == 0)
    def _():
        acc_ref[...] = jnp.zeros_like(acc_ref)

    pre = mm(h1_ref[...], wi_ref[...]) + bi_ref[...]
    pre_ref[...] = pre
    act_ref[...] = 0.5 * pre * (1.0 + lax.erf(pre * ROOT_HALF))
    acc_ref[...] += mm(act_ref[...], wo_ref[...])

    @pl.when(step == pl.num_programs(0) - 1)
    def _():
        slots = h1_ref.shape[0]
        valid = valid_rows(seg_ends(lens_ref, lens_ref.shape[1])[-1], slots)
        summed = h1_ref[...] + (acc_ref[...] + bo_ref[...][None, :])
        unit, inv = norm_stats(summed)
        out_ref[...] = jnp.where(valid, unit * g2_ref[...][None, :] + b2_ref[...][None, :], 0.0)
        e = jnp.where(valid, cot_ref[...], 0.0)
        grad = norm_back(unit, inv, g2_ref[...][None, :], e)
        gs2_ref[...] = grad
        small_ref[...] = jnp.concatenate(
            [
                jnp.sum(e * unit, axis=0, keepdims=True),
                jnp.sum(e, axis=0, keepdims=True),
                jnp.sum(grad, axis=0, keepdims=True),
                jnp.zeros((5, e.shape[1]), f32),
            ],
            axis=0,
        )


def ffn_forward(lens, h1, wi, bi, wo, bo, cot, g2, b2):
    slots, width = h1.shape
    inner = wi.shape[1]
    const = lambda *dims: pl.BlockSpec(dims, lambda j: (0,) * len(dims))
    return pl.pallas_call(
        forward_kernel,
        grid=(inner // width,),
        in_specs=[
            smem(), const(slots, width),
            pl.BlockSpec((width, width), lambda j: (0, j)), pl.BlockSpec((1, width), lambda j: (0, j)),
            pl.BlockSpec((width, width), lambda j: (j, 0)), const(width),
            const(slots, width), const(width), const(width),
        ],
        out_specs=[
            pl.BlockSpec((slots, width), lambda j: (0, j)),
            const(slots, width), const(slots, width), const(8, width),
        ],
        out_shape=[shape(slots, inner), shape(slots, width), shape(slots, width), shape(8, width)],
        scratch_shapes=[pltpu.VMEM((slots, width), f32)] * 2,
        compiler_params=params(),
        name="ffn_forward",
    )(lens, h1, wi, bi, wo, bo, cot, g2, b2)


def put_strips(ref, block, rows=slice(None), first=0):
    for s in range(block.shape[1] // LANES):
        ref[first + s, rows, :] = block[:, s * LANES : (s + 1) * LANES]


def backward_kernel(
    h1_ref, gs2_ref, pre_ref, wi_ref, wo_ref, u1_ref, inv1_ref, g1_ref,
    dwo_ref, dwi_ref, gs1_ref, dbi_ref, small_ref,
    acc_ref, gpre_ref,
):
    step = pl.program_id(0)

    @pl.when(step == 0)
    def _():
        acc_ref[...] = gs2_ref[...]

    def one(g, carry):
        cols = quad(g)
        pre = pre_ref[:, cols]
        phi_big = 0.5 * (1.0 + lax.erf(pre * ROOT_HALF))
        slope = phi_big + pre * (INV_ROOT_TAU * jnp.exp(-0.5 * pre * pre))
        gpre = mm_t(gs2_ref[...], wo_ref[cols, :]) * slope
        gpre_ref[:, cols] = gpre
        dbi_ref[:, cols] = jnp.sum(gpre, axis=0, keepdims=True)
        put_strips(dwo_ref, t_mm(pre * phi_big, gs2_ref[...]), cols)
        return carry

    lax.fori_loop(0, QUADS, one, 0)

    def two(g, carry):
        cols = quad(g)
        put_strips(dwi_ref, t_mm(h1_ref[:, cols], gpre_ref[...]), cols)
        acc_ref[:, cols] += mm_t(gpre_ref[...], wi_ref[cols, :])
        return carry

    lax.fori_loop(0, QUADS, two, 0)

    @pl.when(step == pl.num_programs(0) - 1)
    def _():
        e = acc_ref[...]
        unit = u1_ref[...]
        grad = norm_back(unit, inv1_ref[...], g1_ref[...][None, :], e)
        gs1_ref[...] = grad
        small_ref[...] = jnp.concatenate(
            [
                jnp.sum(e * unit, axis=0, keepdims=True),
                jnp.sum(e, axis=0, keepdims=True),
                jnp.sum(grad, axis=0, keepdims=True),
                jnp.zeros((5, e.shape[1]), f32),
            ],
            axis=0,
        )


def ffn_backward(h1, gs2, pre, wi, wo, u1, inv1, g1):
    slots, width = h1.shape
    inner = wi.shape[1]
    strips = width // LANES
    const = lambda *dims: pl.BlockSpec(dims, lambda j: (0,) * len(dims))
    return pl.pallas_call(
        backward_kernel,
        grid=(inner // width,),
        in_specs=[
            const(slots, width), const(slots, width),
            pl.BlockSpec((slots, width), lambda j: (0, j)),
            pl.BlockSpec((width, width), lambda j: (0, j)),
            pl.BlockSpec((width, width), lambda j: (j, 0)),
            const(slots, width), const(slots, 1), const(width),
        ],
        out_specs=[
            pl.BlockSpec((strips, width, LANES), lambda j: (j, 0, 0)),
            pl.BlockSpec((strips, width, LANES), lambda j: (j, 0, 0)),
            const(slots, width),
            pl.BlockSpec((1, width), lambda j: (0, j)),
            const(8, width),
        ],
        out_shape=[
            shape(inner // LANES, width, LANES), shape(inner // LANES, width, LANES),
            shape(slots, width), shape(1, inner), shape(8, width),
        ],
        scratch_shapes=[pltpu.VMEM((slots, width), f32)] * 2,
        compiler_params=params(),
        name="ffn_backward",
    )(h1, gs2, pre, wi, wo, u1, inv1, g1)


def near_back_quad(g, gctx_ref, near_ref, q_ref, kl_ref, b_ref, gq_ref, gb_ref, gkl_ref):
    mask = head_mask(QUAD)
    ones = jnp.where(mask, 1.0, 0.0)
    cols = quad(g)
    gctx = gctx_ref[:, cols]
    near = near_ref[:, cols]
    gblend = fold(t_mm(gctx, near), mask)
    gb_ref[2 * g] = gblend[:, :LANES]
    gb_ref[2 * g + 1] = gblend[:, LANES:]
    gnear = mm(gctx, spread(pair_rows(b_ref, g, slice(0, DH)), mask))
    gscore = near * (gnear - mm(near * gnear, ones)) * SCALE
    gq_ref[:, cols] = mm(gscore, spread(kl_ref[:, cols], mask))
    gkl_ref[:, cols] = fold(t_mm(gscore, q_ref[:, cols]), mask)


def near_back_kernel(
    lens_ref, gs1_ref, wo_ref, near_ref, q_ref, kl_ref, b_ref,
    gctx_ref, gq_ref, gb_ref, gkl_ref, rim_ref,
):
    count = seg_ends(lens_ref, lens_ref.shape[1])[-1]
    gctx_ref[...] = mm_t(gs1_ref[...], wo_ref[...])
    rim_ref[...] = rims_of(gctx_ref[...], count)
    def one(g, carry):
        near_back_quad(g, gctx_ref, near_ref, q_ref, kl_ref, b_ref, gq_ref, gb_ref, gkl_ref)
        return carry

    lax.fori_loop(0, QUADS, one, 0)


def near_back(lens, gs1, wo, near, q, kl, b):
    slots, width = gs1.shape
    return pl.pallas_call(
        near_back_kernel,
        in_specs=[smem()] + [whole()] * 6,
        out_specs=[whole()] * 5,
        out_shape=[
            shape(slots, width), shape(slots, width), shape(PAIRS, DH, LANES),
            shape(DH, width), shape(2 * RIM, width),
        ],
        compiler_params=params(),
        name="near_back",
    )(lens, gs1, wo, near, q, kl, b)


def far_back_quad(g, k_ref, v_ref, p_ref, m_ref, b_ref, c_ref, ql_ref, gk_ref, gv_ref, gql_ref, add):
    mask = head_mask(QUAD)
    cols = quad(g)
    top = pair_rows(b_ref, g, slice(DH, DH + 1))
    total = pair_rows(b_ref, g, slice(DH + 1, DH + 2))
    prob = p_ref[:, cols] * (jnp.exp(m_ref[:, cols] - top) / total)
    gmixed = spread(pair_rows(c_ref, g, slice(0, DH)), mask)
    dots = pair_rows(c_ref, g, slice(DH, DH + 1))
    gscore = prob * (mm(v_ref[:, cols], gmixed) - dots) * SCALE
    gk_ref[:, cols] = mm(gscore, spread(ql_ref[:, cols], mask))
    gval = mm_t(prob, gmixed)
    if add:
        gv_ref[:, cols] += gval
    else:
        gv_ref[:, cols] = gval
    gql_ref[:, cols] = fold(t_mm(gscore, k_ref[:, cols]), mask)


def land_parts(ret_ref, gql, gkl):
    n, _, segs, _ = ret_ref.shape
    for s in range(n):
        rows = slice(s * segs, (s + 1) * segs)
        ret_ref[s, 0] = gql[rows]
        ret_ref[s, 1] = gkl[rows]


def far_back_kernel(
    k_ref, v_ref, p_ref, m_ref, b_ref, c_ref, ql_ref, gkl_ref, gl_ref,
    gk_ref, gv_ref, ret_ref, gql_ref,
):
    def one(g, carry):
        far_back_quad(g, k_ref, v_ref, p_ref, m_ref, b_ref, c_ref, ql_ref, gk_ref, gv_ref, gql_ref, False)
        return carry

    lax.fori_loop(0, QUADS, one, 0)
    land_parts(ret_ref, gql_ref[...] + gl_ref[0], gkl_ref[...] + gl_ref[1])


def far_back(n, lens, k, v, p, m, b, c, ql, gkl, gl):
    slots, width = k.shape
    segs = lens.shape[1]
    return pl.pallas_call(
        far_back_kernel,
        in_specs=[whole()] * 9,
        out_specs=[whole()] * 3,
        out_shape=[shape(slots, width), shape(slots, width), shape(n, 2, segs, width)],
        scratch_shapes=[pltpu.VMEM((DH, width), f32)],
        compiler_params=params(),
        name="far_back",
    )(k, v, p, m, b, c, ql, gkl, gl)


def taps_sums(scr_ref):
    width = scr_ref.shape[2]
    rows = jnp.concatenate(
        [jnp.sum(scr_ref[c], axis=0, keepdims=True) for c in range(CONV)] + [jnp.zeros((7, width), f32)], axis=0
    )
    row = lax.broadcasted_iota(jnp.int32, (width, LANES), 0) >> 6
    col = lax.broadcasted_iota(jnp.int32, (width, LANES), 1)
    return mm(rows, jnp.where(row == col, 1.0, 0.0), TOP)


def conv_back_kernel(
    lens_ref, values_ref, gctx_ref, gleft_ref, gright_ref, taps_ref, ctx_ref, gs1_ref,
    gv_ref, gtaps_ref, dwo_ref,
    ext_ref, scr_ref,
):
    slots = gctx_ref.shape[0]
    count = seg_ends(lens_ref, lens_ref.shape[1])[-1]
    put_strips(dwo_ref, t_mm(ctx_ref[...], gs1_ref[...]))
    fill_extended(ext_ref, gctx_ref[...], gleft_ref[...], gright_ref[...], count)
    conv_into(gv_ref, ext_ref, taps_ref, slots, True, False)
    taps_grad_into(scr_ref, gctx_ref, values_ref, slots)
    gtaps_ref[...] = taps_sums(scr_ref)


def conv_back(lens, ext, gctx, gleft, gright, taps, ctx, gs1):
    slots, width = gctx.shape
    return pl.pallas_call(
        conv_back_kernel,
        in_specs=[smem()] + [whole()] * 7,
        out_specs=[whole()] * 3,
        out_shape=[shape(slots, width), shape(40, LANES), shape(width // LANES, width, LANES)],
        scratch_shapes=[pltpu.VMEM((slots + 40, width), f32), pltpu.VMEM((CONV, 8, width), f32)],
        compiler_params=params(),
        name="conv_back",
    )(lens, ext, gctx, gleft, gright, taps, ctx, gs1)


def project_back_kernel(
    lens_ref, x_ref, gs1_ref, gqn_ref, gkf_ref, gvc_ref, gvf_ref, own_ref, wq_ref, wk_ref, wv_ref,
    ig_ref, dq_ref, dk_ref, dv_ref, small_ref,
    gq_ref, gk_ref, gv_ref,
):
    @pl.when(pl.program_id(0) == 0)
    def _():
        slots = gqn_ref.shape[0]
        segs = own_ref.shape[1]
        ends = seg_ends(lens_ref, segs)
        member = member_rows(ends, slots)
        inv = inverse_lens(lens_ref, segs)
        gq = gqn_ref[...] + t_mm(member, own_ref[0] * inv)
        gk = gkf_ref[...] + t_mm(member, own_ref[1] * inv)
        gv = jnp.where(valid_rows(ends[-1], slots), gvc_ref[...] + gvf_ref[...], 0.0)
        gq_ref[...] = gq
        gk_ref[...] = gk
        gv_ref[...] = gv
        small_ref[...] = jnp.concatenate(
            [
                jnp.sum(gq, axis=0, keepdims=True),
                jnp.sum(gv, axis=0, keepdims=True),
                jnp.zeros((6, gq.shape[1]), f32),
            ],
            axis=0,
        )

    x = x_ref[...]
    put_strips(dq_ref, t_mm(x, gq_ref[...]))
    put_strips(dk_ref, t_mm(x, gk_ref[...]))
    put_strips(dv_ref, t_mm(x, gv_ref[...]))
    ig_ref[...] = (
        gs1_ref[...]
        + mm_t(gq_ref[...], wq_ref[...])
        + mm_t(gk_ref[...], wk_ref[...])
        + mm_t(gv_ref[...], wv_ref[...])
    )


def project_back(lens, x, gs1, gqn, gkf, gvc, gvf, own, wq, wk, wv):
    slots, width = x.shape
    col = 256
    strips = width // LANES
    const = lambda *dims: pl.BlockSpec(dims, lambda i: (0,) * len(dims))
    part = pl.BlockSpec((slots, col), lambda i: (0, i))
    wspec = pl.BlockSpec((col, width), lambda i: (i, 0))
    dspec = pl.BlockSpec((strips, col, LANES), lambda i: (0, i, 0))
    return pl.pallas_call(
        project_back_kernel,
        grid=(width // col,),
        in_specs=[smem(), part, part] + [const(slots, width)] * 4 + [const(*own.shape), wspec, wspec, wspec],
        out_specs=[part, dspec, dspec, dspec, const(8, width)],
        out_shape=[shape(slots, width)] + [shape(strips, width, LANES)] * 3 + [shape(8, width)],
        scratch_shapes=[pltpu.VMEM((slots, width), f32)] * 3,
        compiler_params=params(),
        name="project_back",
    )(lens, x, gs1, gqn, gkf, gvc, gvf, own, wq, wk, wv)


def sum_plain(parts):
    sizes = [part.size for part in parts]
    shapes = [part.shape for part in parts]
    devices = lax.axis_size(("seq", "dp"))
    flat = jnp.concatenate([part.reshape(-1) for part in parts])
    flat = jnp.pad(flat, (0, -flat.shape[0] % devices))
    own = lax.psum_scatter(flat, ("seq", "dp"), scatter_dimension=0, tiled=True)
    flat = lax.all_gather(own, ("seq", "dp"), axis=0, tiled=True)
    out = []
    at = 0
    for size, dims in zip(sizes, shapes):
        out.append(flat[at : at + size].reshape(dims))
        at += size
    return out


STRIP = 768
HALF = STRIP // 2
PART = HALF // 2
Z_ROWS = PART // 4
OWN = Z_ROWS // 2
STAGES = 13
SMALL_STEPS = 5


def pack_small(sb_ref, small0, small1, small2, inner_bias, taps):
    at = 0
    for ref, count in ((small0, 2), (small1, 3), (small2, 3), (inner_bias, 1)):
        for r in range(count):
            for j in range(ref.shape[1] // LANES):
                sb_ref[0, at : at + 1, :] = ref[r : r + 1, j * LANES : (j + 1) * LANES]
                at += 1
    sb_ref[0, at : at + 40, :] = taps[...]


SMALL_ROWS = 8 * 6 + 24 + 40


def unpack_small(s_ref, outs):
    at = 0
    for ref in outs[:-1]:
        for j in range(ref.shape[0] // LANES):
            ref[pl.ds(j * LANES, LANES)] = s_ref[at, :]
            at += 1
    outs[-1][...] = s_ref[at : at + 40, :].T[:HEADS, :CONV]


def reduce_stages(gw, o_ref, bufs, sems):
    acc, lc, l1, mid, lz, l3, ag = bufs
    cs, cr, s1, r1, ms, zr, r3, r4, gs, gr, r5, keep, es, er = sems
    seq = lax.axis_index("seq")
    dp = lax.axis_index("dp")
    z = seq // 2
    c = lax.rem(seq, 2)
    y = dp // 2
    x = lax.rem(dp, 2)
    zb = 3 - z
    place = lambda z_, c_, y_, x_: (z_ * 2 + c_, y_ * 2 + x_)
    by_core = place(z, 1 - c, y, x)
    by_x = place(z, c, y, 1 - x)
    by_y = place(z, c, 1 - y, x)
    right = place(lax.rem(z + 1, 4), c, y, x)
    left = place(lax.rem(z + 3, 4), c, y, x)
    opposite = place(lax.rem(z + 2, 4), c, y, x)
    near_z = place(z + 1 - 2 * lax.rem(z, 2), c, y, x)

    def remote(src, dst, send, recv, target):
        return pltpu.make_async_remote_copy(src, dst, send, recv, device_id=target, device_id_type=MESH)

    aligned = lambda at: pl.multiple_of(at, 8)
    slot = lambda ref, k: lax.rem(k, ref.shape[0])
    starts = (x * PART, HALF + y * PART)
    others = ((1 - x) * PART, HALF + (1 - y) * PART)
    own_rows = (pl.ds(aligned(y * OWN), OWN), pl.ds(aligned(x * OWN), OWN))
    other_rows = (pl.ds(aligned((1 - y) * OWN), OWN), pl.ds(aligned((1 - x) * OWN), OWN))
    first_to = (by_x, by_y)
    third_to = (by_y, by_x)
    ways = ((0, z, right), (1, zb, left))

    def bytes_of(rows, send, recv, pieces=1):
        part = lc.at[pl.ds(0, pieces), pl.ds(0, rows // pieces)]
        return remote(part, part, send, recv, by_core)

    def strip(k):
        return lax.rem(k // 3, GW_SLOTS) * PAIRS + 2 * lax.rem(k, 3)

    def core_copy(k):
        return remote(gw.at[strip(k) + 1 - c], lc.at[slot(lc, k)], cs.at[k], cr.at[k], by_core)

    def core_out(k):
        core_copy(k).start()

    def first_out(k):
        core_copy(k).wait()
        at = slot(acc, k)
        acc[at] = gw[strip(k) + c] + lc[slot(lc, k)]
        for j in range(2):
            remote(
                acc.at[at, pl.ds(aligned(others[j]), PART)], l1.at[slot(l1, k), j], s1.at[k], r1.at[k], first_to[j]
            ).start()

    def z_copy(k, way, step, block, target):
        return remote(mid.at[slot(mid, k), block], lz.at[slot(lz, k), way, step], ms.at[k], zr.at[k, way, step], target)

    def z_out(k, step):
        if step == 0:
            bytes_of(HALF, s1.at[k], r1.at[k]).wait()
            for j in range(2):
                for block in range(4):
                    here = pl.ds(aligned(starts[j] + block * Z_ROWS), Z_ROWS)
                    there = pl.ds(block * Z_ROWS, Z_ROWS)
                    mid[slot(mid, k), block, j] = acc[slot(acc, k), here] + l1[slot(l1, k), j, there]
        for way, at, target in ways:
            block = 3 - step + z if way == 0 else step - zb
            if step > 0:

                @pl.when((at > 0) & (at <= step))
                def _(way=way, block=block, target=target):
                    z_copy(k, way, step - 1, 0, target).wait_recv()
                    mid[slot(mid, k), block] += lz[slot(lz, k), way, step - 1]

            if step < 3:

                @pl.when((at <= step) & (at < 3))
                def _(way=way, block=block, target=target):
                    z_copy(k, way, step, block, target).start()

    def third_out(k):
        z_out(k, 3)
        for j in range(2):
            remote(
                mid.at[slot(mid, k), z, j, other_rows[j]], l3.at[slot(l3, k), j], ms.at[k], r3.at[k], third_to[j]
            ).start()

    def back_third_out(k):
        bytes_of(2 * OWN, ms.at[k], r3.at[k]).wait_recv()
        for j in range(2):
            ag[slot(ag, k), z, j, own_rows[j]] = mid[slot(mid, k), z, j, own_rows[j]] + l3[slot(l3, k), j]
            part = ag.at[slot(ag, k), z, j, own_rows[j]]
            remote(part, part, gs.at[k], r4.at[k], third_to[j]).start()

    def back_z(k, way, step, block, target):
        part = ag.at[slot(ag, k), block]
        return remote(part, part, gs.at[k], gr.at[k, way, step], target)

    def back_z_out(k, step):
        if step == 0:
            bytes_of(6 * Z_ROWS + 2 * OWN, ms.at[k], r3.at[k]).wait_send()
            bytes_of(2 * OWN, gs.at[k], r4.at[k]).wait_recv()
        for way, at, target in ways:
            block = z - step if way == 0 else z + step
            if step > 0:

                @pl.when(at >= step)
                def _(way=way, target=target):
                    back_z(k, way, step - 1, 0, target).wait_recv()

            if step < 3:

                @pl.when((at >= step) & (at < 3))
                def _(way=way, block=block, target=target):
                    back_z(k, way, step, block, target).start()

    blocks = (pl.ds(x * 4, 4), pl.ds(8 + y * 4, 4))

    def keep_copy(k, j):
        return pltpu.make_async_copy(ag.at[slot(ag, k), :, j], o_ref.at[c, k, blocks[j]], keep.at[k, j])

    def back_first_out(k):
        back_z_out(k, 3)
        for j in range(2):
            remote(ag.at[slot(ag, k), :, j], o_ref.at[c, k, blocks[j]], gs.at[k], r5.at[k], first_to[j]).start()
            keep_copy(k, j).start()

    def back_core(k):
        part = o_ref.at[c, k]
        return remote(part, part, es.at[k], er.at[k], by_core)

    def back_core_out(k):
        bytes_of(HALF, gs.at[k], r5.at[k]).wait_recv()
        for j in range(2):
            keep_copy(k, j).wait()

        @pl.when((z == 0) | (z == 3))
        def _():
            bytes_of(2 * OWN + 2 * Z_ROWS + HALF, gs.at[k], r5.at[k]).wait_send()

        @pl.when((z > 0) & (z < 3))
        def _():
            bytes_of(2 * OWN + 10 * Z_ROWS + HALF, gs.at[k], r5.at[k], 2).wait_send()

        back_core(k).start()

    def finish(k):
        back_core(k).wait()

    stages = [
        core_out, first_out, partial(z_out, step=0), partial(z_out, step=1), partial(z_out, step=2), third_out,
        back_third_out, partial(back_z_out, step=0), partial(back_z_out, step=1), partial(back_z_out, step=2),
        back_first_out, back_core_out, finish,
    ]
    return stages, (by_core, by_x, by_y, near_z, opposite), remote


LAG = (0, 1, 3, 5, 7, 9, 11, 13, 15, 17, 19, 21, 22)
CHUNKS = 36
GW_SLOTS = 4
RING_ACC = 6
RING_LC = 4
RING_MID = 12
RING_Z = 6
RING_AG = 16
SEQ_DEVICES = 8
SMALL_AT = 44
ENTER = 2
HELD = 30
GAP = 2
GS1, GS2, H1, ACT, GPRE, PRE, _, U1, GCTX, IG = range(10)
GV, PROB, CTX, KEYS, NEAR, QUERY, VALS = GS2, H1, ACT, GPRE, PRE, PRE + 1, U1
FFN_AT = (0, 4, 8, 13)
GS1_AT = 17
OUTPUT_AT, VALUE_AT, QUERY_AT, KEY_AT = 21, 28, 32, 33
INPUT_AT = (41, 42, 43)
TAPS_AT = 36


def pick(t, table):
    value = jnp.int32(0)
    hit = t < 0
    for when, what in table.items():
        value = jnp.where(t == when, what, value)
        hit = hit | (t == when)
    return value, hit


def greet_block():
    seq = lax.axis_index("seq")
    dp = lax.axis_index("dp")
    y = dp // 2
    x = lax.rem(dp, 2)
    barrier = pltpu.get_barrier_semaphore()
    for d in range(1, SEQ_DEVICES):
        pl.semaphore_signal(
            barrier, inc=1, device_id=(lax.rem(seq + d, SEQ_DEVICES), dp), device_id_type=MESH
        )
    for other in (y * 2 + 1 - x, (1 - y) * 2 + x):
        pl.semaphore_signal(barrier, inc=1, device_id=(seq, other), device_id_type=MESH)
    pl.semaphore_wait(barrier, SEQ_DEVICES + 1)
    return seq


def tail_kernel(
    lens_ref, gs2_hbm, h1_hbm, u1_hbm, pre_hbm, wout_hbm, win_hbm, wo_hbm, near_hbm, q_hbm, ctx_hbm, ext_hbm,
    k_hbm, v_hbm, p_hbm, x_hbm, wq_hbm, wk_hbm, wv_hbm,
    inv1_ref, g1_ref, m_ref, b_ref, ql_ref, kl_ref, core_ref, zs_ref, ps_ref, rs_ref, qs_ref, mx_ref, taps_ref, small2_ref,
    o_ref, so_ref, ig_hbm,
    acc, lc, l1, mid, lz, l3, ag, sb, sl, gw,
    stack, w, ext, gext, tap_scr, gtaps, small0, small1, dbi,
    gb, rim, gkl, gql, gl, land, cmsg, gleft, gright, ng, ncore, nlead, ret, rland, own,
    loads, ig_sem, b1s, b1r, b2s, b2r, ms, mr, rets, retr, ss, sr,
    *sems,
):
    n = SEQ_DEVICES
    _, slots, width = stack.shape
    segs = own.shape[1]
    gs1, gv, p, ctx, k, near, q, v, gctx, ig = [
        stack.at[i] for i in (GS1, GV, PROB, CTX, KEYS, NEAR, QUERY, VALS, GCTX, IG)
    ]
    moves = []

    def load(src, dst):
        moves.append(pltpu.make_async_copy(src, dst, loads.at[len(moves)]))
        return moves[-1]

    load_gs2 = load(gs2_hbm, stack.at[GS2])
    load_w = []
    load_pre = []
    for j in range(4):
        part = pl.ds(j * width, width)
        load_w.append(load(wout_hbm.at[part, :], w.at[2 * j % 4]))
        load_w.append(load(win_hbm.at[:, part], w.at[(2 * j + 1) % 4]))
        load_pre.append(load(pre_hbm.at[:, part], stack.at[PRE + j % 2]))
    for i, hbm in enumerate((wo_hbm, wv_hbm, wq_hbm, wk_hbm)):
        load_w.append(load(hbm, w.at[i]))
    load_h1, load_u1, load_ext = load(h1_hbm, stack.at[H1]), load(u1_hbm, stack.at[U1]), load(ext_hbm, ext)
    load_near, load_q, load_ctx = load(near_hbm, near), load(q_hbm, q), load(ctx_hbm, ctx)
    load_p, load_k, load_v, load_x = load(p_hbm, p), load(k_hbm, k), load(v_hbm, v), load(x_hbm, q)
    a0, a1, a2, a3 = FFN_AT
    starting = [
        (a0 + 1, load_w[4]), (a0 + 1, load_pre[2]), (a0 + 4, load_w[5]), (a1 + 1, load_w[6]), (a1 + 1, load_pre[3]),
        (a1 + 4, load_w[7]), (a2 + 1, load_w[8]), (a2 + 1, load_near), (a2 + 4, load_w[9]), (a3 + 1, load_w[10]),
        (a3 + 1, load_q), (a3 + 2, load_ctx), (a3 + 3, load_p), (a3 + 4, load_w[11]), (a3 + 4, load_k), (a3 + 4, load_v),
        (GS1_AT + 4, load_x),
    ]
    waiting = [
        (a0, load_gs2), (a0 + 2, load_h1), (a3 + 3, load_u1), (GS1_AT, load_w[8]), (GS1_AT + 1, load_near),
        (GS1_AT + 1, load_q), (OUTPUT_AT, load_ctx), (VALUE_AT, load_x),
    ]
    for j in range(4):
        waiting += [(FFN_AT[j], load_w[2 * j]), (FFN_AT[j], load_pre[j]), (FFN_AT[j] + 3, load_w[2 * j + 1])]
    for i in range(3):
        waiting.append((INPUT_AT[i], load_w[9 + i]))
    for copy in (load_gs2, load_w[0], load_pre[0], load_h1, load_w[1], load_pre[1], load_w[2], load_w[3], load_u1, load_ext):
        copy.start()
    me = greet_block()
    owner, pair_here = pair_at(me, n)
    stages, partners, remote = reduce_stages(gw, o_ref, (acc, lc, l1, mid, lz, l3, ag), sems)
    ends = seg_ends(lens_ref, segs)
    count = ends[-1]

    def weight_event(e, left, right):
        put_strips(gw, t_mm(stack[left], stack[right]), slice(None), lax.rem(e, GW_SLOTS) * PAIRS)

    def through_event(source, target, weight):
        stack[target] += mm_t(stack[source], w[weight])

    def inner_event(j):
        @pl.when(j == 0)
        def _():
            stack[GS1] = stack[GS2]

        at = PRE + lax.rem(j, 2)
        weight = lax.rem(2 * j, 4)

        def one(g, carry):
            cols = quad(g)
            pre = stack[at, :, cols]
            phi_big = 0.5 * (1.0 + lax.erf(pre * ROOT_HALF))
            slope = phi_big + pre * (INV_ROOT_TAU * jnp.exp(-0.5 * pre * pre))
            gpre = mm_t(stack[GS2], w[weight, cols, :]) * slope
            stack[GPRE, :, cols] = gpre
            stack[ACT, :, cols] = pre * phi_big
            dbi[:, pl.ds(pl.multiple_of(j * width + g * QUAD, QUAD), QUAD)] = jnp.sum(gpre, axis=0, keepdims=True)
            return carry

        lax.fori_loop(0, QUADS, one, 0)

    def ev_norm():
        e = gs1[...]
        unit = stack[U1]
        grad = norm_back(unit, inv1_ref[...], g1_ref[...][None, :], e)
        gs1[...] = grad
        ig[...] = grad
        gctx[...] = jnp.zeros_like(grad)
        small1[0:1, :] = jnp.sum(e * unit, axis=0, keepdims=True)
        small1[1:2, :] = jnp.sum(e, axis=0, keepdims=True)
        small1[2:3, :] = jnp.sum(grad, axis=0, keepdims=True)

    def ev_rims():
        rim[...] = rims_of(gctx[...], count)

    def ev_near(g):
        near_back_quad(g, gctx, near, q, kl_ref, b_ref, near, gb, gkl)

    def blend_copy(pair):
        return to_seq(gb.at[pair], land.at[me], b1s.at[pair], b1r.at[me], owner_of(pair, n))

    up, down = rim_copies(n, me, rim, gleft, gright, ms, mr)

    def ev_blend():
        for pair in range(PAIRS):

            @pl.when(me != owner_of(pair, n))
            def _(pair=pair):
                blend_copy(pair).start()

        rim_start(n, me, up, down, gleft, gright)

    def mixed_copy(target):
        return to_seq(cmsg.at[pair_here], cmsg.at[pair_here], b2s.at[target], b2r.at[pair_here], target)

    def ev_owner():
        @pl.when(owner)
        def _():
            land[me] = gb[pair_here]
            for s in range(n):

                @pl.when(me != s)
                def _(s=s):
                    to_seq(gb.at[0], land.at[s], b1s.at[0], b1r.at[s], s).wait_recv()

            gblend = land[0]
            for s in range(1, n):
                gblend = gblend + land[s]
            mixed = mx_ref[...]
            gmixed = mm(gblend, zs_ref[NEWTON], TOP)
            cmsg[pair_here, 0:DH, :] = gmixed
            dots = jnp.sum(gmixed * mixed, axis=0, keepdims=True)
            cmsg[pair_here, DH:MSG, :] = jnp.concatenate([dots, jnp.zeros((MSG - DH - 1, LANES), f32)], axis=0)
            for t in range(n):

                @pl.when(me != t)
                def _(t=t):
                    mixed_copy(t).start()

            ng[...] = inverse_grad(gblend, mixed)
            ncore[...] = jnp.zeros_like(ncore)
            nlead[...] = newton_lead(zs_ref[NEWTON - 1], ps_ref[NEWTON - 1])

        gl[...] = jnp.zeros_like(gl)

    def ev_newton(step):
        @pl.when(owner)
        def _():
            lead = newton_lead(zs_ref[jnp.maximum(step - 1, 0)], ps_ref[jnp.maximum(step - 1, 0)])
            ng[...], ncore[...] = newton_short(
                ng[...], ncore[...], nlead[...], core_ref[...], zs_ref[step], ps_ref[step], rs_ref[step], qs_ref[step]
            )
            nlead[...] = lead

    def ev_core():
        @pl.when(owner)
        def _():
            core_back(ng[...], ncore[...], core_ref[...], zs_ref[0], ql_ref, kl_ref, gl, pair_here)

    quarter = slots // 4

    def ev_taps(part):
        @pl.when(part == 0)
        def _():
            load_ext.wait()
            tap_scr[...] = jnp.zeros_like(tap_scr)

        taps_grad_into(tap_scr, gctx, ext, quarter * (part + 1), quarter * part, False)

        @pl.when(part == 3)
        def _():
            gtaps[...] = taps_sums(tap_scr)

    def ev_conv(part):
        @pl.when(part == 0)
        def _():
            rim_wait(n, me, up, down)
            fill_extended(gext, gctx[...], gleft[...], gright[...], count)

        conv_into(gv, gext, taps_ref, quarter * (part + 1), True, False, quarter * part)

    def ev_mixed():
        for pair in range(PAIRS):

            @pl.when(me != owner_of(pair, n))
            def _(pair=pair):
                to_seq(cmsg.at[pair], cmsg.at[pair], b2s.at[pair], b2r.at[pair], owner_of(pair, n)).wait_recv()

        for copy in (load_k, load_v, load_p):
            copy.wait()

    def ev_far(g):
        far_back_quad(g, k, v, p, m_ref, b_ref, cmsg, ql_ref, p, gv, gql, True)

    def ev_return():
        land_parts(ret, gql[...] + gl[0], gkl[...] + gl[1])
        for d in range(1, n):
            target = lax.rem(me + d, n)
            to_seq(ret.at[target], rland.at[me], rets.at[d], retr.at[me], target).start()

    def ev_own():
        rland[me] = ret[me]
        for d in range(1, n):
            source = lax.rem(me + d, n)
            to_seq(ret.at[0], rland.at[source], rets.at[d], retr.at[source], source).wait_recv()
        total = rland[0]
        for s in range(1, n):
            total = total + rland[s]
        own[...] = total
        inv = inverse_lens(lens_ref, segs)
        member = member_rows(ends, slots)
        near[...] += t_mm(member, own[0] * inv)
        p[...] += t_mm(member, own[1] * inv)
        small0[0:1, :] = jnp.sum(near[...], axis=0, keepdims=True)

    def ev_values():
        masked = jnp.where(valid_rows(count, slots), gv[...], 0.0)
        gv[...] = masked
        small0[1:2, :] = jnp.sum(masked, axis=0, keepdims=True)

    def small(i):
        return remote(sb.at[i], sl.at[i], ss.at[i], sr.at[i], partners[i])

    def ev_small(i):
        if i == 0:
            pack_small(sb, small0, small1, small2_ref, dbi, gtaps)
        else:
            small(i - 1).wait_recv()
            sb[i] = sb[i - 1] + sl[i - 1]
        if i < SMALL_STEPS:
            small(i).start()

    def at_tick(t, when, event):
        @pl.when(t == when)
        def _():
            event()

    def at_ticks(t, start, every, count, event):
        after = t - start

        @pl.when((after >= 0) & (after < every * count) & (lax.rem(after + every, every) == 0))
        def _():
            event(after // every)

    weights = {}
    through = {}
    for j, when in enumerate(FFN_AT):
        weights[when + 1] = (2 * j, ACT, GS2)
        weights[when + 2] = (2 * j + 1, H1, GPRE)
        through[when + 3] = (GPRE, GS1, (2 * j + 1) % 4)
    weights[OUTPUT_AT] = (8, CTX, GS1)
    for i, (when, part) in enumerate(((VALUE_AT, GV), (QUERY_AT, NEAR), (KEY_AT, PROB))):
        weights[when] = (9 + i, QUERY, part)
        through[INPUT_AT[i]] = (part, IG, 1 + i)
    through[GS1_AT] = (GS1, GCTX, 0)

    def by_table(t, table, event):
        columns = [pick(t, {when: row[i] for when, row in table.items()}) for i in range(3)]

        @pl.when(columns[0][1])
        def _():
            event(*[value for value, _ in columns])

    def by_group(t, table, size=6):
        for low in range(0, max(when for when, _ in table) + 1, size):
            mine = [row for row in table if low <= row[0] < low + size]
            if mine:

                @pl.when((t >= low) & (t < low + size))
                def _(mine=mine):
                    for when, event in mine:
                        at_tick(t, when, event)

    copies = [(when, copy.start) for when, copy in starting] + [(when, copy.wait) for when, copy in waiting]
    others = [(FFN_AT[3] + 3, ev_norm), (GS1_AT, ev_rims)]
    last = [
        (GS1_AT + 12, ev_core), (GS1_AT + 12, ev_return), (GS1_AT + 14, ev_own),
        (INPUT_AT[2], lambda: pltpu.make_async_copy(ig, ig_hbm, ig_sem.at[0]).start()),
    ] + [(SMALL_AT + 2 * i, partial(ev_small, i)) for i in range(SMALL_STEPS + 1)]

    def tick(t, carry):
        for stage, run in reversed(list(enumerate(stages))):
            since = t - ENTER - LAG[stage]
            at = jnp.where(since < HELD, since, since - GAP)

            @pl.when((since >= 0) & ((since < HELD) | (since >= HELD + GAP)) & (at < CHUNKS))
            def _(run=run, at=at):
                run(at)

        by_group(t, copies)
        block, hit = pick(t, {when: j for j, when in enumerate(FFN_AT)})

        @pl.when(hit)
        def _():
            inner_event(block)

        by_table(t, through, through_event)
        by_table(t, weights, weight_event)
        by_group(t, others)

        @pl.when((t > GS1_AT) & (t < GS1_AT + 12))
        def _():
            at_ticks(t, GS1_AT + 1, 1, QUADS, ev_near)
            at_tick(t, GS1_AT + 3, ev_blend)
            at_tick(t, GS1_AT + 5, ev_owner)
            at_ticks(t, GS1_AT + 6, 1, NEWTON, lambda i: ev_newton(NEWTON - 1 - i))
            at_ticks(t, GS1_AT + 5, 1, 4, ev_conv)
            at_tick(t, GS1_AT + 8, ev_mixed)
            at_ticks(t, GS1_AT + 8, 1, QUADS, ev_far)
            at_tick(t, GS1_AT + 10, ev_values)

        @pl.when(t >= GS1_AT + 12)
        def _():
            at_ticks(t, TAPS_AT, 1, 4, ev_taps)
            by_group(t, last)

        return carry

    lax.fori_loop(0, CHUNKS + ENTER + GAP + LAG[-1], tick, 0)
    for i in range(SMALL_STEPS):
        small(i).wait_send()
    so_ref[...] = sb[SMALL_STEPS]
    pltpu.make_async_copy(ig, ig_hbm, ig_sem.at[0]).wait()
    for pair in range(PAIRS):

        @pl.when(me != owner_of(pair, n))
        def _(pair=pair):
            blend_copy(pair).wait_send()

    @pl.when(owner)
    def _():
        for t in range(n):

            @pl.when(me != t)
            def _(t=t):
                mixed_copy(t).wait_send()

    for d in range(1, n):
        target = lax.rem(me + d, n)
        to_seq(ret.at[target], rland.at[me], rets.at[d], retr.at[me], target).wait_send()


def tail(lens, big, little):
    slots, width = big[0].shape
    segs = lens.shape[1]
    at = CHUNKS
    n = SEQ_DEVICES
    dma = pltpu.SemaphoreType.DMA
    vm = lambda *dims: pltpu.VMEM(dims, f32)
    anywhere = pl.BlockSpec(memory_space=pl.ANY)
    one = dma((at,))
    zsem = dma((at, 2, 3))
    return pl.pallas_call(
        tail_kernel,
        in_specs=[smem()] + [anywhere] * len(big) + [whole()] * len(little),
        out_specs=[anywhere, whole(), anywhere],
        out_shape=[shape(2, at, STRIP // Z_ROWS, Z_ROWS, LANES), shape(SMALL_ROWS, LANES), shape(slots, width)],
        scratch_shapes=[
            vm(RING_ACC, STRIP, LANES), vm(RING_LC, STRIP, LANES), vm(RING_LC, 2, PART, LANES),
            vm(RING_MID, 4, 2, Z_ROWS, LANES), vm(RING_Z, 2, 3, 2, Z_ROWS, LANES), vm(RING_LC, 2, OWN, LANES),
            vm(RING_AG, 4, 2, Z_ROWS, LANES),
            vm(SMALL_STEPS + 1, SMALL_ROWS, LANES), vm(SMALL_STEPS, SMALL_ROWS, LANES), vm(GW_SLOTS * PAIRS, STRIP, LANES),
            vm(10, slots, width), vm(4, width, width), vm(slots + 40, width), vm(slots + 40, width),
            vm(CONV, 8, width), vm(40, LANES), vm(8, width), vm(8, width), vm(1, 4 * width),
            vm(PAIRS, DH, LANES), vm(2 * RIM, width), vm(DH, width), vm(DH, width), vm(2, DH, width),
            vm(n, DH, LANES), vm(PAIRS, MSG, LANES), vm(RIM, width), vm(RIM, width), vm(LANES, LANES), vm(LANES, LANES),
            vm(3 * LANES, LANES), vm(n, 2, segs, width), vm(n, 2, segs, width), vm(2, segs, width),
            dma((27,)), dma((1,)), dma((PAIRS,)), dma((n,)), dma((n,)), dma((n,)), dma((2,)), dma((2,)),
            dma((n,)), dma((n,)), dma((SMALL_STEPS,)), dma((SMALL_STEPS,)),
            one, one, one, one, one, zsem, one, one, one, zsem, one, dma((at, 2)), one, one,
        ],
        compiler_params=params(collective_id=5, has_side_effects=True),
        name="tail",
    )(lens, *big, *little)


def unstrip(strips):
    count, rows, _ = strips.shape
    return strips.transpose(1, 0, 2).reshape(rows, count * LANES)


def unstrip_tall(strips, across):
    count, rows, _ = strips.shape
    down = count // across
    return strips.reshape(down, across, rows, LANES).transpose(0, 2, 1, 3).reshape(down * rows, across * LANES)


PLACE_SLOTS = 24


def place_strips_kernel(s_ref, small_ref, *refs):
    outs = refs[:6]
    smalls = refs[6:-3]
    buf, in_sem, out_sem = refs[-3:]
    moves = []
    for e in range(CHUNKS // 3):
        if e < 8:
            out, row, col = outs[e % 2], (e // 2) * (1 - e % 2), (e // 2) * (e % 2)
        else:
            out, row, col = outs[e - 6], 0, 0
        for k in range(3):
            for c in range(2):
                rows = pl.ds(row * STRIP, STRIP)
                cols = pl.ds(col * STRIP + (2 * k + c) * LANES, LANES)
                slot = len(moves) % PLACE_SLOTS
                moves.append((
                    pltpu.make_async_copy(s_ref.at[c, 3 * e + k], buf.at[slot], in_sem.at[slot]),
                    pltpu.make_async_copy(buf.at[slot], out.at[rows, cols], out_sem.at[slot]),
                ))
    ahead = PLACE_SLOTS // 2
    for i in range(len(moves) + ahead):
        if i < len(moves):
            if i >= PLACE_SLOTS:
                moves[i - PLACE_SLOTS][1].wait()
            moves[i][0].start()
        if i >= ahead:
            moves[i - ahead][0].wait()
            moves[i - ahead][1].start()
    unpack_small(small_ref, smalls)
    for _, out in moves[-PLACE_SLOTS:]:
        out.wait()


def place_strips(summed, packed, shapes):
    anywhere = pl.BlockSpec(memory_space=pl.ANY)
    dma = pltpu.SemaphoreType.DMA
    width = shapes[0][1]
    return pl.pallas_call(
        place_strips_kernel,
        in_specs=[anywhere, whole()],
        out_specs=[anywhere] * len(shapes) + [whole()] * 10,
        out_shape=[shape(*dims) for dims in shapes] + [shape(width)] * 8 + [shape(shapes[0][0]), shape(HEADS, CONV)],
        scratch_shapes=[pltpu.VMEM((PLACE_SLOTS, STRIP, LANES), f32), dma((PLACE_SLOTS,)), dma((PLACE_SLOTS,))],
        compiler_params=params(),
        name="place_strips",
    )(summed, packed)


def per_device(
    tokens, segment_lens, query_weight, query_bias, key_weight, value_weight, value_bias, conv_taps,
    output_weight, output_bias, first_gain, first_bias, inner_weight, inner_bias, outer_weight, outer_bias,
    second_gain, second_bias, cotangent,
):
    n = lax.axis_size("seq")
    _, slots, width = tokens.shape
    x = tokens.reshape(slots, width)
    cot = cotangent.reshape(slots, width)
    lens = segment_lens

    q, k, v, raised, near, ctx, ext, h1, u1, tops, b, ql, kl, *saved, taps, inv1 = front(
        n, lens, x, conv_taps.T, query_bias, value_bias, output_bias, first_gain, first_bias,
        query_weight, key_weight, value_weight, output_weight,
    )
    pre, layer_out, gs2, small2 = ffn_forward(
        lens, h1, inner_weight, inner_bias.reshape(1, -1), outer_weight, outer_bias, cot, second_gain, second_bias
    )
    weights = [outer_weight, inner_weight, output_weight, value_weight, query_weight, key_weight]
    if n == SEQ_DEVICES and lax.axis_size("dp") == 4:
        big = [
            gs2, h1, u1, pre, outer_weight, inner_weight, output_weight, near, q, ctx, ext, k, v, raised, x,
            query_weight, key_weight, value_weight,
        ]
        little = [inv1, first_gain, tops, b, ql, kl, *saved, taps, small2]
        summed, packed, input_grad = tail(lens, big, little)
        sums = place_strips(summed.reshape(2, CHUNKS, STRIP, LANES), packed, [w.shape for w in weights])
    else:
        d_outer, d_inner, gs1, d_inner_bias, small1 = ffn_backward(
            h1, gs2, pre, inner_weight, outer_weight, u1, inv1, first_gain
        )
        gctx, gqn, gblend, gkl, grim = near_back(lens, gs1, output_weight, near, q, kl, b)
        c, gleft, gright, gl = blend_exchange(n, gblend, grim, ql, kl, saved)
        gkf, gvf, back = far_back(n, lens, k, v, raised, tops, b, c, ql, gkl, gl)
        own = land_return(n, back)
        gvc, gtaps, d_output = conv_back(lens, ext, gctx, gleft, gright, taps, ctx, gs1)
        input_grad, d_query, d_key, d_value, small0 = project_back(
            lens, x, gs1, gqn, gkf, gvc, gvf, own, query_weight, key_weight, value_weight
        )
        grads = [d_outer, d_inner, d_output, d_value, d_query, d_key]
        sums = sum_plain(grads + [small0, small1, small2, d_inner_bias, gtaps])
        small = sums[6:]
        sums = (
            [unstrip_tall(sums[0], width // LANES)] + [unstrip(s) for s in sums[1:6]]
            + [small[0][0], small[0][1], *small[1][:3], *small[2][:3], small[3][0], small[4][:CONV, :HEADS].T]
        )
    d_outer, d_inner, d_output, d_value, d_query, d_key, *vectors = sums
    d_query_bias, d_value_bias, d_first_gain, d_first_bias, d_output_bias = vectors[:5]
    d_second_gain, d_second_bias, d_outer_bias, d_inner_bias, d_taps = vectors[5:]
    return (
        layer_out.reshape(tokens.shape), input_grad.reshape(tokens.shape),
        d_query, d_query_bias, d_key, d_value, d_value_bias, d_taps.T,
        d_output, d_output_bias, d_first_gain, d_first_bias,
        d_inner, d_inner_bias, d_outer, d_outer_bias, d_second_gain, d_second_bias,
    )


def solution(mesh):
    block = P("dp", "seq", None)
    return jax.shard_map(
        per_device,
        mesh=mesh,
        in_specs=(block, P("dp", "seq")) + (P(),) * 16 + (block,),
        out_specs=(block, block) + (P(),) * 16,
        check_vma=False,
    )
```
